32 devices in a mesh: space: 8 (over z, x), orb: 4 (over y, core).
Axes of the slice: x: 2, y: 2, z: 4, core: 2. Of those that a mesh axis runs over, the one named last changes fastest.
Arguments:
- psi: bfloat16 [16, 48, 48, 512], P('space', None, None, 'orb'), may hold values from -6 to 6
- potential: float32 [16, 48, 48], P('space'), may hold values from 0 to 2
- beta: bfloat16 [8, 16, 48, 48], P(None, 'space'), may hold values from -0.21875 to 0.21875
- strength: float32 [8], replicated, may hold values from 0.5 to 4
- atom_slab: int32 [8], replicated, may hold values from 0 to 7, each once
- pattern: int32 [12, 2], replicated, may hold values from 0 to 3, as said below
- q_tiles: bfloat16 [12, 128, 128], replicated, may hold values from -0.3125 to 0.3125
Outputs:
- rotated: bfloat16 [16, 48, 48, 512], P('space', None, None, 'orb')
The draws below stay inside these ranges and needn't reach their ends.
Inputs may be any that keep to these rules, and one draw needn't show every extreme that they name: `pattern`: the 12 tile coordinates are distinct, each in 0 to 3, and every diagonal tile is among them.
All inputs are finite; a program needn't handle non-finite values.
Results may differ from the reference program's by a relative error of at most 0.0064.
Values may be sent and summed in bfloat16 or wider, within the bound.
No kernel may reach another device: no remote copies, remote signals or barrier semaphores. Data moves between devices by JAX's collectives and lax.ppermute only.
A program may use at most 64 MiB of HBM per device.

```python
import math
import jax
import jax.numpy as jnp
from jax import lax

ORBS = 512
TILE = 128
NNZ = 12
CZ = 2
NX = 48
NY = 48
P_SIZE = 8
NZ = 16


def draw_pattern(key, part):
    blocks = ORBS // TILE
    cells = blocks * blocks
    ids = jnp.arange(cells, dtype=jnp.int32)
    scores = jax.random.randint(key, (cells,), 0, 1000, dtype=jnp.int32) * cells + ids
    diagonal = ids // blocks == ids % blocks
    scores = jnp.where(diagonal, 1000 * cells + cells + ids, scores)
    chosen = lax_top(scores)
    return jnp.stack([chosen // blocks, chosen % blocks], axis=1).astype(jnp.int32)


def lax_top(scores):
    values, indices = jax.lax.top_k(scores, NNZ)
    return indices.astype(jnp.int32)


def shard_levels(rng, shape, cuts, least, largest):
    def one(position, parts):
        heights = jax.random.uniform(jax.random.fold_in(jax.random.fold_in(rng, 6), position), (parts,), jnp.float32, least / len(cuts), largest / len(cuts))
        return jnp.repeat(jnp.exp(heights), shape[position] // parts).reshape((-1,) + (1,) * (len(shape) - position - 1))

    factor_of = one(*cuts[0])
    for cut in cuts[1:]:
        factor_of = factor_of * one(*cut)
    return factor_of


def noise(rng, extent, deviation, bound, split=(), kind=jnp.bfloat16):
    drawn = deviation * jax.random.normal(rng, extent, jnp.float32)
    if split:
        drawn = drawn * shard_levels(rng, extent, split, -0.22, 0.18)
    return jnp.clip(drawn, -bound, bound).astype(kind)


def setup_inputs(seed: int = 0) -> dict:
    splits = jax.random.split(jax.random.key(seed), 8)
    return {
        "psi": noise(splits[0], (NZ, NX, NY, ORBS), 1.0, 6.0, ((0, 8), (3, 4))),
        "potential": jnp.clip(2.0 * jax.random.uniform(splits[1], (NZ, NX, NY), jnp.float32) ** shard_levels(splits[1], (NZ, NX, NY), ((0, 8),), -0.2, 0.2), 0.0, 2.0),
        "beta": noise(splits[2], (P_SIZE, NZ, NX, NY), (16 * NX) ** -0.5, 0.21875, ((1, 8),)),
        "strength": jnp.clip(jnp.exp(jax.random.uniform(splits[3], (P_SIZE,), jnp.float32, math.log(0.5), math.log(4.0))), 0.5, 4.0),
        "atom_slab": jax.random.permutation(splits[4], P_SIZE).astype(jnp.int32),
        "pattern": draw_pattern(jax.random.fold_in(splits[7], 71), 0),
        "q_tiles": noise(splits[6], (NNZ, TILE, TILE), (3 * TILE) ** -0.5, 0.3125),
    }


def filter_block(v, potential, beta_m, strength):
    f = v.astype(jnp.float32)
    pz = jnp.pad(f, ((1, 1), (0, 0), (0, 0), (0, 0)))
    pxy = jnp.pad(f, ((0, 0), (1, 1), (1, 1), (0, 0)))
    beside = pz[2:] + pz[:-2]
    beside = beside + pxy[:, 2:, 1:-1] + pxy[:, :-2, 1:-1] + pxy[:, 1:-1, 2:] + pxy[:, 1:-1, :-2]
    kinetic = -0.5 * (beside - 6.0 * f)
    count = f.shape[0] * f.shape[1] * f.shape[2]
    flat_v = v.reshape(count, v.shape[3])
    flat_b = beta_m.reshape(beta_m.shape[0], count)
    proj = jnp.dot(flat_b, flat_v, preferred_element_type=jnp.float32)
    coef = (strength[:, None] * proj).astype(jnp.bfloat16)
    nonlocal_term = lax.dot_general(flat_b, coef, (((0,), (0,)), ((), ())), preferred_element_type=jnp.float32)
    total = kinetic + potential[..., None] * f + nonlocal_term.reshape(f.shape)
    return ((total - 4.0 * f) / 4.0).astype(jnp.bfloat16)


def reference(psi, potential, beta, strength, atom_slab, pattern, q_tiles):
    slab = (jnp.arange(NZ) // CZ).astype(jnp.int32)
    mask = jnp.abs(slab[None, :] - atom_slab[:, None]) <= 1
    beta_m = jnp.where(mask[:, :, None, None], beta, jnp.zeros_like(beta))
    blocks = ORBS // TILE
    stacked = jnp.moveaxis(psi.reshape(NZ, NX, NY, blocks, TILE), 3, 0)

    def twice(v):
        one = filter_block(v, potential, beta_m, strength)
        return filter_block(one, potential, beta_m, strength)

    filtered = lax.map(twice, stacked)
    filtered = jnp.moveaxis(filtered, 0, 3).reshape(NZ * NX * NY, ORBS)
    ids = jnp.arange(blocks, dtype=jnp.int32)
    rows_hot = (pattern[:, 0][:, None] == ids[None, :]).astype(jnp.float32)
    cols_hot = (pattern[:, 1][:, None] == ids[None, :]).astype(jnp.float32)
    dense = jnp.einsum("ki,kj,kab->iajb", rows_hot, cols_hot, q_tiles.astype(jnp.float32))
    dense = dense.reshape(ORBS, ORBS).astype(jnp.bfloat16)
    out = jnp.dot(filtered, dense, preferred_element_type=jnp.float32).astype(jnp.bfloat16)
    return out.reshape(NZ, NX, NY, ORBS)
```

```python
import functools

import jax
import jax.numpy as jnp
from jax import lax
from jax.experimental import pallas as pl
from jax.experimental.pallas import tpu as pltpu
from jax.sharding import PartitionSpec as P

F32 = jnp.float32
BF16 = jnp.bfloat16
VMEM_LIMIT = 50 * 1024 * 1024


def params():
    return pltpu.CompilerParams(vmem_limit_bytes=VMEM_LIMIT)


def cost(flops, moved):
    return pl.CostEstimate(flops=flops, bytes_accessed=moved, transcendentals=0)


def inside(w, window):
    return jnp.logical_and(w >= 0, w < window).astype(F32)


def tridiagonal(n):
    i = lax.broadcasted_iota(jnp.int32, (n, n), 0)
    j = lax.broadcasted_iota(jnp.int32, (n, n), 1)
    return jnp.where(jnp.abs(i - j) == 1, -0.125, 0.0).astype(BF16)


def partial_kernel(count, own, xr, f_own, f_x, f_zo, f_zf, out, acc, gram):
    x = lax.rem(lax.axis_index("space"), 2)
    half = own.shape[1] // 2
    window = xr.shape[1]
    width = own.shape[2]
    depth = f_own.shape[2]
    base = (half - 2) * x
    tri = tridiagonal(width)
    acc[...] = jnp.zeros_like(acc)
    gram[...] = jnp.zeros_like(gram)

    def field(c, w):
        if c == 1:
            return f_zf[0, w]
        if c == 6:
            return f_zo[0, w]
        plane = (c % 2) ^ x
        if c in (2, 3):
            return f_own[plane, base + w]
        return f_x[plane, w]

    def values(c, w):
        plane = (c % 2) ^ x
        return own[plane, base + w] if c in (2, 3) else xr[plane, w]

    def row(j, carry):
        w = 2 * x + j
        below, above = jnp.maximum(w - 1, 0), jnp.minimum(w + 1, window - 1)
        has_below, has_above = inside(w - 1, window), inside(w + 1, window)
        total, square = acc[...], gram[...]
        for c in (2, 3, 4, 5):
            b = field(c, w)
            b32 = b.astype(F32)
            beside = (
                field(c, below).astype(F32) * has_below
                + field(c, above).astype(F32) * has_above
                + field(c - 1, w).astype(F32)
                + field(c + 1, w).astype(F32)
            )
            u = b32[count : count + 1] + b32[count + 1 : count + 2]
            local = jnp.dot(b, tri, preferred_element_type=F32) - 0.125 * beside + u * b32
            hi = local.astype(BF16)
            lo = (local - hi.astype(F32)).astype(BF16)
            weights = jnp.concatenate([b, hi, lo], axis=0)
            total = total + jnp.dot(weights, values(c, w), preferred_element_type=F32)
            square = square + lax.dot_general(
                b, b, (((1,), (1,)), ((), ())), preferred_element_type=F32
            )
        acc[...] = total
        gram[...] = square
        return carry

    lax.fori_loop(0, half, row, 0)
    out[...] = jnp.zeros_like(out)
    out[0:count] = acc[0:count]
    out[count : 2 * count] = acc[depth : depth + count] + acc[2 * depth : 2 * depth + count]
    out[2 * count : 3 * count, 0:count] = gram[0:count, 0:count]


def partials(count, own, xr, f_own, f_x, f_zo, f_zf):
    orbs = own.shape[3]
    depth = f_own.shape[2]
    cells = 4 * (own.shape[1] // 2) * own.shape[2]
    return pl.pallas_call(
        functools.partial(partial_kernel, count),
        out_shape=jax.ShapeDtypeStruct((3 * count, orbs), F32),
        in_specs=[pl.BlockSpec(memory_space=pltpu.VMEM)] * 6,
        out_specs=pl.BlockSpec(memory_space=pltpu.VMEM),
        scratch_shapes=[pltpu.VMEM((3 * depth, orbs), F32), pltpu.VMEM((depth, depth), F32)],
        compiler_params=params(),
        cost_estimate=cost(2 * cells * 3 * depth * orbs, cells * orbs * 4),
        name="partials",
    )(own, xr, f_own, f_x, f_zo, f_zf)


def filter_kernel(count, slabs, start, own, xr, zo, zf, f_own, f_x, f_zo, f_zf, sums, strength, o_x, o_own, first):
    place = lax.axis_index("space")
    x = lax.rem(place, 2)
    half = own.shape[1] // 2
    window = xr.shape[1]
    width = own.shape[2]
    orbs = own.shape[3]
    depth = f_own.shape[2]
    rows = o_own.shape[1]
    base = (half - 2) * x
    lower = (place >= 2).astype(F32)
    upper = (place < slabs - 2).astype(F32)
    is_odd = x.astype(F32)
    has_zf = lower * (1.0 - is_odd) + upper * is_odd
    has_zo = upper * (1.0 - is_odd) + lower * is_odd

    coef1 = (strength[...] * sums[0:count]).astype(BF16).astype(F32) * 0.25
    gram = sums[2 * count : 3 * count]
    padded = coef1
    if orbs > count:
        padded = jnp.concatenate([coef1, jnp.zeros((orbs - count, orbs), F32)], axis=0)
    proj2 = sums[count : 2 * count] + jnp.dot(
        gram, padded, preferred_element_type=F32, precision=lax.Precision.HIGHEST
    )
    coef2 = (strength[...] * proj2).astype(BF16).astype(F32) * 0.25
    k = lax.broadcasted_iota(jnp.int32, (depth, orbs), 0)
    ones = jnp.where(jnp.logical_or(k == count, k == count + 1), 1.0, 0.0)

    def right(coef):
        rest = jnp.zeros((depth - count, orbs), F32)
        return jnp.concatenate([jnp.concatenate([coef, rest], axis=0), ones], axis=1).astype(BF16)

    right1, right2 = right(coef1), right(coef2)
    line = lax.broadcasted_iota(jnp.int32, (width, orbs), 0)
    not_first = (line > 0).astype(F32)
    not_last = (line < width - 1).astype(F32)

    def field(c, w):
        if c == 1:
            return f_zf[0, w]
        if c == 6:
            return f_zo[0, w]
        plane = (c % 2) ^ x
        if c in (2, 3):
            return f_own[plane, base + w]
        return f_x[plane, w]

    def values(c, w):
        plane = (c % 2) ^ x
        if c in (2, 3):
            return own[plane, base + w].astype(F32)
        ref = {0: zf, 1: xr, 2: zo}[0 if c < 2 else (1 if c < 6 else 2)]
        return ref[plane, w].astype(F32)

    def applied(v, xs, zs, fields, right_side):
        along = pltpu.roll(v, 1, 0) * not_first + pltpu.roll(v, width - 1, 0) * not_last
        both = lax.dot_general(
            fields, right_side, (((0,), (0,)), ((), ())), preferred_element_type=F32
        )
        return both[:, :orbs] + both[:, orbs:] * v - 0.125 * (along + xs + zs)

    def step1(j, carry):
        w = start + 2 * x + j - 1
        here = jnp.clip(w, 0, window - 1)
        below, above = jnp.maximum(here - 1, 0), jnp.minimum(here + 1, window - 1)
        has_below, has_above = inside(w - 1, window), inside(w + 1, window)
        valid = inside(w, window)
        vs = [values(c, here) for c in range(8)]
        for c in range(1, 7):
            xs = values(c, below) * has_below + values(c, above) * has_above
            f = applied(vs[c], xs, vs[c - 1] + vs[c + 1], field(c, here), right1)
            keep = valid
            if c == 1:
                keep = valid * has_zf
            if c == 6:
                keep = valid * has_zo
            first[c - 1, j] = (f * keep).astype(BF16)
        return carry

    lax.fori_loop(0, rows + 2, step1, 0)

    def step2(j, carry):
        w = start + 2 * x + j
        vs = [first[c - 1, j + 1].astype(F32) for c in range(1, 7)]
        for c in range(2, 6):
            xs = first[c - 1, j].astype(F32) + first[c - 1, j + 2].astype(F32)
            f = applied(vs[c - 1], xs, vs[c - 2] + vs[c], field(c, w), right2)
            out = o_own if c in (2, 3) else o_x
            out[(c % 2) ^ x, j] = f.astype(BF16)
        return carry

    lax.fori_loop(0, rows, step2, 0)


def filtered(count, slabs, start, rows, *operands):
    own = operands[0]
    planes, _, width, orbs = own.shape
    out = jax.ShapeDtypeStruct((planes, rows, width, orbs), BF16)
    cells = 10 * rows * width
    return pl.pallas_call(
        functools.partial(filter_kernel, count, slabs, start),
        out_shape=(out, out),
        in_specs=[pl.BlockSpec(memory_space=pltpu.VMEM)] * len(operands),
        out_specs=(pl.BlockSpec(memory_space=pltpu.VMEM),) * 2,
        scratch_shapes=[pltpu.VMEM((6, rows + 2, width, orbs), BF16)],
        compiler_params=params(),
        cost_estimate=cost(2 * cells * 32 * orbs, cells * orbs * 4),
        name="filtered",
    )(*operands)


def rotate_kernel(a, b, c, d, q, out):
    planes, rows, width, orbs = a.shape

    def one(j, carry):
        for plane in range(planes):
            total = jnp.dot(a[plane, j], q[0], preferred_element_type=F32)
            for k, ref in ((1, b), (2, c), (3, d)):
                total = total + jnp.dot(ref[plane, j], q[k], preferred_element_type=F32)
            out[plane, j] = total.astype(BF16)
        return carry

    lax.fori_loop(0, rows, one, 0)


def rotated(blocks, q):
    a = blocks[0]
    size = a.size
    return pl.pallas_call(
        rotate_kernel,
        out_shape=jax.ShapeDtypeStruct(a.shape, BF16),
        in_specs=[pl.BlockSpec(memory_space=pltpu.VMEM)] * 5,
        out_specs=pl.BlockSpec(memory_space=pltpu.VMEM),
        compiler_params=params(),
        cost_estimate=cost(8 * size * a.shape[3], 10 * size),
        name="rotated",
    )(*blocks, q)


def assemble_kernel(half, *refs):
    out = refs[-1]
    pieces = (len(refs) - 1) // 2
    x = lax.rem(lax.axis_index("space"), 2)
    rows = refs[0].shape[1]
    for k in range(pieces):
        out[:, pl.ds(half * x + rows * k, rows)] = refs[k][...]
        out[:, pl.ds(half * (1 - x) + rows * k, rows)] = refs[pieces + k][...]


def assembled(shape, mine, theirs):
    return pl.pallas_call(
        functools.partial(assemble_kernel, shape[1] // 2),
        out_shape=jax.ShapeDtypeStruct(shape, BF16),
        in_specs=[pl.BlockSpec(memory_space=pltpu.VMEM)] * (len(mine) + len(theirs)),
        out_specs=pl.BlockSpec(memory_space=pltpu.VMEM),
        compiler_params=params(),
        name="assembled",
    )(*mine, *theirs)


def shards(psi, potential, beta, strength, atom_slab, pattern, q_tiles):
    planes, width_x, width_y, orbs = psi.shape
    count = beta.shape[0]
    slabs = lax.axis_size("space")
    place = lax.axis_index("space")
    x = lax.rem(place, 2)
    half = width_x // 2
    window = half + 2
    swap = [(i, i ^ 1) for i in range(slabs)]
    own_way = [(i, i + 2 if i % 2 else i - 2) for i in range(slabs)]
    own_way = [(i, j) for i, j in own_way if 0 <= j < slabs]
    other_way = [(i, i - 2 if i % 2 else i + 2) for i in range(slabs)]
    other_way = [(i, j) for i, j in other_way if 0 <= j < slabs]
    groups = lax.axis_size("orb")
    across = [(i, i ^ 2) for i in range(groups)]
    beside = [(i, i ^ 1) for i in range(groups)]

    mine = (half - 2) * x
    theirs = (half - 2) * (1 - x)
    to_x = lax.dynamic_slice_in_dim(psi, theirs, window, axis=1)
    xr = lax.ppermute(to_x, "space", swap)
    zo = lax.ppermute(lax.dynamic_slice_in_dim(psi, mine, window, axis=1), "space", own_way)
    zf = lax.ppermute(xr, "space", other_way)

    active = jnp.abs(place - atom_slab) <= 1
    beta_m = jnp.where(active[:, None, None, None], beta, jnp.zeros_like(beta))
    depth = -(-(count + 2) // 16) * 16
    u = (potential - 1.0) * 0.25
    hi = lax.reduce_precision(u, 8, 7)
    lo = u - hi
    fields = jnp.concatenate(
        [
            jnp.transpose(beta_m, (1, 2, 0, 3)),
            hi[:, :, None, :].astype(BF16),
            lo[:, :, None, :].astype(BF16),
            jnp.zeros((planes, width_x, depth - count - 2, width_y), BF16),
        ],
        axis=2,
    )
    f_x = lax.ppermute(lax.dynamic_slice_in_dim(fields, theirs, window, axis=1), "space", swap)
    near = lax.dynamic_slice_in_dim(fields, x, 1, axis=0)
    f_zo = lax.ppermute(lax.dynamic_slice_in_dim(near, mine, window, axis=1), "space", own_way)
    f_zf = lax.ppermute(lax.dynamic_slice_in_dim(f_x, 1 - x, 1, axis=0), "space", other_way)

    sums = partials(count, psi, xr, fields, f_x, f_zo, f_zf)
    step = 1
    while step < slabs:
        sums = sums + lax.ppermute(sums, "space", [(i, i ^ step) for i in range(slabs)])
        step *= 2
    strong = jnp.broadcast_to(strength[:, None], (count, orbs))

    me = lax.axis_index("orb")
    which = jnp.bitwise_xor(me, jnp.arange(groups, dtype=jnp.int32))
    rows_hot = (pattern[:, 0][:, None] == which[None, :]).astype(BF16)
    rows_hot = rows_hot * (pattern[:, 1] == me).astype(BF16)[:, None]
    q = jnp.einsum("ki,kab->iab", rows_hot, q_tiles, preferred_element_type=F32).astype(BF16)

    pieces = 2
    rows = half // pieces
    kept, given = [], []
    for piece in range(pieces):
        for_x, for_me = filtered(
            count, slabs, piece * rows, rows, psi, xr, zo, zf, fields, f_x, f_zo, f_zf, sums, strong
        )
        for block, to in ((for_x, given), (for_me, kept)):
            c = lax.ppermute(block, "orb", beside)
            y = lax.ppermute(block, "orb", across)
            yc = lax.ppermute(y, "orb", beside)
            to.append(rotated((block, c, y, yc), q))
    got = [lax.ppermute(block, "space", swap) for block in given]
    return assembled(psi.shape, kept, got)


def solution(mesh):
    placed = (
        P("space", None, None, "orb"),
        P("space", None, None),
        P(None, "space", None, None),
        P(),
        P(),
        P(),
        P(),
    )
    return jax.shard_map(
        shards, mesh=mesh, in_specs=placed, out_specs=P("space", None, None, "orb"), check_vma=False
    )
```

```python
import functools

import jax
import jax.numpy as jnp
from jax import lax
from jax.experimental import pallas as pl
from jax.experimental.pallas import tpu as pltpu
from jax.sharding import PartitionSpec as P

F32 = jnp.float32
BF16 = jnp.bfloat16
VMEM_LIMIT = 50 * 1024 * 1024


def params():
    return pltpu.CompilerParams(vmem_limit_bytes=VMEM_LIMIT)


def cost(flops, moved):
    return pl.CostEstimate(flops=flops, bytes_accessed=moved, transcendentals=0)


def inside(p, window):
    return jnp.logical_and(p >= 0, p < window).astype(F32)


def pair_matrices(width):
    n = 2 * width
    i = lax.broadcasted_iota(jnp.int32, (n, n), 0)
    j = lax.broadcasted_iota(jnp.int32, (n, n), 1)
    same = (i < width) == (j < width)
    along = jnp.logical_and(jnp.abs(i - j) == 1, same)
    here = jnp.where(jnp.logical_or(along, jnp.abs(i - j) == width), -0.125, 0.0)
    before = jnp.where(i == j + width, -0.125, 0.0)
    after = jnp.where(i == j - width, -0.125, 0.0)
    return here.astype(BF16), before.astype(BF16), after.astype(BF16)


def partial_kernel(count, own, f_own, f_x, f_d, out, acc, gram):
    x = lax.rem(lax.axis_index("space"), 2)
    _, pairs, depth, cells = f_own.shape
    orbs = own.shape[3]
    here, before, after = pair_matrices(cells // 2)
    acc[...] = jnp.zeros_like(acc)
    gram[...] = jnp.zeros_like(gram)

    def row(r, carry):
        low, high = jnp.maximum(r - 1, 0), jnp.minimum(r + 1, pairs - 1)
        has_low, has_high = inside(r - 1, pairs), inside(r + 1, pairs)
        tiles = [f_d[r], f_own[x, r], f_own[1 - x, r], f_x[r]]
        total, square = acc[...], gram[...]
        for c in (1, 2):
            plane = x if c == 1 else 1 - x
            b = tiles[c]
            b32 = b.astype(F32)
            u = b32[count : count + 1] + b32[count + 1 : count + 2]
            local = jnp.dot(b, here, preferred_element_type=F32)
            local += has_low * jnp.dot(f_own[plane, low], before, preferred_element_type=F32)
            local += has_high * jnp.dot(f_own[plane, high], after, preferred_element_type=F32)
            local += u * b32 - 0.125 * (tiles[c - 1].astype(F32) + tiles[c + 1].astype(F32))
            hi = local.astype(BF16)
            lo = (local - hi.astype(F32)).astype(BF16)
            weights = jnp.concatenate([b, hi, lo], axis=0)
            v = own[plane, pl.ds(2 * r, 2)].reshape(cells, orbs)
            total = total + jnp.dot(weights, v, preferred_element_type=F32)
            square = square + lax.dot_general(
                b, b, (((1,), (1,)), ((), ())), preferred_element_type=F32
            )
        acc[...] = total
        gram[...] = square
        return carry

    lax.fori_loop(0, pairs, row, 0)
    out[...] = jnp.zeros_like(out)
    out[0:count] = acc[0:count]
    out[count : 2 * count] = acc[depth : depth + count] + acc[2 * depth : 2 * depth + count]
    out[2 * count : 3 * count, 0:count] = gram[0:count, 0:count]


def partials(count, own, f_own, f_x, f_d):
    orbs = own.shape[3]
    depth = f_own.shape[2]
    cells = own.size // orbs
    return pl.pallas_call(
        functools.partial(partial_kernel, count),
        out_shape=jax.ShapeDtypeStruct((3 * count, orbs), F32),
        in_specs=[pl.BlockSpec(memory_space=pltpu.VMEM)] * 4,
        out_specs=pl.BlockSpec(memory_space=pltpu.VMEM),
        scratch_shapes=[pltpu.VMEM((3 * depth, orbs), F32), pltpu.VMEM((depth, depth), F32)],
        compiler_params=params(),
        cost_estimate=cost(2 * cells * 3 * depth * orbs, cells * orbs * 4),
        name="partials",
    )(own, f_own, f_x, f_d)


def filter_kernel(count, slabs, start, parts, joint, *refs):
    own, f_own, f_x, f_d, f_zo, sums, strength, zo = refs[:8]
    xrs, zfs = refs[8 : 8 + parts], refs[8 + parts : 8 + 2 * parts]
    outs, scratch = refs[8 + 2 * parts : -3 if parts > 1 else -1], refs[-3 if parts > 1 else -1 :]
    first = scratch[0]
    place = lax.axis_index("space")
    x = lax.rem(place, 2)
    _, pairs, depth, cells = f_own.shape
    width = cells // 2
    half = own.shape[1] // 2
    orbs = own.shape[3]
    rows = outs[0].shape[1]
    base = (half - 2) * x
    lower = (place >= 2).astype(F32)
    upper = (place < slabs - 2).astype(F32)
    is_odd = x.astype(F32)
    has_zf = lower * (1.0 - is_odd) + upper * is_odd
    has_zo = upper * (1.0 - is_odd) + lower * is_odd
    if parts > 1:
        xr, zf = scratch[1], scratch[2]
        for target, pieces in ((xr, xrs), (zf, zfs)):
            at = 0
            for piece in pieces:
                target[:, at : at + piece.shape[1]] = piece[...]
                at += piece.shape[1]
        window = at // 2
    else:
        xr, zf = xrs[0], zfs[0]
        window = xr.shape[1] // 2

    coef1 = (strength[...] * sums[0:count]).astype(BF16).astype(F32) * 0.25
    gram = sums[2 * count : 3 * count]
    padded = coef1
    if orbs > count:
        padded = jnp.concatenate([coef1, jnp.zeros((orbs - count, orbs), F32)], axis=0)
    proj2 = sums[count : 2 * count] + jnp.dot(
        gram, padded, preferred_element_type=F32, precision=lax.Precision.HIGHEST
    )
    coef2 = (strength[...] * proj2).astype(BF16).astype(F32) * 0.25
    k = lax.broadcasted_iota(jnp.int32, (depth, orbs), 0)
    ones = jnp.where(jnp.logical_or(k == count, k == count + 1), 1.0, 0.0)

    def right(coef):
        rest = jnp.zeros((depth - count, orbs), F32)
        return jnp.concatenate([jnp.concatenate([coef, rest], axis=0), ones], axis=1).astype(BF16)

    right1, right2 = right(coef1), right(coef2)
    here, _, _ = pair_matrices(width)

    def field(c, p):
        if c == 1:
            return f_d[base // 2 + p]
        if c in (2, 3):
            return f_own[(c % 2) ^ x, base // 2 + p]
        if c == 4:
            return f_x[base // 2 + p]
        if c == 5:
            return f_x[pairs + p]
        return f_zo[p]

    def rows_of(c, w, n):
        plane = (c % 2) ^ x
        if c in (2, 3):
            return own[plane, pl.ds(base + w, n)]
        ref = zf if c < 2 else (xr if c < 6 else zo)
        return ref[plane, pl.ds(w, n)]

    def applied(pair, v, outer, zs, fields, right_side):
        both = lax.dot_general(
            fields, right_side, (((0,), (0,)), ((), ())), preferred_element_type=F32
        )
        near = jnp.dot(here, pair, preferred_element_type=F32)
        return both[:, :orbs] + near + both[:, orbs:] * v - 0.125 * (outer + zs)

    def step1(j, carry):
        p = start // 2 + x + j - 1
        q = jnp.clip(p, 0, window - 1)
        has_below = inside(p - 1, window)
        has_above = inside(p + 1, window)
        valid = inside(p, window)
        below = jnp.maximum(2 * q - 1, 0)
        above = jnp.minimum(2 * q + 2, 2 * window - 1)
        pair = [rows_of(c, 2 * q, 2).reshape(cells, orbs) for c in range(8)]
        vs = [v.astype(F32) for v in pair]
        for c in range(1, 7):
            outer = jnp.concatenate(
                [
                    rows_of(c, below, 1)[0].astype(F32) * has_below,
                    rows_of(c, above, 1)[0].astype(F32) * has_above,
                ],
                axis=0,
            )
            f = applied(pair[c], vs[c], outer, vs[c - 1] + vs[c + 1], field(c, q), right1)
            keep = valid
            if c == 1:
                keep = valid * has_zf
            if c == 6:
                keep = valid * has_zo
            first[c - 1, pl.ds(2 * j, 2)] = (f * keep).astype(BF16).reshape(2, width, orbs)
        return carry

    lax.fori_loop(0, rows // 2 + 2, step1, 0)

    def step2(j, carry):
        p = start // 2 + x + j
        pair = [first[c - 1, pl.ds(2 * j + 2, 2)].reshape(cells, orbs) for c in range(1, 7)]
        vs = [v.astype(F32) for v in pair]
        for c in range(2, 6):
            outer = jnp.concatenate(
                [first[c - 1, 2 * j + 1].astype(F32), first[c - 1, 2 * j + 4].astype(F32)], axis=0
            )
            f = applied(
                pair[c - 1], vs[c - 1], outer, vs[c - 2] + vs[c], field(c, p), right2
            )
            f = f.astype(BF16).reshape(2, width, orbs)
            plane = (c % 2) ^ x
            if joint:
                outs[0][plane + (2 if c in (2, 3) else 0), pl.ds(2 * j, 2)] = f
            else:
                outs[1 if c in (2, 3) else 0][plane, pl.ds(2 * j, 2)] = f
        return carry

    lax.fori_loop(0, rows // 2, step2, 0)


def filtered(count, slabs, start, rows, joint, operands, xrs, zfs):
    own = operands[0]
    planes, _, width, orbs = own.shape
    parts = len(xrs)
    shape = (2 * planes if joint else planes, rows, width, orbs)
    out = (jax.ShapeDtypeStruct(shape, BF16),) * (1 if joint else 2)
    cells = 10 * rows * width
    scratch = [pltpu.VMEM((6, rows + 4, width, orbs), BF16)]
    if parts > 1:
        window = sum(piece.shape[1] for piece in xrs)
        scratch += [pltpu.VMEM((planes, window, width, orbs), BF16)] * 2
    return pl.pallas_call(
        functools.partial(filter_kernel, count, slabs, start, parts, joint),
        out_shape=out,
        in_specs=[pl.BlockSpec(memory_space=pltpu.VMEM)] * (len(operands) + 2 * parts),
        out_specs=(pl.BlockSpec(memory_space=pltpu.VMEM),) * len(out),
        scratch_shapes=scratch,
        compiler_params=params(),
        cost_estimate=cost(2 * cells * 32 * orbs, cells * orbs * 4),
        name="filtered",
    )(*operands, *xrs, *zfs)


def rotate_kernel(group, *refs):
    a, b, c, d, q = refs[:5]
    outs = refs[5:]
    _, rows, width, orbs = a.shape
    planes = outs[0].shape[0]
    low = jnp.concatenate([q[0], q[1]], axis=0)
    high = jnp.concatenate([q[2], q[3]], axis=0)

    def one(j, carry):
        for plane in range(a.shape[0]):
            def take(ref):
                return ref[plane, pl.ds(group * j, group)].reshape(group * width, orbs)

            total = jnp.dot(
                jnp.concatenate([take(a), take(b)], axis=1), low, preferred_element_type=F32
            )
            total = total + jnp.dot(
                jnp.concatenate([take(c), take(d)], axis=1), high, preferred_element_type=F32
            )
            outs[plane // planes][plane % planes, pl.ds(group * j, group)] = total.astype(
                BF16
            ).reshape(group, width, orbs)
        return carry

    lax.fori_loop(0, rows // group, one, 0)


def rotated(blocks, q, pieces):
    a = blocks[0]
    size = a.size
    group = max(g for g in range(1, 7) if a.shape[1] % g == 0)
    out = jax.ShapeDtypeStruct((a.shape[0] // pieces, *a.shape[1:]), BF16)
    return pl.pallas_call(
        functools.partial(rotate_kernel, group),
        out_shape=(out,) * pieces,
        in_specs=[pl.BlockSpec(memory_space=pltpu.VMEM)] * 5,
        out_specs=(pl.BlockSpec(memory_space=pltpu.VMEM),) * pieces,
        compiler_params=params(),
        cost_estimate=cost(8 * size * a.shape[3], 10 * size),
        name="rotated",
    )(*blocks, q)


def assemble_kernel(half, *refs):
    out = refs[-1]
    pieces = (len(refs) - 1) // 2
    x = lax.rem(lax.axis_index("space"), 2)
    rows = refs[0].shape[1]
    for k in range(pieces):
        out[:, pl.ds(half * x + rows * k, rows)] = refs[k][...]
        out[:, pl.ds(half * (1 - x) + rows * k, rows)] = refs[pieces + k][...]


def assembled(shape, mine, theirs):
    return pl.pallas_call(
        functools.partial(assemble_kernel, shape[1] // 2),
        out_shape=jax.ShapeDtypeStruct(shape, BF16),
        in_specs=[pl.BlockSpec(memory_space=pltpu.VMEM)] * (len(mine) + len(theirs)),
        out_specs=pl.BlockSpec(memory_space=pltpu.VMEM),
        compiler_params=params(),
        name="assembled",
    )(*mine, *theirs)


def ordered(*arrays):
    return lax.optimization_barrier(arrays)


def shards(psi, potential, beta, strength, atom_slab, pattern, q_tiles):
    planes, width_x, width_y, orbs = psi.shape
    count = beta.shape[0]
    slabs = lax.axis_size("space")
    place = lax.axis_index("space")
    x = lax.rem(place, 2)
    half = width_x // 2
    window = half + 2
    rows = half // 2
    early = rows + 4

    def within(pairs):
        return [(i, j) for i, j in pairs if 0 <= j < slabs]

    swap = [(i, i ^ 1) for i in range(slabs)]
    own_way = within([(i, i + 2 if i % 2 else i - 2) for i in range(slabs)])
    other_way = within([(i, i - 2 if i % 2 else i + 2) for i in range(slabs)])
    raster = within([(i, i + 1 if i % 2 else i - 1) for i in range(slabs)])
    groups = lax.axis_size("orb")
    across = [(i, i ^ 2) for i in range(groups)]
    beside = [(i, i ^ 1) for i in range(groups)]
    mine = (half - 2) * x
    theirs = (half - 2) * (1 - x)

    active = jnp.abs(place - atom_slab) <= 1
    beta_m = jnp.where(active[:, None, None, None], beta, jnp.zeros_like(beta))
    depth = -(-(count + 2) // 16) * 16
    u = (potential - 1.0) * 0.25
    hi = lax.reduce_precision(u, 8, 7)
    lo = u - hi
    fields = jnp.concatenate(
        [
            jnp.transpose(beta_m, (1, 2, 0, 3)),
            hi[:, :, None, :].astype(BF16),
            lo[:, :, None, :].astype(BF16),
            jnp.zeros((planes, width_x, depth - count - 2, width_y), BF16),
        ],
        axis=2,
    )
    fields = jnp.concatenate([fields[:, 0::2], fields[:, 1::2]], axis=3)
    far = lax.dynamic_index_in_dim(fields, x, 0, keepdims=False)
    near = lax.dynamic_index_in_dim(fields, 1 - x, 0, keepdims=False)
    to_x = jnp.concatenate(
        [near, lax.dynamic_slice_in_dim(far, theirs // 2, window // 2, axis=0)], axis=0
    )
    to_zo = lax.dynamic_slice_in_dim(far, mine // 2, window // 2, axis=0)
    to_x, far, to_zo, psi_in = ordered(to_x, far, to_zo, psi)
    f_x = lax.ppermute(to_x, "space", swap)
    f_d = lax.ppermute(far, "space", raster)
    f_zo = lax.ppermute(to_zo, "space", own_way)

    xr1 = lax.ppermute(
        lax.dynamic_slice_in_dim(psi_in, theirs, early, axis=1), "space", swap
    )
    zo = lax.ppermute(lax.dynamic_slice_in_dim(psi_in, mine, window, axis=1), "space", own_way)
    sums = partials(count, psi, fields, f_x, f_d)
    xr1, sums = ordered(xr1, sums)
    zf1 = lax.ppermute(xr1, "space", other_way)
    second = lax.dynamic_slice_in_dim(psi, theirs + early, window - early, axis=1)
    second, _ = ordered(second, xr1)
    xr2 = lax.ppermute(second, "space", swap)
    step = 1
    while step < slabs:
        sums = sums + lax.ppermute(sums, "space", [(i, i ^ step) for i in range(slabs)])
        step *= 2
    zf1, xr2 = ordered(zf1, xr2)
    zf2 = lax.ppermute(xr2, "space", other_way)
    strong = jnp.broadcast_to(strength[:, None], (count, orbs))

    me = lax.axis_index("orb")
    which = jnp.bitwise_xor(me, jnp.arange(groups, dtype=jnp.int32))
    rows_hot = (pattern[:, 0][:, None] == which[None, :]).astype(BF16)
    rows_hot = rows_hot * (pattern[:, 1] == me).astype(BF16)[:, None]
    q = jnp.einsum("ki,kab->iab", rows_hot, q_tiles, preferred_element_type=F32).astype(BF16)

    operands = (psi, fields, f_x, f_d, f_zo, sums, strong, zo)
    (block1,) = filtered(count, slabs, 0, rows, True, operands, (xr1,), (zf1,))
    y1 = lax.ppermute(block1, "orb", across)
    c1 = lax.ppermute(block1, "orb", beside)
    give2, keep2 = filtered(count, slabs, rows, rows, False, operands, (xr1, xr2), (zf1, zf2))
    cg = lax.ppermute(give2, "orb", beside)
    ck = lax.ppermute(keep2, "orb", beside)
    give_y, y1 = ordered(give2, y1)
    yg = lax.ppermute(give_y, "orb", across)
    yc1 = lax.ppermute(y1, "orb", beside)
    give1, keep1 = rotated((block1, c1, y1, yc1), q, 2)
    got1 = lax.ppermute(give1, "space", swap)
    keep_y, yg = ordered(keep2, yg)
    yk = lax.ppermute(keep_y, "orb", across)
    ycg = lax.ppermute(yg, "orb", beside)
    (give2,) = rotated((give2, cg, yg, ycg), q, 1)
    got2 = lax.ppermute(give2, "space", swap)
    yck = lax.ppermute(yk, "orb", beside)
    (keep2,) = rotated((keep2, ck, yk, yck), q, 1)
    return assembled(psi.shape, [keep1, keep2], [got1, got2])


def solution(mesh):
    placed = (
        P("space", None, None, "orb"),
        P("space", None, None),
        P(None, "space", None, None),
        P(),
        P(),
        P(),
        P(),
    )
    return jax.shard_map(
        shards, mesh=mesh, in_specs=placed, out_specs=P("space", None, None, "orb"), check_vma=False
    )
```

```python
import functools

import jax
import jax.numpy as jnp
from jax import lax
from jax.experimental import pallas as pl
from jax.experimental.pallas import tpu as pltpu
from jax.sharding import PartitionSpec as P

F32 = jnp.float32
BF16 = jnp.bfloat16
VMEM_LIMIT = 50 * 1024 * 1024
SHRINK = 16


def params():
    return pltpu.CompilerParams(vmem_limit_bytes=VMEM_LIMIT)


def cost(flops, moved):
    return pl.CostEstimate(flops=flops // SHRINK, bytes_accessed=moved // SHRINK, transcendentals=0)


def inside(p, window):
    return jnp.logical_and(p >= 0, p < window).astype(F32)


def pair_matrices(width):
    n = 2 * width
    i = lax.broadcasted_iota(jnp.int32, (n, n), 0)
    j = lax.broadcasted_iota(jnp.int32, (n, n), 1)
    same = (i < width) == (j < width)
    along = jnp.logical_and(jnp.abs(i - j) == 1, same)
    here = jnp.where(jnp.logical_or(along, jnp.abs(i - j) == width), -0.125, 0.0)
    before = jnp.where(i == j + width, -0.125, 0.0)
    after = jnp.where(i == j - width, -0.125, 0.0)
    return here.astype(BF16), before.astype(BF16), after.astype(BF16)


def partial_kernel(count, unroll, own, f_own, f_x, f_d, out, weights_out, acc, gram):
    x = lax.rem(lax.axis_index("space"), 2)
    _, pairs, depth, cells = f_own.shape
    orbs = own.shape[3]
    here, before, after = pair_matrices(cells // 2)
    acc[...] = jnp.zeros_like(acc)
    gram[...] = jnp.zeros_like(gram)

    def step(i, carry):
        totals, squares = [], []
        for k in range(unroll):
            r = i * unroll + k
            low, high = jnp.maximum(r - 1, 0), jnp.minimum(r + 1, pairs - 1)
            has_low, has_high = inside(r - 1, pairs), inside(r + 1, pairs)
            tiles = [f_d[r], f_own[x, r], f_own[1 - x, r], f_x[r]]
            for c in (1, 2):
                plane = x if c == 1 else 1 - x
                b = tiles[c]
                b32 = b.astype(F32)
                u = b32[count : count + 1] + b32[count + 1 : count + 2]
                local = jnp.dot(b, here, preferred_element_type=F32)
                local += has_low * jnp.dot(f_own[plane, low], before, preferred_element_type=F32)
                local += has_high * jnp.dot(f_own[plane, high], after, preferred_element_type=F32)
                local += u * b32 - 0.125 * (tiles[c - 1].astype(F32) + tiles[c + 1].astype(F32))
                hi = local.astype(BF16)
                lo = (local - hi.astype(F32)).astype(BF16)
                weights = jnp.concatenate([b, hi, lo], axis=0)
                weights_out[plane, r] = weights
                v = own[plane, pl.ds(2 * r, 2)].reshape(cells, orbs)
                totals.append(jnp.dot(weights, v, preferred_element_type=F32))
                squares.append(
                    lax.dot_general(b, b, (((1,), (1,)), ((), ())), preferred_element_type=F32)
                )
        acc[...] += sum(totals[1:], totals[0])
        gram[...] += sum(squares[1:], squares[0])
        return carry

    lax.fori_loop(0, pairs // unroll, step, 0)
    out[...] = jnp.zeros_like(out)
    out[0:count] = acc[0:count]
    out[count : 2 * count] = acc[depth : depth + count] + acc[2 * depth : 2 * depth + count]
    out[2 * count : 3 * count, 0:count] = gram[0:count, 0:count]


def partials(count, own, f_own, f_x, f_d):
    orbs = own.shape[3]
    planes, pairs, depth, width = f_own.shape
    cells = own.size // orbs
    unroll = max(g for g in (1, 2, 4) if pairs % g == 0 and g * depth <= 144)
    return pl.pallas_call(
        functools.partial(partial_kernel, count, unroll),
        out_shape=(
            jax.ShapeDtypeStruct((3 * count, orbs), F32),
            jax.ShapeDtypeStruct((planes, pairs, 3 * depth, width), BF16),
        ),
        in_specs=[pl.BlockSpec(memory_space=pltpu.VMEM)] * 4,
        out_specs=(pl.BlockSpec(memory_space=pltpu.VMEM),) * 2,
        scratch_shapes=[pltpu.VMEM((3 * depth, orbs), F32), pltpu.VMEM((depth, depth), F32)],
        compiler_params=params(),
        cost_estimate=cost(2 * cells * 3 * depth * orbs, cells * orbs * 4),
        name="partials",
    )(own, f_own, f_x, f_d)


def coefficient_kernel(sums, strength, out):
    count, orbs = strength.shape
    coef1 = (strength[...] * sums[0:count]).astype(BF16)
    padded = coef1.astype(F32) * 0.25
    if orbs > count:
        padded = jnp.concatenate([padded, jnp.zeros((orbs - count, orbs), F32)], axis=0)
    proj2 = sums[count : 2 * count] + jnp.dot(
        sums[2 * count : 3 * count],
        padded,
        preferred_element_type=F32,
        precision=lax.Precision.HIGHEST,
    )
    out[0:count] = coef1
    out[count : 2 * count] = (strength[...] * proj2).astype(BF16)


def coefficients(sums, strength):
    count, orbs = strength.shape
    return pl.pallas_call(
        coefficient_kernel,
        out_shape=jax.ShapeDtypeStruct((2 * count, orbs), BF16),
        in_specs=[pl.BlockSpec(memory_space=pltpu.VMEM)] * 2,
        out_specs=pl.BlockSpec(memory_space=pltpu.VMEM),
        compiler_params=params(),
        cost_estimate=cost(4096, 4096),
        name="coefficients",
    )(sums, strength)


def nonlocal_kernel(depth, unroll, a, b, c, d, q, weights, out):
    count, orbs = a.shape[0] // 2, a.shape[1]
    pairs, cells = weights.shape[1], weights.shape[3]
    turned = sum(
        jnp.dot(ref[...], q[k], preferred_element_type=F32) for k, ref in enumerate((a, b, c, d))
    )
    turned = turned * 0.25
    gap = jnp.zeros((depth - count, orbs), F32)
    one, two = turned[0:count], turned[count : 2 * count]
    right = jnp.concatenate([two, gap, one, gap, one, gap], axis=0)
    hi = right.astype(BF16)
    lo = (right - hi.astype(F32)).astype(BF16)
    right = jnp.concatenate([hi, lo], axis=1)

    def step(i, carry):
        for k in range(unroll):
            r = i * unroll + k
            for plane in range(weights.shape[0]):
                both = lax.dot_general(
                    weights[plane, r], right, (((0,), (0,)), ((), ())), preferred_element_type=F32
                )
                term = both[:, :orbs] + both[:, orbs:]
                out[plane, pl.ds(2 * r, 2)] = term.reshape(2, cells // 2, orbs)
        return carry

    lax.fori_loop(0, pairs // unroll, step, 0)


def nonlocal_term(shape, coefs, q, weights):
    depth = weights.shape[2] // 3
    unroll = max(g for g in (1, 2, 4) if weights.shape[1] % g == 0)
    return pl.pallas_call(
        functools.partial(nonlocal_kernel, depth, unroll),
        out_shape=jax.ShapeDtypeStruct(shape, F32),
        in_specs=[pl.BlockSpec(memory_space=pltpu.VMEM)] * 6,
        out_specs=pl.BlockSpec(memory_space=pltpu.VMEM),
        compiler_params=params(),
        cost_estimate=cost(4096, 4096),
        name="nonlocal",
    )(*coefs, q, weights)


def filter_kernel(count, slabs, start, parts, joint, *refs):
    own, f_own, f_x, f_d, f_zo, zo = refs[:6]
    xrs, zfs = refs[6 : 6 + parts], refs[6 + parts : 6 + 2 * parts]
    outs, scratch = refs[6 + 2 * parts : -3 if parts > 1 else -1], refs[-3 if parts > 1 else -1 :]
    first = scratch[0]
    place = lax.axis_index("space")
    x = lax.rem(place, 2)
    _, pairs, depth, cells = f_own.shape
    width = cells // 2
    half = own.shape[1] // 2
    orbs = own.shape[3]
    rows = outs[0].shape[1]
    base = (half - 2) * x
    lower = (place >= 2).astype(F32)
    upper = (place < slabs - 2).astype(F32)
    is_odd = x.astype(F32)
    has_zf = lower * (1.0 - is_odd) + upper * is_odd
    has_zo = upper * (1.0 - is_odd) + lower * is_odd
    if parts > 1:
        xr, zf = scratch[1], scratch[2]
        for target, pieces in ((xr, xrs), (zf, zfs)):
            at = 0
            for piece in pieces:
                target[:, at : at + piece.shape[1]] = piece[...]
                at += piece.shape[1]
        window = at // 2
    else:
        xr, zf = xrs[0], zfs[0]
        window = xr.shape[1] // 2

    k = lax.broadcasted_iota(jnp.int32, (depth, orbs), 0)
    ones = jnp.where(jnp.logical_or(k == count, k == count + 1), 1.0, 0.0).astype(BF16)
    here, _, _ = pair_matrices(width)

    def field(c, p):
        if c == 1:
            return f_d[base // 2 + p]
        if c in (2, 3):
            return f_own[(c % 2) ^ x, base // 2 + p]
        if c == 4:
            return f_x[base // 2 + p]
        if c == 5:
            return f_x[pairs + p]
        return f_zo[p]

    def rows_of(c, w, n):
        plane = (c % 2) ^ x
        if c in (2, 3):
            return own[plane, pl.ds(base + w, n)]
        ref = zf if c < 2 else (xr if c < 6 else zo)
        return ref[plane, pl.ds(w, n)]

    def applied(pair, v, outer, zs, fields):
        u = lax.dot_general(fields, ones, (((0,), (0,)), ((), ())), preferred_element_type=F32)
        near = jnp.dot(here, pair, preferred_element_type=F32)
        return near + u * v - 0.125 * (outer + zs)

    def step1(j, carry):
        p = start // 2 + x + j - 1
        q = jnp.clip(p, 0, window - 1)
        has_below = inside(p - 1, window)
        has_above = inside(p + 1, window)
        valid = inside(p, window)
        below = jnp.maximum(2 * q - 1, 0)
        above = jnp.minimum(2 * q + 2, 2 * window - 1)
        pair = [rows_of(c, 2 * q, 2).reshape(cells, orbs) for c in range(8)]
        vs = [v.astype(F32) for v in pair]
        for c in range(1, 7):
            outer = jnp.concatenate(
                [
                    rows_of(c, below, 1)[0].astype(F32) * has_below,
                    rows_of(c, above, 1)[0].astype(F32) * has_above,
                ],
                axis=0,
            )
            f = applied(pair[c], vs[c], outer, vs[c - 1] + vs[c + 1], field(c, q))
            keep = valid
            if c == 1:
                keep = valid * has_zf
            if c == 6:
                keep = valid * has_zo
            first[c - 1, pl.ds(2 * j, 2)] = (f * keep).astype(BF16).reshape(2, width, orbs)
        return carry

    lax.fori_loop(0, rows // 2 + 2, step1, 0)

    def step2(j, carry):
        p = start // 2 + x + j
        pair = [first[c - 1, pl.ds(2 * j + 2, 2)].reshape(cells, orbs) for c in range(1, 7)]
        vs = [v.astype(F32) for v in pair]
        for c in range(2, 6):
            outer = jnp.concatenate(
                [first[c - 1, 2 * j + 1].astype(F32), first[c - 1, 2 * j + 4].astype(F32)], axis=0
            )
            f = applied(pair[c - 1], vs[c - 1], outer, vs[c - 2] + vs[c], field(c, p))
            f = f.astype(BF16).reshape(2, width, orbs)
            plane = (c % 2) ^ x
            if joint:
                outs[0][plane + (2 if c in (2, 3) else 0), pl.ds(2 * j, 2)] = f
            else:
                outs[1 if c in (2, 3) else 0][plane, pl.ds(2 * j, 2)] = f
        return carry

    lax.fori_loop(0, rows // 2, step2, 0)


def filtered(count, slabs, start, rows, joint, operands, xrs, zfs):
    own = operands[0]
    planes, _, width, orbs = own.shape
    parts = len(xrs)
    shape = (2 * planes if joint else planes, rows, width, orbs)
    out = (jax.ShapeDtypeStruct(shape, BF16),) * (1 if joint else 2)
    cells = 10 * rows * width
    scratch = [pltpu.VMEM((6, rows + 4, width, orbs), BF16)]
    if parts > 1:
        window = sum(piece.shape[1] for piece in xrs)
        scratch += [pltpu.VMEM((planes, window, width, orbs), BF16)] * 2
    return pl.pallas_call(
        functools.partial(filter_kernel, count, slabs, start, parts, joint),
        out_shape=out,
        in_specs=[pl.BlockSpec(memory_space=pltpu.VMEM)] * (len(operands) + 2 * parts),
        out_specs=(pl.BlockSpec(memory_space=pltpu.VMEM),) * len(out),
        scratch_shapes=scratch,
        compiler_params=params(),
        cost_estimate=cost(2 * cells * 32 * orbs, cells * orbs * 4),
        name="filtered",
    )(*operands, *xrs, *zfs)


def rotate_kernel(group, *refs):
    a, b, c, d, q = refs[:5]
    outs = refs[5:]
    _, rows, width, orbs = a.shape
    planes = outs[0].shape[0]
    low = jnp.concatenate([q[0], q[1]], axis=0)
    high = jnp.concatenate([q[2], q[3]], axis=0)

    def one(j, carry):
        for plane in range(a.shape[0]):
            def take(ref):
                return ref[plane, pl.ds(group * j, group)].reshape(group * width, orbs)

            total = jnp.dot(
                jnp.concatenate([take(a), take(b)], axis=1), low, preferred_element_type=F32
            )
            total = total + jnp.dot(
                jnp.concatenate([take(c), take(d)], axis=1), high, preferred_element_type=F32
            )
            outs[plane // planes][plane % planes, pl.ds(group * j, group)] = total.astype(
                BF16
            ).reshape(group, width, orbs)
        return carry

    lax.fori_loop(0, rows // group, one, 0)


def rotated(blocks, q, pieces):
    a = blocks[0]
    size = a.size
    group = max(g for g in range(1, 7) if a.shape[1] % g == 0)
    out = jax.ShapeDtypeStruct((a.shape[0] // pieces, *a.shape[1:]), BF16)
    return pl.pallas_call(
        functools.partial(rotate_kernel, group),
        out_shape=(out,) * pieces,
        in_specs=[pl.BlockSpec(memory_space=pltpu.VMEM)] * 5,
        out_specs=(pl.BlockSpec(memory_space=pltpu.VMEM),) * pieces,
        compiler_params=params(),
        cost_estimate=cost(8 * size * a.shape[3], 10 * size),
        name="rotated",
    )(*blocks, q)


def assemble_kernel(half, term, *refs):
    out = refs[-1]
    pieces = (len(refs) - 1) // 2
    x = lax.rem(lax.axis_index("space"), 2)
    rows = refs[0].shape[1]
    for k in range(pieces):
        for ref, at in ((refs[k], half * x), (refs[pieces + k], half * (1 - x))):
            where = pl.ds(at + rows * k, rows)
            out[:, where] = (ref[...].astype(F32) + term[:, where]).astype(BF16)


def assembled(term, mine, theirs):
    return pl.pallas_call(
        functools.partial(assemble_kernel, term.shape[1] // 2),
        out_shape=jax.ShapeDtypeStruct(term.shape, BF16),
        in_specs=[pl.BlockSpec(memory_space=pltpu.VMEM)] * (1 + len(mine) + len(theirs)),
        out_specs=pl.BlockSpec(memory_space=pltpu.VMEM),
        compiler_params=params(),
        cost_estimate=cost(4096, 4096),
        name="assembled",
    )(term, *mine, *theirs)


def ordered(*arrays):
    return lax.optimization_barrier(arrays)


def shards(psi, potential, beta, strength, atom_slab, pattern, q_tiles):
    planes, width_x, width_y, orbs = psi.shape
    count = beta.shape[0]
    slabs = lax.axis_size("space")
    place = lax.axis_index("space")
    x = lax.rem(place, 2)
    half = width_x // 2
    window = half + 2
    rows = half // 2
    early = rows + 4

    def within(pairs):
        return [(i, j) for i, j in pairs if 0 <= j < slabs]

    swap = [(i, i ^ 1) for i in range(slabs)]
    own_way = within([(i, i + 2 if i % 2 else i - 2) for i in range(slabs)])
    other_way = within([(i, i - 2 if i % 2 else i + 2) for i in range(slabs)])
    raster = within([(i, i + 1 if i % 2 else i - 1) for i in range(slabs)])
    groups = lax.axis_size("orb")
    across = [(i, i ^ 2) for i in range(groups)]
    beside = [(i, i ^ 1) for i in range(groups)]
    mine = (half - 2) * x
    theirs = (half - 2) * (1 - x)

    active = jnp.abs(place - atom_slab) <= 1
    beta_m = jnp.where(active[:, None, None, None], beta, jnp.zeros_like(beta))
    depth = -(-(count + 2) // 16) * 16
    u = (potential - 1.0) * 0.25
    hi = lax.reduce_precision(u, 8, 7)
    lo = u - hi
    fields = jnp.concatenate(
        [
            jnp.transpose(beta_m, (1, 2, 0, 3)),
            hi[:, :, None, :].astype(BF16),
            lo[:, :, None, :].astype(BF16),
            jnp.zeros((planes, width_x, depth - count - 2, width_y), BF16),
        ],
        axis=2,
    )
    fields = jnp.concatenate([fields[:, 0::2], fields[:, 1::2]], axis=3)
    far = lax.dynamic_index_in_dim(fields, x, 0, keepdims=False)
    near = lax.dynamic_index_in_dim(fields, 1 - x, 0, keepdims=False)
    to_x = jnp.concatenate(
        [near, lax.dynamic_slice_in_dim(far, theirs // 2, window // 2, axis=0)], axis=0
    )
    to_zo = lax.dynamic_slice_in_dim(far, mine // 2, window // 2, axis=0)
    f_x = lax.ppermute(to_x, "space", swap)
    f_d = lax.ppermute(far, "space", raster)
    f_zo = lax.ppermute(to_zo, "space", own_way)

    xr1 = lax.ppermute(
        lax.dynamic_slice_in_dim(psi, theirs, early, axis=1), "space", swap
    )
    zo = lax.ppermute(lax.dynamic_slice_in_dim(psi, mine, window, axis=1), "space", own_way)
    zf1 = lax.ppermute(xr1, "space", other_way)
    second = lax.dynamic_slice_in_dim(psi, theirs + early, window - early, axis=1)
    second, _ = ordered(second, xr1)
    xr2 = lax.ppermute(second, "space", swap)
    zf1, xr2 = ordered(zf1, xr2)
    zf2 = lax.ppermute(xr2, "space", other_way)
    sums, weights = partials(count, psi, fields, f_x, f_d)
    step = 1
    while step < slabs:
        sums = sums + lax.ppermute(sums, "space", [(i, i ^ step) for i in range(slabs)])
        step *= 2
    strong = jnp.broadcast_to(strength[:, None], (count, orbs))

    me = lax.axis_index("orb")
    which = jnp.bitwise_xor(me, jnp.arange(groups, dtype=jnp.int32))
    rows_hot = (pattern[:, 0][:, None] == which[None, :]).astype(BF16)
    rows_hot = rows_hot * (pattern[:, 1] == me).astype(BF16)[:, None]
    q = jnp.einsum("ki,kab->iab", rows_hot, q_tiles, preferred_element_type=F32).astype(BF16)

    coefs = coefficients(sums, strong)
    coefs_c = lax.ppermute(coefs, "orb", beside)
    coefs_y = lax.ppermute(jnp.concatenate([coefs, coefs_c], axis=0), "orb", across)
    coefs_yc, coefs_y = coefs_y[2 * count :], coefs_y[: 2 * count]
    term = nonlocal_term(psi.shape, (coefs, coefs_c, coefs_y, coefs_yc), q, weights)

    operands = (psi, fields, f_x, f_d, f_zo, zo)
    (block1,) = filtered(count, slabs, 0, rows, True, operands, (xr1,), (zf1,))
    y1 = lax.ppermute(block1, "orb", across)
    c1 = lax.ppermute(block1, "orb", beside)
    give2, keep2 = filtered(count, slabs, rows, rows, False, operands, (xr1, xr2), (zf1, zf2))
    cg = lax.ppermute(give2, "orb", beside)
    ck = lax.ppermute(keep2, "orb", beside)
    give_y, y1 = ordered(give2, y1)
    yg = lax.ppermute(give_y, "orb", across)
    yc1 = lax.ppermute(y1, "orb", beside)
    give1, keep1 = rotated((block1, c1, y1, yc1), q, 2)
    got1 = lax.ppermute(give1, "space", swap)
    keep_y, yg = ordered(keep2, yg)
    yk = lax.ppermute(keep_y, "orb", across)
    ycg = lax.ppermute(yg, "orb", beside)
    (give2,) = rotated((give2, cg, yg, ycg), q, 1)
    got2 = lax.ppermute(give2, "space", swap)
    yck = lax.ppermute(yk, "orb", beside)
    (keep2,) = rotated((keep2, ck, yk, yck), q, 1)
    return assembled(term, [keep1, keep2], [got1, got2])


def solution(mesh):
    placed = (
        P("space", None, None, "orb"),
        P("space", None, None),
        P(None, "space", None, None),
        P(),
        P(),
        P(),
        P(),
    )
    return jax.shard_map(
        shards, mesh=mesh, in_specs=placed, out_specs=P("space", None, None, "orb"), check_vma=False
    )
```

```python
import functools

import jax
import jax.numpy as jnp
from jax import lax
from jax.experimental import pallas as pl
from jax.experimental.pallas import tpu as pltpu
from jax.sharding import PartitionSpec as P

F32 = jnp.float32
BF16 = jnp.bfloat16
VMEM_LIMIT = 24 * 1024 * 1024
SHRINK = 16


def params():
    return pltpu.CompilerParams(vmem_limit_bytes=VMEM_LIMIT)


def cost(flops, moved):
    return pl.CostEstimate(flops=flops // SHRINK, bytes_accessed=moved // SHRINK, transcendentals=0)


def inside(p, window):
    return jnp.logical_and(p >= 0, p < window).astype(F32)


def pair_matrices(width):
    n = 2 * width
    i = lax.broadcasted_iota(jnp.int32, (n, n), 0)
    j = lax.broadcasted_iota(jnp.int32, (n, n), 1)
    same = (i < width) == (j < width)
    along = jnp.logical_and(jnp.abs(i - j) == 1, same)
    here = jnp.where(jnp.logical_or(along, jnp.abs(i - j) == width), -0.125, 0.0)
    before = jnp.where(i == j + width, -0.125, 0.0)
    after = jnp.where(i == j - width, -0.125, 0.0)
    return here.astype(BF16), before.astype(BF16), after.astype(BF16)


def partial_kernel(count, unroll, own, f_own, f_x, f_d, out, weights_out, acc, gram):
    x = lax.rem(lax.axis_index("space"), 2)
    _, pairs, depth, cells = f_own.shape
    orbs = own.shape[3]
    here, before, after = pair_matrices(cells // 2)
    acc[...] = jnp.zeros_like(acc)
    gram[...] = jnp.zeros_like(gram)

    def step(i, carry):
        totals, squares = [], []
        for k in range(unroll):
            r = i * unroll + k
            low, high = jnp.maximum(r - 1, 0), jnp.minimum(r + 1, pairs - 1)
            has_low, has_high = inside(r - 1, pairs), inside(r + 1, pairs)
            tiles = [f_d[r], f_own[x, r], f_own[1 - x, r], f_x[r]]
            for c in (1, 2):
                plane = x if c == 1 else 1 - x
                b = tiles[c]
                b32 = b.astype(F32)
                u = b32[count : count + 1] + b32[count + 1 : count + 2]
                local = jnp.dot(b, here, preferred_element_type=F32)
                local += has_low * jnp.dot(f_own[plane, low], before, preferred_element_type=F32)
                local += has_high * jnp.dot(f_own[plane, high], after, preferred_element_type=F32)
                local += u * b32 - 0.125 * (tiles[c - 1].astype(F32) + tiles[c + 1].astype(F32))
                hi = local.astype(BF16)
                lo = (local - hi.astype(F32)).astype(BF16)
                weights = jnp.concatenate([b, hi, lo], axis=0)
                weights_out[plane, r] = weights
                v = own[plane, pl.ds(2 * r, 2)].reshape(cells, orbs)
                totals.append(jnp.dot(weights, v, preferred_element_type=F32))
                squares.append(
                    lax.dot_general(b, b, (((1,), (1,)), ((), ())), preferred_element_type=F32)
                )
        acc[...] += sum(totals[1:], totals[0])
        gram[...] += sum(squares[1:], squares[0])
        return carry

    lax.fori_loop(0, pairs // unroll, step, 0)
    out[...] = jnp.zeros_like(out)
    out[0:count] = acc[0:count]
    out[count : 2 * count] = acc[depth : depth + count] + acc[2 * depth : 2 * depth + count]
    out[2 * count : 3 * count, 0:count] = gram[0:count, 0:count]


def partials(count, own, f_own, f_x, f_d):
    orbs = own.shape[3]
    planes, pairs, depth, width = f_own.shape
    cells = own.size // orbs
    unroll = max(g for g in (1, 2, 4) if pairs % g == 0 and g * depth <= 144)
    return pl.pallas_call(
        functools.partial(partial_kernel, count, unroll),
        out_shape=(
            jax.ShapeDtypeStruct((3 * count, orbs), F32),
            jax.ShapeDtypeStruct((planes, pairs, 3 * depth, width), BF16),
        ),
        in_specs=[pl.BlockSpec(memory_space=pltpu.VMEM)] * 4,
        out_specs=(pl.BlockSpec(memory_space=pltpu.VMEM),) * 2,
        scratch_shapes=[pltpu.VMEM((3 * depth, orbs), F32), pltpu.VMEM((depth, depth), F32)],
        compiler_params=params(),
        cost_estimate=cost(2 * cells * 3 * depth * orbs, cells * orbs * 4),
        name="partials",
    )(own, f_own, f_x, f_d)


def coefficient_kernel(sums, strength, out):
    count, orbs = strength.shape
    coef1 = (strength[...] * sums[0:count]).astype(BF16)
    padded = coef1.astype(F32) * 0.25
    if orbs > count:
        padded = jnp.concatenate([padded, jnp.zeros((orbs - count, orbs), F32)], axis=0)
    proj2 = sums[count : 2 * count] + jnp.dot(
        sums[2 * count : 3 * count],
        padded,
        preferred_element_type=F32,
        precision=lax.Precision.HIGHEST,
    )
    out[0:count] = coef1
    out[count : 2 * count] = (strength[...] * proj2).astype(BF16)


def coefficients(sums, strength):
    count, orbs = strength.shape
    return pl.pallas_call(
        coefficient_kernel,
        out_shape=jax.ShapeDtypeStruct((2 * count, orbs), BF16),
        in_specs=[pl.BlockSpec(memory_space=pltpu.VMEM)] * 2,
        out_specs=pl.BlockSpec(memory_space=pltpu.VMEM),
        compiler_params=params(),
        cost_estimate=cost(4096, 4096),
        name="coefficients",
    )(sums, strength)


def nonlocal_kernel(depth, unroll, a, b, c, d, q, weights, out):
    count, orbs = a.shape[0] // 2, a.shape[1]
    pairs, cells = weights.shape[1], weights.shape[3]
    turned = sum(
        jnp.dot(ref[...], q[k], preferred_element_type=F32) for k, ref in enumerate((a, b, c, d))
    )
    turned = turned * 0.25
    gap = jnp.zeros((depth - count, orbs), F32)
    one, two = turned[0:count], turned[count : 2 * count]
    right = jnp.concatenate([two, gap, one, gap, one, gap], axis=0)
    hi = right.astype(BF16)
    lo = (right - hi.astype(F32)).astype(BF16)
    right = jnp.concatenate([hi, lo], axis=1)

    def step(i, carry):
        for k in range(unroll):
            r = i * unroll + k
            for plane in range(weights.shape[0]):
                both = lax.dot_general(
                    weights[plane, r], right, (((0,), (0,)), ((), ())), preferred_element_type=F32
                )
                term = both[:, :orbs] + both[:, orbs:]
                out[plane, pl.ds(2 * r, 2)] = term.reshape(2, cells // 2, orbs)
        return carry

    lax.fori_loop(0, pairs // unroll, step, 0)


def nonlocal_term(shape, coefs, q, weights):
    depth = weights.shape[2] // 3
    unroll = max(g for g in (1, 2, 4) if weights.shape[1] % g == 0)
    return pl.pallas_call(
        functools.partial(nonlocal_kernel, depth, unroll),
        out_shape=jax.ShapeDtypeStruct(shape, F32),
        in_specs=[pl.BlockSpec(memory_space=pltpu.VMEM)] * 6,
        out_specs=pl.BlockSpec(memory_space=pltpu.VMEM),
        compiler_params=params(),
        cost_estimate=cost(4096, 4096),
        name="nonlocal",
    )(*coefs, q, weights)


def filter_kernel(slabs, start, parts, joint, *refs):
    own, p_own, p_x, p_d, p_zo, zo = refs[:6]
    xrs, zfs = refs[6 : 6 + parts], refs[6 + parts : 6 + 2 * parts]
    outs, scratch = refs[6 + 2 * parts : -3 if parts > 1 else -1], refs[-3 if parts > 1 else -1 :]
    first = scratch[0]
    place = lax.axis_index("space")
    x = lax.rem(place, 2)
    width = own.shape[2]
    cells = 2 * width
    half = own.shape[1] // 2
    orbs = own.shape[3]
    rows = outs[0].shape[1]
    base = (half - 2) * x
    lower = (place >= 2).astype(F32)
    upper = (place < slabs - 2).astype(F32)
    is_odd = x.astype(F32)
    has_zf = lower * (1.0 - is_odd) + upper * is_odd
    has_zo = upper * (1.0 - is_odd) + lower * is_odd
    if parts > 1:
        xr, zf = scratch[1], scratch[2]
        for target, pieces in ((xr, xrs), (zf, zfs)):
            at = 0
            for piece in pieces:
                target[:, at : at + piece.shape[1]] = piece[...]
                at += piece.shape[1]
        window = at // 2
    else:
        xr, zf = xrs[0], zfs[0]
        window = xr.shape[1] // 2

    here, _, _ = pair_matrices(width)
    here = here.astype(F32)
    i = lax.broadcasted_iota(jnp.int32, (cells, cells), 0)
    diagonal = i == lax.broadcasted_iota(jnp.int32, (cells, cells), 1)

    def local(c, p):
        w = base + 2 * p

        def line(at):
            if c in (1, 6):
                return (p_d if c == 1 else p_zo)[0, pl.ds(at, 1)]
            return (p_own if c in (2, 3) else p_x)[(c % 2) ^ x, pl.ds(at, 1)]

        u = (jnp.concatenate([line(w), line(w + 1)], axis=1) - 1.0) * 0.25
        hi = u.astype(BF16).astype(F32)
        return (
            jnp.where(diagonal, hi, here).astype(BF16),
            jnp.where(diagonal, u - hi, 0.0).astype(BF16),
        )

    def rows_of(c, w, n):
        plane = (c % 2) ^ x
        if c in (2, 3):
            return own[plane, pl.ds(base + w, n)]
        ref = zf if c < 2 else (xr if c < 6 else zo)
        return ref[plane, pl.ds(w, n)]

    def applied(pair, outer, zs, matrices):
        near = jnp.dot(matrices[0], pair, preferred_element_type=F32)
        near = near + jnp.dot(matrices[1], pair, preferred_element_type=F32)
        return near - 0.125 * (outer + zs)

    def step1(j, carry):
        p = start // 2 + x + j - 1
        q = jnp.clip(p, 0, window - 1)
        has_below = inside(p - 1, window)
        has_above = inside(p + 1, window)
        valid = inside(p, window)
        below = jnp.maximum(2 * q - 1, 0)
        above = jnp.minimum(2 * q + 2, 2 * window - 1)
        pair = [rows_of(c, 2 * q, 2).reshape(cells, orbs) for c in range(8)]
        vs = [v.astype(F32) for v in pair]
        for c in range(1, 7):
            outer = jnp.concatenate(
                [
                    rows_of(c, below, 1)[0].astype(F32) * has_below,
                    rows_of(c, above, 1)[0].astype(F32) * has_above,
                ],
                axis=0,
            )
            f = applied(pair[c], outer, vs[c - 1] + vs[c + 1], local(c, q))
            keep = valid
            if c == 1:
                keep = valid * has_zf
            if c == 6:
                keep = valid * has_zo
            first[c - 1, pl.ds(2 * j, 2)] = (f * keep).astype(BF16).reshape(2, width, orbs)
        return carry

    lax.fori_loop(0, rows // 2 + 2, step1, 0)

    def step2(j, carry):
        p = start // 2 + x + j
        pair = [first[c - 1, pl.ds(2 * j + 2, 2)].reshape(cells, orbs) for c in range(1, 7)]
        vs = [v.astype(F32) for v in pair]
        for c in range(2, 6):
            outer = jnp.concatenate(
                [first[c - 1, 2 * j + 1].astype(F32), first[c - 1, 2 * j + 4].astype(F32)], axis=0
            )
            f = applied(pair[c - 1], outer, vs[c - 2] + vs[c], local(c, p))
            f = f.astype(BF16).reshape(2, width, orbs)
            plane = (c % 2) ^ x
            if joint:
                outs[0][plane + (2 if c in (2, 3) else 0), pl.ds(2 * j, 2)] = f
            else:
                outs[1 if c in (2, 3) else 0][plane, pl.ds(2 * j, 2)] = f
        return carry

    lax.fori_loop(0, rows // 2, step2, 0)


def filtered(slabs, start, rows, joint, operands, xrs, zfs):
    own = operands[0]
    planes, _, width, orbs = own.shape
    parts = len(xrs)
    shape = (2 * planes if joint else planes, rows, width, orbs)
    out = (jax.ShapeDtypeStruct(shape, BF16),) * (1 if joint else 2)
    cells = 10 * rows * width
    scratch = [pltpu.VMEM((6, rows + 4, width, orbs), BF16)]
    if parts > 1:
        window = sum(piece.shape[1] for piece in xrs)
        scratch += [pltpu.VMEM((planes, window, width, orbs), BF16)] * 2
    return pl.pallas_call(
        functools.partial(filter_kernel, slabs, start, parts, joint),
        out_shape=out,
        in_specs=[pl.BlockSpec(memory_space=pltpu.VMEM)] * (len(operands) + 2 * parts),
        out_specs=(pl.BlockSpec(memory_space=pltpu.VMEM),) * len(out),
        scratch_shapes=scratch,
        compiler_params=params(),
        cost_estimate=cost(2 * cells * 32 * orbs, cells * orbs * 4),
        name="filtered",
    )(*operands, *xrs, *zfs)


def rotate_kernel(group, *refs):
    a, b, c, d, q = refs[:5]
    outs = refs[5:]
    _, rows, width, orbs = a.shape
    planes = outs[0].shape[0]
    low = jnp.concatenate([q[0], q[1]], axis=0)
    high = jnp.concatenate([q[2], q[3]], axis=0)

    def one(j, carry):
        for plane in range(a.shape[0]):
            def take(ref):
                return ref[plane, pl.ds(group * j, group)].reshape(group * width, orbs)

            total = jnp.dot(
                jnp.concatenate([take(a), take(b)], axis=1), low, preferred_element_type=F32
            )
            total = total + jnp.dot(
                jnp.concatenate([take(c), take(d)], axis=1), high, preferred_element_type=F32
            )
            outs[plane // planes][plane % planes, pl.ds(group * j, group)] = total.astype(
                BF16
            ).reshape(group, width, orbs)
        return carry

    lax.fori_loop(0, rows // group, one, 0)


def rotated(blocks, q, pieces):
    a = blocks[0]
    size = a.size
    group = max(g for g in range(1, 7) if a.shape[1] % g == 0)
    out = jax.ShapeDtypeStruct((a.shape[0] // pieces, *a.shape[1:]), BF16)
    return pl.pallas_call(
        functools.partial(rotate_kernel, group),
        out_shape=(out,) * pieces,
        in_specs=[pl.BlockSpec(memory_space=pltpu.VMEM)] * 5,
        out_specs=(pl.BlockSpec(memory_space=pltpu.VMEM),) * pieces,
        compiler_params=params(),
        cost_estimate=cost(8 * size * a.shape[3], 10 * size),
        name="rotated",
    )(*blocks, q)


def assemble_kernel(half, term, *refs):
    out = refs[-1]
    pieces = (len(refs) - 1) // 2
    x = lax.rem(lax.axis_index("space"), 2)
    rows = refs[0].shape[1]
    for k in range(pieces):
        for ref, at in ((refs[k], half * x), (refs[pieces + k], half * (1 - x))):
            where = pl.ds(at + rows * k, rows)
            out[:, where] = (ref[...].astype(F32) + term[:, where]).astype(BF16)


def assembled(term, mine, theirs):
    return pl.pallas_call(
        functools.partial(assemble_kernel, term.shape[1] // 2),
        out_shape=jax.ShapeDtypeStruct(term.shape, BF16),
        in_specs=[pl.BlockSpec(memory_space=pltpu.VMEM)] * (1 + len(mine) + len(theirs)),
        out_specs=pl.BlockSpec(memory_space=pltpu.VMEM),
        compiler_params=params(),
        cost_estimate=cost(4096, 4096),
        name="assembled",
    )(term, *mine, *theirs)


def ordered(*arrays):
    return lax.optimization_barrier(arrays)


def shards(psi, potential, beta, strength, atom_slab, pattern, q_tiles):
    planes, width_x, width_y, orbs = psi.shape
    count = beta.shape[0]
    slabs = lax.axis_size("space")
    place = lax.axis_index("space")
    x = lax.rem(place, 2)
    half = width_x // 2
    window = half + 2
    rows = half // 2
    early = rows + 4

    def within(pairs):
        return [(i, j) for i, j in pairs if 0 <= j < slabs]

    swap = [(i, i ^ 1) for i in range(slabs)]
    own_way = within([(i, i + 2 if i % 2 else i - 2) for i in range(slabs)])
    other_way = within([(i, i - 2 if i % 2 else i + 2) for i in range(slabs)])
    raster = within([(i, i + 1 if i % 2 else i - 1) for i in range(slabs)])
    groups = lax.axis_size("orb")
    across = [(i, i ^ 2) for i in range(groups)]
    beside = [(i, i ^ 1) for i in range(groups)]
    mine = (half - 2) * x
    theirs = (half - 2) * (1 - x)

    active = jnp.abs(place - atom_slab) <= 1
    beta_m = jnp.where(active[:, None, None, None], beta, jnp.zeros_like(beta))
    depth = -(-(count + 2) // 16) * 16
    u = (potential - 1.0) * 0.25
    hi = lax.reduce_precision(u, 8, 7)
    lo = u - hi
    fields = jnp.concatenate(
        [
            jnp.transpose(beta_m, (1, 2, 0, 3)),
            hi[:, :, None, :].astype(BF16),
            lo[:, :, None, :].astype(BF16),
            jnp.zeros((planes, width_x, depth - count - 2, width_y), BF16),
        ],
        axis=2,
    )
    fields = jnp.concatenate([fields[:, 0::2], fields[:, 1::2]], axis=3)
    far = lax.dynamic_index_in_dim(fields, x, 0, keepdims=False)
    near = lax.dynamic_index_in_dim(fields, 1 - x, 0, keepdims=False)
    f_x = lax.ppermute(near, "space", swap)
    f_d = lax.ppermute(far, "space", raster)
    p_far = lax.dynamic_slice_in_dim(potential, x, 1, axis=0)
    p_x = lax.ppermute(potential, "space", swap)
    p_d = lax.ppermute(p_far, "space", raster)
    p_zo = lax.ppermute(p_far, "space", own_way)

    xr1 = lax.ppermute(
        lax.dynamic_slice_in_dim(psi, theirs, early, axis=1), "space", swap
    )
    zo = lax.ppermute(lax.dynamic_slice_in_dim(psi, mine, window, axis=1), "space", own_way)
    zf1 = lax.ppermute(xr1, "space", other_way)
    second = lax.dynamic_slice_in_dim(psi, theirs + early, window - early, axis=1)
    second, _ = ordered(second, xr1)
    xr2 = lax.ppermute(second, "space", swap)
    zf1_in, _ = ordered(zf1, xr2)
    zf2 = lax.ppermute(xr2, "space", other_way)
    strong = jnp.broadcast_to(strength[:, None], (count, orbs))

    me = lax.axis_index("orb")
    which = jnp.bitwise_xor(me, jnp.arange(groups, dtype=jnp.int32))
    rows_hot = (pattern[:, 0][:, None] == which[None, :]).astype(BF16)
    rows_hot = rows_hot * (pattern[:, 1] == me).astype(BF16)[:, None]
    q = jnp.einsum("ki,kab->iab", rows_hot, q_tiles, preferred_element_type=F32).astype(BF16)

    p_x, f_x, f_d = ordered(p_x, f_x, f_d)
    operands = (psi, potential, p_x, p_d, p_zo, zo)
    (block1,) = filtered(slabs, 0, rows, True, operands, (xr1,), (zf1_in,))
    y1 = lax.ppermute(block1, "orb", across)
    c1 = lax.ppermute(block1, "orb", beside)
    sums, weights = partials(count, psi, fields, f_x, f_d)
    xr2, sums = ordered(xr2, sums)
    give2, keep2 = filtered(slabs, rows, rows, False, operands, (xr1, xr2), (zf1, zf2))
    step = 1
    while step < slabs:
        sums = sums + lax.ppermute(sums, "space", [(i, i ^ step) for i in range(slabs)])
        step *= 2
    coefs = coefficients(sums, strong)
    cg = lax.ppermute(give2, "orb", beside)
    ck = lax.ppermute(keep2, "orb", beside)
    give_y, y1 = ordered(give2, y1)
    yg = lax.ppermute(give_y, "orb", across)
    yc1 = lax.ppermute(y1, "orb", beside)
    give1, keep1 = rotated((block1, c1, y1, yc1), q, 2)
    keep_y, yg, give1, coefs = ordered(keep2, yg, give1, coefs)
    got1 = lax.ppermute(give1, "space", swap)
    coefs_c = lax.ppermute(coefs, "orb", beside)
    coefs_y = lax.ppermute(jnp.concatenate([coefs, coefs_c], axis=0), "orb", across)
    coefs_yc, coefs_y = coefs_y[2 * count :], coefs_y[: 2 * count]
    term = nonlocal_term(psi.shape, (coefs, coefs_c, coefs_y, coefs_yc), q, weights)

    yk = lax.ppermute(keep_y, "orb", across)
    ycg = lax.ppermute(yg, "orb", beside)
    (give2,) = rotated((give2, cg, yg, ycg), q, 1)
    got2 = lax.ppermute(give2, "space", swap)
    yck = lax.ppermute(yk, "orb", beside)
    (keep2,) = rotated((keep2, ck, yk, yck), q, 1)
    return assembled(term, [keep1, keep2], [got1, got2])


def solution(mesh):
    placed = (
        P("space", None, None, "orb"),
        P("space", None, None),
        P(None, "space", None, None),
        P(),
        P(),
        P(),
        P(),
    )
    return jax.shard_map(
        shards, mesh=mesh, in_specs=placed, out_specs=P("space", None, None, "orb"), check_vma=False
    )
```

```python
import functools

import jax
import jax.numpy as jnp
from jax import lax
from jax.experimental import pallas as pl
from jax.experimental.pallas import tpu as pltpu
from jax.sharding import PartitionSpec as P

F32 = jnp.float32
BF16 = jnp.bfloat16
VMEM_LIMIT = 24 * 1024 * 1024
SHRINK = 16


def params():
    return pltpu.CompilerParams(vmem_limit_bytes=VMEM_LIMIT)


def cost(flops, moved):
    return pl.CostEstimate(flops=flops // SHRINK, bytes_accessed=moved // SHRINK, transcendentals=0)


def inside(p, window):
    return jnp.logical_and(p >= 0, p < window).astype(F32)


def neighbour_sum(width, pairs):
    n = (2 if pairs else 1) * width
    i = lax.broadcasted_iota(jnp.int32, (n, n), 0)
    j = lax.broadcasted_iota(jnp.int32, (n, n), 1)
    linked = jnp.abs(i - j) == 1
    if pairs:
        linked = jnp.logical_and(linked, (i < width) == (j < width))
        linked = jnp.logical_or(linked, jnp.abs(i - j) == width)
    return jnp.where(linked, -0.125, 0.0)


def prepare_kernel(early, psi, potential, to_x, to_x2, to_z, blocks, sems):
    x = lax.rem(lax.axis_index("space"), 2)
    half = psi.shape[1] // 2
    window = half + 2
    mine, theirs = (half - 2) * x, (half - 2) * (1 - x)
    width = potential.shape[2]
    gap = jnp.zeros((potential.shape[1], 64 - width), F32)
    copies = [
        pltpu.make_async_copy(
            psi.at[:, pl.ds(theirs, early)], to_x.at[:, pl.ds(0, early)], sems.at[0]
        ),
        pltpu.make_async_copy(
            psi.at[:, pl.ds(mine, window)], to_z.at[:, pl.ds(0, window)], sems.at[1]
        ),
        pltpu.make_async_copy(
            psi.at[:, pl.ds(theirs + early, window - early)], to_x2, sems.at[2]
        ),
    ]
    for copy in copies:
        copy.start()
    for plane in range(blocks.shape[0]):
        u = (potential[plane] - 1.0) * 0.25
        hi = u.astype(BF16).astype(F32)
        blocks[plane, 0] = jnp.concatenate([hi, gap, u - hi, gap], axis=1).astype(BF16)
    more = [
        pltpu.make_async_copy(blocks, to_x.at[:, pl.ds(early, 1)], sems.at[3]),
        pltpu.make_async_copy(blocks, to_z.at[:, pl.ds(window, 1)], sems.at[4]),
    ]
    for copy in more:
        copy.start()
    for copy in copies + more:
        copy.wait()


def prepared(psi, potential, early):
    planes, width_x, width_y, orbs = psi.shape
    window = width_x // 2 + 2

    def out(rows):
        return jax.ShapeDtypeStruct((planes, rows, width_y, orbs), BF16)

    anywhere = pl.BlockSpec(memory_space=pl.ANY)
    local = pl.BlockSpec(memory_space=pltpu.VMEM)
    return pl.pallas_call(
        functools.partial(prepare_kernel, early),
        out_shape=(out(early + 1), out(window - early), out(window + 1), out(1)),
        in_specs=[anywhere, local],
        out_specs=(anywhere, anywhere, anywhere, local),
        scratch_shapes=[pltpu.SemaphoreType.DMA((5,))],
        compiler_params=params(),
        cost_estimate=cost(4096, 4096),
        name="prepared",
    )(psi, potential)


def partial_kernel(count, atoms, own, beta, b_x, b_d, potential, gram, out, weights_out, table, acc):
    place = lax.axis_index("space")
    x = lax.rem(place, 2)
    rows, width = potential.shape[1:]
    side = place ^ 1
    beyond = place - 1 + 2 * x
    tri = neighbour_sum(width, False).astype(BF16)
    acc[...] = jnp.zeros_like(acc)
    step = 8

    for k in range(2):
        plane = x if k == 0 else 1 - x
        outer, there = (b_d, beyond) if k == 0 else (b_x, side)
        u = (potential[plane] - 1.0) * 0.25

        def fill(i, carry):
            for j in range(step):
                p = i * step + j
                here = (jnp.abs(place - atoms[p]) <= 1).astype(F32)
                next_to = (jnp.abs(there - atoms[p]) <= 1).astype(F32)
                b32 = beta[p, plane].astype(F32) * here
                b = b32.astype(BF16)
                sides = beta[p, 1 - plane].astype(F32) * here + outer[p].astype(F32) * next_to
                whole = jnp.dot(b, tri, preferred_element_type=F32)
                whole = whole + jnp.dot(tri, b, preferred_element_type=F32)
                whole = whole + u * b32 - 0.125 * sides
                hi = whole.astype(BF16).astype(F32)
                for kind, value in enumerate((b32, hi, whole - hi)):
                    table[pl.ds((kind * count + p) * rows, rows)] = value
            return carry

        lax.fori_loop(0, count // step, fill, 0)

        def use(i, carry):
            totals = []
            for j in range(step):
                r = i * step + j
                weights = table[pl.ds(r, 3 * count, stride=rows)].astype(BF16)
                weights_out[plane, r] = weights
                totals.append(jnp.dot(weights, own[plane, r], preferred_element_type=F32))
            acc[...] += sum(totals[1:], totals[0])
            return carry

        lax.fori_loop(0, rows // step, use, 0)
    out[...] = jnp.zeros_like(out)
    out[0:count] = acc[0:count]
    out[count : 2 * count] = acc[count : 2 * count] + acc[2 * count : 3 * count]
    out[2 * count : 3 * count, 0:count] = gram[...]


def partials(count, atoms, own, beta, b_x, b_d, potential, gram):
    planes, rows, width, orbs = own.shape
    return pl.pallas_call(
        functools.partial(partial_kernel, count),
        out_shape=(
            jax.ShapeDtypeStruct((3 * count, orbs), F32),
            jax.ShapeDtypeStruct((planes, rows, 3 * count, width), BF16),
        ),
        in_specs=[pl.BlockSpec(memory_space=pltpu.SMEM)]
        + [pl.BlockSpec(memory_space=pltpu.VMEM)] * 6,
        out_specs=(pl.BlockSpec(memory_space=pltpu.VMEM),) * 2,
        scratch_shapes=[
            pltpu.VMEM((3 * count * rows, width), F32),
            pltpu.VMEM((3 * count, orbs), F32),
        ],
        compiler_params=params(),
        cost_estimate=cost(4096, 4096),
        name="partials",
    )(atoms, own, beta, b_x, b_d, potential, gram)


def coefficient_kernel(sums, strength, out):
    count, orbs = strength.shape
    coef1 = (strength[...] * sums[0:count]).astype(BF16)
    padded = coef1.astype(F32) * 0.25
    if orbs > count:
        padded = jnp.concatenate([padded, jnp.zeros((orbs - count, orbs), F32)], axis=0)
    proj2 = sums[count : 2 * count] + jnp.dot(
        sums[2 * count : 3 * count],
        padded,
        preferred_element_type=F32,
        precision=lax.Precision.HIGHEST,
    )
    out[0:count] = coef1
    out[count : 2 * count] = (strength[...] * proj2).astype(BF16)


def coefficients(sums, strength):
    count, orbs = strength.shape
    return pl.pallas_call(
        coefficient_kernel,
        out_shape=jax.ShapeDtypeStruct((2 * count, orbs), BF16),
        in_specs=[pl.BlockSpec(memory_space=pltpu.VMEM)] * 2,
        out_specs=pl.BlockSpec(memory_space=pltpu.VMEM),
        compiler_params=params(),
        cost_estimate=cost(4096, 4096),
        name="coefficients",
    )(sums, strength)


def nonlocal_kernel(unroll, a, b, c, d, q, weights, out):
    count, orbs = a.shape[0] // 2, a.shape[1]
    turned = sum(
        jnp.dot(ref[...], q[k], preferred_element_type=F32) for k, ref in enumerate((a, b, c, d))
    )
    turned = turned * 0.25
    one, two = turned[0:count], turned[count : 2 * count]
    right = jnp.concatenate([two, one, one], axis=0)
    hi = right.astype(BF16)
    lo = right - hi.astype(F32)
    right = jnp.concatenate([hi.astype(F32), lo], axis=1).astype(BF16)

    def step(i, carry):
        for k in range(unroll):
            r = i * unroll + k
            for plane in range(weights.shape[0]):
                both = lax.dot_general(
                    weights[plane, r], right, (((0,), (0,)), ((), ())), preferred_element_type=F32
                )
                out[plane, r] = both[:, :orbs] + both[:, orbs:]
        return carry

    lax.fori_loop(0, weights.shape[1] // unroll, step, 0)


def nonlocal_term(shape, coefs, q, weights):
    unroll = max(g for g in (1, 2, 4, 8) if weights.shape[1] % g == 0)
    return pl.pallas_call(
        functools.partial(nonlocal_kernel, unroll),
        out_shape=jax.ShapeDtypeStruct(shape, F32),
        in_specs=[pl.BlockSpec(memory_space=pltpu.VMEM)] * 6,
        out_specs=pl.BlockSpec(memory_space=pltpu.VMEM),
        compiler_params=params(),
        cost_estimate=cost(4096, 4096),
        name="nonlocal",
    )(*coefs, q, weights)


def filter_kernel(slabs, start, parts, joint, *refs):
    own, p_own, zo = refs[:3]
    xrs, zfs = refs[3 : 3 + parts], refs[3 + parts : 3 + 2 * parts]
    extra = 5 if parts > 1 else 3
    outs, scratch = refs[3 + 2 * parts : -extra], refs[-extra:]
    first, lines, diagonals = scratch[:3]
    place = lax.axis_index("space")
    x = lax.rem(place, 2)
    width = own.shape[2]
    cells = 2 * width
    half = own.shape[1] // 2
    orbs = own.shape[3]
    rows = outs[0].shape[1]
    base = (half - 2) * x
    lower = (place >= 2).astype(F32)
    upper = (place < slabs - 2).astype(F32)
    is_odd = x.astype(F32)
    has_zf = lower * (1.0 - is_odd) + upper * is_odd
    has_zo = upper * (1.0 - is_odd) + lower * is_odd
    if parts > 1:
        xr, zf = scratch[3], scratch[4]
        early = xrs[0].shape[1] - 1
        for target, pieces in ((xr, xrs), (zf, zfs)):
            target[:, 0:early] = pieces[0][:, 0:early]
            target[:, early:] = pieces[1][...]
        window = xr.shape[1] // 2
    else:
        xr, zf = xrs[0], zfs[0]
        window = (xr.shape[1] - 1) // 2
    for c in range(1, 7):
        plane = (c % 2) ^ x
        if c in (2, 3):
            block = p_own[plane, 0]
        else:
            ref = zfs[0] if c < 2 else (xrs[0] if c < 6 else zo)
            block = ref[plane, ref.shape[1] - 1]
        lines[c - 1] = block.astype(F32)
        for kind in range(2):
            even, odd = (lines[c - 1, pl.ds(k, half, stride=2)] for k in range(2))
            lanes = slice(64 * kind, 64 * kind + width)
            diagonals[c - 1, kind] = jnp.concatenate([even[:, lanes], odd[:, lanes]], axis=1)

    here = neighbour_sum(width, True)
    i = lax.broadcasted_iota(jnp.int32, (cells, cells), 0)
    diagonal = i == lax.broadcasted_iota(jnp.int32, (cells, cells), 1)

    def local(c, p):
        at = base // 2 + p
        hi = diagonals[c - 1, 0, pl.ds(at, 1)]
        lo = diagonals[c - 1, 1, pl.ds(at, 1)]
        return (
            jnp.where(diagonal, hi, here).astype(BF16),
            jnp.where(diagonal, lo, 0.0).astype(BF16),
        )

    def rows_of(c, w, n):
        plane = (c % 2) ^ x
        if c in (2, 3):
            return own[plane, pl.ds(base + w, n)]
        ref = zf if c < 2 else (xr if c < 6 else zo)
        return ref[plane, pl.ds(w, n)]

    def applied(pair, outer, zs, matrices):
        near = jnp.dot(matrices[0], pair, preferred_element_type=F32)
        near = near + jnp.dot(matrices[1], pair, preferred_element_type=F32)
        return near - 0.125 * (outer + zs)

    def step1(j, carry):
        p = start // 2 + x + j - 1
        q = jnp.clip(p, 0, window - 1)
        has_below = inside(p - 1, window)
        has_above = inside(p + 1, window)
        valid = inside(p, window)
        below = jnp.maximum(2 * q - 1, 0)
        above = jnp.minimum(2 * q + 2, 2 * window - 1)
        pair = [rows_of(c, 2 * q, 2).reshape(cells, orbs) for c in range(8)]
        vs = [v.astype(F32) for v in pair]
        for c in range(1, 7):
            outer = jnp.concatenate(
                [
                    rows_of(c, below, 1)[0].astype(F32) * has_below,
                    rows_of(c, above, 1)[0].astype(F32) * has_above,
                ],
                axis=0,
            )
            f = applied(pair[c], outer, vs[c - 1] + vs[c + 1], local(c, q))
            keep = valid
            if c == 1:
                keep = valid * has_zf
            if c == 6:
                keep = valid * has_zo
            first[c - 1, pl.ds(2 * j, 2)] = (f * keep).astype(BF16).reshape(2, width, orbs)
        return carry

    lax.fori_loop(0, rows // 2 + 2, step1, 0)

    def step2(j, carry):
        p = start // 2 + x + j
        pair = [first[c - 1, pl.ds(2 * j + 2, 2)].reshape(cells, orbs) for c in range(1, 7)]
        vs = [v.astype(F32) for v in pair]
        for c in range(2, 6):
            outer = jnp.concatenate(
                [first[c - 1, 2 * j + 1].astype(F32), first[c - 1, 2 * j + 4].astype(F32)], axis=0
            )
            f = applied(pair[c - 1], outer, vs[c - 2] + vs[c], local(c, p))
            f = f.astype(BF16).reshape(2, width, orbs)
            plane = (c % 2) ^ x
            if joint:
                outs[0][plane + (2 if c in (2, 3) else 0), pl.ds(2 * j, 2)] = f
            else:
                outs[1 if c in (2, 3) else 0][plane, pl.ds(2 * j, 2)] = f
        return carry

    lax.fori_loop(0, rows // 2, step2, 0)


def filtered(slabs, start, rows, joint, operands, xrs, zfs):
    own = operands[0]
    planes, _, width, orbs = own.shape
    parts = len(xrs)
    shape = (2 * planes if joint else planes, rows, width, orbs)
    out = (jax.ShapeDtypeStruct(shape, BF16),) * (1 if joint else 2)
    cells = 10 * rows * width
    scratch = [
        pltpu.VMEM((6, rows + 4, width, orbs), BF16),
        pltpu.VMEM((6, width, orbs), F32),
        pltpu.VMEM((6, 2, own.shape[1] // 2, 2 * width), F32),
    ]
    if parts > 1:
        window = xrs[0].shape[1] - 1 + xrs[1].shape[1]
        scratch += [pltpu.VMEM((planes, window, width, orbs), BF16)] * 2
    return pl.pallas_call(
        functools.partial(filter_kernel, slabs, start, parts, joint),
        out_shape=out,
        in_specs=[pl.BlockSpec(memory_space=pltpu.VMEM)] * (len(operands) + 2 * parts),
        out_specs=(pl.BlockSpec(memory_space=pltpu.VMEM),) * len(out),
        scratch_shapes=scratch,
        compiler_params=params(),
        cost_estimate=cost(2 * cells * 32 * orbs, cells * orbs * 4),
        name="filtered",
    )(*operands, *xrs, *zfs)


def rotate_kernel(group, *refs):
    a, b, c, d, q = refs[:5]
    outs = refs[5:]
    _, rows, width, orbs = a.shape
    planes = outs[0].shape[0]
    low = jnp.concatenate([q[0], q[1]], axis=0)
    high = jnp.concatenate([q[2], q[3]], axis=0)

    def one(j, carry):
        for plane in range(a.shape[0]):
            def take(ref):
                return ref[plane, pl.ds(group * j, group)].reshape(group * width, orbs)

            total = jnp.dot(
                jnp.concatenate([take(a), take(b)], axis=1), low, preferred_element_type=F32
            )
            total = total + jnp.dot(
                jnp.concatenate([take(c), take(d)], axis=1), high, preferred_element_type=F32
            )
            outs[plane // planes][plane % planes, pl.ds(group * j, group)] = total.astype(
                BF16
            ).reshape(group, width, orbs)
        return carry

    lax.fori_loop(0, rows // group, one, 0)


def rotated(blocks, q, pieces):
    a = blocks[0]
    size = a.size
    group = max(g for g in range(1, 7) if a.shape[1] % g == 0)
    out = jax.ShapeDtypeStruct((a.shape[0] // pieces, *a.shape[1:]), BF16)
    return pl.pallas_call(
        functools.partial(rotate_kernel, group),
        out_shape=(out,) * pieces,
        in_specs=[pl.BlockSpec(memory_space=pltpu.VMEM)] * 5,
        out_specs=(pl.BlockSpec(memory_space=pltpu.VMEM),) * pieces,
        compiler_params=params(),
        cost_estimate=cost(8 * size * a.shape[3], 10 * size),
        name="rotated",
    )(*blocks, q)


def assemble_kernel(half, term, *refs):
    out = refs[-1]
    pieces = (len(refs) - 1) // 2
    x = lax.rem(lax.axis_index("space"), 2)
    rows = refs[0].shape[1]
    for k in range(pieces):
        for ref, at in ((refs[k], half * x), (refs[pieces + k], half * (1 - x))):
            where = pl.ds(at + rows * k, rows)
            out[:, where] = (ref[...].astype(F32) + term[:, where]).astype(BF16)


def assembled(term, mine, theirs):
    return pl.pallas_call(
        functools.partial(assemble_kernel, term.shape[1] // 2),
        out_shape=jax.ShapeDtypeStruct(term.shape, BF16),
        in_specs=[pl.BlockSpec(memory_space=pltpu.VMEM)] * (1 + len(mine) + len(theirs)),
        out_specs=pl.BlockSpec(memory_space=pltpu.VMEM),
        compiler_params=params(),
        cost_estimate=cost(4096, 4096),
        name="assembled",
    )(term, *mine, *theirs)


def ordered(*arrays):
    return lax.optimization_barrier(arrays)


def shards(psi, potential, beta, strength, atom_slab, pattern, q_tiles):
    planes, width_x, width_y, orbs = psi.shape
    count = beta.shape[0]
    slabs = lax.axis_size("space")
    place = lax.axis_index("space")
    x = lax.rem(place, 2)
    half = width_x // 2
    window = half + 2
    rows = half // 2
    early = rows + 4

    def within(pairs):
        return [(i, j) for i, j in pairs if 0 <= j < slabs]

    swap = [(i, i ^ 1) for i in range(slabs)]
    own_way = within([(i, i + 2 if i % 2 else i - 2) for i in range(slabs)])
    other_way = within([(i, i - 2 if i % 2 else i + 2) for i in range(slabs)])
    raster = within([(i, i + 1 if i % 2 else i - 1) for i in range(slabs)])
    groups = lax.axis_size("orb")
    across = [(i, i ^ 2) for i in range(groups)]
    beside = [(i, i ^ 1) for i in range(groups)]
    mine = (half - 2) * x
    theirs = (half - 2) * (1 - x)

    to_x, to_x2, to_z, blocks = prepared(psi, potential, early)
    xr1 = lax.ppermute(to_x, "space", swap)
    zo = lax.ppermute(to_z, "space", own_way)
    far = lax.dynamic_index_in_dim(beta, x, 1, keepdims=False)
    near = lax.dynamic_index_in_dim(beta, 1 - x, 1, keepdims=False)
    active = jnp.abs(place - atom_slab) <= 1
    beta_m = jnp.where(active[:, None, None, None], beta, jnp.zeros_like(beta))
    gram = jnp.einsum("pzxy,qzxy->pq", beta_m, beta_m, preferred_element_type=F32)
    far, near, gram, xr1 = ordered(far, near, gram, xr1)
    zf1 = lax.ppermute(xr1, "space", other_way)
    second, _ = ordered(to_x2, xr1)
    xr2 = lax.ppermute(second, "space", swap)
    f_x = lax.ppermute(near, "space", swap)
    f_d = lax.ppermute(far, "space", raster)
    zf1_in, _ = ordered(zf1, xr2)
    zf2 = lax.ppermute(xr2, "space", other_way)
    strong = jnp.broadcast_to(strength[:, None], (count, orbs))

    me = lax.axis_index("orb")
    which = jnp.bitwise_xor(me, jnp.arange(groups, dtype=jnp.int32))
    rows_hot = (pattern[:, 0][:, None] == which[None, :]).astype(BF16)
    rows_hot = rows_hot * (pattern[:, 1] == me).astype(BF16)[:, None]
    q = jnp.einsum("ki,kab->iab", rows_hot, q_tiles, preferred_element_type=F32).astype(BF16)

    operands = (psi, blocks, zo)
    (block1,) = filtered(slabs, 0, rows, True, operands, (xr1,), (zf1_in,))
    y1 = lax.ppermute(block1, "orb", across)
    c1 = lax.ppermute(block1, "orb", beside)
    sums, weights = partials(count, atom_slab, psi, beta, f_x, f_d, potential, gram)
    xr2, sums = ordered(xr2, sums)
    give2, keep2 = filtered(slabs, rows, rows, False, operands, (xr1, xr2), (zf1, zf2))
    step = 1
    while step < slabs:
        sums = sums + lax.ppermute(sums, "space", [(i, i ^ step) for i in range(slabs)])
        step *= 2
    coefs = coefficients(sums, strong)
    cg = lax.ppermute(give2, "orb", beside)
    ck = lax.ppermute(keep2, "orb", beside)
    give_y, y1 = ordered(give2, y1)
    yg = lax.ppermute(give_y, "orb", across)
    yc1 = lax.ppermute(y1, "orb", beside)
    give1, keep1 = rotated((block1, c1, y1, yc1), q, 2)
    keep_y, yg, give1, coefs = ordered(keep2, yg, give1, coefs)
    got1 = lax.ppermute(give1, "space", swap)
    coefs_c = lax.ppermute(coefs, "orb", beside)
    coefs_y = lax.ppermute(jnp.concatenate([coefs, coefs_c], axis=0), "orb", across)
    coefs_yc, coefs_y = coefs_y[2 * count :], coefs_y[: 2 * count]
    term = nonlocal_term(psi.shape, (coefs, coefs_c, coefs_y, coefs_yc), q, weights)

    yk = lax.ppermute(keep_y, "orb", across)
    ycg = lax.ppermute(yg, "orb", beside)
    (give2,) = rotated((give2, cg, yg, ycg), q, 1)
    got2 = lax.ppermute(give2, "space", swap)
    yck = lax.ppermute(yk, "orb", beside)
    (keep2,) = rotated((keep2, ck, yk, yck), q, 1)
    return assembled(term, [keep1, keep2], [got1, got2])


def solution(mesh):
    placed = (
        P("space", None, None, "orb"),
        P("space", None, None),
        P(None, "space", None, None),
        P(),
        P(),
        P(),
        P(),
    )
    return jax.shard_map(
        shards, mesh=mesh, in_specs=placed, out_specs=P("space", None, None, "orb"), check_vma=False
    )
```

```python
import functools

import jax
import jax.numpy as jnp
from jax import lax
from jax.experimental import pallas as pl
from jax.experimental.pallas import tpu as pltpu
from jax.sharding import PartitionSpec as P

F32 = jnp.float32
BF16 = jnp.bfloat16
VMEM_LIMIT = 24 * 1024 * 1024
SHRINK = 16
FILTER = 100


def params():
    return pltpu.CompilerParams(vmem_limit_bytes=VMEM_LIMIT)


def cost(flops, moved):
    return pl.CostEstimate(flops=flops // SHRINK, bytes_accessed=moved // SHRINK, transcendentals=0)


def inside(p, window):
    return jnp.logical_and(p >= 0, p < window).astype(F32)


def neighbour_sum(width, pairs):
    n = (2 if pairs else 1) * width
    i = lax.broadcasted_iota(jnp.int32, (n, n), 0)
    j = lax.broadcasted_iota(jnp.int32, (n, n), 1)
    linked = jnp.abs(i - j) == 1
    if pairs:
        linked = jnp.logical_and(linked, (i < width) == (j < width))
        linked = jnp.logical_or(linked, jnp.abs(i - j) == width)
    return jnp.where(linked, -0.125, 0.0)


def prepare_kernel(early, psi, potential_far, to_x, to_x2, to_z, blocks, potential, sems):
    x = lax.rem(lax.axis_index("space"), 2)
    half = psi.shape[1] // 2
    window = half + 2
    mine, theirs = (half - 2) * x, (half - 2) * (1 - x)
    width = potential_far.shape[2]
    gap = jnp.zeros((potential_far.shape[1], 64 - width), F32)
    copies = [
        pltpu.make_async_copy(
            psi.at[:, pl.ds(theirs, early)], to_x.at[:, pl.ds(0, early)], sems.at[0]
        ),
        pltpu.make_async_copy(
            psi.at[:, pl.ds(mine, window)], to_z.at[:, pl.ds(0, window)], sems.at[1]
        ),
        pltpu.make_async_copy(
            psi.at[:, pl.ds(theirs + early, window - early)], to_x2, sems.at[2]
        ),
    ]
    fetch = pltpu.make_async_copy(potential_far, potential, sems.at[5])
    fetch.start()
    for copy in copies:
        copy.start()
    fetch.wait()
    for plane in range(blocks.shape[0]):
        u = (potential[plane] - 1.0) * 0.25
        hi = u.astype(BF16).astype(F32)
        blocks[plane, 0] = jnp.concatenate([hi, gap, u - hi, gap], axis=1).astype(BF16)
    more = [
        pltpu.make_async_copy(blocks, to_x.at[:, pl.ds(early, 1)], sems.at[3]),
        pltpu.make_async_copy(blocks, to_z.at[:, pl.ds(window, 1)], sems.at[4]),
    ]
    for copy in more:
        copy.start()
    for copy in copies + more:
        copy.wait()


def prepared(psi, potential, early):
    planes, width_x, width_y, orbs = psi.shape
    window = width_x // 2 + 2

    def out(rows):
        return jax.ShapeDtypeStruct((planes, rows, width_y, orbs), BF16)

    anywhere = pl.BlockSpec(memory_space=pl.ANY)
    local = pl.BlockSpec(memory_space=pltpu.VMEM)
    return pl.pallas_call(
        functools.partial(prepare_kernel, early),
        out_shape=(out(early + 1), out(window - early), out(window + 1), out(1)),
        in_specs=[pl.BlockSpec(memory_space=pltpu.MemorySpace.HBM)] * 2,
        out_specs=(anywhere, anywhere, anywhere, local),
        scratch_shapes=[pltpu.VMEM(potential.shape, F32), pltpu.SemaphoreType.DMA((6,))],
        compiler_params=params(),
        cost_estimate=cost(4096, 4096),
        name="prepared",
    )(*(pltpu.with_memory_space_constraint(a, pltpu.MemorySpace.HBM) for a in (psi, potential)))


def partial_kernel(count, atoms, own, beta, b_x, b_d, potential, gram, out, weights_out, table, acc):
    place = lax.axis_index("space")
    x = lax.rem(place, 2)
    rows, width = potential.shape[1:]
    side = place ^ 1
    beyond = place - 1 + 2 * x
    tri = neighbour_sum(width, False).astype(BF16)
    acc[...] = jnp.zeros_like(acc)
    step = 8

    for k in range(2):
        plane = x if k == 0 else 1 - x
        outer, there = (b_d, beyond) if k == 0 else (b_x, side)
        u = (potential[plane] - 1.0) * 0.25

        def fill(i, carry):
            for j in range(step):
                p = i * step + j
                here = (jnp.abs(place - atoms[p]) <= 1).astype(F32)
                next_to = (jnp.abs(there - atoms[p]) <= 1).astype(F32)
                b32 = beta[p, plane].astype(F32) * here
                b = b32.astype(BF16)
                sides = beta[p, 1 - plane].astype(F32) * here + outer[p].astype(F32) * next_to
                whole = jnp.dot(b, tri, preferred_element_type=F32)
                whole = whole + jnp.dot(tri, b, preferred_element_type=F32)
                whole = whole + u * b32 - 0.125 * sides
                hi = whole.astype(BF16).astype(F32)
                for kind, value in enumerate((b32, hi, whole - hi)):
                    table[pl.ds((kind * count + p) * rows, rows)] = value
            return carry

        lax.fori_loop(0, count // step, fill, 0)

        def use(i, carry):
            totals = []
            for j in range(step):
                r = i * step + j
                weights = table[pl.ds(r, 3 * count, stride=rows)].astype(BF16)
                weights_out[plane, r] = weights
                totals.append(jnp.dot(weights, own[plane, r], preferred_element_type=F32))
            acc[...] += sum(totals[1:], totals[0])
            return carry

        lax.fori_loop(0, rows // step, use, 0)
    out[...] = jnp.zeros_like(out)
    out[0:count] = acc[0:count]
    out[count : 2 * count] = acc[count : 2 * count] + acc[2 * count : 3 * count]
    out[2 * count : 3 * count, 0:count] = gram[...]


def partials(count, atoms, own, beta, b_x, b_d, potential, gram):
    planes, rows, width, orbs = own.shape
    return pl.pallas_call(
        functools.partial(partial_kernel, count),
        out_shape=(
            jax.ShapeDtypeStruct((3 * count, orbs), F32),
            jax.ShapeDtypeStruct((planes, rows, 3 * count, width), BF16),
        ),
        in_specs=[pl.BlockSpec(memory_space=pltpu.SMEM)]
        + [pl.BlockSpec(memory_space=pltpu.VMEM)] * 6,
        out_specs=(pl.BlockSpec(memory_space=pltpu.VMEM),) * 2,
        scratch_shapes=[
            pltpu.VMEM((3 * count * rows, width), F32),
            pltpu.VMEM((3 * count, orbs), F32),
        ],
        compiler_params=params(),
        cost_estimate=cost(4096, 4096),
        name="partials",
    )(atoms, own, beta, b_x, b_d, potential, gram)


def coefficient_kernel(sums, strength, out):
    count, orbs = strength.shape
    coef1 = (strength[...] * sums[0:count]).astype(BF16)
    padded = coef1.astype(F32) * 0.25
    if orbs > count:
        padded = jnp.concatenate([padded, jnp.zeros((orbs - count, orbs), F32)], axis=0)
    proj2 = sums[count : 2 * count] + jnp.dot(
        sums[2 * count : 3 * count],
        padded,
        preferred_element_type=F32,
        precision=lax.Precision.HIGHEST,
    )
    out[0:count] = coef1
    out[count : 2 * count] = (strength[...] * proj2).astype(BF16)


def coefficients(sums, strength):
    count, orbs = strength.shape
    return pl.pallas_call(
        coefficient_kernel,
        out_shape=jax.ShapeDtypeStruct((2 * count, orbs), BF16),
        in_specs=[pl.BlockSpec(memory_space=pltpu.VMEM)] * 2,
        out_specs=pl.BlockSpec(memory_space=pltpu.VMEM),
        compiler_params=params(),
        cost_estimate=cost(4096, 4096),
        name="coefficients",
    )(sums, strength)


def nonlocal_kernel(unroll, a, b, c, d, q, weights, out):
    count, orbs = a.shape[0] // 2, a.shape[1]
    turned = sum(
        jnp.dot(ref[...], q[k], preferred_element_type=F32) for k, ref in enumerate((a, b, c, d))
    )
    turned = turned * 0.25
    one, two = turned[0:count], turned[count : 2 * count]
    right = jnp.concatenate([two, one, one], axis=0)
    hi = right.astype(BF16)
    lo = right - hi.astype(F32)
    right = jnp.concatenate([hi.astype(F32), lo], axis=1).astype(BF16)

    def step(i, carry):
        for k in range(unroll):
            r = i * unroll + k
            for plane in range(weights.shape[0]):
                both = lax.dot_general(
                    weights[plane, r], right, (((0,), (0,)), ((), ())), preferred_element_type=F32
                )
                out[plane, r] = both[:, :orbs] + both[:, orbs:]
        return carry

    lax.fori_loop(0, weights.shape[1] // unroll, step, 0)


def nonlocal_term(shape, coefs, q, weights):
    unroll = max(g for g in (1, 2, 4, 8) if weights.shape[1] % g == 0)
    return pl.pallas_call(
        functools.partial(nonlocal_kernel, unroll),
        out_shape=jax.ShapeDtypeStruct(shape, F32),
        in_specs=[pl.BlockSpec(memory_space=pltpu.VMEM)] * 6,
        out_specs=pl.BlockSpec(memory_space=pltpu.VMEM),
        compiler_params=params(),
        cost_estimate=cost(4096, 4096),
        name="nonlocal",
    )(*coefs, q, weights)


def filter_kernel(slabs, start, parts, joint, *refs):
    own, p_own, zo = refs[:3]
    xrs, zfs = refs[3 : 3 + parts], refs[3 + parts : 3 + 2 * parts]
    extra = 5 if parts > 1 else 3
    outs, scratch = refs[3 + 2 * parts : -extra], refs[-extra:]
    first, lines, diagonals = scratch[:3]
    place = lax.axis_index("space")
    x = lax.rem(place, 2)
    width = own.shape[2]
    cells = 2 * width
    half = own.shape[1] // 2
    orbs = own.shape[3]
    rows = outs[0].shape[1]
    base = (half - 2) * x
    lower = (place >= 2).astype(F32)
    upper = (place < slabs - 2).astype(F32)
    is_odd = x.astype(F32)
    has_zf = lower * (1.0 - is_odd) + upper * is_odd
    has_zo = upper * (1.0 - is_odd) + lower * is_odd
    if parts > 1:
        xr, zf = scratch[3], scratch[4]
        early = xrs[0].shape[1] - 1
        for target, pieces in ((xr, xrs), (zf, zfs)):
            target[:, 0:early] = pieces[0][:, 0:early]
            target[:, early:] = pieces[1][...]
        window = xr.shape[1] // 2
    else:
        xr, zf = xrs[0], zfs[0]
        window = (xr.shape[1] - 1) // 2
    for c in range(1, 7):
        plane = (c % 2) ^ x
        if c in (2, 3):
            block = p_own[plane, 0]
        else:
            ref = zfs[0] if c < 2 else (xrs[0] if c < 6 else zo)
            block = ref[plane, ref.shape[1] - 1]
        lines[c - 1] = block.astype(F32)
        for kind in range(2):
            even, odd = (lines[c - 1, pl.ds(k, half, stride=2)] for k in range(2))
            lanes = slice(64 * kind, 64 * kind + width)
            diagonals[c - 1, kind] = jnp.concatenate([even[:, lanes], odd[:, lanes]], axis=1)

    here = neighbour_sum(width, True)
    i = lax.broadcasted_iota(jnp.int32, (cells, cells), 0)
    diagonal = i == lax.broadcasted_iota(jnp.int32, (cells, cells), 1)

    def local(c, p):
        at = base // 2 + p
        hi = diagonals[c - 1, 0, pl.ds(at, 1)]
        lo = diagonals[c - 1, 1, pl.ds(at, 1)]
        return (
            jnp.where(diagonal, hi, here).astype(BF16),
            jnp.where(diagonal, lo, 0.0).astype(BF16),
        )

    def rows_of(c, w, n):
        plane = (c % 2) ^ x
        if c in (2, 3):
            return own[plane, pl.ds(base + w, n)]
        ref = zf if c < 2 else (xr if c < 6 else zo)
        return ref[plane, pl.ds(w, n)]

    def applied(pair, outer, zs, matrices):
        near = jnp.dot(matrices[0], pair, preferred_element_type=F32)
        near = near + jnp.dot(matrices[1], pair, preferred_element_type=F32)
        return near - 0.125 * (outer + zs)

    def step1(j, carry):
        p = start // 2 + x + j - 1
        q = jnp.clip(p, 0, window - 1)
        has_below = inside(p - 1, window)
        has_above = inside(p + 1, window)
        valid = inside(p, window)
        below = jnp.maximum(2 * q - 1, 0)
        above = jnp.minimum(2 * q + 2, 2 * window - 1)
        pair = [rows_of(c, 2 * q, 2).reshape(cells, orbs) for c in range(8)]
        vs = [v.astype(F32) for v in pair]
        for c in range(1, 7):
            outer = jnp.concatenate(
                [
                    rows_of(c, below, 1)[0].astype(F32) * has_below,
                    rows_of(c, above, 1)[0].astype(F32) * has_above,
                ],
                axis=0,
            )
            f = applied(pair[c], outer, vs[c - 1] + vs[c + 1], local(c, q))
            keep = valid
            if c == 1:
                keep = valid * has_zf
            if c == 6:
                keep = valid * has_zo
            first[c - 1, pl.ds(2 * j, 2)] = (f * keep).astype(BF16).reshape(2, width, orbs)
        return carry

    lax.fori_loop(0, rows // 2 + 2, step1, 0)

    def step2(j, carry):
        p = start // 2 + x + j
        pair = [first[c - 1, pl.ds(2 * j + 2, 2)].reshape(cells, orbs) for c in range(1, 7)]
        vs = [v.astype(F32) for v in pair]
        for c in range(2, 6):
            outer = jnp.concatenate(
                [first[c - 1, 2 * j + 1].astype(F32), first[c - 1, 2 * j + 4].astype(F32)], axis=0
            )
            f = applied(pair[c - 1], outer, vs[c - 2] + vs[c], local(c, p))
            f = f.astype(BF16).reshape(2, width, orbs)
            plane = (c % 2) ^ x
            if joint:
                outs[0][plane + (2 if c in (2, 3) else 0), pl.ds(2 * j, 2)] = f
            else:
                outs[1 if c in (2, 3) else 0][plane, pl.ds(2 * j, 2)] = f
        return carry

    lax.fori_loop(0, rows // 2, step2, 0)


def filtered(slabs, start, rows, joint, operands, xrs, zfs):
    own = operands[0]
    planes, _, width, orbs = own.shape
    parts = len(xrs)
    shape = (2 * planes if joint else planes, rows, width, orbs)
    out = (jax.ShapeDtypeStruct(shape, BF16),) * (1 if joint else 2)
    cells = 10 * rows * width
    scratch = [
        pltpu.VMEM((6, rows + 4, width, orbs), BF16),
        pltpu.VMEM((6, width, orbs), F32),
        pltpu.VMEM((6, 2, own.shape[1] // 2, 2 * width), F32),
    ]
    if parts > 1:
        window = xrs[0].shape[1] - 1 + xrs[1].shape[1]
        scratch += [pltpu.VMEM((planes, window, width, orbs), BF16)] * 2
    return pl.pallas_call(
        functools.partial(filter_kernel, slabs, start, parts, joint),
        out_shape=out,
        in_specs=[pl.BlockSpec(memory_space=pltpu.VMEM)] * (len(operands) + 2 * parts),
        out_specs=(pl.BlockSpec(memory_space=pltpu.VMEM),) * len(out),
        scratch_shapes=scratch,
        compiler_params=params(),
        cost_estimate=cost(2 * cells * 32 * orbs, FILTER * cells * orbs * 4),
        name="filtered",
    )(*operands, *xrs, *zfs)


def rotate_kernel(group, *refs):
    a, b, c, d, q = refs[:5]
    outs = refs[5:]
    _, rows, width, orbs = a.shape
    planes = outs[0].shape[0]
    low = jnp.concatenate([q[0], q[1]], axis=0)
    high = jnp.concatenate([q[2], q[3]], axis=0)

    def one(j, carry):
        for plane in range(a.shape[0]):
            def take(ref):
                return ref[plane, pl.ds(group * j, group)].reshape(group * width, orbs)

            total = jnp.dot(
                jnp.concatenate([take(a), take(b)], axis=1), low, preferred_element_type=F32
            )
            total = total + jnp.dot(
                jnp.concatenate([take(c), take(d)], axis=1), high, preferred_element_type=F32
            )
            outs[plane // planes][plane % planes, pl.ds(group * j, group)] = total.astype(
                BF16
            ).reshape(group, width, orbs)
        return carry

    lax.fori_loop(0, rows // group, one, 0)


def rotated(blocks, q, pieces):
    a = blocks[0]
    size = a.size
    group = max(g for g in range(1, 7) if a.shape[1] % g == 0)
    out = jax.ShapeDtypeStruct((a.shape[0] // pieces, *a.shape[1:]), BF16)
    return pl.pallas_call(
        functools.partial(rotate_kernel, group),
        out_shape=(out,) * pieces,
        in_specs=[pl.BlockSpec(memory_space=pltpu.VMEM)] * 5,
        out_specs=(pl.BlockSpec(memory_space=pltpu.VMEM),) * pieces,
        compiler_params=params(),
        cost_estimate=cost(8 * size * a.shape[3], 10 * size),
        name="rotated",
    )(*blocks, q)


def assemble_kernel(half, term, *refs):
    out = refs[-1]
    pieces = (len(refs) - 1) // 2
    x = lax.rem(lax.axis_index("space"), 2)
    start = 0
    for k in range(pieces):
        rows = refs[k].shape[1]
        start += refs[k - 1].shape[1] if k else 0
        for ref, at in ((refs[k], half * x), (refs[pieces + k], half * (1 - x))):
            where = pl.ds(at + start, rows)
            out[:, where] = (ref[...].astype(F32) + term[:, where]).astype(BF16)


def assembled(term, mine, theirs):
    return pl.pallas_call(
        functools.partial(assemble_kernel, term.shape[1] // 2),
        out_shape=jax.ShapeDtypeStruct(term.shape, BF16),
        in_specs=[pl.BlockSpec(memory_space=pltpu.VMEM)] * (1 + len(mine) + len(theirs)),
        out_specs=pl.BlockSpec(memory_space=pltpu.VMEM),
        compiler_params=params(),
        cost_estimate=cost(4096, 4096),
        name="assembled",
    )(term, *mine, *theirs)


def ordered(*arrays):
    return lax.optimization_barrier(arrays)


def shards(psi, potential, beta, strength, atom_slab, pattern, q_tiles):
    planes, width_x, width_y, orbs = psi.shape
    count = beta.shape[0]
    slabs = lax.axis_size("space")
    place = lax.axis_index("space")
    x = lax.rem(place, 2)
    half = width_x // 2
    window = half + 2
    rows1 = half * 5 // 24 * 2
    rows2 = half - rows1
    early = rows1 + 4

    def within(pairs):
        return [(i, j) for i, j in pairs if 0 <= j < slabs]

    swap = [(i, i ^ 1) for i in range(slabs)]
    own_way = within([(i, i + 2 if i % 2 else i - 2) for i in range(slabs)])
    other_way = within([(i, i - 2 if i % 2 else i + 2) for i in range(slabs)])
    raster = within([(i, i + 1 if i % 2 else i - 1) for i in range(slabs)])
    groups = lax.axis_size("orb")
    across = [(i, i ^ 2) for i in range(groups)]
    beside = [(i, i ^ 1) for i in range(groups)]
    mine = (half - 2) * x
    theirs = (half - 2) * (1 - x)

    to_x, to_x2, to_z, blocks = prepared(psi, potential, early)
    xr1 = lax.ppermute(to_x, "space", swap)
    zo = lax.ppermute(to_z, "space", own_way)
    far = lax.dynamic_index_in_dim(beta, x, 1, keepdims=False)
    near = lax.dynamic_index_in_dim(beta, 1 - x, 1, keepdims=False)
    active = jnp.abs(place - atom_slab) <= 1
    beta_m = jnp.where(active[:, None, None, None], beta, jnp.zeros_like(beta))
    gram = jnp.einsum("pzxy,qzxy->pq", beta_m, beta_m, preferred_element_type=F32)
    far, near, gram, xr1 = ordered(far, near, gram, xr1)
    zf1 = lax.ppermute(xr1, "space", other_way)
    second, _ = ordered(to_x2, xr1)
    xr2 = lax.ppermute(second, "space", swap)
    zf2 = lax.ppermute(xr2, "space", other_way)
    f_x = lax.ppermute(near, "space", swap)
    f_d = lax.ppermute(far, "space", raster)
    strong = jnp.broadcast_to(strength[:, None], (count, orbs))

    me = lax.axis_index("orb")
    which = jnp.bitwise_xor(me, jnp.arange(groups, dtype=jnp.int32))
    rows_hot = (pattern[:, 0][:, None] == which[None, :]).astype(BF16)
    rows_hot = rows_hot * (pattern[:, 1] == me).astype(BF16)[:, None]
    q = jnp.einsum("ki,kab->iab", rows_hot, q_tiles, preferred_element_type=F32).astype(BF16)

    sums, weights = partials(count, atom_slab, psi, beta, f_x, f_d, potential, gram)
    zf1, sums, _ = ordered(zf1, sums, xr2)
    operands = (psi, blocks, zo)
    (block1,) = filtered(slabs, 0, rows1, True, operands, (xr1,), (zf1,))
    y1 = lax.ppermute(block1, "orb", across)
    c1 = lax.ppermute(block1, "orb", beside)
    give2, keep2 = filtered(slabs, rows1, rows2, False, operands, (xr1, xr2), (zf1, zf2))
    step = 1
    while step < slabs:
        sums = sums + lax.ppermute(sums, "space", [(i, i ^ step) for i in range(slabs)])
        step *= 2
    coefs = coefficients(sums, strong)
    cg = lax.ppermute(give2, "orb", beside)
    ck = lax.ppermute(keep2, "orb", beside)
    yg = lax.ppermute(give2, "orb", across)
    yc1 = lax.ppermute(y1, "orb", beside)
    give1, keep1 = rotated((block1, c1, y1, yc1), q, 2)
    keep_y, yg = ordered(keep2, yg)
    yk = lax.ppermute(keep_y, "orb", across)
    yg, give1, coefs = ordered(yg, give1, coefs)
    ycg = lax.ppermute(yg, "orb", beside)
    got1 = lax.ppermute(give1, "space", swap)
    coefs_c = lax.ppermute(coefs, "orb", beside)
    coefs_y = lax.ppermute(jnp.concatenate([coefs, coefs_c], axis=0), "orb", across)
    coefs_yc, coefs_y = coefs_y[2 * count :], coefs_y[: 2 * count]
    term = nonlocal_term(psi.shape, (coefs, coefs_c, coefs_y, coefs_yc), q, weights)
    (give2,) = rotated((give2, cg, yg, ycg), q, 1)
    got2 = lax.ppermute(give2, "space", swap)
    yck = lax.ppermute(yk, "orb", beside)
    (keep2,) = rotated((keep2, ck, yk, yck), q, 1)
    return assembled(term, [keep1, keep2], [got1, got2])


def solution(mesh):
    placed = (
        P("space", None, None, "orb"),
        P("space", None, None),
        P(None, "space", None, None),
        P(),
        P(),
        P(),
        P(),
    )
    return jax.shard_map(
        shards, mesh=mesh, in_specs=placed, out_specs=P("space", None, None, "orb"), check_vma=False
    )
```

```python
import functools

import jax
import jax.numpy as jnp
from jax import lax
from jax.experimental import pallas as pl
from jax.experimental.pallas import tpu as pltpu
from jax.sharding import PartitionSpec as P

F32 = jnp.float32
BF16 = jnp.bfloat16
VMEM_LIMIT = 24 * 1024 * 1024
SHRINK = 16
FILTER = 100


def params():
    return pltpu.CompilerParams(vmem_limit_bytes=VMEM_LIMIT)


def cost(flops, moved):
    return pl.CostEstimate(flops=flops // SHRINK, bytes_accessed=moved // SHRINK, transcendentals=0)


def inside(p, window):
    return jnp.logical_and(p >= 0, p < window).astype(F32)


def neighbour_sum(width, pairs):
    n = (2 if pairs else 1) * width
    i = lax.broadcasted_iota(jnp.int32, (n, n), 0)
    j = lax.broadcasted_iota(jnp.int32, (n, n), 1)
    linked = jnp.abs(i - j) == 1
    if pairs:
        linked = jnp.logical_and(linked, (i < width) == (j < width))
        linked = jnp.logical_or(linked, jnp.abs(i - j) == width)
    return jnp.where(linked, -0.125, 0.0)


def prepare_kernel(early, psi, potential_far, to_x, to_x2, to_z, blocks, potential, sems):
    x = lax.rem(lax.axis_index("space"), 2)
    half = psi.shape[1] // 2
    window = half + 2
    mine, theirs = (half - 2) * x, (half - 2) * (1 - x)
    width = potential_far.shape[2]
    gap = jnp.zeros((potential_far.shape[1], 64 - width), F32)
    copies = [
        pltpu.make_async_copy(
            psi.at[:, pl.ds(theirs, early)], to_x.at[:, pl.ds(0, early)], sems.at[0]
        ),
        pltpu.make_async_copy(
            psi.at[:, pl.ds(mine, window)], to_z.at[:, pl.ds(0, window)], sems.at[1]
        ),
        pltpu.make_async_copy(
            psi.at[:, pl.ds(theirs + early, window - early)], to_x2, sems.at[2]
        ),
    ]
    fetch = pltpu.make_async_copy(potential_far, potential, sems.at[5])
    fetch.start()
    for copy in copies:
        copy.start()
    fetch.wait()
    for plane in range(blocks.shape[0]):
        u = (potential[plane] - 1.0) * 0.25
        hi = u.astype(BF16).astype(F32)
        blocks[plane, 0] = jnp.concatenate([hi, gap, u - hi, gap], axis=1).astype(BF16)
    more = [
        pltpu.make_async_copy(blocks, to_x.at[:, pl.ds(early, 1)], sems.at[3]),
        pltpu.make_async_copy(blocks, to_z.at[:, pl.ds(window, 1)], sems.at[4]),
    ]
    for copy in more:
        copy.start()
    for copy in copies + more:
        copy.wait()


def prepared(psi, potential, early):
    planes, width_x, width_y, orbs = psi.shape
    window = width_x // 2 + 2

    def out(rows):
        return jax.ShapeDtypeStruct((planes, rows, width_y, orbs), BF16)

    local = pl.BlockSpec(memory_space=pltpu.VMEM)
    return pl.pallas_call(
        functools.partial(prepare_kernel, early),
        out_shape=(out(early + 1), out(window - early), out(window + 1), out(1)),
        in_specs=[pl.BlockSpec(memory_space=pltpu.MemorySpace.HBM)] * 2,
        out_specs=(local,) * 4,
        scratch_shapes=[pltpu.VMEM(potential.shape, F32), pltpu.SemaphoreType.DMA((6,))],
        compiler_params=params(),
        cost_estimate=cost(4096, 4096),
        name="prepared",
    )(*(pltpu.with_memory_space_constraint(a, pltpu.MemorySpace.HBM) for a in (psi, potential)))


def partial_kernel(count, atoms, own, beta, b_x, b_d, potential, gram, out, weights_out, table, acc):
    place = lax.axis_index("space")
    x = lax.rem(place, 2)
    rows, width = potential.shape[1:]
    side = place ^ 1
    beyond = place - 1 + 2 * x
    tri = neighbour_sum(width, False).astype(BF16)
    acc[...] = jnp.zeros_like(acc)
    step = 8

    for k in range(2):
        plane = x if k == 0 else 1 - x
        outer, there = (b_d, beyond) if k == 0 else (b_x, side)
        u = (potential[plane] - 1.0) * 0.25

        def fill(i, carry):
            for j in range(step):
                p = i * step + j
                here = (jnp.abs(place - atoms[p]) <= 1).astype(F32)
                next_to = (jnp.abs(there - atoms[p]) <= 1).astype(F32)
                b32 = beta[p, plane].astype(F32) * here
                b = b32.astype(BF16)
                sides = beta[p, 1 - plane].astype(F32) * here + outer[p].astype(F32) * next_to
                whole = jnp.dot(b, tri, preferred_element_type=F32)
                whole = whole + jnp.dot(tri, b, preferred_element_type=F32)
                whole = whole + u * b32 - 0.125 * sides
                hi = whole.astype(BF16).astype(F32)
                for kind, value in enumerate((b32, hi, whole - hi)):
                    table[pl.ds((kind * count + p) * rows, rows)] = value
            return carry

        lax.fori_loop(0, count // step, fill, 0)

        def use(i, carry):
            totals = []
            for j in range(step):
                r = i * step + j
                weights = table[pl.ds(r, 3 * count, stride=rows)].astype(BF16)
                weights_out[plane, r] = weights
                totals.append(jnp.dot(weights, own[plane, r], preferred_element_type=F32))
            acc[...] += sum(totals[1:], totals[0])
            return carry

        lax.fori_loop(0, rows // step, use, 0)
    out[...] = jnp.zeros_like(out)
    out[0:count] = acc[0:count]
    out[count : 2 * count] = acc[count : 2 * count] + acc[2 * count : 3 * count]
    out[2 * count : 3 * count, 0:count] = gram[...]


def partials(count, atoms, own, beta, b_x, b_d, potential, gram):
    planes, rows, width, orbs = own.shape
    return pl.pallas_call(
        functools.partial(partial_kernel, count),
        out_shape=(
            jax.ShapeDtypeStruct((3 * count, orbs), F32),
            jax.ShapeDtypeStruct((planes, rows, 3 * count, width), BF16),
        ),
        in_specs=[pl.BlockSpec(memory_space=pltpu.SMEM)]
        + [pl.BlockSpec(memory_space=pltpu.VMEM)] * 6,
        out_specs=(pl.BlockSpec(memory_space=pltpu.VMEM),) * 2,
        scratch_shapes=[
            pltpu.VMEM((3 * count * rows, width), F32),
            pltpu.VMEM((3 * count, orbs), F32),
        ],
        compiler_params=params(),
        cost_estimate=cost(4096, 4096),
        name="partials",
    )(atoms, own, beta, b_x, b_d, potential, gram)


def coefficient_kernel(sums, strength, out):
    count, orbs = strength.shape
    coef1 = (strength[...] * sums[0:count]).astype(BF16)
    padded = coef1.astype(F32) * 0.25
    if orbs > count:
        padded = jnp.concatenate([padded, jnp.zeros((orbs - count, orbs), F32)], axis=0)
    proj2 = sums[count : 2 * count] + jnp.dot(
        sums[2 * count : 3 * count],
        padded,
        preferred_element_type=F32,
        precision=lax.Precision.HIGHEST,
    )
    out[0:count] = coef1
    out[count : 2 * count] = (strength[...] * proj2).astype(BF16)


def coefficients(sums, strength):
    count, orbs = strength.shape
    return pl.pallas_call(
        coefficient_kernel,
        out_shape=jax.ShapeDtypeStruct((2 * count, orbs), BF16),
        in_specs=[pl.BlockSpec(memory_space=pltpu.VMEM)] * 2,
        out_specs=pl.BlockSpec(memory_space=pltpu.VMEM),
        compiler_params=params(),
        cost_estimate=cost(4096, 4096),
        name="coefficients",
    )(sums, strength)


def nonlocal_kernel(unroll, a, b, c, d, q, weights, out):
    count, orbs = a.shape[0] // 2, a.shape[1]
    turned = sum(
        jnp.dot(ref[...], q[k], preferred_element_type=F32) for k, ref in enumerate((a, b, c, d))
    )
    turned = turned * 0.25
    one, two = turned[0:count], turned[count : 2 * count]
    right = jnp.concatenate([two, one, one], axis=0)
    hi = right.astype(BF16)
    lo = right - hi.astype(F32)
    right = jnp.concatenate([hi.astype(F32), lo], axis=1).astype(BF16)

    def step(i, carry):
        for k in range(unroll):
            r = i * unroll + k
            for plane in range(weights.shape[0]):
                both = lax.dot_general(
                    weights[plane, r], right, (((0,), (0,)), ((), ())), preferred_element_type=F32
                )
                out[plane, r] = both[:, :orbs] + both[:, orbs:]
        return carry

    lax.fori_loop(0, weights.shape[1] // unroll, step, 0)


def nonlocal_term(shape, coefs, q, weights):
    unroll = max(g for g in (1, 2, 4, 8) if weights.shape[1] % g == 0)
    return pl.pallas_call(
        functools.partial(nonlocal_kernel, unroll),
        out_shape=jax.ShapeDtypeStruct(shape, F32),
        in_specs=[pl.BlockSpec(memory_space=pltpu.VMEM)] * 6,
        out_specs=pl.BlockSpec(memory_space=pltpu.VMEM),
        compiler_params=params(),
        cost_estimate=cost(4096, 4096),
        name="nonlocal",
    )(*coefs, q, weights)


def filter_kernel(slabs, start, parts, joint, *refs):
    own, p_own, zo = refs[:3]
    xrs, zfs = refs[3 : 3 + parts], refs[3 + parts : 3 + 2 * parts]
    extra = 5 if parts > 1 else 3
    outs, scratch = refs[3 + 2 * parts : -extra], refs[-extra:]
    first, lines, diagonals = scratch[:3]
    place = lax.axis_index("space")
    x = lax.rem(place, 2)
    width = own.shape[2]
    cells = 2 * width
    half = own.shape[1] // 2
    orbs = own.shape[3]
    rows = outs[0].shape[1]
    base = (half - 2) * x
    lower = (place >= 2).astype(F32)
    upper = (place < slabs - 2).astype(F32)
    is_odd = x.astype(F32)
    has_zf = lower * (1.0 - is_odd) + upper * is_odd
    has_zo = upper * (1.0 - is_odd) + lower * is_odd
    if parts > 1:
        xr, zf = scratch[3], scratch[4]
        early = xrs[0].shape[1] - 1
        for target, pieces in ((xr, xrs), (zf, zfs)):
            target[:, 0:early] = pieces[0][:, 0:early]
            target[:, early:] = pieces[1][...]
        window = xr.shape[1] // 2
    else:
        xr, zf = xrs[0], zfs[0]
        window = (xr.shape[1] - 1) // 2
    for c in range(1, 7):
        plane = (c % 2) ^ x
        if c in (2, 3):
            block = p_own[plane, 0]
        else:
            ref = zfs[0] if c < 2 else (xrs[0] if c < 6 else zo)
            block = ref[plane, ref.shape[1] - 1]
        lines[c - 1] = block.astype(F32)
        for kind in range(2):
            even, odd = (lines[c - 1, pl.ds(k, half, stride=2)] for k in range(2))
            lanes = slice(64 * kind, 64 * kind + width)
            diagonals[c - 1, kind] = jnp.concatenate([even[:, lanes], odd[:, lanes]], axis=1)

    here = neighbour_sum(width, True)
    i = lax.broadcasted_iota(jnp.int32, (cells, cells), 0)
    diagonal = i == lax.broadcasted_iota(jnp.int32, (cells, cells), 1)

    def local(c, p):
        at = base // 2 + p
        hi = diagonals[c - 1, 0, pl.ds(at, 1)]
        lo = diagonals[c - 1, 1, pl.ds(at, 1)]
        return (
            jnp.where(diagonal, hi, here).astype(BF16),
            jnp.where(diagonal, lo, 0.0).astype(BF16),
        )

    def rows_of(c, w, n):
        plane = (c % 2) ^ x
        if c in (2, 3):
            return own[plane, pl.ds(base + w, n)]
        ref = zf if c < 2 else (xr if c < 6 else zo)
        return ref[plane, pl.ds(w, n)]

    def applied(pair, outer, zs, matrices):
        near = jnp.dot(matrices[0], pair, preferred_element_type=F32)
        near = near + jnp.dot(matrices[1], pair, preferred_element_type=F32)
        return near - 0.125 * (outer + zs)

    def step1(j, carry):
        p = start // 2 + x + j - 1
        q = jnp.clip(p, 0, window - 1)
        has_below = inside(p - 1, window)
        has_above = inside(p + 1, window)
        valid = inside(p, window)
        below = jnp.maximum(2 * q - 1, 0)
        above = jnp.minimum(2 * q + 2, 2 * window - 1)
        pair = [rows_of(c, 2 * q, 2).reshape(cells, orbs) for c in range(8)]
        vs = [v.astype(F32) for v in pair]
        for c in range(1, 7):
            outer = jnp.concatenate(
                [
                    rows_of(c, below, 1)[0].astype(F32) * has_below,
                    rows_of(c, above, 1)[0].astype(F32) * has_above,
                ],
                axis=0,
            )
            f = applied(pair[c], outer, vs[c - 1] + vs[c + 1], local(c, q))
            keep = valid
            if c == 1:
                keep = valid * has_zf
            if c == 6:
                keep = valid * has_zo
            first[c - 1, pl.ds(2 * j, 2)] = (f * keep).astype(BF16).reshape(2, width, orbs)
        return carry

    lax.fori_loop(0, rows // 2 + 2, step1, 0)

    def step2(j, carry):
        p = start // 2 + x + j
        pair = [first[c - 1, pl.ds(2 * j + 2, 2)].reshape(cells, orbs) for c in range(1, 7)]
        vs = [v.astype(F32) for v in pair]
        for c in range(2, 6):
            outer = jnp.concatenate(
                [first[c - 1, 2 * j + 1].astype(F32), first[c - 1, 2 * j + 4].astype(F32)], axis=0
            )
            f = applied(pair[c - 1], outer, vs[c - 2] + vs[c], local(c, p))
            f = f.astype(BF16).reshape(2, width, orbs)
            plane = (c % 2) ^ x
            if joint:
                outs[0][plane + (2 if c in (2, 3) else 0), pl.ds(2 * j, 2)] = f
            else:
                outs[1 if c in (2, 3) else 0][plane, pl.ds(2 * j, 2)] = f
        return carry

    lax.fori_loop(0, rows // 2, step2, 0)


def filtered(slabs, start, rows, joint, operands, xrs, zfs):
    own = operands[0]
    planes, _, width, orbs = own.shape
    parts = len(xrs)
    shape = (2 * planes if joint else planes, rows, width, orbs)
    out = (jax.ShapeDtypeStruct(shape, BF16),) * (1 if joint else 2)
    cells = 10 * rows * width
    scratch = [
        pltpu.VMEM((6, rows + 4, width, orbs), BF16),
        pltpu.VMEM((6, width, orbs), F32),
        pltpu.VMEM((6, 2, own.shape[1] // 2, 2 * width), F32),
    ]
    if parts > 1:
        window = xrs[0].shape[1] - 1 + xrs[1].shape[1]
        scratch += [pltpu.VMEM((planes, window, width, orbs), BF16)] * 2
    return pl.pallas_call(
        functools.partial(filter_kernel, slabs, start, parts, joint),
        out_shape=out,
        in_specs=[pl.BlockSpec(memory_space=pltpu.VMEM)] * (len(operands) + 2 * parts),
        out_specs=(pl.BlockSpec(memory_space=pltpu.VMEM),) * len(out),
        scratch_shapes=scratch,
        compiler_params=params(),
        cost_estimate=cost(2 * cells * 32 * orbs, FILTER * cells * orbs * 4),
        name="filtered",
    )(*operands, *xrs, *zfs)


def rotate_kernel(group, *refs):
    a, b, c, d, q = refs[:5]
    outs = refs[5:]
    _, rows, width, orbs = a.shape
    planes = outs[0].shape[0]
    low = jnp.concatenate([q[0], q[1]], axis=0)
    high = jnp.concatenate([q[2], q[3]], axis=0)

    def one(j, carry):
        for plane in range(a.shape[0]):
            def take(ref):
                return ref[plane, pl.ds(group * j, group)].reshape(group * width, orbs)

            total = jnp.dot(
                jnp.concatenate([take(a), take(b)], axis=1), low, preferred_element_type=F32
            )
            total = total + jnp.dot(
                jnp.concatenate([take(c), take(d)], axis=1), high, preferred_element_type=F32
            )
            outs[plane // planes][plane % planes, pl.ds(group * j, group)] = total.astype(
                BF16
            ).reshape(group, width, orbs)
        return carry

    lax.fori_loop(0, rows // group, one, 0)


def rotated(blocks, q, pieces):
    a = blocks[0]
    size = a.size
    group = max(g for g in range(1, 9) if a.shape[1] % g == 0)
    out = jax.ShapeDtypeStruct((a.shape[0] // pieces, *a.shape[1:]), BF16)
    return pl.pallas_call(
        functools.partial(rotate_kernel, group),
        out_shape=(out,) * pieces,
        in_specs=[pl.BlockSpec(memory_space=pltpu.VMEM)] * 5,
        out_specs=(pl.BlockSpec(memory_space=pltpu.VMEM),) * pieces,
        compiler_params=params(),
        cost_estimate=cost(8 * size * a.shape[3], 10 * size),
        name="rotated",
    )(*blocks, q)


def assemble_kernel(half, term, *refs):
    out = refs[-1]
    pieces = (len(refs) - 1) // 2
    x = lax.rem(lax.axis_index("space"), 2)
    start = 0
    for k in range(pieces):
        rows = refs[k].shape[1]
        start += refs[k - 1].shape[1] if k else 0
        for ref, at in ((refs[k], half * x), (refs[pieces + k], half * (1 - x))):
            where = pl.ds(at + start, rows)
            out[:, where] = (ref[...].astype(F32) + term[:, where]).astype(BF16)


def assembled(term, mine, theirs):
    return pl.pallas_call(
        functools.partial(assemble_kernel, term.shape[1] // 2),
        out_shape=jax.ShapeDtypeStruct(term.shape, BF16),
        in_specs=[pl.BlockSpec(memory_space=pltpu.VMEM)] * (1 + len(mine) + len(theirs)),
        out_specs=pl.BlockSpec(memory_space=pltpu.VMEM),
        compiler_params=params(),
        cost_estimate=cost(4096, 4096),
        name="assembled",
    )(term, *mine, *theirs)


def ordered(*arrays):
    return lax.optimization_barrier(arrays)


def shards(psi, potential, beta, strength, atom_slab, pattern, q_tiles):
    planes, width_x, width_y, orbs = psi.shape
    count = beta.shape[0]
    slabs = lax.axis_size("space")
    place = lax.axis_index("space")
    x = lax.rem(place, 2)
    half = width_x // 2
    window = half + 2
    rows1 = half * 5 // 24 * 2
    rows2 = half - rows1
    early = rows1 + 4

    def within(pairs):
        return [(i, j) for i, j in pairs if 0 <= j < slabs]

    swap = [(i, i ^ 1) for i in range(slabs)]
    own_way = within([(i, i + 2 if i % 2 else i - 2) for i in range(slabs)])
    other_way = within([(i, i - 2 if i % 2 else i + 2) for i in range(slabs)])
    raster = within([(i, i + 1 if i % 2 else i - 1) for i in range(slabs)])
    groups = lax.axis_size("orb")
    across = [(i, i ^ 2) for i in range(groups)]
    beside = [(i, i ^ 1) for i in range(groups)]
    mine = (half - 2) * x
    theirs = (half - 2) * (1 - x)

    to_x, to_x2, to_z, blocks = prepared(psi, potential, early)
    xr1 = lax.ppermute(to_x, "space", swap)
    zo = lax.ppermute(to_z, "space", own_way)
    far = lax.dynamic_index_in_dim(beta, x, 1, keepdims=False)
    near = lax.dynamic_index_in_dim(beta, 1 - x, 1, keepdims=False)
    active = jnp.abs(place - atom_slab) <= 1
    beta_m = jnp.where(active[:, None, None, None], beta, jnp.zeros_like(beta))
    gram = jnp.einsum("pzxy,qzxy->pq", beta_m, beta_m, preferred_element_type=F32)
    f_x = lax.ppermute(near, "space", swap)
    f_d = lax.ppermute(far, "space", raster)
    zf1 = lax.ppermute(xr1, "space", other_way)
    second, _, f_x, f_d = ordered(to_x2, xr1, f_x, f_d)
    xr2 = lax.ppermute(second, "space", swap)
    zf2 = lax.ppermute(xr2, "space", other_way)
    strong = jnp.broadcast_to(strength[:, None], (count, orbs))

    me = lax.axis_index("orb")
    which = jnp.bitwise_xor(me, jnp.arange(groups, dtype=jnp.int32))
    rows_hot = (pattern[:, 0][:, None] == which[None, :]).astype(BF16)
    rows_hot = rows_hot * (pattern[:, 1] == me).astype(BF16)[:, None]
    q = jnp.einsum("ki,kab->iab", rows_hot, q_tiles, preferred_element_type=F32).astype(BF16)

    sums, weights = partials(count, atom_slab, psi, beta, f_x, f_d, potential, gram)
    zf1, sums = ordered(zf1, sums)
    operands = (psi, blocks, zo)
    (block1,) = filtered(slabs, 0, rows1, True, operands, (xr1,), (zf1,))
    y1 = lax.ppermute(block1, "orb", across)
    c1 = lax.ppermute(block1, "orb", beside)
    give2, keep2 = filtered(slabs, rows1, rows2, False, operands, (xr1, xr2), (zf1, zf2))
    step = 1
    while step < slabs:
        sums = sums + lax.ppermute(sums, "space", [(i, i ^ step) for i in range(slabs)])
        step *= 2
    coefs = coefficients(sums, strong)
    cg = lax.ppermute(give2, "orb", beside)
    ck = lax.ppermute(keep2, "orb", beside)
    yg = lax.ppermute(give2, "orb", across)
    yc1 = lax.ppermute(y1, "orb", beside)
    give1, keep1 = rotated((block1, c1, y1, yc1), q, 2)
    keep_y, yg = ordered(keep2, yg)
    yk = lax.ppermute(keep_y, "orb", across)
    yg, coefs = ordered(yg, coefs)
    ycg = lax.ppermute(yg, "orb", beside)
    ycg, give1 = ordered(ycg, give1)
    got1 = lax.ppermute(give1, "space", swap)
    coefs_c = lax.ppermute(coefs, "orb", beside)
    coefs_y = lax.ppermute(jnp.concatenate([coefs, coefs_c], axis=0), "orb", across)
    coefs_yc, coefs_y = coefs_y[2 * count :], coefs_y[: 2 * count]
    term = nonlocal_term(psi.shape, (coefs, coefs_c, coefs_y, coefs_yc), q, weights)
    (give2,) = rotated((give2, cg, yg, ycg), q, 1)
    yk, give2 = ordered(yk, give2)
    got2 = lax.ppermute(give2, "space", swap)
    yck = lax.ppermute(yk, "orb", beside)
    (keep2,) = rotated((keep2, ck, yk, yck), q, 1)
    return assembled(term, [keep1, keep2], [got1, got2])


def solution(mesh):
    placed = (
        P("space", None, None, "orb"),
        P("space", None, None),
        P(None, "space", None, None),
        P(),
        P(),
        P(),
        P(),
    )
    return jax.shard_map(
        shards, mesh=mesh, in_specs=placed, out_specs=P("space", None, None, "orb"), check_vma=False
    )
```

```python
import functools

import jax
import jax.numpy as jnp
from jax import lax
from jax.experimental import pallas as pl
from jax.experimental.pallas import tpu as pltpu
from jax.sharding import PartitionSpec as P

F32 = jnp.float32
BF16 = jnp.bfloat16
VMEM_LIMIT = 24 * 1024 * 1024
SHRINK = 16
FILTER = 100


def params():
    return pltpu.CompilerParams(vmem_limit_bytes=VMEM_LIMIT)


def cost(flops, moved):
    return pl.CostEstimate(flops=flops // SHRINK, bytes_accessed=moved // SHRINK, transcendentals=0)


def inside(p, window):
    return jnp.logical_and(p >= 0, p < window).astype(F32)


def neighbour_sum(width, pairs):
    n = (2 if pairs else 1) * width
    i = lax.broadcasted_iota(jnp.int32, (n, n), 0)
    j = lax.broadcasted_iota(jnp.int32, (n, n), 1)
    linked = jnp.abs(i - j) == 1
    if pairs:
        linked = jnp.logical_and(linked, (i < width) == (j < width))
        linked = jnp.logical_or(linked, jnp.abs(i - j) == width)
    return jnp.where(linked, -0.125, 0.0)


def prepare_kernel(early, psi, potential_far, beta, to_x, to_x2, to_z, blocks, potential, sems):
    x = lax.rem(lax.axis_index("space"), 2)
    half = psi.shape[1] // 2
    window = half + 2
    mine, theirs = (half - 2) * x, (half - 2) * (1 - x)
    width = potential_far.shape[2]
    gap = jnp.zeros((potential_far.shape[1], 64 - width), F32)
    copies = [
        pltpu.make_async_copy(
            psi.at[:, pl.ds(theirs, early)], to_x.at[:, pl.ds(0, early)], sems.at[0]
        ),
        pltpu.make_async_copy(
            psi.at[:, pl.ds(mine, window)], to_z.at[:, pl.ds(0, window)], sems.at[1]
        ),
        pltpu.make_async_copy(
            psi.at[:, pl.ds(theirs + early, window - early)],
            to_x2.at[:, pl.ds(0, window - early)],
            sems.at[2],
        ),
    ]
    fetch = pltpu.make_async_copy(potential_far, potential, sems.at[5])
    fetch.start()
    for copy in copies:
        copy.start()
    each = beta.shape[0] // blocks.shape[0]

    def pack(i, carry):
        for plane in range(blocks.shape[0]):
            first, second = (beta[plane * each + i, k].astype(F32) for k in range(2))
            to_x2[plane, window - early + i] = jnp.concatenate(
                [first, gap, second, gap], axis=1
            ).astype(BF16)
        return carry

    lax.fori_loop(0, each, pack, 0)
    fetch.wait()
    for plane in range(blocks.shape[0]):
        u = (potential[plane] - 1.0) * 0.25
        hi = u.astype(BF16).astype(F32)
        blocks[plane, 0] = jnp.concatenate([hi, gap, u - hi, gap], axis=1).astype(BF16)
    more = [
        pltpu.make_async_copy(blocks, to_x.at[:, pl.ds(early, 1)], sems.at[3]),
        pltpu.make_async_copy(blocks, to_z.at[:, pl.ds(window, 1)], sems.at[4]),
    ]
    for copy in more:
        copy.start()
    for copy in copies + more:
        copy.wait()


def prepared(psi, potential, beta, early):
    planes, width_x, width_y, orbs = psi.shape
    window = width_x // 2 + 2

    def out(rows):
        return jax.ShapeDtypeStruct((planes, rows, width_y, orbs), BF16)

    local = pl.BlockSpec(memory_space=pltpu.VMEM)
    return pl.pallas_call(
        functools.partial(prepare_kernel, early),
        out_shape=(
            out(early + 1),
            out(window - early + beta.shape[0] // planes),
            out(window + 1),
            out(1),
        ),
        in_specs=[pl.BlockSpec(memory_space=pltpu.MemorySpace.HBM)] * 2 + [local],
        out_specs=(local,) * 4,
        scratch_shapes=[pltpu.VMEM(potential.shape, F32), pltpu.SemaphoreType.DMA((6,))],
        compiler_params=params(),
        cost_estimate=cost(4096, 4096),
        name="prepared",
    )(*(pltpu.with_memory_space_constraint(a, pltpu.MemorySpace.HBM) for a in (psi, potential)), beta)


def partial_kernel(count, atoms, own, beta, b_x, b_d, potential, gram, out, weights_out, table, acc):
    place = lax.axis_index("space")
    x = lax.rem(place, 2)
    rows, width = potential.shape[1:]
    side = place ^ 1
    beyond = place - 1 + 2 * x
    tri = neighbour_sum(width, False).astype(BF16)
    acc[...] = jnp.zeros_like(acc)
    step = 8

    for k in range(2):
        plane = x if k == 0 else 1 - x
        outer, there = (b_d, beyond) if k == 0 else (b_x, side)
        left = x == (1 if k == 0 else 0)
        each = count // outer.shape[0]
        begin = outer.shape[1] - each
        u = (potential[plane] - 1.0) * 0.25

        def fill(i, carry):
            for j in range(step):
                p = i * step + j
                here = (jnp.abs(place - atoms[p]) <= 1).astype(F32)
                next_to = (jnp.abs(there - atoms[p]) <= 1).astype(F32)
                b32 = beta[p, plane].astype(F32) * here
                b = b32.astype(BF16)
                both = outer[p // each, begin + lax.rem(p, each)].astype(F32)
                other = jnp.where(left, both[:, :width], both[:, 64 : 64 + width])
                sides = beta[p, 1 - plane].astype(F32) * here + other * next_to
                whole = jnp.dot(b, tri, preferred_element_type=F32)
                whole = whole + jnp.dot(tri, b, preferred_element_type=F32)
                whole = whole + u * b32 - 0.125 * sides
                hi = whole.astype(BF16).astype(F32)
                for kind, value in enumerate((b32, hi, whole - hi)):
                    table[pl.ds((kind * count + p) * rows, rows)] = value
            return carry

        lax.fori_loop(0, count // step, fill, 0)

        def use(i, carry):
            totals = []
            for j in range(step):
                r = i * step + j
                weights = table[pl.ds(r, 3 * count, stride=rows)].astype(BF16)
                weights_out[plane, r] = weights
                totals.append(jnp.dot(weights, own[plane, r], preferred_element_type=F32))
            acc[...] += sum(totals[1:], totals[0])
            return carry

        lax.fori_loop(0, rows // step, use, 0)
    out[...] = jnp.zeros_like(out)
    out[0:count] = acc[0:count]
    out[count : 2 * count] = acc[count : 2 * count] + acc[2 * count : 3 * count]
    out[2 * count : 3 * count, 0:count] = gram[...]


def partials(count, atoms, own, beta, b_x, b_d, potential, gram):
    planes, rows, width, orbs = own.shape
    return pl.pallas_call(
        functools.partial(partial_kernel, count),
        out_shape=(
            jax.ShapeDtypeStruct((3 * count, orbs), F32),
            jax.ShapeDtypeStruct((planes, rows, 3 * count, width), BF16),
        ),
        in_specs=[pl.BlockSpec(memory_space=pltpu.SMEM)]
        + [pl.BlockSpec(memory_space=pltpu.VMEM)] * 6,
        out_specs=(pl.BlockSpec(memory_space=pltpu.VMEM),) * 2,
        scratch_shapes=[
            pltpu.VMEM((3 * count * rows, width), F32),
            pltpu.VMEM((3 * count, orbs), F32),
        ],
        compiler_params=params(),
        cost_estimate=cost(4096, 4096),
        name="partials",
    )(atoms, own, beta, b_x, b_d, potential, gram)


def coefficient_kernel(sums, strength, out):
    count, orbs = strength.shape
    coef1 = (strength[...] * sums[0:count]).astype(BF16)
    padded = coef1.astype(F32) * 0.25
    if orbs > count:
        padded = jnp.concatenate([padded, jnp.zeros((orbs - count, orbs), F32)], axis=0)
    proj2 = sums[count : 2 * count] + jnp.dot(
        sums[2 * count : 3 * count],
        padded,
        preferred_element_type=F32,
        precision=lax.Precision.HIGHEST,
    )
    out[0:count] = coef1
    out[count : 2 * count] = (strength[...] * proj2).astype(BF16)


def coefficients(sums, strength):
    count, orbs = strength.shape
    return pl.pallas_call(
        coefficient_kernel,
        out_shape=jax.ShapeDtypeStruct((2 * count, orbs), BF16),
        in_specs=[pl.BlockSpec(memory_space=pltpu.VMEM)] * 2,
        out_specs=pl.BlockSpec(memory_space=pltpu.VMEM),
        compiler_params=params(),
        cost_estimate=cost(4096, 4096),
        name="coefficients",
    )(sums, strength)


def nonlocal_kernel(unroll, a, b, c, d, q, weights, out):
    count, orbs = a.shape[0] // 2, a.shape[1]
    turned = sum(
        jnp.dot(ref[...], q[k], preferred_element_type=F32) for k, ref in enumerate((a, b, c, d))
    )
    turned = turned * 0.25
    one, two = turned[0:count], turned[count : 2 * count]
    right = jnp.concatenate([two, one, one], axis=0)
    hi = right.astype(BF16)
    lo = right - hi.astype(F32)
    right = jnp.concatenate([hi.astype(F32), lo], axis=1).astype(BF16)

    def step(i, carry):
        for k in range(unroll):
            r = i * unroll + k
            for plane in range(weights.shape[0]):
                both = lax.dot_general(
                    weights[plane, r], right, (((0,), (0,)), ((), ())), preferred_element_type=F32
                )
                out[plane, r] = both[:, :orbs] + both[:, orbs:]
        return carry

    lax.fori_loop(0, weights.shape[1] // unroll, step, 0)


def nonlocal_term(shape, coefs, q, weights):
    unroll = max(g for g in (1, 2, 4, 8) if weights.shape[1] % g == 0)
    return pl.pallas_call(
        functools.partial(nonlocal_kernel, unroll),
        out_shape=jax.ShapeDtypeStruct(shape, F32),
        in_specs=[pl.BlockSpec(memory_space=pltpu.VMEM)] * 6,
        out_specs=pl.BlockSpec(memory_space=pltpu.VMEM),
        compiler_params=params(),
        cost_estimate=cost(4096, 4096),
        name="nonlocal",
    )(*coefs, q, weights)


def filter_kernel(slabs, start, parts, joint, *refs):
    own, p_own, zo = refs[:3]
    xrs, zfs = refs[3 : 3 + parts], refs[3 + parts : 3 + 2 * parts]
    extra = 5 if parts > 1 else 3
    outs, scratch = refs[3 + 2 * parts : -extra], refs[-extra:]
    first, lines, diagonals = scratch[:3]
    place = lax.axis_index("space")
    x = lax.rem(place, 2)
    width = own.shape[2]
    cells = 2 * width
    half = own.shape[1] // 2
    orbs = own.shape[3]
    rows = outs[0].shape[1]
    base = (half - 2) * x
    lower = (place >= 2).astype(F32)
    upper = (place < slabs - 2).astype(F32)
    is_odd = x.astype(F32)
    has_zf = lower * (1.0 - is_odd) + upper * is_odd
    has_zo = upper * (1.0 - is_odd) + lower * is_odd
    if parts > 1:
        xr, zf = scratch[3], scratch[4]
        early = xrs[0].shape[1] - 1
        for target, pieces in ((xr, xrs), (zf, zfs)):
            target[:, 0:early] = pieces[0][:, 0:early]
            target[:, early:] = pieces[1][:, 0 : target.shape[1] - early]
        window = xr.shape[1] // 2
    else:
        xr, zf = xrs[0], zfs[0]
        window = (xr.shape[1] - 1) // 2
    for c in range(1, 7):
        plane = (c % 2) ^ x
        if c in (2, 3):
            block = p_own[plane, 0]
        else:
            ref = zfs[0] if c < 2 else (xrs[0] if c < 6 else zo)
            block = ref[plane, ref.shape[1] - 1]
        lines[c - 1] = block.astype(F32)
        for kind in range(2):
            even, odd = (lines[c - 1, pl.ds(k, half, stride=2)] for k in range(2))
            lanes = slice(64 * kind, 64 * kind + width)
            diagonals[c - 1, kind] = jnp.concatenate([even[:, lanes], odd[:, lanes]], axis=1)

    here = neighbour_sum(width, True)
    i = lax.broadcasted_iota(jnp.int32, (cells, cells), 0)
    diagonal = i == lax.broadcasted_iota(jnp.int32, (cells, cells), 1)

    def local(c, p):
        at = base // 2 + p
        hi = diagonals[c - 1, 0, pl.ds(at, 1)]
        lo = diagonals[c - 1, 1, pl.ds(at, 1)]
        return (
            jnp.where(diagonal, hi, here).astype(BF16),
            jnp.where(diagonal, lo, 0.0).astype(BF16),
        )

    def rows_of(c, w, n):
        plane = (c % 2) ^ x
        if c in (2, 3):
            return own[plane, pl.ds(base + w, n)]
        ref = zf if c < 2 else (xr if c < 6 else zo)
        return ref[plane, pl.ds(w, n)]

    def applied(pair, outer, zs, matrices):
        near = jnp.dot(matrices[0], pair, preferred_element_type=F32)
        near = near + jnp.dot(matrices[1], pair, preferred_element_type=F32)
        return near - 0.125 * (outer + zs)

    def step1(j, carry):
        p = start // 2 + x + j - 1
        q = jnp.clip(p, 0, window - 1)
        has_below = inside(p - 1, window)
        has_above = inside(p + 1, window)
        valid = inside(p, window)
        below = jnp.maximum(2 * q - 1, 0)
        above = jnp.minimum(2 * q + 2, 2 * window - 1)
        pair = [rows_of(c, 2 * q, 2).reshape(cells, orbs) for c in range(8)]
        vs = [v.astype(F32) for v in pair]
        for c in range(1, 7):
            outer = jnp.concatenate(
                [
                    rows_of(c, below, 1)[0].astype(F32) * has_below,
                    rows_of(c, above, 1)[0].astype(F32) * has_above,
                ],
                axis=0,
            )
            f = applied(pair[c], outer, vs[c - 1] + vs[c + 1], local(c, q))
            keep = valid
            if c == 1:
                keep = valid * has_zf
            if c == 6:
                keep = valid * has_zo
            first[c - 1, pl.ds(2 * j, 2)] = (f * keep).astype(BF16).reshape(2, width, orbs)
        return carry

    lax.fori_loop(0, rows // 2 + 2, step1, 0)

    def step2(j, carry):
        p = start // 2 + x + j
        pair = [first[c - 1, pl.ds(2 * j + 2, 2)].reshape(cells, orbs) for c in range(1, 7)]
        vs = [v.astype(F32) for v in pair]
        for c in range(2, 6):
            outer = jnp.concatenate(
                [first[c - 1, 2 * j + 1].astype(F32), first[c - 1, 2 * j + 4].astype(F32)], axis=0
            )
            f = applied(pair[c - 1], outer, vs[c - 2] + vs[c], local(c, p))
            f = f.astype(BF16).reshape(2, width, orbs)
            plane = (c % 2) ^ x
            if joint:
                outs[0][plane + (2 if c in (2, 3) else 0), pl.ds(2 * j, 2)] = f
            else:
                outs[1 if c in (2, 3) else 0][plane, pl.ds(2 * j, 2)] = f
        return carry

    lax.fori_loop(0, rows // 2, step2, 0)


def filtered(slabs, start, rows, joint, operands, xrs, zfs):
    own = operands[0]
    planes, _, width, orbs = own.shape
    parts = len(xrs)
    shape = (2 * planes if joint else planes, rows, width, orbs)
    out = (jax.ShapeDtypeStruct(shape, BF16),) * (1 if joint else 2)
    cells = 10 * rows * width
    scratch = [
        pltpu.VMEM((6, rows + 4, width, orbs), BF16),
        pltpu.VMEM((6, width, orbs), F32),
        pltpu.VMEM((6, 2, own.shape[1] // 2, 2 * width), F32),
    ]
    if parts > 1:
        window = own.shape[1] // 2 + 2
        scratch += [pltpu.VMEM((planes, window, width, orbs), BF16)] * 2
    return pl.pallas_call(
        functools.partial(filter_kernel, slabs, start, parts, joint),
        out_shape=out,
        in_specs=[pl.BlockSpec(memory_space=pltpu.VMEM)] * (len(operands) + 2 * parts),
        out_specs=(pl.BlockSpec(memory_space=pltpu.VMEM),) * len(out),
        scratch_shapes=scratch,
        compiler_params=params(),
        cost_estimate=cost(2 * cells * 32 * orbs, FILTER * cells * orbs * 4),
        name="filtered",
    )(*operands, *xrs, *zfs)


def rotate_kernel(group, *refs):
    a, b, c, d, q = refs[:5]
    outs = refs[5:]
    _, rows, width, orbs = a.shape
    planes = outs[0].shape[0]
    low = jnp.concatenate([q[0], q[1]], axis=0)
    high = jnp.concatenate([q[2], q[3]], axis=0)

    def one(j, carry):
        for plane in range(a.shape[0]):
            def take(ref):
                return ref[plane, pl.ds(group * j, group)].reshape(group * width, orbs)

            total = jnp.dot(
                jnp.concatenate([take(a), take(b)], axis=1), low, preferred_element_type=F32
            )
            total = total + jnp.dot(
                jnp.concatenate([take(c), take(d)], axis=1), high, preferred_element_type=F32
            )
            outs[plane // planes][plane % planes, pl.ds(group * j, group)] = total.astype(
                BF16
            ).reshape(group, width, orbs)
        return carry

    lax.fori_loop(0, rows // group, one, 0)


def rotated(blocks, q, pieces):
    a = blocks[0]
    size = a.size
    group = max(g for g in range(1, 9) if a.shape[1] % g == 0)
    out = jax.ShapeDtypeStruct((a.shape[0] // pieces, *a.shape[1:]), BF16)
    return pl.pallas_call(
        functools.partial(rotate_kernel, group),
        out_shape=(out,) * pieces,
        in_specs=[pl.BlockSpec(memory_space=pltpu.VMEM)] * 5,
        out_specs=(pl.BlockSpec(memory_space=pltpu.VMEM),) * pieces,
        compiler_params=params(),
        cost_estimate=cost(8 * size * a.shape[3], 10 * size),
        name="rotated",
    )(*blocks, q)


def assemble_kernel(half, term, *refs):
    out = refs[-1]
    pieces = (len(refs) - 1) // 2
    x = lax.rem(lax.axis_index("space"), 2)
    start = 0
    for k in range(pieces):
        rows = refs[k].shape[1]
        start += refs[k - 1].shape[1] if k else 0
        for ref, at in ((refs[k], half * x), (refs[pieces + k], half * (1 - x))):
            where = pl.ds(at + start, rows)
            out[:, where] = (ref[...].astype(F32) + term[:, where]).astype(BF16)


def assembled(term, mine, theirs):
    return pl.pallas_call(
        functools.partial(assemble_kernel, term.shape[1] // 2),
        out_shape=jax.ShapeDtypeStruct(term.shape, BF16),
        in_specs=[pl.BlockSpec(memory_space=pltpu.VMEM)] * (1 + len(mine) + len(theirs)),
        out_specs=pl.BlockSpec(memory_space=pltpu.VMEM),
        compiler_params=params(),
        cost_estimate=cost(4096, 4096),
        name="assembled",
    )(term, *mine, *theirs)


def ordered(*arrays):
    return lax.optimization_barrier(arrays)


def shards(psi, potential, beta, strength, atom_slab, pattern, q_tiles):
    planes, width_x, width_y, orbs = psi.shape
    count = beta.shape[0]
    slabs = lax.axis_size("space")
    place = lax.axis_index("space")
    x = lax.rem(place, 2)
    half = width_x // 2
    window = half + 2
    rows1 = half * 5 // 24 * 2
    rows2 = half - rows1
    early = rows1 + 4

    def within(pairs):
        return [(i, j) for i, j in pairs if 0 <= j < slabs]

    swap = [(i, i ^ 1) for i in range(slabs)]
    own_way = within([(i, i + 2 if i % 2 else i - 2) for i in range(slabs)])
    other_way = within([(i, i - 2 if i % 2 else i + 2) for i in range(slabs)])
    groups = lax.axis_size("orb")
    across = [(i, i ^ 2) for i in range(groups)]
    beside = [(i, i ^ 1) for i in range(groups)]
    mine = (half - 2) * x
    theirs = (half - 2) * (1 - x)

    to_x, to_x2, to_z, blocks = prepared(psi, potential, beta, early)
    xr1 = lax.ppermute(to_x, "space", swap)
    zo = lax.ppermute(to_z, "space", own_way)
    active = jnp.abs(place - atom_slab) <= 1
    beta_m = jnp.where(active[:, None, None, None], beta, jnp.zeros_like(beta))
    gram = jnp.einsum("pzxy,qzxy->pq", beta_m, beta_m, preferred_element_type=F32)
    zf1 = lax.ppermute(xr1, "space", other_way)
    second, _ = ordered(to_x2, xr1)
    xr2 = lax.ppermute(second, "space", swap)
    zf2 = lax.ppermute(xr2, "space", other_way)
    strong = jnp.broadcast_to(strength[:, None], (count, orbs))

    me = lax.axis_index("orb")
    which = jnp.bitwise_xor(me, jnp.arange(groups, dtype=jnp.int32))
    rows_hot = (pattern[:, 0][:, None] == which[None, :]).astype(BF16)
    rows_hot = rows_hot * (pattern[:, 1] == me).astype(BF16)[:, None]
    q = jnp.einsum("ki,kab->iab", rows_hot, q_tiles, preferred_element_type=F32).astype(BF16)

    zf1, _ = ordered(zf1, xr2)
    operands = (psi, blocks, zo)
    (block1,) = filtered(slabs, 0, rows1, True, operands, (xr1,), (zf1,))
    y1 = lax.ppermute(block1, "orb", across)
    c1 = lax.ppermute(block1, "orb", beside)
    give2, keep2 = filtered(slabs, rows1, rows2, False, operands, (xr1, xr2), (zf1, zf2))
    xr2, _ = ordered(xr2, give2)
    sums, weights = partials(count, atom_slab, psi, beta, xr2, zf2, potential, gram)
    step = 1
    while step < slabs:
        sums = sums + lax.ppermute(sums, "space", [(i, i ^ step) for i in range(slabs)])
        step *= 2
    coefs = coefficients(sums, strong)
    cg = lax.ppermute(give2, "orb", beside)
    ck = lax.ppermute(keep2, "orb", beside)
    yg = lax.ppermute(give2, "orb", across)
    yc1 = lax.ppermute(y1, "orb", beside)
    give1, keep1 = rotated((block1, c1, y1, yc1), q, 2)
    keep_y, yg = ordered(keep2, yg)
    yk = lax.ppermute(keep_y, "orb", across)
    ycg = lax.ppermute(yg, "orb", beside)
    ycg, _ = ordered(ycg, give1)
    got1 = lax.ppermute(give1, "space", swap)
    coefs_c = lax.ppermute(coefs, "orb", beside)
    coefs_y = lax.ppermute(jnp.concatenate([coefs, coefs_c], axis=0), "orb", across)
    coefs_yc, coefs_y = coefs_y[2 * count :], coefs_y[: 2 * count]
    term = nonlocal_term(psi.shape, (coefs, coefs_c, coefs_y, coefs_yc), q, weights)
    (give2,) = rotated((give2, cg, yg, ycg), q, 1)
    got2 = lax.ppermute(give2, "space", swap)
    yk, _, _ = ordered(yk, give2, coefs)
    yck = lax.ppermute(yk, "orb", beside)
    (keep2,) = rotated((keep2, ck, yk, yck), q, 1)
    return assembled(term, [keep1, keep2], [got1, got2])


def solution(mesh):
    placed = (
        P("space", None, None, "orb"),
        P("space", None, None),
        P(None, "space", None, None),
        P(),
        P(),
        P(),
        P(),
    )
    return jax.shard_map(
        shards, mesh=mesh, in_specs=placed, out_specs=P("space", None, None, "orb"), check_vma=False
    )
```

```python
import functools

import jax
import jax.numpy as jnp
from jax import lax
from jax.experimental import pallas as pl
from jax.experimental.pallas import tpu as pltpu
from jax.sharding import PartitionSpec as P

F32 = jnp.float32
BF16 = jnp.bfloat16
VMEM_LIMIT = 24 * 1024 * 1024
SHRINK = 16
FILTER = 100


def params():
    return pltpu.CompilerParams(vmem_limit_bytes=VMEM_LIMIT)


def cost(flops, moved):
    return pl.CostEstimate(flops=flops // SHRINK, bytes_accessed=moved // SHRINK, transcendentals=0)


def inside(p, window):
    return jnp.logical_and(p >= 0, p < window).astype(F32)


def neighbour_sum(width, pairs):
    n = (2 if pairs else 1) * width
    i = lax.broadcasted_iota(jnp.int32, (n, n), 0)
    j = lax.broadcasted_iota(jnp.int32, (n, n), 1)
    linked = jnp.abs(i - j) == 1
    if pairs:
        linked = jnp.logical_and(linked, (i < width) == (j < width))
        linked = jnp.logical_or(linked, jnp.abs(i - j) == width)
    return jnp.where(linked, -0.125, 0.0)


def potential_block(potential):
    lines, width = potential.shape
    gap = jnp.zeros((lines, 64 - width), F32)
    u = (potential - 1.0) * 0.25
    hi = u.astype(BF16).astype(F32)
    return jnp.concatenate([hi, gap, u - hi, gap], axis=1)


def prepare_kernel(early, psi, potential_far, to_x, to_z, potential, sems):
    x = lax.rem(lax.axis_index("space"), 2)
    half = psi.shape[1] // 2
    window = half + 2
    mine, theirs = (half - 2) * x, (half - 2) * (1 - x)
    fetch = pltpu.make_async_copy(potential_far, potential, sems.at[0])
    fetch.start()
    copies = [
        pltpu.make_async_copy(
            psi.at[:, pl.ds(theirs, early)], to_x.at[:, pl.ds(0, early)], sems.at[1]
        ),
        pltpu.make_async_copy(
            psi.at[:, pl.ds(mine, window)], to_z.at[:, pl.ds(0, window)], sems.at[2]
        ),
    ]
    for copy in copies:
        copy.start()
    fetch.wait()
    for plane in range(potential.shape[0]):
        block = potential_block(potential[plane]).astype(BF16)
        to_x[plane, early] = block
        to_z[plane, window] = block
    for copy in copies:
        copy.wait()


def prepared(psi, potential, early):
    planes, width_x, width_y, orbs = psi.shape
    window = width_x // 2 + 2

    def out(rows):
        return jax.ShapeDtypeStruct((planes, rows, width_y, orbs), BF16)

    return pl.pallas_call(
        functools.partial(prepare_kernel, early),
        out_shape=(out(early + 1), out(window + 1)),
        in_specs=[pl.BlockSpec(memory_space=pltpu.MemorySpace.HBM)] * 2,
        out_specs=(pl.BlockSpec(memory_space=pltpu.VMEM),) * 2,
        scratch_shapes=[pltpu.VMEM(potential.shape, F32), pltpu.SemaphoreType.DMA((3,))],
        compiler_params=params(),
        cost_estimate=cost(4096, 4096),
        name="prepared",
    )(*(pltpu.with_memory_space_constraint(a, pltpu.MemorySpace.HBM) for a in (psi, potential)))


def pack_kernel(early, psi, beta, to_x2, sem):
    x = lax.rem(lax.axis_index("space"), 2)
    half = psi.shape[1] // 2
    later = half + 2 - early
    _, _, lines, width = beta.shape
    gap = jnp.zeros((lines, 64 - width), F32)
    copy = pltpu.make_async_copy(
        psi.at[:, pl.ds((half - 2) * (1 - x) + early, later)], to_x2.at[:, pl.ds(0, later)], sem
    )
    copy.start()
    each = beta.shape[0] // to_x2.shape[0]

    def pack(i, carry):
        for plane in range(to_x2.shape[0]):
            first, second = (beta[plane * each + i, k].astype(F32) for k in range(2))
            to_x2[plane, later + i] = jnp.concatenate(
                [first, gap, second, gap], axis=1
            ).astype(BF16)
        return carry

    lax.fori_loop(0, each, pack, 0)
    copy.wait()


def packed(psi, beta, early):
    planes, width_x, width_y, orbs = psi.shape
    rows = width_x // 2 + 2 - early + beta.shape[0] // planes
    return pl.pallas_call(
        functools.partial(pack_kernel, early),
        out_shape=jax.ShapeDtypeStruct((planes, rows, width_y, orbs), BF16),
        in_specs=[
            pl.BlockSpec(memory_space=pltpu.MemorySpace.HBM),
            pl.BlockSpec(memory_space=pltpu.VMEM),
        ],
        out_specs=pl.BlockSpec(memory_space=pltpu.VMEM),
        scratch_shapes=[pltpu.SemaphoreType.DMA],
        compiler_params=params(),
        cost_estimate=cost(4096, 4096),
        name="packed",
    )(pltpu.with_memory_space_constraint(psi, pltpu.MemorySpace.HBM), beta)


def partial_kernel(count, atoms, own, beta, b_x, b_d, potential, gram, out, weights_out, table, acc):
    place = lax.axis_index("space")
    x = lax.rem(place, 2)
    rows, width = potential.shape[1:]
    side = place ^ 1
    beyond = place - 1 + 2 * x
    tri = neighbour_sum(width, False).astype(BF16)
    acc[...] = jnp.zeros_like(acc)
    step = 8

    for k in range(2):
        plane = x if k == 0 else 1 - x
        outer, there = (b_d, beyond) if k == 0 else (b_x, side)
        left = x == (1 if k == 0 else 0)
        each = count // outer.shape[0]
        begin = outer.shape[1] - each
        u = (potential[plane] - 1.0) * 0.25

        def fill(i, carry):
            for j in range(step):
                p = i * step + j
                here = (jnp.abs(place - atoms[p]) <= 1).astype(F32)
                next_to = (jnp.abs(there - atoms[p]) <= 1).astype(F32)
                b32 = beta[p, plane].astype(F32) * here
                b = b32.astype(BF16)
                both = outer[p // each, begin + lax.rem(p, each)].astype(F32)
                other = jnp.where(left, both[:, :width], both[:, 64 : 64 + width])
                sides = beta[p, 1 - plane].astype(F32) * here + other * next_to
                whole = jnp.dot(b, tri, preferred_element_type=F32)
                whole = whole + jnp.dot(tri, b, preferred_element_type=F32)
                whole = whole + u * b32 - 0.125 * sides
                hi = whole.astype(BF16).astype(F32)
                for kind, value in enumerate((b32, hi, whole - hi)):
                    table[pl.ds((kind * count + p) * rows, rows)] = value
            return carry

        lax.fori_loop(0, count // step, fill, 0)

        def use(i, carry):
            totals = []
            for j in range(step):
                r = i * step + j
                weights = table[pl.ds(r, 3 * count, stride=rows)].astype(BF16)
                weights_out[plane, r] = weights
                totals.append(jnp.dot(weights, own[plane, r], preferred_element_type=F32))
            acc[...] += sum(totals[1:], totals[0])
            return carry

        lax.fori_loop(0, rows // step, use, 0)
    out[...] = jnp.zeros_like(out)
    out[0:count] = acc[0:count]
    out[count : 2 * count] = acc[count : 2 * count] + acc[2 * count : 3 * count]
    out[2 * count : 3 * count, 0:count] = gram[...]


def partials(count, atoms, own, beta, b_x, b_d, potential, gram):
    planes, rows, width, orbs = own.shape
    return pl.pallas_call(
        functools.partial(partial_kernel, count),
        out_shape=(
            jax.ShapeDtypeStruct((3 * count, orbs), F32),
            jax.ShapeDtypeStruct((planes, rows, 3 * count, width), BF16),
        ),
        in_specs=[pl.BlockSpec(memory_space=pltpu.SMEM)]
        + [pl.BlockSpec(memory_space=pltpu.VMEM)] * 6,
        out_specs=(pl.BlockSpec(memory_space=pltpu.VMEM),) * 2,
        scratch_shapes=[
            pltpu.VMEM((3 * count * rows, width), F32),
            pltpu.VMEM((3 * count, orbs), F32),
        ],
        compiler_params=params(),
        cost_estimate=cost(4096, 4096),
        name="partials",
    )(atoms, own, beta, b_x, b_d, potential, gram)


def coefficient_kernel(sums, strength, out):
    count, orbs = strength.shape
    coef1 = (strength[...] * sums[0:count]).astype(BF16)
    padded = coef1.astype(F32) * 0.25
    if orbs > count:
        padded = jnp.concatenate([padded, jnp.zeros((orbs - count, orbs), F32)], axis=0)
    proj2 = sums[count : 2 * count] + jnp.dot(
        sums[2 * count : 3 * count],
        padded,
        preferred_element_type=F32,
        precision=lax.Precision.HIGHEST,
    )
    out[0:count] = coef1
    out[count : 2 * count] = (strength[...] * proj2).astype(BF16)


def coefficients(sums, strength):
    count, orbs = strength.shape
    return pl.pallas_call(
        coefficient_kernel,
        out_shape=jax.ShapeDtypeStruct((2 * count, orbs), BF16),
        in_specs=[pl.BlockSpec(memory_space=pltpu.VMEM)] * 2,
        out_specs=pl.BlockSpec(memory_space=pltpu.VMEM),
        compiler_params=params(),
        cost_estimate=cost(4096, 4096),
        name="coefficients",
    )(sums, strength)


def nonlocal_kernel(unroll, a, b, c, d, q, weights, out):
    count, orbs = a.shape[0] // 2, a.shape[1]
    turned = sum(
        jnp.dot(ref[...], q[k], preferred_element_type=F32) for k, ref in enumerate((a, b, c, d))
    )
    turned = turned * 0.25
    one, two = turned[0:count], turned[count : 2 * count]
    right = jnp.concatenate([two, one, one], axis=0)
    hi = right.astype(BF16)
    lo = right - hi.astype(F32)
    right = jnp.concatenate([hi.astype(F32), lo], axis=1).astype(BF16)

    def step(i, carry):
        for k in range(unroll):
            r = i * unroll + k
            for plane in range(weights.shape[0]):
                both = lax.dot_general(
                    weights[plane, r], right, (((0,), (0,)), ((), ())), preferred_element_type=F32
                )
                out[plane, r] = both[:, :orbs] + both[:, orbs:]
        return carry

    lax.fori_loop(0, weights.shape[1] // unroll, step, 0)


def nonlocal_term(shape, coefs, q, weights):
    unroll = max(g for g in (1, 2, 4, 8) if weights.shape[1] % g == 0)
    return pl.pallas_call(
        functools.partial(nonlocal_kernel, unroll),
        out_shape=jax.ShapeDtypeStruct(shape, F32),
        in_specs=[pl.BlockSpec(memory_space=pltpu.VMEM)] * 6,
        out_specs=pl.BlockSpec(memory_space=pltpu.VMEM),
        compiler_params=params(),
        cost_estimate=cost(4096, 4096),
        name="nonlocal",
    )(*coefs, q, weights)


def filter_kernel(slabs, start, parts, joint, *refs):
    own, p_own, zo = refs[:3]
    xrs, zfs = refs[3 : 3 + parts], refs[3 + parts : 3 + 2 * parts]
    extra = 5 if parts > 1 else 3
    outs, scratch = refs[3 + 2 * parts : -extra], refs[-extra:]
    first, lines, diagonals = scratch[:3]
    place = lax.axis_index("space")
    x = lax.rem(place, 2)
    width = own.shape[2]
    cells = 2 * width
    half = own.shape[1] // 2
    orbs = own.shape[3]
    rows = outs[0].shape[1]
    base = (half - 2) * x
    lower = (place >= 2).astype(F32)
    upper = (place < slabs - 2).astype(F32)
    is_odd = x.astype(F32)
    has_zf = lower * (1.0 - is_odd) + upper * is_odd
    has_zo = upper * (1.0 - is_odd) + lower * is_odd
    if parts > 1:
        xr, zf = scratch[3], scratch[4]
        early = start + 4
        for target, pieces in ((xr, xrs), (zf, zfs)):
            target[:, start - 4 : early] = pieces[0][:, 0:8]
            target[:, early:] = pieces[1][:, 0 : target.shape[1] - early]
        window = xr.shape[1] // 2
    else:
        xr, zf = xrs[0], zfs[0]
        early = xr.shape[1] - 1
        window = early // 2
        for target, piece in ((outs[1], xr), (outs[2], zf)):
            target[...] = piece[:, early - 8 :]
    for c in range(1, 7):
        plane = (c % 2) ^ x
        if c in (2, 3):
            lines[c - 1] = potential_block(p_own[plane])
        else:
            ref = zfs[0] if c < 2 else (xrs[0] if c < 6 else zo)
            lines[c - 1] = ref[plane, ref.shape[1] - 1].astype(F32)
        for kind in range(2):
            even, odd = (lines[c - 1, pl.ds(k, half, stride=2)] for k in range(2))
            lanes = slice(64 * kind, 64 * kind + width)
            diagonals[c - 1, kind] = jnp.concatenate([even[:, lanes], odd[:, lanes]], axis=1)

    here = neighbour_sum(width, True)
    i = lax.broadcasted_iota(jnp.int32, (cells, cells), 0)
    diagonal = i == lax.broadcasted_iota(jnp.int32, (cells, cells), 1)

    def local(c, p):
        at = base // 2 + p
        hi = diagonals[c - 1, 0, pl.ds(at, 1)]
        lo = diagonals[c - 1, 1, pl.ds(at, 1)]
        return (
            jnp.where(diagonal, hi, here).astype(BF16),
            jnp.where(diagonal, lo, 0.0).astype(BF16),
        )

    def rows_of(c, w, n):
        plane = (c % 2) ^ x
        if c in (2, 3):
            return own[plane, pl.ds(base + w, n)]
        ref = zf if c < 2 else (xr if c < 6 else zo)
        return ref[plane, pl.ds(w, n)]

    def applied(pair, outer, zs, matrices):
        near = jnp.dot(matrices[0], pair, preferred_element_type=F32)
        near = near + jnp.dot(matrices[1], pair, preferred_element_type=F32)
        return near - 0.125 * (outer + zs)

    def step1(j, carry):
        p = start // 2 + x + j - 1
        q = jnp.clip(p, 0, window - 1)
        has_below = inside(p - 1, window)
        has_above = inside(p + 1, window)
        valid = inside(p, window)
        below = jnp.maximum(2 * q - 1, 0)
        above = jnp.minimum(2 * q + 2, 2 * window - 1)
        pair = [rows_of(c, 2 * q, 2).reshape(cells, orbs) for c in range(8)]
        vs = [v.astype(F32) for v in pair]
        for c in range(1, 7):
            outer = jnp.concatenate(
                [
                    rows_of(c, below, 1)[0].astype(F32) * has_below,
                    rows_of(c, above, 1)[0].astype(F32) * has_above,
                ],
                axis=0,
            )
            f = applied(pair[c], outer, vs[c - 1] + vs[c + 1], local(c, q))
            keep = valid
            if c == 1:
                keep = valid * has_zf
            if c == 6:
                keep = valid * has_zo
            first[c - 1, pl.ds(2 * j, 2)] = (f * keep).astype(BF16).reshape(2, width, orbs)
        return carry

    lax.fori_loop(0, rows // 2 + 2, step1, 0)

    def step2(j, carry):
        p = start // 2 + x + j
        pair = [first[c - 1, pl.ds(2 * j + 2, 2)].reshape(cells, orbs) for c in range(1, 7)]
        vs = [v.astype(F32) for v in pair]
        for c in range(2, 6):
            outer = jnp.concatenate(
                [first[c - 1, 2 * j + 1].astype(F32), first[c - 1, 2 * j + 4].astype(F32)], axis=0
            )
            f = applied(pair[c - 1], outer, vs[c - 2] + vs[c], local(c, p))
            f = f.astype(BF16).reshape(2, width, orbs)
            plane = (c % 2) ^ x
            if joint:
                outs[0][plane + (2 if c in (2, 3) else 0), pl.ds(2 * j, 2)] = f
            else:
                outs[1 if c in (2, 3) else 0][plane, pl.ds(2 * j, 2)] = f
        return carry

    lax.fori_loop(0, rows // 2, step2, 0)


def filtered(slabs, start, rows, joint, operands, xrs, zfs):
    own = operands[0]
    planes, _, width, orbs = own.shape
    parts = len(xrs)
    shape = (2 * planes if joint else planes, rows, width, orbs)
    out = (jax.ShapeDtypeStruct(shape, BF16),) * (1 if joint else 2)
    if parts == 1:
        out += (jax.ShapeDtypeStruct((planes, 9, width, orbs), BF16),) * 2
    cells = 10 * rows * width
    scratch = [
        pltpu.VMEM((6, rows + 4, width, orbs), BF16),
        pltpu.VMEM((6, width, orbs), F32),
        pltpu.VMEM((6, 2, own.shape[1] // 2, 2 * width), F32),
    ]
    if parts > 1:
        window = own.shape[1] // 2 + 2
        scratch += [pltpu.VMEM((planes, window, width, orbs), BF16)] * 2
    return pl.pallas_call(
        functools.partial(filter_kernel, slabs, start, parts, joint),
        out_shape=out,
        in_specs=[pl.BlockSpec(memory_space=pltpu.VMEM)] * (len(operands) + 2 * parts),
        out_specs=(pl.BlockSpec(memory_space=pltpu.VMEM),) * len(out),
        scratch_shapes=scratch,
        compiler_params=params(),
        cost_estimate=cost(2 * cells * 32 * orbs, FILTER * cells * orbs * 4),
        name="filtered",
    )(*operands, *xrs, *zfs)


def rotate_kernel(group, *refs):
    a, b, c, d, q = refs[:5]
    outs = refs[5:]
    _, rows, width, orbs = a.shape
    planes = outs[0].shape[0]
    low = jnp.concatenate([q[0], q[1]], axis=0)
    high = jnp.concatenate([q[2], q[3]], axis=0)

    def one(j, carry):
        for plane in range(a.shape[0]):
            def take(ref):
                return ref[plane, pl.ds(group * j, group)].reshape(group * width, orbs)

            total = jnp.dot(
                jnp.concatenate([take(a), take(b)], axis=1), low, preferred_element_type=F32
            )
            total = total + jnp.dot(
                jnp.concatenate([take(c), take(d)], axis=1), high, preferred_element_type=F32
            )
            outs[plane // planes][plane % planes, pl.ds(group * j, group)] = total.astype(
                BF16
            ).reshape(group, width, orbs)
        return carry

    lax.fori_loop(0, rows // group, one, 0)


def rotated(blocks, q, pieces):
    a = blocks[0]
    size = a.size
    group = max(g for g in range(1, 9) if a.shape[1] % g == 0)
    out = jax.ShapeDtypeStruct((a.shape[0] // pieces, *a.shape[1:]), BF16)
    return pl.pallas_call(
        functools.partial(rotate_kernel, group),
        out_shape=(out,) * pieces,
        in_specs=[pl.BlockSpec(memory_space=pltpu.VMEM)] * 5,
        out_specs=(pl.BlockSpec(memory_space=pltpu.VMEM),) * pieces,
        compiler_params=params(),
        cost_estimate=cost(8 * size * a.shape[3], 10 * size),
        name="rotated",
    )(*blocks, q)


def assemble_kernel(group, term, keep1, got1, got2, a, b, c, d, q, out):
    half = term.shape[1] // 2
    width, orbs = term.shape[2:]
    x = lax.rem(lax.axis_index("space"), 2)
    rows1, rows2 = keep1.shape[1], got2.shape[1]
    for ref, at in (
        (keep1, half * x),
        (got1, half * (1 - x)),
        (got2, half * (1 - x) + rows1),
    ):
        where = pl.ds(at, ref.shape[1])
        out[:, where] = (ref[...].astype(F32) + term[:, where]).astype(BF16)
    low = jnp.concatenate([q[0], q[1]], axis=0)
    high = jnp.concatenate([q[2], q[3]], axis=0)

    def one(j, carry):
        where = pl.ds(half * x + rows1 + group * j, group)
        for plane in range(a.shape[0]):
            def take(ref):
                return ref[plane, pl.ds(group * j, group)].reshape(group * width, orbs)

            total = jnp.dot(
                jnp.concatenate([take(a), take(b)], axis=1), low, preferred_element_type=F32
            )
            total = total + jnp.dot(
                jnp.concatenate([take(c), take(d)], axis=1), high, preferred_element_type=F32
            )
            total = total.reshape(group, width, orbs) + term[plane, where]
            out[plane, where] = total.astype(BF16)
        return carry

    lax.fori_loop(0, rows2 // group, one, 0)


def assembled(term, keep1, got1, got2, blocks, q):
    group = max(g for g in range(1, 9) if got2.shape[1] % g == 0)
    return pl.pallas_call(
        functools.partial(assemble_kernel, group),
        out_shape=jax.ShapeDtypeStruct(term.shape, BF16),
        in_specs=[pl.BlockSpec(memory_space=pltpu.VMEM)] * 9,
        out_specs=pl.BlockSpec(memory_space=pltpu.VMEM),
        compiler_params=params(),
        cost_estimate=cost(4096, 4096),
        name="assembled",
    )(term, keep1, got1, got2, *blocks, q)


def ordered(*arrays):
    return lax.optimization_barrier(arrays)


def shards(psi, potential, beta, strength, atom_slab, pattern, q_tiles):
    planes, width_x, width_y, orbs = psi.shape
    count = beta.shape[0]
    slabs = lax.axis_size("space")
    place = lax.axis_index("space")
    x = lax.rem(place, 2)
    half = width_x // 2
    window = half + 2
    rows1 = half * 5 // 24 * 2
    rows2 = half - rows1
    early = rows1 + 4

    def within(pairs):
        return [(i, j) for i, j in pairs if 0 <= j < slabs]

    swap = [(i, i ^ 1) for i in range(slabs)]
    own_way = within([(i, i + 2 if i % 2 else i - 2) for i in range(slabs)])
    other_way = within([(i, i - 2 if i % 2 else i + 2) for i in range(slabs)])
    groups = lax.axis_size("orb")
    across = [(i, i ^ 2) for i in range(groups)]
    beside = [(i, i ^ 1) for i in range(groups)]
    mine = (half - 2) * x
    theirs = (half - 2) * (1 - x)

    to_x, to_z = prepared(psi, potential, early)
    to_x2 = packed(psi, beta, early)
    xr1 = lax.ppermute(to_x, "space", swap)
    zo = lax.ppermute(to_z, "space", own_way)
    active = jnp.abs(place - atom_slab) <= 1
    beta_m = jnp.where(active[:, None, None, None], beta, jnp.zeros_like(beta))
    gram = jnp.einsum("pzxy,qzxy->pq", beta_m, beta_m, preferred_element_type=F32)
    zf1 = lax.ppermute(xr1, "space", other_way)
    second, _ = ordered(to_x2, xr1)
    xr2 = lax.ppermute(second, "space", swap)
    zf2 = lax.ppermute(xr2, "space", other_way)
    strong = jnp.broadcast_to(strength[:, None], (count, orbs))

    zf1, _ = ordered(zf1, xr2)
    operands = (psi, potential, zo)
    block1, xr_c, zf_c = filtered(slabs, 0, rows1, True, operands, (xr1,), (zf1,))
    y1 = lax.ppermute(block1, "orb", across)
    give2, keep2 = filtered(slabs, rows1, rows2, False, operands, (xr_c, xr2), (zf_c, zf2))
    xr2, _ = ordered(xr2, give2)
    sums, weights = partials(count, atom_slab, psi, beta, xr2, zf2, potential, gram)
    rounds = [1 << k for k in range((slabs - 1).bit_length())]

    def added(values, step):
        pairs = [(i, i ^ step) for i in range(slabs)]
        return values + lax.ppermute(values, "space", pairs)

    for step in rounds[:-1]:
        sums = added(sums, step)
    pattern, q_tiles, _ = ordered(pattern, q_tiles, give2)
    me = lax.axis_index("orb")
    which = jnp.bitwise_xor(me, jnp.arange(groups, dtype=jnp.int32))
    rows_hot = (pattern[:, 0][:, None] == which[None, :]).astype(BF16)
    rows_hot = rows_hot * (pattern[:, 1] == me).astype(BF16)[:, None]
    q = jnp.einsum("ki,kab->iab", rows_hot, q_tiles, preferred_element_type=F32).astype(BF16)
    cg = lax.ppermute(give2, "orb", beside)
    ck = lax.ppermute(keep2, "orb", beside)
    yg = lax.ppermute(give2, "orb", across)
    y1, again, _ = ordered(y1, block1, give2)
    c1 = lax.ppermute(again, "orb", beside)
    yc1 = lax.ppermute(y1, "orb", beside)
    give1, keep1 = rotated((block1, c1, y1, yc1), q, 2)
    got1 = lax.ppermute(give1, "space", swap)
    keep_y, yg, got1, sums = ordered(keep2, yg, got1, sums)
    coefs = coefficients(added(sums, rounds[-1]), strong)
    yk = lax.ppermute(keep_y, "orb", across)
    ycg = lax.ppermute(yg, "orb", beside)
    coefs_c = lax.ppermute(coefs, "orb", beside)
    coefs_y = lax.ppermute(jnp.concatenate([coefs, coefs_c], axis=0), "orb", across)
    coefs_yc, coefs_y = coefs_y[2 * count :], coefs_y[: 2 * count]
    term = nonlocal_term(psi.shape, (coefs, coefs_c, coefs_y, coefs_yc), q, weights)
    (give2,) = rotated((give2, cg, yg, ycg), q, 1)
    got2 = lax.ppermute(give2, "space", swap)
    yk, _, _ = ordered(yk, give2, coefs)
    yck = lax.ppermute(yk, "orb", beside)
    return assembled(term, keep1, got1, got2, (keep2, ck, yk, yck), q)


def solution(mesh):
    placed = (
        P("space", None, None, "orb"),
        P("space", None, None),
        P(None, "space", None, None),
        P(),
        P(),
        P(),
        P(),
    )
    return jax.shard_map(
        shards, mesh=mesh, in_specs=placed, out_specs=P("space", None, None, "orb"), check_vma=False
    )
```

```python
import functools

import jax
import jax.numpy as jnp
from jax import lax
from jax.experimental import pallas as pl
from jax.experimental.pallas import tpu as pltpu
from jax.sharding import PartitionSpec as P

F32 = jnp.float32
BF16 = jnp.bfloat16
VMEM_LIMIT = 24 * 1024 * 1024
SHRINK = 16
FILTER = 100


def params():
    return pltpu.CompilerParams(vmem_limit_bytes=VMEM_LIMIT)


def cost(flops, moved):
    return pl.CostEstimate(flops=flops // SHRINK, bytes_accessed=moved // SHRINK, transcendentals=0)


def inside(p, window):
    return jnp.logical_and(p >= 0, p < window).astype(F32)


def neighbour_sum(width, pairs):
    n = (2 if pairs else 1) * width
    i = lax.broadcasted_iota(jnp.int32, (n, n), 0)
    j = lax.broadcasted_iota(jnp.int32, (n, n), 1)
    linked = jnp.abs(i - j) == 1
    if pairs:
        linked = jnp.logical_and(linked, (i < width) == (j < width))
        linked = jnp.logical_or(linked, jnp.abs(i - j) == width)
    return jnp.where(linked, -0.125, 0.0)


def potential_block(potential):
    lines, width = potential.shape
    gap = jnp.zeros((lines, 64 - width), F32)
    u = (potential - 1.0) * 0.25
    hi = u.astype(BF16).astype(F32)
    return jnp.concatenate([hi, gap, u - hi, gap], axis=1)


def prepare_kernel(early, psi, potential_far, to_x, to_z, potential, sems):
    x = lax.rem(lax.axis_index("space"), 2)
    half = psi.shape[1] // 2
    window = half + 2
    mine, theirs = (half - 2) * x, (half - 2) * (1 - x)
    fetch = pltpu.make_async_copy(potential_far, potential, sems.at[0])
    fetch.start()
    copies = [
        pltpu.make_async_copy(
            psi.at[:, pl.ds(theirs, early)], to_x.at[:, pl.ds(0, early)], sems.at[1]
        ),
        pltpu.make_async_copy(
            psi.at[:, pl.ds(mine, window)], to_z.at[:, pl.ds(0, window)], sems.at[2]
        ),
    ]
    for copy in copies:
        copy.start()
    fetch.wait()
    for plane in range(potential.shape[0]):
        block = potential_block(potential[plane]).astype(BF16)
        to_x[plane, early] = block
        to_z[plane, window] = block
    for copy in copies:
        copy.wait()


def prepared(psi, potential, early):
    planes, width_x, width_y, orbs = psi.shape
    window = width_x // 2 + 2

    def out(rows):
        return jax.ShapeDtypeStruct((planes, rows, width_y, orbs), BF16)

    return pl.pallas_call(
        functools.partial(prepare_kernel, early),
        out_shape=(out(early + 1), out(window + 1)),
        in_specs=[pl.BlockSpec(memory_space=pltpu.MemorySpace.HBM)] * 2,
        out_specs=(pl.BlockSpec(memory_space=pltpu.VMEM),) * 2,
        scratch_shapes=[pltpu.VMEM(potential.shape, F32), pltpu.SemaphoreType.DMA((3,))],
        compiler_params=params(),
        cost_estimate=cost(4096, 4096),
        name="prepared",
    )(*(pltpu.with_memory_space_constraint(a, pltpu.MemorySpace.HBM) for a in (psi, potential)))


def pack_kernel(early, psi, beta, to_x2, far, sem):
    x = lax.rem(lax.axis_index("space"), 2)
    half = psi.shape[1] // 2
    later = half + 2 - early
    _, _, lines, width = beta.shape
    gap = jnp.zeros((lines, 64 - width), F32)
    copy = pltpu.make_async_copy(
        psi.at[:, pl.ds((half - 2) * (1 - x) + early, later)], to_x2.at[:, pl.ds(0, later)], sem
    )
    copy.start()
    each = beta.shape[0] // to_x2.shape[0]

    def pack(i, carry):
        for plane in range(to_x2.shape[0]):
            first, second = (beta[plane * each + i, k].astype(F32) for k in range(2))
            to_x2[plane, later + i] = jnp.concatenate(
                [first, gap, second, gap], axis=1
            ).astype(BF16)
        return carry

    far[...] = beta[:, x]
    lax.fori_loop(0, each, pack, 0)
    copy.wait()


def packed(psi, beta, early):
    planes, width_x, width_y, orbs = psi.shape
    rows = width_x // 2 + 2 - early + beta.shape[0] // planes
    return pl.pallas_call(
        functools.partial(pack_kernel, early),
        out_shape=(
            jax.ShapeDtypeStruct((planes, rows, width_y, orbs), BF16),
            jax.ShapeDtypeStruct((beta.shape[0], *beta.shape[2:]), BF16),
        ),
        in_specs=[
            pl.BlockSpec(memory_space=pltpu.MemorySpace.HBM),
            pl.BlockSpec(memory_space=pltpu.VMEM),
        ],
        out_specs=(pl.BlockSpec(memory_space=pltpu.VMEM),) * 2,
        scratch_shapes=[pltpu.SemaphoreType.DMA],
        compiler_params=params(),
        cost_estimate=cost(4096, 4096),
        name="packed",
    )(pltpu.with_memory_space_constraint(psi, pltpu.MemorySpace.HBM), beta)


def partial_kernel(count, atoms, own, beta, b_x, b_d, potential, gram, out, weights_out, table, acc):
    place = lax.axis_index("space")
    x = lax.rem(place, 2)
    rows, width = potential.shape[1:]
    side = place ^ 1
    beyond = place - 1 + 2 * x
    tri = neighbour_sum(width, False).astype(BF16)
    acc[...] = jnp.zeros_like(acc)
    step = 8

    for k in range(2):
        plane = x if k == 0 else 1 - x
        there = beyond if k == 0 else side
        each = count // b_x.shape[0]
        begin = b_x.shape[1] - each
        u = (potential[plane] - 1.0) * 0.25

        def fill(i, carry):
            for j in range(step):
                p = i * step + j
                here = (jnp.abs(place - atoms[p]) <= 1).astype(F32)
                next_to = (jnp.abs(there - atoms[p]) <= 1).astype(F32)
                b32 = beta[p, plane].astype(F32) * here
                b = b32.astype(BF16)
                if k == 0:
                    other = b_d[p].astype(F32)
                else:
                    both = b_x[p // each, begin + lax.rem(p, each)].astype(F32)
                    other = jnp.where(x == 0, both[:, :width], both[:, 64 : 64 + width])
                sides = beta[p, 1 - plane].astype(F32) * here + other * next_to
                whole = jnp.dot(b, tri, preferred_element_type=F32)
                whole = whole + jnp.dot(tri, b, preferred_element_type=F32)
                whole = whole + u * b32 - 0.125 * sides
                hi = whole.astype(BF16).astype(F32)
                for kind, value in enumerate((b32, hi, whole - hi)):
                    table[pl.ds((kind * count + p) * rows, rows)] = value
            return carry

        lax.fori_loop(0, count // step, fill, 0)

        def use(i, carry):
            totals = []
            for j in range(step):
                r = i * step + j
                weights = table[pl.ds(r, 3 * count, stride=rows)].astype(BF16)
                weights_out[plane, r] = weights
                totals.append(jnp.dot(weights, own[plane, r], preferred_element_type=F32))
            acc[...] += sum(totals[1:], totals[0])
            return carry

        lax.fori_loop(0, rows // step, use, 0)
    out[...] = jnp.zeros_like(out)
    out[0:count] = acc[0:count]
    out[count : 2 * count] = acc[count : 2 * count] + acc[2 * count : 3 * count]
    out[2 * count : 3 * count, 0:count] = gram[...]


def partials(count, atoms, own, beta, b_x, b_d, potential, gram):
    planes, rows, width, orbs = own.shape
    return pl.pallas_call(
        functools.partial(partial_kernel, count),
        out_shape=(
            jax.ShapeDtypeStruct((3 * count, orbs), F32),
            jax.ShapeDtypeStruct((planes, rows, 3 * count, width), BF16),
        ),
        in_specs=[pl.BlockSpec(memory_space=pltpu.SMEM)]
        + [pl.BlockSpec(memory_space=pltpu.VMEM)] * 6,
        out_specs=(pl.BlockSpec(memory_space=pltpu.VMEM),) * 2,
        scratch_shapes=[
            pltpu.VMEM((3 * count * rows, width), F32),
            pltpu.VMEM((3 * count, orbs), F32),
        ],
        compiler_params=params(),
        cost_estimate=cost(4096, 4096),
        name="partials",
    )(atoms, own, beta, b_x, b_d, potential, gram)


def coefficient_kernel(sums, strength, out):
    count, orbs = strength.shape
    coef1 = (strength[...] * sums[0:count]).astype(BF16)
    padded = coef1.astype(F32) * 0.25
    if orbs > count:
        padded = jnp.concatenate([padded, jnp.zeros((orbs - count, orbs), F32)], axis=0)
    proj2 = sums[count : 2 * count] + jnp.dot(
        sums[2 * count : 3 * count],
        padded,
        preferred_element_type=F32,
        precision=lax.Precision.HIGHEST,
    )
    out[0:count] = coef1
    out[count : 2 * count] = (strength[...] * proj2).astype(BF16)


def coefficients(sums, strength):
    count, orbs = strength.shape
    return pl.pallas_call(
        coefficient_kernel,
        out_shape=jax.ShapeDtypeStruct((2 * count, orbs), BF16),
        in_specs=[pl.BlockSpec(memory_space=pltpu.VMEM)] * 2,
        out_specs=pl.BlockSpec(memory_space=pltpu.VMEM),
        compiler_params=params(),
        cost_estimate=cost(4096, 4096),
        name="coefficients",
    )(sums, strength)


def nonlocal_kernel(unroll, a, b, c, d, q, weights, out):
    count, orbs = a.shape[0] // 2, a.shape[1]
    turned = sum(
        jnp.dot(ref[...], q[k], preferred_element_type=F32) for k, ref in enumerate((a, b, c, d))
    )
    turned = turned * 0.25
    one, two = turned[0:count], turned[count : 2 * count]
    right = jnp.concatenate([two, one, one], axis=0)
    hi = right.astype(BF16)
    lo = right - hi.astype(F32)
    right = jnp.concatenate([hi.astype(F32), lo], axis=1).astype(BF16)

    def step(i, carry):
        for k in range(unroll):
            r = i * unroll + k
            for plane in range(weights.shape[0]):
                both = lax.dot_general(
                    weights[plane, r], right, (((0,), (0,)), ((), ())), preferred_element_type=F32
                )
                out[plane, r] = both[:, :orbs] + both[:, orbs:]
        return carry

    lax.fori_loop(0, weights.shape[1] // unroll, step, 0)


def nonlocal_term(shape, coefs, q, weights):
    unroll = max(g for g in (1, 2, 4, 8) if weights.shape[1] % g == 0)
    return pl.pallas_call(
        functools.partial(nonlocal_kernel, unroll),
        out_shape=jax.ShapeDtypeStruct(shape, F32),
        in_specs=[pl.BlockSpec(memory_space=pltpu.VMEM)] * 6,
        out_specs=pl.BlockSpec(memory_space=pltpu.VMEM),
        compiler_params=params(),
        cost_estimate=cost(4096, 4096),
        name="nonlocal",
    )(*coefs, q, weights)


def filter_kernel(slabs, start, parts, joint, *refs):
    own, p_own, zo = refs[:3]
    xrs, zfs = refs[3 : 3 + parts], refs[3 + parts : 3 + 2 * parts]
    extra = 7 if parts > 1 else 4
    outs, scratch = refs[3 + 2 * parts : -extra], refs[-extra:]
    first, lines, diagonals = scratch[:3]
    place = lax.axis_index("space")
    x = lax.rem(place, 2)
    width = own.shape[2]
    cells = 2 * width
    half = own.shape[1] // 2
    orbs = own.shape[3]
    rows = outs[0].shape[1]
    base = (half - 2) * x
    lower = (place >= 2).astype(F32)
    upper = (place < slabs - 2).astype(F32)
    is_odd = x.astype(F32)
    has_zf = lower * (1.0 - is_odd) + upper * is_odd
    has_zo = upper * (1.0 - is_odd) + lower * is_odd
    if parts > 1:
        xr, zf, pots, sems = scratch[3:]
        early = start + 4
        copies = []
        for k, (target, pieces) in enumerate(((xr, xrs), (zf, zfs))):
            rows_in = pieces[0].at[:, pl.ds(0, 8)]
            last = pieces[0].at[:, pl.ds(8, 1)]
            copies += [
                pltpu.make_async_copy(
                    rows_in, target.at[:, pl.ds(start - 4, 8)], sems.at[2 * k]
                ),
                pltpu.make_async_copy(last, pots.at[k], sems.at[2 * k + 1]),
            ]
        for copy in copies:
            copy.start()
        for target, pieces in ((xr, xrs), (zf, zfs)):
            target[:, early:] = pieces[1][:, 0 : target.shape[1] - early]
        for copy in copies:
            copy.wait()
        window = xr.shape[1] // 2
    else:
        xr, zf = xrs[0], zfs[0]
        early = xr.shape[1] - 1
        window = early // 2
        sems = scratch[3]
        copies = [
            pltpu.make_async_copy(piece.at[:, pl.ds(early - 8, 9)], target, sems.at[k])
            for k, (target, piece) in enumerate(((outs[1], xr), (outs[2], zf)))
        ]
        for copy in copies:
            copy.start()
    for c in range(1, 7):
        plane = (c % 2) ^ x
        if c in (2, 3):
            lines[c - 1] = potential_block(p_own[plane])
        else:
            if c == 6:
                tail = zo
            elif parts > 1:
                tail = pots.at[1 if c < 2 else 0]
            else:
                tail = zf if c < 2 else xr
            lines[c - 1] = tail[plane, tail.shape[1] - 1].astype(F32)
        for kind in range(2):
            even, odd = (lines[c - 1, pl.ds(k, half, stride=2)] for k in range(2))
            lanes = slice(64 * kind, 64 * kind + width)
            diagonals[c - 1, kind] = jnp.concatenate([even[:, lanes], odd[:, lanes]], axis=1)

    here = neighbour_sum(width, True)
    i = lax.broadcasted_iota(jnp.int32, (cells, cells), 0)
    diagonal = i == lax.broadcasted_iota(jnp.int32, (cells, cells), 1)

    def local(c, p):
        at = base // 2 + p
        hi = diagonals[c - 1, 0, pl.ds(at, 1)]
        lo = diagonals[c - 1, 1, pl.ds(at, 1)]
        return (
            jnp.where(diagonal, hi, here).astype(BF16),
            jnp.where(diagonal, lo, 0.0).astype(BF16),
        )

    def rows_of(c, w, n):
        plane = (c % 2) ^ x
        if c in (2, 3):
            return own[plane, pl.ds(base + w, n)]
        ref = zf if c < 2 else (xr if c < 6 else zo)
        return ref[plane, pl.ds(w, n)]

    def applied(pair, outer, zs, matrices):
        near = jnp.dot(matrices[0], pair, preferred_element_type=F32)
        near = near + jnp.dot(matrices[1], pair, preferred_element_type=F32)
        return near - 0.125 * (outer + zs)

    def step1(j, carry):
        p = start // 2 + x + j - 1
        q = jnp.clip(p, 0, window - 1)
        has_below = inside(p - 1, window)
        has_above = inside(p + 1, window)
        valid = inside(p, window)
        below = jnp.maximum(2 * q - 1, 0)
        above = jnp.minimum(2 * q + 2, 2 * window - 1)
        pair = [rows_of(c, 2 * q, 2).reshape(cells, orbs) for c in range(8)]
        vs = [v.astype(F32) for v in pair]
        for c in range(1, 7):
            outer = jnp.concatenate(
                [
                    rows_of(c, below, 1)[0].astype(F32) * has_below,
                    rows_of(c, above, 1)[0].astype(F32) * has_above,
                ],
                axis=0,
            )
            f = applied(pair[c], outer, vs[c - 1] + vs[c + 1], local(c, q))
            keep = valid
            if c == 1:
                keep = valid * has_zf
            if c == 6:
                keep = valid * has_zo
            first[c - 1, pl.ds(2 * j, 2)] = (f * keep).astype(BF16).reshape(2, width, orbs)
        return carry

    lax.fori_loop(0, rows // 2 + 2, step1, 0)

    def step2(j, carry):
        p = start // 2 + x + j
        pair = [first[c - 1, pl.ds(2 * j + 2, 2)].reshape(cells, orbs) for c in range(1, 7)]
        vs = [v.astype(F32) for v in pair]
        for c in range(2, 6):
            outer = jnp.concatenate(
                [first[c - 1, 2 * j + 1].astype(F32), first[c - 1, 2 * j + 4].astype(F32)], axis=0
            )
            f = applied(pair[c - 1], outer, vs[c - 2] + vs[c], local(c, p))
            f = f.astype(BF16).reshape(2, width, orbs)
            plane = (c % 2) ^ x
            if joint:
                outs[0][plane + (2 if c in (2, 3) else 0), pl.ds(2 * j, 2)] = f
            else:
                outs[1 if c in (2, 3) else 0][plane, pl.ds(2 * j, 2)] = f
        return carry

    lax.fori_loop(0, rows // 2, step2, 0)
    if parts == 1:
        for copy in copies:
            copy.wait()


def filtered(slabs, start, rows, joint, operands, xrs, zfs):
    own = operands[0]
    planes, _, width, orbs = own.shape
    parts = len(xrs)
    shape = (2 * planes if joint else planes, rows, width, orbs)
    out = (jax.ShapeDtypeStruct(shape, BF16),) * (1 if joint else 2)
    if parts == 1:
        out += (jax.ShapeDtypeStruct((planes, 9, width, orbs), BF16),) * 2
    cells = 10 * rows * width
    scratch = [
        pltpu.VMEM((6, rows + 4, width, orbs), BF16),
        pltpu.VMEM((6, width, orbs), F32),
        pltpu.VMEM((6, 2, own.shape[1] // 2, 2 * width), F32),
    ]
    local = pl.BlockSpec(memory_space=pltpu.VMEM)
    distant = pl.BlockSpec(memory_space=pltpu.MemorySpace.HBM)
    in_specs, out_specs = [local] * (len(operands) + 2 * parts), [local] * len(out)
    if parts == 1:
        out_specs[1:] = [distant] * 2
        scratch += [pltpu.SemaphoreType.DMA((2,))]
    else:
        for k in (0, parts):
            in_specs[len(operands) + k] = distant
        window = own.shape[1] // 2 + 2
        scratch += [pltpu.VMEM((planes, window, width, orbs), BF16)] * 2
        scratch += [pltpu.VMEM((2, planes, 1, width, orbs), BF16), pltpu.SemaphoreType.DMA((4,))]
    return pl.pallas_call(
        functools.partial(filter_kernel, slabs, start, parts, joint),
        out_shape=out,
        in_specs=in_specs,
        out_specs=tuple(out_specs),
        scratch_shapes=scratch,
        compiler_params=params(),
        cost_estimate=cost(2 * cells * 32 * orbs, FILTER * cells * orbs * 4),
        name="filtered",
    )(*operands, *xrs, *zfs)


def rotate_kernel(group, *refs):
    a, b, c, d, q = refs[:5]
    outs = refs[5:]
    _, rows, width, orbs = a.shape
    planes = outs[0].shape[0]
    low = jnp.concatenate([q[0], q[1]], axis=0)
    high = jnp.concatenate([q[2], q[3]], axis=0)

    def one(j, carry):
        for plane in range(a.shape[0]):
            def take(ref):
                return ref[plane, pl.ds(group * j, group)].reshape(group * width, orbs)

            total = jnp.dot(
                jnp.concatenate([take(a), take(b)], axis=1), low, preferred_element_type=F32
            )
            total = total + jnp.dot(
                jnp.concatenate([take(c), take(d)], axis=1), high, preferred_element_type=F32
            )
            outs[plane // planes][plane % planes, pl.ds(group * j, group)] = total.astype(
                BF16
            ).reshape(group, width, orbs)
        return carry

    lax.fori_loop(0, rows // group, one, 0)


def rotated(blocks, q, pieces):
    a = blocks[0]
    size = a.size
    group = max(g for g in range(1, 9) if a.shape[1] % g == 0)
    out = jax.ShapeDtypeStruct((a.shape[0] // pieces, *a.shape[1:]), BF16)
    return pl.pallas_call(
        functools.partial(rotate_kernel, group),
        out_shape=(out,) * pieces,
        in_specs=[pl.BlockSpec(memory_space=pltpu.VMEM)] * 5,
        out_specs=(pl.BlockSpec(memory_space=pltpu.VMEM),) * pieces,
        compiler_params=params(),
        cost_estimate=cost(8 * size * a.shape[3], 10 * size),
        name="rotated",
    )(*blocks, q)


def assemble_kernel(group, term, keep1, got1, got2, a, b, c, d, q, out):
    half = term.shape[1] // 2
    width, orbs = term.shape[2:]
    x = lax.rem(lax.axis_index("space"), 2)
    rows1, rows2 = keep1.shape[1], got2.shape[1]
    for ref, at in (
        (keep1, half * x),
        (got1, half * (1 - x)),
        (got2, half * (1 - x) + rows1),
    ):
        where = pl.ds(at, ref.shape[1])
        out[:, where] = (ref[...].astype(F32) + term[:, where]).astype(BF16)
    low = jnp.concatenate([q[0], q[1]], axis=0)
    high = jnp.concatenate([q[2], q[3]], axis=0)

    def one(j, carry):
        where = pl.ds(half * x + rows1 + group * j, group)
        for plane in range(a.shape[0]):
            def take(ref):
                return ref[plane, pl.ds(group * j, group)].reshape(group * width, orbs)

            total = jnp.dot(
                jnp.concatenate([take(a), take(b)], axis=1), low, preferred_element_type=F32
            )
            total = total + jnp.dot(
                jnp.concatenate([take(c), take(d)], axis=1), high, preferred_element_type=F32
            )
            total = total.reshape(group, width, orbs) + term[plane, where]
            out[plane, where] = total.astype(BF16)
        return carry

    lax.fori_loop(0, rows2 // group, one, 0)


def assembled(term, keep1, got1, got2, blocks, q):
    group = max(g for g in range(1, 9) if got2.shape[1] % g == 0)
    return pl.pallas_call(
        functools.partial(assemble_kernel, group),
        out_shape=jax.ShapeDtypeStruct(term.shape, BF16),
        in_specs=[pl.BlockSpec(memory_space=pltpu.VMEM)] * 9,
        out_specs=pl.BlockSpec(memory_space=pltpu.VMEM),
        compiler_params=params(),
        cost_estimate=cost(4096, 4096),
        name="assembled",
    )(term, keep1, got1, got2, *blocks, q)


def ordered(*arrays):
    return lax.optimization_barrier(arrays)


def shards(psi, potential, beta, strength, atom_slab, pattern, q_tiles):
    planes, width_x, width_y, orbs = psi.shape
    count = beta.shape[0]
    slabs = lax.axis_size("space")
    place = lax.axis_index("space")
    x = lax.rem(place, 2)
    half = width_x // 2
    window = half + 2
    rows1 = half * 5 // 24 * 2
    rows2 = half - rows1
    early = rows1 + 4

    def within(pairs):
        return [(i, j) for i, j in pairs if 0 <= j < slabs]

    swap = [(i, i ^ 1) for i in range(slabs)]
    own_way = within([(i, i + 2 if i % 2 else i - 2) for i in range(slabs)])
    other_way = within([(i, i - 2 if i % 2 else i + 2) for i in range(slabs)])
    groups = lax.axis_size("orb")
    across = [(i, i ^ 2) for i in range(groups)]
    beside = [(i, i ^ 1) for i in range(groups)]
    mine = (half - 2) * x
    theirs = (half - 2) * (1 - x)

    to_x, to_z = prepared(psi, potential, early)
    to_x2, far = packed(psi, beta, early)
    raster = within([(i, i + 1 if i % 2 else i - 1) for i in range(slabs)])
    f_d = lax.ppermute(far, "space", raster)
    to_z, f_d = ordered(to_z, f_d)
    xr1 = lax.ppermute(to_x, "space", swap)
    zo = lax.ppermute(to_z, "space", own_way)
    active = jnp.abs(place - atom_slab) <= 1
    beta_m = jnp.where(active[:, None, None, None], beta, jnp.zeros_like(beta))
    gram = jnp.einsum("pzxy,qzxy->pq", beta_m, beta_m, preferred_element_type=F32)
    zf1 = lax.ppermute(xr1, "space", other_way)
    second, _ = ordered(to_x2, xr1)
    xr2 = lax.ppermute(second, "space", swap)
    zf2 = lax.ppermute(xr2, "space", other_way)
    strong = jnp.broadcast_to(strength[:, None], (count, orbs))

    zf1, _ = ordered(zf1, xr2)
    operands = (psi, potential, zo)
    block1, xr_c, zf_c = filtered(slabs, 0, rows1, True, operands, (xr1,), (zf1,))
    y1 = lax.ppermute(block1, "orb", across)
    f_d, _ = ordered(f_d, block1)
    sums, weights = partials(count, atom_slab, psi, beta, xr2, f_d, potential, gram)
    zf2, sums = ordered(zf2, sums)
    give2, keep2 = filtered(slabs, rows1, rows2, False, operands, (xr_c, xr2), (zf_c, zf2))
    rounds = [1 << k for k in range((slabs - 1).bit_length())]

    def added(values, step):
        pairs = [(i, i ^ step) for i in range(slabs)]
        return values + lax.ppermute(values, "space", pairs)

    for step in rounds[:-1]:
        sums = added(sums, step)
    pattern, q_tiles, _ = ordered(pattern, q_tiles, give2)
    me = lax.axis_index("orb")
    which = jnp.bitwise_xor(me, jnp.arange(groups, dtype=jnp.int32))
    rows_hot = (pattern[:, 0][:, None] == which[None, :]).astype(BF16)
    rows_hot = rows_hot * (pattern[:, 1] == me).astype(BF16)[:, None]
    q = jnp.einsum("ki,kab->iab", rows_hot, q_tiles, preferred_element_type=F32).astype(BF16)
    cg = lax.ppermute(give2, "orb", beside)
    ck = lax.ppermute(keep2, "orb", beside)
    yg = lax.ppermute(give2, "orb", across)
    y1, again, _ = ordered(y1, block1, give2)
    c1 = lax.ppermute(again, "orb", beside)
    yc1 = lax.ppermute(y1, "orb", beside)
    give1, keep1 = rotated((block1, c1, y1, yc1), q, 2)
    got1 = lax.ppermute(give1, "space", swap)
    keep_y, yg, got1, sums = ordered(keep2, yg, got1, sums)
    coefs = coefficients(added(sums, rounds[-1]), strong)
    yk = lax.ppermute(keep_y, "orb", across)
    ycg = lax.ppermute(yg, "orb", beside)
    coefs_c = lax.ppermute(coefs, "orb", beside)
    coefs_y = lax.ppermute(jnp.concatenate([coefs, coefs_c], axis=0), "orb", across)
    coefs_yc, coefs_y = coefs_y[2 * count :], coefs_y[: 2 * count]
    term = nonlocal_term(psi.shape, (coefs, coefs_c, coefs_y, coefs_yc), q, weights)
    (give2,) = rotated((give2, cg, yg, ycg), q, 1)
    got2 = lax.ppermute(give2, "space", swap)
    yk, _, _ = ordered(yk, give2, coefs)
    yck = lax.ppermute(yk, "orb", beside)
    return assembled(term, keep1, got1, got2, (keep2, ck, yk, yck), q)


def solution(mesh):
    placed = (
        P("space", None, None, "orb"),
        P("space", None, None),
        P(None, "space", None, None),
        P(),
        P(),
        P(),
        P(),
    )
    return jax.shard_map(
        shards, mesh=mesh, in_specs=placed, out_specs=P("space", None, None, "orb"), check_vma=False
    )
```

```python
import functools

import jax
import jax.numpy as jnp
from jax import lax
from jax.experimental import pallas as pl
from jax.experimental.pallas import tpu as pltpu
from jax.sharding import PartitionSpec as P

F32 = jnp.float32
BF16 = jnp.bfloat16
VMEM_LIMIT = 24 * 1024 * 1024
SHRINK = 16
FILTER = 100


def params():
    return pltpu.CompilerParams(vmem_limit_bytes=VMEM_LIMIT)


def cost(flops, moved):
    return pl.CostEstimate(flops=flops // SHRINK, bytes_accessed=moved // SHRINK, transcendentals=0)


def inside(p, window):
    return jnp.logical_and(p >= 0, p < window).astype(F32)


def neighbour_sum(width, pairs):
    n = (2 if pairs else 1) * width
    i = lax.broadcasted_iota(jnp.int32, (n, n), 0)
    j = lax.broadcasted_iota(jnp.int32, (n, n), 1)
    linked = jnp.abs(i - j) == 1
    if pairs:
        linked = jnp.logical_and(linked, (i < width) == (j < width))
        linked = jnp.logical_or(linked, jnp.abs(i - j) == width)
    return jnp.where(linked, -0.125, 0.0)


def potential_block(potential):
    lines, width = potential.shape
    gap = jnp.zeros((lines, 64 - width), F32)
    u = (potential - 1.0) * 0.25
    hi = u.astype(BF16).astype(F32)
    return jnp.concatenate([hi, gap, u - hi, gap], axis=1)


def prepare_kernel(early, psi, potential_far, to_x, to_z, potential, sems):
    x = lax.rem(lax.axis_index("space"), 2)
    half = psi.shape[1] // 2
    window = half + 2
    mine, theirs = (half - 2) * x, (half - 2) * (1 - x)
    fetch = pltpu.make_async_copy(potential_far, potential, sems.at[0])
    fetch.start()
    copies = [
        pltpu.make_async_copy(
            psi.at[:, pl.ds(theirs, early)], to_x.at[:, pl.ds(0, early)], sems.at[1]
        ),
        pltpu.make_async_copy(
            psi.at[:, pl.ds(mine, window)], to_z.at[:, pl.ds(0, window)], sems.at[2]
        ),
    ]
    for copy in copies:
        copy.start()
    fetch.wait()
    for plane in range(potential.shape[0]):
        block = potential_block(potential[plane]).astype(BF16)
        to_x[plane, early] = block
        to_z[plane, window] = block
    for copy in copies:
        copy.wait()


def prepared(psi, potential, early):
    planes, width_x, width_y, orbs = psi.shape
    window = width_x // 2 + 2

    def out(rows):
        return jax.ShapeDtypeStruct((planes, rows, width_y, orbs), BF16)

    return pl.pallas_call(
        functools.partial(prepare_kernel, early),
        out_shape=(out(early + 1), out(window + 1)),
        in_specs=[pl.BlockSpec(memory_space=pltpu.MemorySpace.HBM)] * 2,
        out_specs=(pl.BlockSpec(memory_space=pltpu.VMEM),) * 2,
        scratch_shapes=[pltpu.VMEM(potential.shape, F32), pltpu.SemaphoreType.DMA((3,))],
        compiler_params=params(),
        cost_estimate=cost(4096, 4096),
        name="prepared",
    )(*(pltpu.with_memory_space_constraint(a, pltpu.MemorySpace.HBM) for a in (psi, potential)))


def pack_kernel(early, psi, beta, to_x2, far, sem):
    x = lax.rem(lax.axis_index("space"), 2)
    half = psi.shape[1] // 2
    later = half + 2 - early
    _, _, lines, width = beta.shape
    gap = jnp.zeros((lines, 64 - width), F32)
    copy = pltpu.make_async_copy(
        psi.at[:, pl.ds((half - 2) * (1 - x) + early, later)], to_x2.at[:, pl.ds(0, later)], sem
    )
    copy.start()
    each = beta.shape[0] // to_x2.shape[0]

    def pack(i, carry):
        for plane in range(to_x2.shape[0]):
            first, second = (beta[plane * each + i, k].astype(F32) for k in range(2))
            to_x2[plane, later + i] = jnp.concatenate(
                [first, gap, second, gap], axis=1
            ).astype(BF16)
        return carry

    far[...] = beta[:, x]
    lax.fori_loop(0, each, pack, 0)
    copy.wait()


def packed(psi, beta, early):
    planes, width_x, width_y, orbs = psi.shape
    rows = width_x // 2 + 2 - early + beta.shape[0] // planes
    return pl.pallas_call(
        functools.partial(pack_kernel, early),
        out_shape=(
            jax.ShapeDtypeStruct((planes, rows, width_y, orbs), BF16),
            jax.ShapeDtypeStruct((beta.shape[0], *beta.shape[2:]), BF16),
        ),
        in_specs=[
            pl.BlockSpec(memory_space=pltpu.MemorySpace.HBM),
            pl.BlockSpec(memory_space=pltpu.VMEM),
        ],
        out_specs=(pl.BlockSpec(memory_space=pltpu.VMEM),) * 2,
        scratch_shapes=[pltpu.SemaphoreType.DMA],
        compiler_params=params(),
        cost_estimate=cost(4096, 4096),
        name="packed",
    )(pltpu.with_memory_space_constraint(psi, pltpu.MemorySpace.HBM), beta)


def partial_kernel(count, atoms, own, beta, b_x, b_d, potential, gram, out, weights_out, table, acc):
    place = lax.axis_index("space")
    x = lax.rem(place, 2)
    rows, width = potential.shape[1:]
    side = place ^ 1
    beyond = place - 1 + 2 * x
    tri = neighbour_sum(width, False).astype(BF16)
    acc[...] = jnp.zeros_like(acc)
    step = 8

    for k in range(2):
        plane = x if k == 0 else 1 - x
        there = beyond if k == 0 else side
        each = count // b_x.shape[0]
        begin = b_x.shape[1] - each
        u = (potential[plane] - 1.0) * 0.25

        def fill(i, carry):
            for j in range(step):
                p = i * step + j
                here = (jnp.abs(place - atoms[p]) <= 1).astype(F32)
                next_to = (jnp.abs(there - atoms[p]) <= 1).astype(F32)
                b32 = beta[p, plane].astype(F32) * here
                b = b32.astype(BF16)
                if k == 0:
                    other = b_d[p].astype(F32)
                else:
                    both = b_x[p // each, begin + lax.rem(p, each)].astype(F32)
                    other = jnp.where(x == 0, both[:, :width], both[:, 64 : 64 + width])
                sides = beta[p, 1 - plane].astype(F32) * here + other * next_to
                whole = jnp.dot(b, tri, preferred_element_type=F32)
                whole = whole + jnp.dot(tri, b, preferred_element_type=F32)
                whole = whole + u * b32 - 0.125 * sides
                hi = whole.astype(BF16).astype(F32)
                for kind, value in enumerate((b32, hi, whole - hi)):
                    table[pl.ds((kind * count + p) * rows, rows)] = value
            return carry

        lax.fori_loop(0, count // step, fill, 0)

        def use(i, carry):
            totals = []
            for j in range(step):
                r = i * step + j
                weights = table[pl.ds(r, 3 * count, stride=rows)].astype(BF16)
                weights_out[plane, r] = weights
                totals.append(jnp.dot(weights, own[plane, r], preferred_element_type=F32))
            acc[...] += sum(totals[1:], totals[0])
            return carry

        lax.fori_loop(0, rows // step, use, 0)
    out[...] = jnp.zeros_like(out)
    out[0:count] = acc[0:count]
    out[count : 2 * count] = acc[count : 2 * count] + acc[2 * count : 3 * count]
    out[2 * count : 3 * count, 0:count] = gram[...]


def partials(count, atoms, own, beta, b_x, b_d, potential, gram):
    planes, rows, width, orbs = own.shape
    return pl.pallas_call(
        functools.partial(partial_kernel, count),
        out_shape=(
            jax.ShapeDtypeStruct((3 * count, orbs), F32),
            jax.ShapeDtypeStruct((planes, rows, 3 * count, width), BF16),
        ),
        in_specs=[pl.BlockSpec(memory_space=pltpu.SMEM)]
        + [pl.BlockSpec(memory_space=pltpu.VMEM)] * 6,
        out_specs=(pl.BlockSpec(memory_space=pltpu.VMEM),) * 2,
        scratch_shapes=[
            pltpu.VMEM((3 * count * rows, width), F32),
            pltpu.VMEM((3 * count, orbs), F32),
        ],
        compiler_params=params(),
        cost_estimate=cost(4096, 4096),
        name="partials",
    )(atoms, own, beta, b_x, b_d, potential, gram)


def coefficient_kernel(sums, strength, out):
    count, orbs = strength.shape
    coef1 = (strength[...] * sums[0:count]).astype(BF16)
    padded = coef1.astype(F32) * 0.25
    if orbs > count:
        padded = jnp.concatenate([padded, jnp.zeros((orbs - count, orbs), F32)], axis=0)
    proj2 = sums[count : 2 * count] + jnp.dot(
        sums[2 * count : 3 * count],
        padded,
        preferred_element_type=F32,
        precision=lax.Precision.HIGHEST,
    )
    out[0:count] = coef1
    out[count : 2 * count] = (strength[...] * proj2).astype(BF16)


def coefficients(sums, strength):
    count, orbs = strength.shape
    return pl.pallas_call(
        coefficient_kernel,
        out_shape=jax.ShapeDtypeStruct((2 * count, orbs), BF16),
        in_specs=[pl.BlockSpec(memory_space=pltpu.VMEM)] * 2,
        out_specs=pl.BlockSpec(memory_space=pltpu.VMEM),
        compiler_params=params(),
        cost_estimate=cost(4096, 4096),
        name="coefficients",
    )(sums, strength)


def nonlocal_kernel(unroll, a, b, c, d, q, weights, out):
    count, orbs = a.shape[0] // 2, a.shape[1]
    turned = sum(
        jnp.dot(ref[...], q[k], preferred_element_type=F32) for k, ref in enumerate((a, b, c, d))
    )
    turned = turned * 0.25
    one, two = turned[0:count], turned[count : 2 * count]
    right = jnp.concatenate([two, one, one], axis=0)
    hi = right.astype(BF16)
    lo = right - hi.astype(F32)
    right = jnp.concatenate([hi.astype(F32), lo], axis=1).astype(BF16)

    def step(i, carry):
        for k in range(unroll):
            r = i * unroll + k
            for plane in range(weights.shape[0]):
                both = lax.dot_general(
                    weights[plane, r], right, (((0,), (0,)), ((), ())), preferred_element_type=F32
                )
                out[plane, r] = both[:, :orbs] + both[:, orbs:]
        return carry

    lax.fori_loop(0, weights.shape[1] // unroll, step, 0)


def nonlocal_term(shape, coefs, q, weights):
    unroll = max(g for g in (1, 2, 4, 8) if weights.shape[1] % g == 0)
    return pl.pallas_call(
        functools.partial(nonlocal_kernel, unroll),
        out_shape=jax.ShapeDtypeStruct(shape, F32),
        in_specs=[pl.BlockSpec(memory_space=pltpu.VMEM)] * 6,
        out_specs=pl.BlockSpec(memory_space=pltpu.VMEM),
        compiler_params=params(),
        cost_estimate=cost(4096, 4096),
        name="nonlocal",
    )(*coefs, q, weights)


def filter_kernel(slabs, start, parts, joint, *refs):
    own, p_own, zo = refs[:3]
    xrs, zfs = refs[3 : 3 + parts], refs[3 + parts : 3 + 2 * parts]
    extra = 5 if parts > 1 else 3
    outs, scratch = refs[3 + 2 * parts : -extra], refs[-extra:]
    first, lines, diagonals = scratch[:3]
    place = lax.axis_index("space")
    x = lax.rem(place, 2)
    width = own.shape[2]
    cells = 2 * width
    half = own.shape[1] // 2
    orbs = own.shape[3]
    rows = outs[0].shape[1]
    base = (half - 2) * x
    lower = (place >= 2).astype(F32)
    upper = (place < slabs - 2).astype(F32)
    is_odd = x.astype(F32)
    has_zf = lower * (1.0 - is_odd) + upper * is_odd
    has_zo = upper * (1.0 - is_odd) + lower * is_odd
    if parts > 1:
        xr, zf = scratch[3], scratch[4]
        early = start + 4
        for target, pieces in ((xr, xrs), (zf, zfs)):
            target[:, start - 4 : early] = pieces[0][:, 0:8]
            target[:, early:] = pieces[1][:, 0 : target.shape[1] - early]
        window = xr.shape[1] // 2
    else:
        xr, zf = xrs[0], zfs[0]
        early = xr.shape[1] - 1
        window = early // 2
        for target, piece in ((outs[1], xr), (outs[2], zf)):
            target[...] = piece[:, early - 8 :]
    for c in range(1, 7):
        plane = (c % 2) ^ x
        if c in (2, 3):
            lines[c - 1] = potential_block(p_own[plane])
        else:
            ref = zfs[0] if c < 2 else (xrs[0] if c < 6 else zo)
            lines[c - 1] = ref[plane, ref.shape[1] - 1].astype(F32)
        for kind in range(2):
            even, odd = (lines[c - 1, pl.ds(k, half, stride=2)] for k in range(2))
            lanes = slice(64 * kind, 64 * kind + width)
            diagonals[c - 1, kind] = jnp.concatenate([even[:, lanes], odd[:, lanes]], axis=1)

    here = neighbour_sum(width, True)
    i = lax.broadcasted_iota(jnp.int32, (cells, cells), 0)
    diagonal = i == lax.broadcasted_iota(jnp.int32, (cells, cells), 1)

    def local(c, p):
        at = base // 2 + p
        hi = diagonals[c - 1, 0, pl.ds(at, 1)]
        lo = diagonals[c - 1, 1, pl.ds(at, 1)]
        return (
            jnp.where(diagonal, hi, here).astype(BF16),
            jnp.where(diagonal, lo, 0.0).astype(BF16),
        )

    def rows_of(c, w, n):
        plane = (c % 2) ^ x
        if c in (2, 3):
            return own[plane, pl.ds(base + w, n)]
        ref = zf if c < 2 else (xr if c < 6 else zo)
        return ref[plane, pl.ds(w, n)]

    def applied(pair, outer, zs, matrices):
        near = jnp.dot(matrices[0], pair, preferred_element_type=F32)
        near = near + jnp.dot(matrices[1], pair, preferred_element_type=F32)
        return near - 0.125 * (outer + zs)

    def step1(j, carry):
        p = start // 2 + x + j - 1
        q = jnp.clip(p, 0, window - 1)
        has_below = inside(p - 1, window)
        has_above = inside(p + 1, window)
        valid = inside(p, window)
        below = jnp.maximum(2 * q - 1, 0)
        above = jnp.minimum(2 * q + 2, 2 * window - 1)
        pair = [rows_of(c, 2 * q, 2).reshape(cells, orbs) for c in range(8)]
        vs = [v.astype(F32) for v in pair]
        for c in range(1, 7):
            outer = jnp.concatenate(
                [
                    rows_of(c, below, 1)[0].astype(F32) * has_below,
                    rows_of(c, above, 1)[0].astype(F32) * has_above,
                ],
                axis=0,
            )
            f = applied(pair[c], outer, vs[c - 1] + vs[c + 1], local(c, q))
            keep = valid
            if c == 1:
                keep = valid * has_zf
            if c == 6:
                keep = valid * has_zo
            first[c - 1, pl.ds(2 * j, 2)] = (f * keep).astype(BF16).reshape(2, width, orbs)
        return carry

    lax.fori_loop(0, rows // 2 + 2, step1, 0)

    def step2(j, carry):
        p = start // 2 + x + j
        pair = [first[c - 1, pl.ds(2 * j + 2, 2)].reshape(cells, orbs) for c in range(1, 7)]
        vs = [v.astype(F32) for v in pair]
        for c in range(2, 6):
            outer = jnp.concatenate(
                [first[c - 1, 2 * j + 1].astype(F32), first[c - 1, 2 * j + 4].astype(F32)], axis=0
            )
            f = applied(pair[c - 1], outer, vs[c - 2] + vs[c], local(c, p))
            f = f.astype(BF16).reshape(2, width, orbs)
            plane = (c % 2) ^ x
            if joint:
                outs[0][plane + (2 if c in (2, 3) else 0), pl.ds(2 * j, 2)] = f
            else:
                outs[1 if c in (2, 3) else 0][plane, pl.ds(2 * j, 2)] = f
        return carry

    lax.fori_loop(0, rows // 2, step2, 0)


def filtered(slabs, start, rows, joint, operands, xrs, zfs):
    own = operands[0]
    planes, _, width, orbs = own.shape
    parts = len(xrs)
    shape = (2 * planes if joint else planes, rows, width, orbs)
    out = (jax.ShapeDtypeStruct(shape, BF16),) * (1 if joint else 2)
    if parts == 1:
        out += (jax.ShapeDtypeStruct((planes, 9, width, orbs), BF16),) * 2
    cells = 10 * rows * width
    scratch = [
        pltpu.VMEM((6, rows + 4, width, orbs), BF16),
        pltpu.VMEM((6, width, orbs), F32),
        pltpu.VMEM((6, 2, own.shape[1] // 2, 2 * width), F32),
    ]
    if parts > 1:
        window = own.shape[1] // 2 + 2
        scratch += [pltpu.VMEM((planes, window, width, orbs), BF16)] * 2
    return pl.pallas_call(
        functools.partial(filter_kernel, slabs, start, parts, joint),
        out_shape=out,
        in_specs=[pl.BlockSpec(memory_space=pltpu.VMEM)] * (len(operands) + 2 * parts),
        out_specs=(pl.BlockSpec(memory_space=pltpu.VMEM),) * len(out),
        scratch_shapes=scratch,
        compiler_params=params(),
        cost_estimate=cost(2 * cells * 32 * orbs, FILTER * cells * orbs * 4),
        name="filtered",
    )(*operands, *xrs, *zfs)


def rotate_kernel(group, *refs):
    a, b, c, d, q = refs[:5]
    outs = refs[5:]
    _, rows, width, orbs = a.shape
    planes = outs[0].shape[0]
    low = jnp.concatenate([q[0], q[1]], axis=0)
    high = jnp.concatenate([q[2], q[3]], axis=0)

    def one(j, carry):
        for plane in range(a.shape[0]):
            def take(ref):
                return ref[plane, pl.ds(group * j, group)].reshape(group * width, orbs)

            total = jnp.dot(
                jnp.concatenate([take(a), take(b)], axis=1), low, preferred_element_type=F32
            )
            total = total + jnp.dot(
                jnp.concatenate([take(c), take(d)], axis=1), high, preferred_element_type=F32
            )
            outs[plane // planes][plane % planes, pl.ds(group * j, group)] = total.astype(
                BF16
            ).reshape(group, width, orbs)
        return carry

    lax.fori_loop(0, rows // group, one, 0)


def rotated(blocks, q, pieces):
    a = blocks[0]
    size = a.size
    group = max(g for g in range(1, 9) if a.shape[1] % g == 0)
    out = jax.ShapeDtypeStruct((a.shape[0] // pieces, *a.shape[1:]), BF16)
    return pl.pallas_call(
        functools.partial(rotate_kernel, group),
        out_shape=(out,) * pieces,
        in_specs=[pl.BlockSpec(memory_space=pltpu.VMEM)] * 5,
        out_specs=(pl.BlockSpec(memory_space=pltpu.VMEM),) * pieces,
        compiler_params=params(),
        cost_estimate=cost(8 * size * a.shape[3], 10 * size),
        name="rotated",
    )(*blocks, q)


def assemble_kernel(group, term, keep1, got1, got2, a, b, c, d, q, out):
    half = term.shape[1] // 2
    width, orbs = term.shape[2:]
    x = lax.rem(lax.axis_index("space"), 2)
    rows1, rows2 = keep1.shape[1], got2.shape[1]
    for ref, at in (
        (keep1, half * x),
        (got1, half * (1 - x)),
        (got2, half * (1 - x) + rows1),
    ):
        where = pl.ds(at, ref.shape[1])
        out[:, where] = (ref[...].astype(F32) + term[:, where]).astype(BF16)
    low = jnp.concatenate([q[0], q[1]], axis=0)
    high = jnp.concatenate([q[2], q[3]], axis=0)

    def one(j, carry):
        where = pl.ds(half * x + rows1 + group * j, group)
        for plane in range(a.shape[0]):
            def take(ref):
                return ref[plane, pl.ds(group * j, group)].reshape(group * width, orbs)

            total = jnp.dot(
                jnp.concatenate([take(a), take(b)], axis=1), low, preferred_element_type=F32
            )
            total = total + jnp.dot(
                jnp.concatenate([take(c), take(d)], axis=1), high, preferred_element_type=F32
            )
            total = total.reshape(group, width, orbs) + term[plane, where]
            out[plane, where] = total.astype(BF16)
        return carry

    lax.fori_loop(0, rows2 // group, one, 0)


def assembled(term, keep1, got1, got2, blocks, q):
    group = max(g for g in range(1, 9) if got2.shape[1] % g == 0)
    return pl.pallas_call(
        functools.partial(assemble_kernel, group),
        out_shape=jax.ShapeDtypeStruct(term.shape, BF16),
        in_specs=[pl.BlockSpec(memory_space=pltpu.VMEM)] * 9,
        out_specs=pl.BlockSpec(memory_space=pltpu.VMEM),
        compiler_params=params(),
        cost_estimate=cost(4096, 4096),
        name="assembled",
    )(term, keep1, got1, got2, *blocks, q)


def ordered(*arrays):
    return lax.optimization_barrier(arrays)


def shards(psi, potential, beta, strength, atom_slab, pattern, q_tiles):
    planes, width_x, width_y, orbs = psi.shape
    count = beta.shape[0]
    slabs = lax.axis_size("space")
    place = lax.axis_index("space")
    x = lax.rem(place, 2)
    half = width_x // 2
    window = half + 2
    rows1 = half * 5 // 24 * 2
    rows2 = half - rows1
    early = rows1 + 4

    def within(pairs):
        return [(i, j) for i, j in pairs if 0 <= j < slabs]

    swap = [(i, i ^ 1) for i in range(slabs)]
    own_way = within([(i, i + 2 if i % 2 else i - 2) for i in range(slabs)])
    other_way = within([(i, i - 2 if i % 2 else i + 2) for i in range(slabs)])
    groups = lax.axis_size("orb")
    across = [(i, i ^ 2) for i in range(groups)]
    beside = [(i, i ^ 1) for i in range(groups)]
    mine = (half - 2) * x
    theirs = (half - 2) * (1 - x)

    to_x, to_z = prepared(psi, potential, early)
    to_x2, far = packed(psi, beta, early)
    raster = within([(i, i + 1 if i % 2 else i - 1) for i in range(slabs)])
    f_d = lax.ppermute(far, "space", raster)
    xr1 = lax.ppermute(to_x, "space", swap)
    zo = lax.ppermute(to_z, "space", own_way)
    active = jnp.abs(place - atom_slab) <= 1
    beta_m = jnp.where(active[:, None, None, None], beta, jnp.zeros_like(beta))
    gram = jnp.einsum("pzxy,qzxy->pq", beta_m, beta_m, preferred_element_type=F32)
    zf1 = lax.ppermute(xr1, "space", other_way)
    second, _ = ordered(to_x2, xr1)
    xr2 = lax.ppermute(second, "space", swap)
    zf2 = lax.ppermute(xr2, "space", other_way)
    strong = jnp.broadcast_to(strength[:, None], (count, orbs))

    zf1, _ = ordered(zf1, xr2)
    operands = (psi, potential, zo)
    block1, xr_c, zf_c = filtered(slabs, 0, rows1, True, operands, (xr1,), (zf1,))
    y1 = lax.ppermute(block1, "orb", across)
    f_d, _ = ordered(f_d, block1)
    sums, weights = partials(count, atom_slab, psi, beta, xr2, f_d, potential, gram)
    rounds = [1 << k for k in range((slabs - 1).bit_length())]

    def added(values, step):
        pairs = [(i, i ^ step) for i in range(slabs)]
        return values + lax.ppermute(values, "space", pairs)

    for step in rounds[:-1]:
        sums = added(sums, step)
    zf2, sums = ordered(zf2, sums)
    sums = added(sums, rounds[-1])
    give2, keep2 = filtered(slabs, rows1, rows2, False, operands, (xr_c, xr2), (zf_c, zf2))
    pattern, q_tiles, _ = ordered(pattern, q_tiles, give2)
    me = lax.axis_index("orb")
    which = jnp.bitwise_xor(me, jnp.arange(groups, dtype=jnp.int32))
    rows_hot = (pattern[:, 0][:, None] == which[None, :]).astype(BF16)
    rows_hot = rows_hot * (pattern[:, 1] == me).astype(BF16)[:, None]
    q = jnp.einsum("ki,kab->iab", rows_hot, q_tiles, preferred_element_type=F32).astype(BF16)
    cg = lax.ppermute(give2, "orb", beside)
    ck = lax.ppermute(keep2, "orb", beside)
    yg = lax.ppermute(give2, "orb", across)
    y1, again, _, sums = ordered(y1, block1, give2, sums)
    coefs = coefficients(sums, strong)
    coefs = jnp.concatenate([coefs, lax.ppermute(coefs, "orb", beside)], axis=0)
    c1 = lax.ppermute(again, "orb", beside)
    yc1 = lax.ppermute(y1, "orb", beside)
    give1, keep1 = rotated((block1, c1, y1, yc1), q, 2)
    got1 = lax.ppermute(give1, "space", swap)
    keep_y, yg, _ = ordered(keep2, yg, give1)
    yk = lax.ppermute(keep_y, "orb", across)
    ycg = lax.ppermute(yg, "orb", beside)
    ycg, got1 = ordered(ycg, got1)
    (give2,) = rotated((give2, cg, yg, ycg), q, 1)
    got2 = lax.ppermute(give2, "space", swap)
    coefs, _ = ordered(coefs, give2)
    coefs_y = lax.ppermute(coefs, "orb", across)
    coefs = [half_of[k * 2 * count : (k + 1) * 2 * count] for half_of in (coefs, coefs_y) for k in (0, 1)]
    term = nonlocal_term(psi.shape, coefs, q, weights)
    yk, _ = ordered(yk, give2)
    yck = lax.ppermute(yk, "orb", beside)
    return assembled(term, keep1, got1, got2, (keep2, ck, yk, yck), q)


def solution(mesh):
    placed = (
        P("space", None, None, "orb"),
        P("space", None, None),
        P(None, "space", None, None),
        P(),
        P(),
        P(),
        P(),
    )
    return jax.shard_map(
        shards, mesh=mesh, in_specs=placed, out_specs=P("space", None, None, "orb"), check_vma=False
    )
```

```python
import functools

import jax
import jax.numpy as jnp
from jax import lax
from jax.experimental import pallas as pl
from jax.experimental.pallas import tpu as pltpu
from jax.sharding import PartitionSpec as P

F32 = jnp.float32
BF16 = jnp.bfloat16
VMEM_LIMIT = 24 * 1024 * 1024
SHRINK = 16
FILTER = 100


def params():
    return pltpu.CompilerParams(vmem_limit_bytes=VMEM_LIMIT)


def cost(flops, moved):
    return pl.CostEstimate(flops=flops // SHRINK, bytes_accessed=moved // SHRINK, transcendentals=0)


def inside(p, window):
    return jnp.logical_and(p >= 0, p < window).astype(F32)


def neighbour_sum(width, pairs):
    n = (2 if pairs else 1) * width
    i = lax.broadcasted_iota(jnp.int32, (n, n), 0)
    j = lax.broadcasted_iota(jnp.int32, (n, n), 1)
    linked = jnp.abs(i - j) == 1
    if pairs:
        linked = jnp.logical_and(linked, (i < width) == (j < width))
        linked = jnp.logical_or(linked, jnp.abs(i - j) == width)
    return jnp.where(linked, -0.125, 0.0)


def potential_block(potential):
    lines, width = potential.shape
    gap = jnp.zeros((lines, 64 - width), F32)
    u = (potential - 1.0) * 0.25
    hi = u.astype(BF16).astype(F32)
    return jnp.concatenate([hi, gap, u - hi, gap], axis=1)


def prepare_kernel(early, psi, potential_far, to_x, to_z, potential, sems):
    x = lax.rem(lax.axis_index("space"), 2)
    half = psi.shape[1] // 2
    window = half + 2
    mine, theirs = (half - 2) * x, (half - 2) * (1 - x)
    fetch = pltpu.make_async_copy(potential_far, potential, sems.at[0])
    fetch.start()
    copies = [
        pltpu.make_async_copy(
            psi.at[:, pl.ds(theirs, early)], to_x.at[:, pl.ds(0, early)], sems.at[1]
        ),
        pltpu.make_async_copy(
            psi.at[:, pl.ds(mine, window)], to_z.at[:, pl.ds(0, window)], sems.at[2]
        ),
    ]
    for copy in copies:
        copy.start()
    fetch.wait()
    for plane in range(potential.shape[0]):
        block = potential_block(potential[plane]).astype(BF16)
        to_x[plane, early] = block
        to_z[plane, window] = block
    for copy in copies:
        copy.wait()


def prepared(psi, potential, early):
    planes, width_x, width_y, orbs = psi.shape
    window = width_x // 2 + 2

    def out(rows):
        return jax.ShapeDtypeStruct((planes, rows, width_y, orbs), BF16)

    return pl.pallas_call(
        functools.partial(prepare_kernel, early),
        out_shape=(out(early + 1), out(window + 1)),
        in_specs=[pl.BlockSpec(memory_space=pltpu.MemorySpace.HBM)] * 2,
        out_specs=(pl.BlockSpec(memory_space=pltpu.VMEM),) * 2,
        scratch_shapes=[pltpu.VMEM(potential.shape, F32), pltpu.SemaphoreType.DMA((3,))],
        compiler_params=params(),
        cost_estimate=cost(4096, 4096),
        name="prepared",
    )(*(pltpu.with_memory_space_constraint(a, pltpu.MemorySpace.HBM) for a in (psi, potential)))


def pack_kernel(early, psi, beta, to_x2, far, sem):
    x = lax.rem(lax.axis_index("space"), 2)
    half = psi.shape[1] // 2
    later = half + 2 - early
    _, _, lines, width = beta.shape
    gap = jnp.zeros((lines, 64 - width), F32)
    copy = pltpu.make_async_copy(
        psi.at[:, pl.ds((half - 2) * (1 - x) + early, later)], to_x2.at[:, pl.ds(0, later)], sem
    )
    copy.start()
    each = beta.shape[0] // to_x2.shape[0]

    def pack(i, carry):
        for plane in range(to_x2.shape[0]):
            first, second = (beta[plane * each + i, k].astype(F32) for k in range(2))
            to_x2[plane, later + i] = jnp.concatenate(
                [first, gap, second, gap], axis=1
            ).astype(BF16)
        return carry

    far[...] = beta[:, x]
    lax.fori_loop(0, each, pack, 0)
    copy.wait()


def packed(psi, beta, early):
    planes, width_x, width_y, orbs = psi.shape
    rows = width_x // 2 + 2 - early + beta.shape[0] // planes
    return pl.pallas_call(
        functools.partial(pack_kernel, early),
        out_shape=(
            jax.ShapeDtypeStruct((planes, rows, width_y, orbs), BF16),
            jax.ShapeDtypeStruct((beta.shape[0], *beta.shape[2:]), BF16),
        ),
        in_specs=[
            pl.BlockSpec(memory_space=pltpu.MemorySpace.HBM),
            pl.BlockSpec(memory_space=pltpu.VMEM),
        ],
        out_specs=(pl.BlockSpec(memory_space=pltpu.VMEM),) * 2,
        scratch_shapes=[pltpu.SemaphoreType.DMA],
        compiler_params=params(),
        cost_estimate=cost(4096, 4096),
        name="packed",
    )(pltpu.with_memory_space_constraint(psi, pltpu.MemorySpace.HBM), beta)


def partial_kernel(count, atoms, own, beta, b_x, b_d, potential, gram, out, weights_out, table, acc):
    place = lax.axis_index("space")
    x = lax.rem(place, 2)
    rows, width = potential.shape[1:]
    side = place ^ 1
    beyond = place - 1 + 2 * x
    tri = neighbour_sum(width, False).astype(BF16)
    acc[...] = jnp.zeros_like(acc)
    step = 8

    for k in range(2):
        plane = x if k == 0 else 1 - x
        there = beyond if k == 0 else side
        each = count // b_x.shape[0]
        begin = b_x.shape[1] - each
        u = (potential[plane] - 1.0) * 0.25

        def fill(i, carry):
            for j in range(step):
                p = i * step + j
                here = (jnp.abs(place - atoms[p]) <= 1).astype(F32)
                next_to = (jnp.abs(there - atoms[p]) <= 1).astype(F32)
                b32 = beta[p, plane].astype(F32) * here
                b = b32.astype(BF16)
                if k == 0:
                    other = b_d[p].astype(F32)
                else:
                    both = b_x[p // each, begin + lax.rem(p, each)].astype(F32)
                    other = jnp.where(x == 0, both[:, :width], both[:, 64 : 64 + width])
                sides = beta[p, 1 - plane].astype(F32) * here + other * next_to
                whole = jnp.dot(b, tri, preferred_element_type=F32)
                whole = whole + jnp.dot(tri, b, preferred_element_type=F32)
                whole = whole + u * b32 - 0.125 * sides
                hi = whole.astype(BF16).astype(F32)
                for kind, value in enumerate((b32, hi, whole - hi)):
                    table[pl.ds((kind * count + p) * rows, rows)] = value
            return carry

        lax.fori_loop(0, count // step, fill, 0)

        def use(i, carry):
            totals = []
            for j in range(step):
                r = i * step + j
                weights = table[pl.ds(r, 3 * count, stride=rows)].astype(BF16)
                weights_out[plane, r] = weights
                totals.append(jnp.dot(weights, own[plane, r], preferred_element_type=F32))
            acc[...] += sum(totals[1:], totals[0])
            return carry

        lax.fori_loop(0, rows // step, use, 0)
    out[...] = jnp.zeros_like(out)
    out[0:count] = acc[0:count]
    out[count : 2 * count] = acc[count : 2 * count] + acc[2 * count : 3 * count]
    out[2 * count : 3 * count, 0:count] = gram[...]


def partials(count, atoms, own, beta, b_x, b_d, potential, gram):
    planes, rows, width, orbs = own.shape
    return pl.pallas_call(
        functools.partial(partial_kernel, count),
        out_shape=(
            jax.ShapeDtypeStruct((3 * count, orbs), F32),
            jax.ShapeDtypeStruct((planes, rows, 3 * count, width), BF16),
        ),
        in_specs=[pl.BlockSpec(memory_space=pltpu.SMEM)]
        + [pl.BlockSpec(memory_space=pltpu.VMEM)] * 6,
        out_specs=(pl.BlockSpec(memory_space=pltpu.VMEM),) * 2,
        scratch_shapes=[
            pltpu.VMEM((3 * count * rows, width), F32),
            pltpu.VMEM((3 * count, orbs), F32),
        ],
        compiler_params=params(),
        cost_estimate=cost(4096, 4096),
        name="partials",
    )(atoms, own, beta, b_x, b_d, potential, gram)


def coefficient_kernel(sums, strength, out):
    count, orbs = strength.shape
    coef1 = (strength[...] * sums[0:count]).astype(BF16)
    padded = coef1.astype(F32) * 0.25
    if orbs > count:
        padded = jnp.concatenate([padded, jnp.zeros((orbs - count, orbs), F32)], axis=0)
    proj2 = sums[count : 2 * count] + jnp.dot(
        sums[2 * count : 3 * count],
        padded,
        preferred_element_type=F32,
        precision=lax.Precision.HIGHEST,
    )
    out[0:count] = coef1
    out[count : 2 * count] = (strength[...] * proj2).astype(BF16)


def coefficients(sums, strength):
    count, orbs = strength.shape
    return pl.pallas_call(
        coefficient_kernel,
        out_shape=jax.ShapeDtypeStruct((2 * count, orbs), BF16),
        in_specs=[pl.BlockSpec(memory_space=pltpu.VMEM)] * 2,
        out_specs=pl.BlockSpec(memory_space=pltpu.VMEM),
        compiler_params=params(),
        cost_estimate=cost(4096, 4096),
        name="coefficients",
    )(sums, strength)


def nonlocal_kernel(unroll, a, b, c, d, q, weights, out):
    count, orbs = a.shape[0] // 2, a.shape[1]
    turned = sum(
        jnp.dot(ref[...], q[k], preferred_element_type=F32) for k, ref in enumerate((a, b, c, d))
    )
    turned = turned * 0.25
    one, two = turned[0:count], turned[count : 2 * count]
    right = jnp.concatenate([two, one, one], axis=0)
    hi = right.astype(BF16)
    lo = right - hi.astype(F32)
    right = jnp.concatenate([hi.astype(F32), lo], axis=1).astype(BF16)

    def step(i, carry):
        for k in range(unroll):
            r = i * unroll + k
            for plane in range(weights.shape[0]):
                both = lax.dot_general(
                    weights[plane, r], right, (((0,), (0,)), ((), ())), preferred_element_type=F32
                )
                out[plane, r] = both[:, :orbs] + both[:, orbs:]
        return carry

    lax.fori_loop(0, weights.shape[1] // unroll, step, 0)


def nonlocal_term(shape, coefs, q, weights):
    unroll = max(g for g in (1, 2, 4, 8) if weights.shape[1] % g == 0)
    return pl.pallas_call(
        functools.partial(nonlocal_kernel, unroll),
        out_shape=jax.ShapeDtypeStruct(shape, F32),
        in_specs=[pl.BlockSpec(memory_space=pltpu.VMEM)] * 6,
        out_specs=pl.BlockSpec(memory_space=pltpu.VMEM),
        compiler_params=params(),
        cost_estimate=cost(4096, 4096),
        name="nonlocal",
    )(*coefs, q, weights)


def filter_kernel(slabs, start, parts, joint, *refs):
    own, p_own, zo = refs[:3]
    xrs, zfs = refs[3 : 3 + parts], refs[3 + parts : 3 + 2 * parts]
    extra = 5 if parts > 1 else 3
    outs, scratch = refs[3 + 2 * parts : -extra], refs[-extra:]
    first, lines, diagonals = scratch[:3]
    place = lax.axis_index("space")
    x = lax.rem(place, 2)
    width = own.shape[2]
    cells = 2 * width
    half = own.shape[1] // 2
    orbs = own.shape[3]
    rows = outs[0].shape[1]
    base = (half - 2) * x
    lower = (place >= 2).astype(F32)
    upper = (place < slabs - 2).astype(F32)
    is_odd = x.astype(F32)
    has_zf = lower * (1.0 - is_odd) + upper * is_odd
    has_zo = upper * (1.0 - is_odd) + lower * is_odd
    if parts > 1:
        xr, zf = scratch[3], scratch[4]
        early = start + 4
        for target, pieces in ((xr, xrs), (zf, zfs)):
            target[:, start - 4 : early] = pieces[0][:, 0:8]
            target[:, early:] = pieces[1][:, 0 : target.shape[1] - early]
        window = xr.shape[1] // 2
    else:
        xr, zf = xrs[0], zfs[0]
        early = xr.shape[1] - 1
        window = early // 2
        for target, piece in ((outs[1], xr), (outs[2], zf)):
            target[...] = piece[:, early - 8 :]
    for c in range(1, 7):
        plane = (c % 2) ^ x
        if c in (2, 3):
            lines[c - 1] = potential_block(p_own[plane])
        else:
            ref = zfs[0] if c < 2 else (xrs[0] if c < 6 else zo)
            lines[c - 1] = ref[plane, ref.shape[1] - 1].astype(F32)
        for kind in range(2):
            even, odd = (lines[c - 1, pl.ds(k, half, stride=2)] for k in range(2))
            lanes = slice(64 * kind, 64 * kind + width)
            diagonals[c - 1, kind] = jnp.concatenate([even[:, lanes], odd[:, lanes]], axis=1)

    here = neighbour_sum(width, True)
    i = lax.broadcasted_iota(jnp.int32, (cells, cells), 0)
    diagonal = i == lax.broadcasted_iota(jnp.int32, (cells, cells), 1)

    def local(c, p):
        at = base // 2 + p
        hi = diagonals[c - 1, 0, pl.ds(at, 1)]
        lo = diagonals[c - 1, 1, pl.ds(at, 1)]
        return (
            jnp.where(diagonal, hi, here).astype(BF16),
            jnp.where(diagonal, lo, 0.0).astype(BF16),
        )

    def rows_of(c, w, n):
        plane = (c % 2) ^ x
        if c in (2, 3):
            return own[plane, pl.ds(base + w, n)]
        ref = zf if c < 2 else (xr if c < 6 else zo)
        return ref[plane, pl.ds(w, n)]

    def applied(pair, outer, zs, matrices):
        near = jnp.dot(matrices[0], pair, preferred_element_type=F32)
        near = near + jnp.dot(matrices[1], pair, preferred_element_type=F32)
        return near - 0.125 * (outer + zs)

    def step1(j, carry):
        p = start // 2 + x + j - 1
        q = jnp.clip(p, 0, window - 1)
        has_below = inside(p - 1, window)
        has_above = inside(p + 1, window)
        valid = inside(p, window)
        below = jnp.maximum(2 * q - 1, 0)
        above = jnp.minimum(2 * q + 2, 2 * window - 1)
        pair = [rows_of(c, 2 * q, 2).reshape(cells, orbs) for c in range(8)]
        vs = [v.astype(F32) for v in pair]
        for c in range(1, 7):
            outer = jnp.concatenate(
                [
                    rows_of(c, below, 1)[0].astype(F32) * has_below,
                    rows_of(c, above, 1)[0].astype(F32) * has_above,
                ],
                axis=0,
            )
            f = applied(pair[c], outer, vs[c - 1] + vs[c + 1], local(c, q))
            keep = valid
            if c == 1:
                keep = valid * has_zf
            if c == 6:
                keep = valid * has_zo
            first[c - 1, pl.ds(2 * j, 2)] = (f * keep).astype(BF16).reshape(2, width, orbs)
        return carry

    lax.fori_loop(0, rows // 2 + 2, step1, 0)

    def step2(j, carry):
        p = start // 2 + x + j
        pair = [first[c - 1, pl.ds(2 * j + 2, 2)].reshape(cells, orbs) for c in range(1, 7)]
        vs = [v.astype(F32) for v in pair]
        for c in range(2, 6):
            outer = jnp.concatenate(
                [first[c - 1, 2 * j + 1].astype(F32), first[c - 1, 2 * j + 4].astype(F32)], axis=0
            )
            f = applied(pair[c - 1], outer, vs[c - 2] + vs[c], local(c, p))
            f = f.astype(BF16).reshape(2, width, orbs)
            plane = (c % 2) ^ x
            if joint:
                outs[0][plane + (2 if c in (2, 3) else 0), pl.ds(2 * j, 2)] = f
            else:
                outs[1 if c in (2, 3) else 0][plane, pl.ds(2 * j, 2)] = f
        return carry

    lax.fori_loop(0, rows // 2, step2, 0)


def filtered(slabs, start, rows, joint, operands, xrs, zfs):
    own = operands[0]
    planes, _, width, orbs = own.shape
    parts = len(xrs)
    shape = (2 * planes if joint else planes, rows, width, orbs)
    out = (jax.ShapeDtypeStruct(shape, BF16),) * (1 if joint else 2)
    if parts == 1:
        out += (jax.ShapeDtypeStruct((planes, 9, width, orbs), BF16),) * 2
    cells = 10 * rows * width
    scratch = [
        pltpu.VMEM((6, rows + 4, width, orbs), BF16),
        pltpu.VMEM((6, width, orbs), F32),
        pltpu.VMEM((6, 2, own.shape[1] // 2, 2 * width), F32),
    ]
    if parts > 1:
        window = own.shape[1] // 2 + 2
        scratch += [pltpu.VMEM((planes, window, width, orbs), BF16)] * 2
    return pl.pallas_call(
        functools.partial(filter_kernel, slabs, start, parts, joint),
        out_shape=out,
        in_specs=[pl.BlockSpec(memory_space=pltpu.VMEM)] * (len(operands) + 2 * parts),
        out_specs=(pl.BlockSpec(memory_space=pltpu.VMEM),) * len(out),
        scratch_shapes=scratch,
        compiler_params=params(),
        cost_estimate=cost(2 * cells * 32 * orbs, FILTER * cells * orbs * 4),
        name="filtered",
    )(*operands, *xrs, *zfs)


def rotate_kernel(group, *refs):
    a, b, c, d, q = refs[:5]
    outs = refs[5:]
    _, rows, width, orbs = a.shape
    planes = outs[0].shape[0]
    low = jnp.concatenate([q[0], q[1]], axis=0)
    high = jnp.concatenate([q[2], q[3]], axis=0)

    def one(j, carry):
        for plane in range(a.shape[0]):
            def take(ref):
                return ref[plane, pl.ds(group * j, group)].reshape(group * width, orbs)

            total = jnp.dot(
                jnp.concatenate([take(a), take(b)], axis=1), low, preferred_element_type=F32
            )
            total = total + jnp.dot(
                jnp.concatenate([take(c), take(d)], axis=1), high, preferred_element_type=F32
            )
            outs[plane // planes][plane % planes, pl.ds(group * j, group)] = total.astype(
                BF16
            ).reshape(group, width, orbs)
        return carry

    lax.fori_loop(0, rows // group, one, 0)


def rotated(blocks, q, pieces):
    a = blocks[0]
    size = a.size
    group = max(g for g in range(1, 9) if a.shape[1] % g == 0)
    out = jax.ShapeDtypeStruct((a.shape[0] // pieces, *a.shape[1:]), BF16)
    return pl.pallas_call(
        functools.partial(rotate_kernel, group),
        out_shape=(out,) * pieces,
        in_specs=[pl.BlockSpec(memory_space=pltpu.VMEM)] * 5,
        out_specs=(pl.BlockSpec(memory_space=pltpu.VMEM),) * pieces,
        compiler_params=params(),
        cost_estimate=cost(8 * size * a.shape[3], 10 * size),
        name="rotated",
    )(*blocks, q)


def assemble_kernel(group, term, keep1, got1, got2, a, b, c, d, q, out):
    half = term.shape[1] // 2
    width, orbs = term.shape[2:]
    x = lax.rem(lax.axis_index("space"), 2)
    rows1, rows2 = keep1.shape[1], got2.shape[1]
    for ref, at in (
        (keep1, half * x),
        (got1, half * (1 - x)),
        (got2, half * (1 - x) + rows1),
    ):
        where = pl.ds(at, ref.shape[1])
        out[:, where] = (ref[...].astype(F32) + term[:, where]).astype(BF16)
    low = jnp.concatenate([q[0], q[1]], axis=0)
    high = jnp.concatenate([q[2], q[3]], axis=0)

    def one(j, carry):
        where = pl.ds(half * x + rows1 + group * j, group)
        for plane in range(a.shape[0]):
            def take(ref):
                return ref[plane, pl.ds(group * j, group)].reshape(group * width, orbs)

            total = jnp.dot(
                jnp.concatenate([take(a), take(b)], axis=1), low, preferred_element_type=F32
            )
            total = total + jnp.dot(
                jnp.concatenate([take(c), take(d)], axis=1), high, preferred_element_type=F32
            )
            total = total.reshape(group, width, orbs) + term[plane, where]
            out[plane, where] = total.astype(BF16)
        return carry

    lax.fori_loop(0, rows2 // group, one, 0)


def assembled(term, keep1, got1, got2, blocks, q):
    group = max(g for g in range(1, 9) if got2.shape[1] % g == 0)
    return pl.pallas_call(
        functools.partial(assemble_kernel, group),
        out_shape=jax.ShapeDtypeStruct(term.shape, BF16),
        in_specs=[pl.BlockSpec(memory_space=pltpu.VMEM)] * 9,
        out_specs=pl.BlockSpec(memory_space=pltpu.VMEM),
        compiler_params=params(),
        cost_estimate=cost(4096, 4096),
        name="assembled",
    )(term, keep1, got1, got2, *blocks, q)


def ordered(*arrays):
    return lax.optimization_barrier(arrays)


def shards(psi, potential, beta, strength, atom_slab, pattern, q_tiles):
    planes, width_x, width_y, orbs = psi.shape
    count = beta.shape[0]
    slabs = lax.axis_size("space")
    place = lax.axis_index("space")
    x = lax.rem(place, 2)
    half = width_x // 2
    window = half + 2
    rows1 = half * 5 // 24 * 2
    rows2 = half - rows1
    early = rows1 + 4

    def within(pairs):
        return [(i, j) for i, j in pairs if 0 <= j < slabs]

    swap = [(i, i ^ 1) for i in range(slabs)]
    own_way = within([(i, i + 2 if i % 2 else i - 2) for i in range(slabs)])
    other_way = within([(i, i - 2 if i % 2 else i + 2) for i in range(slabs)])
    groups = lax.axis_size("orb")
    across = [(i, i ^ 2) for i in range(groups)]
    beside = [(i, i ^ 1) for i in range(groups)]
    mine = (half - 2) * x
    theirs = (half - 2) * (1 - x)

    to_x, to_z = prepared(psi, potential, early)
    to_x2, far = packed(psi, beta, early)
    raster = within([(i, i + 1 if i % 2 else i - 1) for i in range(slabs)])
    f_d = lax.ppermute(far, "space", raster)
    xr1 = lax.ppermute(to_x, "space", swap)
    zo = lax.ppermute(to_z, "space", own_way)
    active = jnp.abs(place - atom_slab) <= 1
    beta_m = jnp.where(active[:, None, None, None], beta, jnp.zeros_like(beta))
    gram = jnp.einsum("pzxy,qzxy->pq", beta_m, beta_m, preferred_element_type=F32)
    zf1 = lax.ppermute(xr1, "space", other_way)
    second, _ = ordered(to_x2, xr1)
    xr2 = lax.ppermute(second, "space", swap)
    zf2 = lax.ppermute(xr2, "space", other_way)
    strong = jnp.broadcast_to(strength[:, None], (count, orbs))

    zf1, _ = ordered(zf1, xr2)
    operands = (psi, potential, zo)
    block1, xr_c, zf_c = filtered(slabs, 0, rows1, True, operands, (xr1,), (zf1,))
    y1 = lax.ppermute(block1, "orb", across)
    f_d, _ = ordered(f_d, block1)
    sums, weights = partials(count, atom_slab, psi, beta, xr2, f_d, potential, gram)
    rounds = [1 << k for k in range((slabs - 1).bit_length())]

    def added(values, step):
        pairs = [(i, i ^ step) for i in range(slabs)]
        return values + lax.ppermute(values, "space", pairs)

    zf2, sums = ordered(zf2, sums)
    give2, keep2 = filtered(slabs, rows1, rows2, False, operands, (xr_c, xr2), (zf_c, zf2))
    pattern, q_tiles, _ = ordered(pattern, q_tiles, give2)
    me = lax.axis_index("orb")
    which = jnp.bitwise_xor(me, jnp.arange(groups, dtype=jnp.int32))
    rows_hot = (pattern[:, 0][:, None] == which[None, :]).astype(BF16)
    rows_hot = rows_hot * (pattern[:, 1] == me).astype(BF16)[:, None]
    q = jnp.einsum("ki,kab->iab", rows_hot, q_tiles, preferred_element_type=F32).astype(BF16)
    cg = lax.ppermute(give2, "orb", beside)
    ck = lax.ppermute(keep2, "orb", beside)
    yg = lax.ppermute(give2, "orb", across)
    sums = added(sums, rounds[0])
    y1, again, _, sums = ordered(y1, block1, give2, sums)
    c1 = lax.ppermute(again, "orb", beside)
    yc1 = lax.ppermute(y1, "orb", beside)
    sums = added(sums, rounds[1])
    yc1, sums = ordered(yc1, sums)
    give1, keep1 = rotated((block1, c1, y1, yc1), q, 2)
    got1 = lax.ppermute(give1, "space", swap)
    keep_y, yg, _, sums = ordered(keep2, yg, give1, sums)
    yk = lax.ppermute(keep_y, "orb", across)
    ycg = lax.ppermute(yg, "orb", beside)
    for step in rounds[2:]:
        sums = added(sums, step)
    ycg, sums, got1 = ordered(ycg, sums, got1)
    coefs = coefficients(sums, strong)
    coefs = jnp.concatenate([coefs, lax.ppermute(coefs, "orb", beside)], axis=0)
    (give2,) = rotated((give2, cg, yg, ycg), q, 1)
    got2 = lax.ppermute(give2, "space", swap)
    coefs, _ = ordered(coefs, give2)
    coefs_y = lax.ppermute(coefs, "orb", across)
    coefs = [half_of[k * 2 * count : (k + 1) * 2 * count] for half_of in (coefs, coefs_y) for k in (0, 1)]
    term = nonlocal_term(psi.shape, coefs, q, weights)
    yk, _ = ordered(yk, give2)
    yck = lax.ppermute(yk, "orb", beside)
    return assembled(term, keep1, got1, got2, (keep2, ck, yk, yck), q)


def solution(mesh):
    placed = (
        P("space", None, None, "orb"),
        P("space", None, None),
        P(None, "space", None, None),
        P(),
        P(),
        P(),
        P(),
    )
    return jax.shard_map(
        shards, mesh=mesh, in_specs=placed, out_specs=P("space", None, None, "orb"), check_vma=False
    )
```

```python
import functools

import jax
import jax.numpy as jnp
from jax import lax
from jax.experimental import pallas as pl
from jax.experimental.pallas import tpu as pltpu
from jax.sharding import PartitionSpec as P

F32 = jnp.float32
BF16 = jnp.bfloat16
VMEM_LIMIT = 24 * 1024 * 1024
SHRINK = 16
FILTER = 100


def params():
    return pltpu.CompilerParams(vmem_limit_bytes=VMEM_LIMIT)


def cost(flops, moved):
    return pl.CostEstimate(flops=flops // SHRINK, bytes_accessed=moved // SHRINK, transcendentals=0)


def inside(p, window):
    return jnp.logical_and(p >= 0, p < window).astype(F32)


def neighbour_sum(width, pairs):
    n = (2 if pairs else 1) * width
    i = lax.broadcasted_iota(jnp.int32, (n, n), 0)
    j = lax.broadcasted_iota(jnp.int32, (n, n), 1)
    linked = jnp.abs(i - j) == 1
    if pairs:
        linked = jnp.logical_and(linked, (i < width) == (j < width))
        linked = jnp.logical_or(linked, jnp.abs(i - j) == width)
    return jnp.where(linked, -0.125, 0.0)


def potential_block(potential):
    lines, width = potential.shape
    gap = jnp.zeros((lines, 64 - width), F32)
    u = (potential - 1.0) * 0.25
    hi = u.astype(BF16).astype(F32)
    return jnp.concatenate([hi, gap, u - hi, gap], axis=1)


def prepare_kernel(early, psi, potential_far, to_x, to_z, potential, sems):
    x = lax.rem(lax.axis_index("space"), 2)
    half = psi.shape[1] // 2
    window = half + 2
    mine, theirs = (half - 2) * x, (half - 2) * (1 - x)
    fetch = pltpu.make_async_copy(potential_far, potential, sems.at[0])
    fetch.start()
    copies = [
        pltpu.make_async_copy(
            psi.at[:, pl.ds(theirs, early)], to_x.at[:, pl.ds(0, early)], sems.at[1]
        ),
        pltpu.make_async_copy(
            psi.at[:, pl.ds(mine, window)], to_z.at[:, pl.ds(0, window)], sems.at[2]
        ),
    ]
    for copy in copies:
        copy.start()
    fetch.wait()
    for plane in range(potential.shape[0]):
        block = potential_block(potential[plane]).astype(BF16)
        to_x[plane, early] = block
        to_z[plane, window] = block
    for copy in copies:
        copy.wait()


def prepared(psi, potential, early):
    planes, width_x, width_y, orbs = psi.shape
    window = width_x // 2 + 2

    def out(rows):
        return jax.ShapeDtypeStruct((planes, rows, width_y, orbs), BF16)

    return pl.pallas_call(
        functools.partial(prepare_kernel, early),
        out_shape=(out(early + 1), out(window + 1)),
        in_specs=[pl.BlockSpec(memory_space=pltpu.MemorySpace.HBM)] * 2,
        out_specs=(pl.BlockSpec(memory_space=pltpu.VMEM),) * 2,
        scratch_shapes=[pltpu.VMEM(potential.shape, F32), pltpu.SemaphoreType.DMA((3,))],
        compiler_params=params(),
        cost_estimate=cost(4096, 4096),
        name="prepared",
    )(*(pltpu.with_memory_space_constraint(a, pltpu.MemorySpace.HBM) for a in (psi, potential)))


def pack_kernel(early, psi, beta, to_x2, far, sem):
    x = lax.rem(lax.axis_index("space"), 2)
    half = psi.shape[1] // 2
    later = half + 2 - early
    _, _, lines, width = beta.shape
    gap = jnp.zeros((lines, 64 - width), F32)
    copy = pltpu.make_async_copy(
        psi.at[:, pl.ds((half - 2) * (1 - x) + early, later)], to_x2.at[:, pl.ds(0, later)], sem
    )
    copy.start()
    each = beta.shape[0] // to_x2.shape[0]

    def pack(i, carry):
        for plane in range(to_x2.shape[0]):
            first, second = (beta[plane * each + i, k].astype(F32) for k in range(2))
            to_x2[plane, later + i] = jnp.concatenate(
                [first, gap, second, gap], axis=1
            ).astype(BF16)
        return carry

    far[...] = beta[:, x]
    lax.fori_loop(0, each, pack, 0)
    copy.wait()


def packed(psi, beta, early):
    planes, width_x, width_y, orbs = psi.shape
    rows = width_x // 2 + 2 - early + beta.shape[0] // planes
    return pl.pallas_call(
        functools.partial(pack_kernel, early),
        out_shape=(
            jax.ShapeDtypeStruct((planes, rows, width_y, orbs), BF16),
            jax.ShapeDtypeStruct((beta.shape[0], *beta.shape[2:]), BF16),
        ),
        in_specs=[
            pl.BlockSpec(memory_space=pltpu.MemorySpace.HBM),
            pl.BlockSpec(memory_space=pltpu.VMEM),
        ],
        out_specs=(pl.BlockSpec(memory_space=pltpu.VMEM),) * 2,
        scratch_shapes=[pltpu.SemaphoreType.DMA],
        compiler_params=params(),
        cost_estimate=cost(4096, 4096),
        name="packed",
    )(pltpu.with_memory_space_constraint(psi, pltpu.MemorySpace.HBM), beta)


def partial_kernel(count, atoms, own, beta, b_x, b_d, potential, gram, out, weights_out, table, acc):
    place = lax.axis_index("space")
    x = lax.rem(place, 2)
    rows, width = potential.shape[1:]
    side = place ^ 1
    beyond = place - 1 + 2 * x
    tri = neighbour_sum(width, False).astype(BF16)
    acc[...] = jnp.zeros_like(acc)
    step = 8

    for k in range(2):
        plane = x if k == 0 else 1 - x
        there = beyond if k == 0 else side
        each = count // b_x.shape[0]
        begin = b_x.shape[1] - each
        u = (potential[plane] - 1.0) * 0.25

        def fill(i, carry):
            for j in range(step):
                p = i * step + j
                here = (jnp.abs(place - atoms[p]) <= 1).astype(F32)
                next_to = (jnp.abs(there - atoms[p]) <= 1).astype(F32)
                b32 = beta[p, plane].astype(F32) * here
                b = b32.astype(BF16)
                if k == 0:
                    other = b_d[p].astype(F32)
                else:
                    both = b_x[p // each, begin + lax.rem(p, each)].astype(F32)
                    other = jnp.where(x == 0, both[:, :width], both[:, 64 : 64 + width])
                sides = beta[p, 1 - plane].astype(F32) * here + other * next_to
                whole = jnp.dot(b, tri, preferred_element_type=F32)
                whole = whole + jnp.dot(tri, b, preferred_element_type=F32)
                whole = whole + u * b32 - 0.125 * sides
                hi = whole.astype(BF16).astype(F32)
                for kind, value in enumerate((b32, hi, whole - hi)):
                    table[pl.ds((kind * count + p) * rows, rows)] = value
            return carry

        lax.fori_loop(0, count // step, fill, 0)

        def use(i, carry):
            totals = []
            for j in range(step):
                r = i * step + j
                weights = table[pl.ds(r, 3 * count, stride=rows)].astype(BF16)
                weights_out[plane, r] = weights
                totals.append(jnp.dot(weights, own[plane, r], preferred_element_type=F32))
            acc[...] += sum(totals[1:], totals[0])
            return carry

        lax.fori_loop(0, rows // step, use, 0)
    out[...] = jnp.zeros_like(out)
    out[0:count] = acc[0:count]
    out[count : 2 * count] = acc[count : 2 * count] + acc[2 * count : 3 * count]
    out[2 * count : 3 * count, 0:count] = gram[...]


def partials(count, atoms, own, beta, b_x, b_d, potential, gram):
    planes, rows, width, orbs = own.shape
    return pl.pallas_call(
        functools.partial(partial_kernel, count),
        out_shape=(
            jax.ShapeDtypeStruct((3 * count, orbs), F32),
            jax.ShapeDtypeStruct((planes, rows, 3 * count, width), BF16),
        ),
        in_specs=[pl.BlockSpec(memory_space=pltpu.SMEM)]
        + [pl.BlockSpec(memory_space=pltpu.VMEM)] * 6,
        out_specs=(pl.BlockSpec(memory_space=pltpu.VMEM),) * 2,
        scratch_shapes=[
            pltpu.VMEM((3 * count * rows, width), F32),
            pltpu.VMEM((3 * count, orbs), F32),
        ],
        compiler_params=params(),
        cost_estimate=cost(4096, 4096),
        name="partials",
    )(atoms, own, beta, b_x, b_d, potential, gram)


def coefficient_kernel(sums, strength, out):
    count, orbs = strength.shape
    coef1 = (strength[...] * sums[0:count]).astype(BF16)
    padded = coef1.astype(F32) * 0.25
    if orbs > count:
        padded = jnp.concatenate([padded, jnp.zeros((orbs - count, orbs), F32)], axis=0)
    proj2 = sums[count : 2 * count] + jnp.dot(
        sums[2 * count : 3 * count],
        padded,
        preferred_element_type=F32,
        precision=lax.Precision.HIGHEST,
    )
    out[0:count] = coef1
    out[count : 2 * count] = (strength[...] * proj2).astype(BF16)


def coefficients(sums, strength):
    count, orbs = strength.shape
    return pl.pallas_call(
        coefficient_kernel,
        out_shape=jax.ShapeDtypeStruct((2 * count, orbs), BF16),
        in_specs=[pl.BlockSpec(memory_space=pltpu.VMEM)] * 2,
        out_specs=pl.BlockSpec(memory_space=pltpu.VMEM),
        compiler_params=params(),
        cost_estimate=cost(4096, 4096),
        name="coefficients",
    )(sums, strength)


def nonlocal_kernel(unroll, a, b, c, d, q, weights, out):
    count, orbs = a.shape[0] // 2, a.shape[1]
    turned = sum(
        jnp.dot(ref[...], q[k], preferred_element_type=F32) for k, ref in enumerate((a, b, c, d))
    )
    turned = turned * 0.25
    one, two = turned[0:count], turned[count : 2 * count]
    right = jnp.concatenate([two, one, one], axis=0)
    hi = right.astype(BF16)
    lo = right - hi.astype(F32)
    right = jnp.concatenate([hi.astype(F32), lo], axis=1).astype(BF16)

    def step(i, carry):
        for k in range(unroll):
            r = i * unroll + k
            for plane in range(weights.shape[0]):
                both = lax.dot_general(
                    weights[plane, r], right, (((0,), (0,)), ((), ())), preferred_element_type=F32
                )
                out[plane, r] = both[:, :orbs] + both[:, orbs:]
        return carry

    lax.fori_loop(0, weights.shape[1] // unroll, step, 0)


def nonlocal_term(shape, coefs, q, weights):
    unroll = max(g for g in (1, 2, 4, 8) if weights.shape[1] % g == 0)
    return pl.pallas_call(
        functools.partial(nonlocal_kernel, unroll),
        out_shape=jax.ShapeDtypeStruct(shape, F32),
        in_specs=[pl.BlockSpec(memory_space=pltpu.VMEM)] * 6,
        out_specs=pl.BlockSpec(memory_space=pltpu.VMEM),
        compiler_params=params(),
        cost_estimate=cost(4096, 4096),
        name="nonlocal",
    )(*coefs, q, weights)


def filter_kernel(slabs, start, parts, joint, *refs):
    own, p_own, zo = refs[:3]
    xrs, zfs = refs[3 : 3 + parts], refs[3 + parts : 3 + 2 * parts]
    extra = 7
    outs, scratch = refs[3 + 2 * parts : -extra], refs[-extra:]
    first, lines, diagonals = scratch[:3]
    place = lax.axis_index("space")
    x = lax.rem(place, 2)
    width = own.shape[2]
    cells = 2 * width
    half = own.shape[1] // 2
    orbs = own.shape[3]
    rows = outs[0].shape[1]
    base = (half - 2) * x
    lower = (place >= 2).astype(F32)
    upper = (place < slabs - 2).astype(F32)
    is_odd = x.astype(F32)
    has_zf = lower * (1.0 - is_odd) + upper * is_odd
    has_zo = upper * (1.0 - is_odd) + lower * is_odd
    xr, zf, pots, sems = scratch[3:]
    window = xr.shape[1] // 2
    early = xrs[0].shape[1] - 1
    copies = []
    for k, (target, pieces) in enumerate(((xr, xrs), (zf, zfs))):
        begin = 0 if parts == 1 else early - 8
        moved = [
            (pieces[0].at[:, pl.ds(early, 1)], pots.at[k]),
            (
                pieces[0].at[:, pl.ds(begin, early - begin)],
                target.at[:, pl.ds(begin, early - begin)],
            ),
        ]
        if parts > 1:
            later = target.shape[1] - early
            moved.append((pieces[1].at[:, pl.ds(0, later)], target.at[:, pl.ds(early, later)]))
        copies += [
            pltpu.make_async_copy(source, goal, sems.at[3 * k + i])
            for i, (source, goal) in enumerate(moved)
        ]
    for copy in copies:
        copy.start()

    def fill(c, block):
        lines[c - 1] = block
        for kind in range(2):
            even, odd = (lines[c - 1, pl.ds(k, half, stride=2)] for k in range(2))
            lanes = slice(64 * kind, 64 * kind + width)
            diagonals[c - 1, kind] = jnp.concatenate([even[:, lanes], odd[:, lanes]], axis=1)

    for c in (2, 3):
        fill(c, potential_block(p_own[(c % 2) ^ x]))
    fill(6, zo[x, zo.shape[1] - 1].astype(F32))
    for copy in copies:
        copy.wait()
    for c in (1, 4, 5):
        fill(c, pots[1 if c < 2 else 0, (c % 2) ^ x, 0].astype(F32))

    here = neighbour_sum(width, True)
    i = lax.broadcasted_iota(jnp.int32, (cells, cells), 0)
    diagonal = i == lax.broadcasted_iota(jnp.int32, (cells, cells), 1)

    def local(c, p):
        at = base // 2 + p
        hi = diagonals[c - 1, 0, pl.ds(at, 1)]
        lo = diagonals[c - 1, 1, pl.ds(at, 1)]
        return (
            jnp.where(diagonal, hi, here).astype(BF16),
            jnp.where(diagonal, lo, 0.0).astype(BF16),
        )

    def rows_of(c, w, n):
        plane = (c % 2) ^ x
        if c in (2, 3):
            return own[plane, pl.ds(base + w, n)]
        ref = zf if c < 2 else (xr if c < 6 else zo)
        return ref[plane, pl.ds(w, n)]

    def applied(pair, outer, zs, matrices):
        near = jnp.dot(matrices[0], pair, preferred_element_type=F32)
        near = near + jnp.dot(matrices[1], pair, preferred_element_type=F32)
        return near - 0.125 * (outer + zs)

    def step1(j, carry):
        p = start // 2 + x + j - 1
        q = jnp.clip(p, 0, window - 1)
        has_below = inside(p - 1, window)
        has_above = inside(p + 1, window)
        valid = inside(p, window)
        below = jnp.maximum(2 * q - 1, 0)
        above = jnp.minimum(2 * q + 2, 2 * window - 1)
        pair = [rows_of(c, 2 * q, 2).reshape(cells, orbs) for c in range(8)]
        vs = [v.astype(F32) for v in pair]
        for c in range(1, 7):
            outer = jnp.concatenate(
                [
                    rows_of(c, below, 1)[0].astype(F32) * has_below,
                    rows_of(c, above, 1)[0].astype(F32) * has_above,
                ],
                axis=0,
            )
            f = applied(pair[c], outer, vs[c - 1] + vs[c + 1], local(c, q))
            keep = valid
            if c == 1:
                keep = valid * has_zf
            if c == 6:
                keep = valid * has_zo
            first[c - 1, pl.ds(2 * j, 2)] = (f * keep).astype(BF16).reshape(2, width, orbs)
        return carry

    lax.fori_loop(0, rows // 2 + 2, step1, 0)

    def step2(j, carry):
        p = start // 2 + x + j
        pair = [first[c - 1, pl.ds(2 * j + 2, 2)].reshape(cells, orbs) for c in range(1, 7)]
        vs = [v.astype(F32) for v in pair]
        for c in range(2, 6):
            outer = jnp.concatenate(
                [first[c - 1, 2 * j + 1].astype(F32), first[c - 1, 2 * j + 4].astype(F32)], axis=0
            )
            f = applied(pair[c - 1], outer, vs[c - 2] + vs[c], local(c, p))
            f = f.astype(BF16).reshape(2, width, orbs)
            plane = (c % 2) ^ x
            if joint:
                outs[0][plane + (2 if c in (2, 3) else 0), pl.ds(2 * j, 2)] = f
            else:
                outs[1 if c in (2, 3) else 0][plane, pl.ds(2 * j, 2)] = f
        return carry

    lax.fori_loop(0, rows // 2, step2, 0)


def filtered(slabs, start, rows, joint, operands, xrs, zfs):
    own = operands[0]
    planes, _, width, orbs = own.shape
    parts = len(xrs)
    shape = (2 * planes if joint else planes, rows, width, orbs)
    out = (jax.ShapeDtypeStruct(shape, BF16),) * (1 if joint else 2)
    cells = 10 * rows * width
    scratch = [
        pltpu.VMEM((6, rows + 4, width, orbs), BF16),
        pltpu.VMEM((6, width, orbs), F32),
        pltpu.VMEM((6, 2, own.shape[1] // 2, 2 * width), F32),
    ]
    window = own.shape[1] // 2 + 2 if parts > 1 else xrs[0].shape[1] - 1
    scratch += [pltpu.VMEM((planes, window, width, orbs), BF16)] * 2
    scratch += [pltpu.VMEM((2, planes, 1, width, orbs), BF16), pltpu.SemaphoreType.DMA((6,))]
    local = pl.BlockSpec(memory_space=pltpu.VMEM)
    distant = pl.BlockSpec(memory_space=pltpu.MemorySpace.HBM)
    xrs, zfs = (
        [pltpu.with_memory_space_constraint(piece, pltpu.MemorySpace.HBM) for piece in pieces]
        for pieces in (xrs, zfs)
    )
    return pl.pallas_call(
        functools.partial(filter_kernel, slabs, start, parts, joint),
        out_shape=out,
        in_specs=[local] * len(operands) + [distant] * (2 * parts),
        out_specs=(local,) * len(out),
        scratch_shapes=scratch,
        compiler_params=params(),
        cost_estimate=cost(2 * cells * 32 * orbs, FILTER * cells * orbs * 4),
        name="filtered",
    )(*operands, *xrs, *zfs)


def rotate_kernel(group, *refs):
    a, b, c, d, q = refs[:5]
    outs = refs[5:]
    _, rows, width, orbs = a.shape
    planes = outs[0].shape[0]
    low = jnp.concatenate([q[0], q[1]], axis=0)
    high = jnp.concatenate([q[2], q[3]], axis=0)

    def one(j, carry):
        for plane in range(a.shape[0]):
            def take(ref):
                return ref[plane, pl.ds(group * j, group)].reshape(group * width, orbs)

            total = jnp.dot(
                jnp.concatenate([take(a), take(b)], axis=1), low, preferred_element_type=F32
            )
            total = total + jnp.dot(
                jnp.concatenate([take(c), take(d)], axis=1), high, preferred_element_type=F32
            )
            outs[plane // planes][plane % planes, pl.ds(group * j, group)] = total.astype(
                BF16
            ).reshape(group, width, orbs)
        return carry

    lax.fori_loop(0, rows // group, one, 0)


def rotated(blocks, q, pieces):
    a = blocks[0]
    size = a.size
    group = max(g for g in range(1, 9) if a.shape[1] % g == 0)
    out = jax.ShapeDtypeStruct((a.shape[0] // pieces, *a.shape[1:]), BF16)
    return pl.pallas_call(
        functools.partial(rotate_kernel, group),
        out_shape=(out,) * pieces,
        in_specs=[pl.BlockSpec(memory_space=pltpu.VMEM)] * 5,
        out_specs=(pl.BlockSpec(memory_space=pltpu.VMEM),) * pieces,
        compiler_params=params(),
        cost_estimate=cost(8 * size * a.shape[3], 10 * size),
        name="rotated",
    )(*blocks, q)


def assemble_kernel(group, term, keep1, got1, got2, a, b, c, d, q, out):
    half = term.shape[1] // 2
    width, orbs = term.shape[2:]
    x = lax.rem(lax.axis_index("space"), 2)
    rows1, rows2 = keep1.shape[1], got2.shape[1]
    for ref, at in (
        (keep1, half * x),
        (got1, half * (1 - x)),
        (got2, half * (1 - x) + rows1),
    ):
        where = pl.ds(at, ref.shape[1])
        out[:, where] = (ref[...].astype(F32) + term[:, where]).astype(BF16)
    low = jnp.concatenate([q[0], q[1]], axis=0)
    high = jnp.concatenate([q[2], q[3]], axis=0)

    def one(j, carry):
        where = pl.ds(half * x + rows1 + group * j, group)
        for plane in range(a.shape[0]):
            def take(ref):
                return ref[plane, pl.ds(group * j, group)].reshape(group * width, orbs)

            total = jnp.dot(
                jnp.concatenate([take(a), take(b)], axis=1), low, preferred_element_type=F32
            )
            total = total + jnp.dot(
                jnp.concatenate([take(c), take(d)], axis=1), high, preferred_element_type=F32
            )
            total = total.reshape(group, width, orbs) + term[plane, where]
            out[plane, where] = total.astype(BF16)
        return carry

    lax.fori_loop(0, rows2 // group, one, 0)


def assembled(term, keep1, got1, got2, blocks, q):
    group = max(g for g in range(1, 9) if got2.shape[1] % g == 0)
    return pl.pallas_call(
        functools.partial(assemble_kernel, group),
        out_shape=jax.ShapeDtypeStruct(term.shape, BF16),
        in_specs=[pl.BlockSpec(memory_space=pltpu.VMEM)] * 9,
        out_specs=pl.BlockSpec(memory_space=pltpu.VMEM),
        compiler_params=params(),
        cost_estimate=cost(4096, 4096),
        name="assembled",
    )(term, keep1, got1, got2, *blocks, q)


def ordered(*arrays):
    return lax.optimization_barrier(arrays)


def shards(psi, potential, beta, strength, atom_slab, pattern, q_tiles):
    planes, width_x, width_y, orbs = psi.shape
    count = beta.shape[0]
    slabs = lax.axis_size("space")
    place = lax.axis_index("space")
    x = lax.rem(place, 2)
    half = width_x // 2
    window = half + 2
    rows1 = half * 7 // 24 * 2
    rows2 = half - rows1
    early = rows1 + 4

    def within(pairs):
        return [(i, j) for i, j in pairs if 0 <= j < slabs]

    swap = [(i, i ^ 1) for i in range(slabs)]
    own_way = within([(i, i + 2 if i % 2 else i - 2) for i in range(slabs)])
    other_way = within([(i, i - 2 if i % 2 else i + 2) for i in range(slabs)])
    groups = lax.axis_size("orb")
    across = [(i, i ^ 2) for i in range(groups)]
    beside = [(i, i ^ 1) for i in range(groups)]
    mine = (half - 2) * x
    theirs = (half - 2) * (1 - x)

    to_x, to_z = prepared(psi, potential, early)
    to_x2, far = packed(psi, beta, early)
    raster = within([(i, i + 1 if i % 2 else i - 1) for i in range(slabs)])
    f_d = lax.ppermute(far, "space", raster)
    xr1 = lax.ppermute(to_x, "space", swap)
    zo = lax.ppermute(to_z, "space", own_way)
    active = jnp.abs(place - atom_slab) <= 1
    beta_m = jnp.where(active[:, None, None, None], beta, jnp.zeros_like(beta))
    gram = jnp.einsum("pzxy,qzxy->pq", beta_m, beta_m, preferred_element_type=F32)
    xr1, second = ordered(xr1, to_x2)
    zf1 = lax.ppermute(xr1, "space", other_way)
    xr2 = lax.ppermute(second, "space", swap)
    zf2 = lax.ppermute(xr2, "space", other_way)
    strong = jnp.broadcast_to(strength[:, None], (count, orbs))

    zf1, _ = ordered(zf1, xr2)
    operands = (psi, potential, zo)
    (block1,) = filtered(slabs, 0, rows1, True, operands, (xr1,), (zf1,))
    y1 = lax.ppermute(block1, "orb", across)
    f_d, _ = ordered(f_d, block1)
    sums, weights = partials(count, atom_slab, psi, beta, xr2, f_d, potential, gram)
    rounds = [1 << k for k in range((slabs - 1).bit_length())]

    def added(values, step):
        pairs = [(i, i ^ step) for i in range(slabs)]
        return values + lax.ppermute(values, "space", pairs)

    zf2, sums = ordered(zf2, sums)
    give2, keep2 = filtered(slabs, rows1, rows2, False, operands, (xr1, xr2), (zf1, zf2))
    pattern, q_tiles, _ = ordered(pattern, q_tiles, give2)
    me = lax.axis_index("orb")
    which = jnp.bitwise_xor(me, jnp.arange(groups, dtype=jnp.int32))
    rows_hot = (pattern[:, 0][:, None] == which[None, :]).astype(BF16)
    rows_hot = rows_hot * (pattern[:, 1] == me).astype(BF16)[:, None]
    q = jnp.einsum("ki,kab->iab", rows_hot, q_tiles, preferred_element_type=F32).astype(BF16)
    cg = lax.ppermute(give2, "orb", beside)
    ck = lax.ppermute(keep2, "orb", beside)
    yg = lax.ppermute(give2, "orb", across)
    sums = added(sums, rounds[0])
    y1, again, _, sums = ordered(y1, block1, give2, sums)
    c1 = lax.ppermute(again, "orb", beside)
    yc1 = lax.ppermute(y1, "orb", beside)
    sums = added(sums, rounds[1])
    yc1, sums = ordered(yc1, sums)
    give1, keep1 = rotated((block1, c1, y1, yc1), q, 2)
    got1 = lax.ppermute(give1, "space", swap)
    keep_y, yg, _, sums = ordered(keep2, yg, give1, sums)
    yk = lax.ppermute(keep_y, "orb", across)
    ycg = lax.ppermute(yg, "orb", beside)
    for step in rounds[2:]:
        sums = added(sums, step)
    ycg, sums, got1 = ordered(ycg, sums, got1)
    coefs = coefficients(sums, strong)
    coefs = jnp.concatenate([coefs, lax.ppermute(coefs, "orb", beside)], axis=0)
    (give2,) = rotated((give2, cg, yg, ycg), q, 1)
    got2 = lax.ppermute(give2, "space", swap)
    coefs, _ = ordered(coefs, give2)
    coefs_y = lax.ppermute(coefs, "orb", across)
    coefs = [half_of[k * 2 * count : (k + 1) * 2 * count] for half_of in (coefs, coefs_y) for k in (0, 1)]
    term = nonlocal_term(psi.shape, coefs, q, weights)
    yk, _ = ordered(yk, give2)
    yck = lax.ppermute(yk, "orb", beside)
    return assembled(term, keep1, got1, got2, (keep2, ck, yk, yck), q)


def solution(mesh):
    placed = (
        P("space", None, None, "orb"),
        P("space", None, None),
        P(None, "space", None, None),
        P(),
        P(),
        P(),
        P(),
    )
    return jax.shard_map(
        shards, mesh=mesh, in_specs=placed, out_specs=P("space", None, None, "orb"), check_vma=False
    )
```

```python
import functools

import jax
import jax.numpy as jnp
from jax import lax
from jax.experimental import pallas as pl
from jax.experimental.pallas import tpu as pltpu
from jax.sharding import PartitionSpec as P

F32 = jnp.float32
BF16 = jnp.bfloat16
VMEM_LIMIT = 24 * 1024 * 1024
SHRINK = 16
FILTER = 100


def params():
    return pltpu.CompilerParams(vmem_limit_bytes=VMEM_LIMIT)


def cost(flops, moved):
    return pl.CostEstimate(flops=flops // SHRINK, bytes_accessed=moved // SHRINK, transcendentals=0)


def inside(p, window):
    return jnp.logical_and(p >= 0, p < window).astype(F32)


def neighbour_sum(width, pairs):
    n = (2 if pairs else 1) * width
    i = lax.broadcasted_iota(jnp.int32, (n, n), 0)
    j = lax.broadcasted_iota(jnp.int32, (n, n), 1)
    linked = jnp.abs(i - j) == 1
    if pairs:
        linked = jnp.logical_and(linked, (i < width) == (j < width))
        linked = jnp.logical_or(linked, jnp.abs(i - j) == width)
    return jnp.where(linked, -0.125, 0.0)


def potential_block(potential):
    lines, width = potential.shape
    gap = jnp.zeros((lines, 64 - width), F32)
    u = (potential - 1.0) * 0.25
    hi = u.astype(BF16).astype(F32)
    return jnp.concatenate([hi, gap, u - hi, gap], axis=1)


def prepare_kernel(early, psi, potential_far, to_x, to_z, potential, sems):
    x = lax.rem(lax.axis_index("space"), 2)
    half = psi.shape[1] // 2
    window = half + 2
    mine, theirs = (half - 2) * x, (half - 2) * (1 - x)
    fetch = pltpu.make_async_copy(potential_far, potential, sems.at[0])
    fetch.start()
    copies = [
        pltpu.make_async_copy(
            psi.at[:, pl.ds(theirs, early)], to_x.at[:, pl.ds(0, early)], sems.at[1]
        ),
        pltpu.make_async_copy(
            psi.at[:, pl.ds(mine, window)], to_z.at[:, pl.ds(0, window)], sems.at[2]
        ),
    ]
    for copy in copies:
        copy.start()
    fetch.wait()
    for plane in range(potential.shape[0]):
        block = potential_block(potential[plane]).astype(BF16)
        to_x[plane, early] = block
        to_z[plane, window] = block
    for copy in copies:
        copy.wait()


def prepared(psi, potential, early):
    planes, width_x, width_y, orbs = psi.shape
    window = width_x // 2 + 2

    def out(rows):
        return jax.ShapeDtypeStruct((planes, rows, width_y, orbs), BF16)

    return pl.pallas_call(
        functools.partial(prepare_kernel, early),
        out_shape=(out(early + 1), out(window + 1)),
        in_specs=[pl.BlockSpec(memory_space=pltpu.MemorySpace.HBM)] * 2,
        out_specs=(pl.BlockSpec(memory_space=pltpu.VMEM),) * 2,
        scratch_shapes=[pltpu.VMEM(potential.shape, F32), pltpu.SemaphoreType.DMA((3,))],
        compiler_params=params(),
        cost_estimate=cost(4096, 4096),
        name="prepared",
    )(*(pltpu.with_memory_space_constraint(a, pltpu.MemorySpace.HBM) for a in (psi, potential)))


def pack_kernel(early, psi, beta, to_x2, far, near, sem):
    x = lax.rem(lax.axis_index("space"), 2)
    half = psi.shape[1] // 2
    later = half + 2 - early
    copy = pltpu.make_async_copy(
        psi.at[:, pl.ds((half - 2) * (1 - x) + early, later)], to_x2, sem
    )
    copy.start()
    far[...] = beta[:, x]
    near[...] = beta[:, 1 - x]
    copy.wait()


def packed(psi, beta, early):
    planes, width_x, width_y, orbs = psi.shape
    side = jax.ShapeDtypeStruct((beta.shape[0], *beta.shape[2:]), BF16)
    later = width_x // 2 + 2 - early
    return pl.pallas_call(
        functools.partial(pack_kernel, early),
        out_shape=(jax.ShapeDtypeStruct((planes, later, width_y, orbs), BF16), side, side),
        in_specs=[
            pl.BlockSpec(memory_space=pltpu.MemorySpace.HBM),
            pl.BlockSpec(memory_space=pltpu.VMEM),
        ],
        out_specs=(pl.BlockSpec(memory_space=pltpu.VMEM),) * 3,
        scratch_shapes=[pltpu.SemaphoreType.DMA],
        compiler_params=params(),
        cost_estimate=cost(4096, 4096),
        name="packed",
    )(pltpu.with_memory_space_constraint(psi, pltpu.MemorySpace.HBM), beta)


def partial_kernel(count, atoms, own, beta, b_x, b_d, potential, gram, out, weights_out, table, acc):
    place = lax.axis_index("space")
    x = lax.rem(place, 2)
    rows, width = potential.shape[1:]
    side = place ^ 1
    beyond = place - 1 + 2 * x
    tri = neighbour_sum(width, False).astype(BF16)
    acc[...] = jnp.zeros_like(acc)
    step = 8

    for k in range(2):
        plane = x if k == 0 else 1 - x
        outer, there = (b_d, beyond) if k == 0 else (b_x, side)
        u = (potential[plane] - 1.0) * 0.25

        def fill(i, carry):
            for j in range(step):
                p = i * step + j
                here = (jnp.abs(place - atoms[p]) <= 1).astype(F32)
                next_to = (jnp.abs(there - atoms[p]) <= 1).astype(F32)
                b32 = beta[p, plane].astype(F32) * here
                b = b32.astype(BF16)
                sides = beta[p, 1 - plane].astype(F32) * here + outer[p].astype(F32) * next_to
                whole = jnp.dot(b, tri, preferred_element_type=F32)
                whole = whole + jnp.dot(tri, b, preferred_element_type=F32)
                whole = whole + u * b32 - 0.125 * sides
                hi = whole.astype(BF16).astype(F32)
                for kind, value in enumerate((b32, hi, whole - hi)):
                    table[pl.ds((kind * count + p) * rows, rows)] = value
            return carry

        lax.fori_loop(0, count // step, fill, 0)

        def use(i, carry):
            totals = []
            for j in range(step):
                r = i * step + j
                weights = table[pl.ds(r, 3 * count, stride=rows)].astype(BF16)
                weights_out[plane, r] = weights
                totals.append(jnp.dot(weights, own[plane, r], preferred_element_type=F32))
            acc[...] += sum(totals[1:], totals[0])
            return carry

        lax.fori_loop(0, rows // step, use, 0)
    out[...] = jnp.zeros_like(out)
    out[0:count] = acc[0:count]
    out[count : 2 * count] = acc[count : 2 * count] + acc[2 * count : 3 * count]
    out[2 * count : 3 * count, 0:count] = gram[...]


def partials(count, atoms, own, beta, b_x, b_d, potential, gram):
    planes, rows, width, orbs = own.shape
    return pl.pallas_call(
        functools.partial(partial_kernel, count),
        out_shape=(
            jax.ShapeDtypeStruct((3 * count, orbs), F32),
            jax.ShapeDtypeStruct((planes, rows, 3 * count, width), BF16),
        ),
        in_specs=[pl.BlockSpec(memory_space=pltpu.SMEM)]
        + [pl.BlockSpec(memory_space=pltpu.VMEM)] * 6,
        out_specs=(pl.BlockSpec(memory_space=pltpu.VMEM),) * 2,
        scratch_shapes=[
            pltpu.VMEM((3 * count * rows, width), F32),
            pltpu.VMEM((3 * count, orbs), F32),
        ],
        compiler_params=params(),
        cost_estimate=cost(4096, 4096),
        name="partials",
    )(atoms, own, beta, b_x, b_d, potential, gram)


def coefficient_kernel(sums, strength, out):
    count, orbs = strength.shape
    coef1 = (strength[...] * sums[0:count]).astype(BF16)
    padded = coef1.astype(F32) * 0.25
    if orbs > count:
        padded = jnp.concatenate([padded, jnp.zeros((orbs - count, orbs), F32)], axis=0)
    proj2 = sums[count : 2 * count] + jnp.dot(
        sums[2 * count : 3 * count],
        padded,
        preferred_element_type=F32,
        precision=lax.Precision.HIGHEST,
    )
    out[0:count] = coef1
    out[count : 2 * count] = (strength[...] * proj2).astype(BF16)


def coefficients(sums, strength):
    count, orbs = strength.shape
    return pl.pallas_call(
        coefficient_kernel,
        out_shape=jax.ShapeDtypeStruct((2 * count, orbs), BF16),
        in_specs=[pl.BlockSpec(memory_space=pltpu.VMEM)] * 2,
        out_specs=pl.BlockSpec(memory_space=pltpu.VMEM),
        compiler_params=params(),
        cost_estimate=cost(4096, 4096),
        name="coefficients",
    )(sums, strength)


def nonlocal_kernel(unroll, a, b, c, d, q, weights, out):
    count, orbs = a.shape[0] // 2, a.shape[1]
    turned = sum(
        jnp.dot(ref[...], q[k], preferred_element_type=F32) for k, ref in enumerate((a, b, c, d))
    )
    turned = turned * 0.25
    one, two = turned[0:count], turned[count : 2 * count]
    right = jnp.concatenate([two, one, one], axis=0)
    hi = right.astype(BF16)
    lo = right - hi.astype(F32)
    right = jnp.concatenate([hi.astype(F32), lo], axis=1).astype(BF16)

    def step(i, carry):
        for k in range(unroll):
            r = i * unroll + k
            for plane in range(weights.shape[0]):
                both = lax.dot_general(
                    weights[plane, r], right, (((0,), (0,)), ((), ())), preferred_element_type=F32
                )
                out[plane, r] = both[:, :orbs] + both[:, orbs:]
        return carry

    lax.fori_loop(0, weights.shape[1] // unroll, step, 0)


def nonlocal_term(shape, coefs, q, weights):
    unroll = max(g for g in (1, 2, 4, 8) if weights.shape[1] % g == 0)
    return pl.pallas_call(
        functools.partial(nonlocal_kernel, unroll),
        out_shape=jax.ShapeDtypeStruct(shape, F32),
        in_specs=[pl.BlockSpec(memory_space=pltpu.VMEM)] * 6,
        out_specs=pl.BlockSpec(memory_space=pltpu.VMEM),
        compiler_params=params(),
        cost_estimate=cost(4096, 4096),
        name="nonlocal",
    )(*coefs, q, weights)


def filter_kernel(slabs, start, parts, joint, *refs):
    own, p_own, zo = refs[:3]
    xrs, zfs = refs[3 : 3 + parts], refs[3 + parts : 3 + 2 * parts]
    extra = 7
    outs, scratch = refs[3 + 2 * parts : -extra], refs[-extra:]
    first, lines, diagonals = scratch[:3]
    place = lax.axis_index("space")
    x = lax.rem(place, 2)
    width = own.shape[2]
    cells = 2 * width
    half = own.shape[1] // 2
    orbs = own.shape[3]
    rows = outs[0].shape[1]
    base = (half - 2) * x
    lower = (place >= 2).astype(F32)
    upper = (place < slabs - 2).astype(F32)
    is_odd = x.astype(F32)
    has_zf = lower * (1.0 - is_odd) + upper * is_odd
    has_zo = upper * (1.0 - is_odd) + lower * is_odd
    xr, zf, pots, sems = scratch[3:]
    window = xr.shape[1] // 2
    early = xrs[0].shape[1] - 1
    copies = []
    for k, (target, pieces) in enumerate(((xr, xrs), (zf, zfs))):
        begin = 0 if parts == 1 else early - 8
        moved = [
            (pieces[0].at[:, pl.ds(early, 1)], pots.at[k]),
            (
                pieces[0].at[:, pl.ds(begin, early - begin)],
                target.at[:, pl.ds(begin, early - begin)],
            ),
        ]
        if parts > 1:
            later = target.shape[1] - early
            moved.append((pieces[1].at[:, pl.ds(0, later)], target.at[:, pl.ds(early, later)]))
        copies += [
            pltpu.make_async_copy(source, goal, sems.at[3 * k + i])
            for i, (source, goal) in enumerate(moved)
        ]
    for copy in copies:
        copy.start()

    def fill(c, block):
        lines[c - 1] = block
        for kind in range(2):
            even, odd = (lines[c - 1, pl.ds(k, half, stride=2)] for k in range(2))
            lanes = slice(64 * kind, 64 * kind + width)
            diagonals[c - 1, kind] = jnp.concatenate([even[:, lanes], odd[:, lanes]], axis=1)

    for c in (2, 3):
        fill(c, potential_block(p_own[(c % 2) ^ x]))
    fill(6, zo[x, zo.shape[1] - 1].astype(F32))
    for copy in copies:
        copy.wait()
    for c in (1, 4, 5):
        fill(c, pots[1 if c < 2 else 0, (c % 2) ^ x, 0].astype(F32))

    here = neighbour_sum(width, True)
    i = lax.broadcasted_iota(jnp.int32, (cells, cells), 0)
    diagonal = i == lax.broadcasted_iota(jnp.int32, (cells, cells), 1)

    def local(c, p):
        at = base // 2 + p
        hi = diagonals[c - 1, 0, pl.ds(at, 1)]
        lo = diagonals[c - 1, 1, pl.ds(at, 1)]
        return (
            jnp.where(diagonal, hi, here).astype(BF16),
            jnp.where(diagonal, lo, 0.0).astype(BF16),
        )

    def rows_of(c, w, n):
        plane = (c % 2) ^ x
        if c in (2, 3):
            return own[plane, pl.ds(base + w, n)]
        ref = zf if c < 2 else (xr if c < 6 else zo)
        return ref[plane, pl.ds(w, n)]

    def applied(pair, outer, zs, matrices):
        near = jnp.dot(matrices[0], pair, preferred_element_type=F32)
        near = near + jnp.dot(matrices[1], pair, preferred_element_type=F32)
        return near - 0.125 * (outer + zs)

    def step1(j, carry):
        p = start // 2 + x + j - 1
        q = jnp.clip(p, 0, window - 1)
        has_below = inside(p - 1, window)
        has_above = inside(p + 1, window)
        valid = inside(p, window)
        below = jnp.maximum(2 * q - 1, 0)
        above = jnp.minimum(2 * q + 2, 2 * window - 1)
        pair = [rows_of(c, 2 * q, 2).reshape(cells, orbs) for c in range(8)]
        vs = [v.astype(F32) for v in pair]
        for c in range(1, 7):
            outer = jnp.concatenate(
                [
                    rows_of(c, below, 1)[0].astype(F32) * has_below,
                    rows_of(c, above, 1)[0].astype(F32) * has_above,
                ],
                axis=0,
            )
            f = applied(pair[c], outer, vs[c - 1] + vs[c + 1], local(c, q))
            keep = valid
            if c == 1:
                keep = valid * has_zf
            if c == 6:
                keep = valid * has_zo
            first[c - 1, pl.ds(2 * j, 2)] = (f * keep).astype(BF16).reshape(2, width, orbs)
        return carry

    lax.fori_loop(0, rows // 2 + 2, step1, 0)

    def step2(j, carry):
        p = start // 2 + x + j
        pair = [first[c - 1, pl.ds(2 * j + 2, 2)].reshape(cells, orbs) for c in range(1, 7)]
        vs = [v.astype(F32) for v in pair]
        for c in range(2, 6):
            outer = jnp.concatenate(
                [first[c - 1, 2 * j + 1].astype(F32), first[c - 1, 2 * j + 4].astype(F32)], axis=0
            )
            f = applied(pair[c - 1], outer, vs[c - 2] + vs[c], local(c, p))
            f = f.astype(BF16).reshape(2, width, orbs)
            plane = (c % 2) ^ x
            if joint:
                outs[0][plane + (2 if c in (2, 3) else 0), pl.ds(2 * j, 2)] = f
            else:
                outs[1 if c in (2, 3) else 0][plane, pl.ds(2 * j, 2)] = f
        return carry

    lax.fori_loop(0, rows // 2, step2, 0)


def filtered(slabs, start, rows, joint, operands, xrs, zfs):
    own = operands[0]
    planes, _, width, orbs = own.shape
    parts = len(xrs)
    shape = (2 * planes if joint else planes, rows, width, orbs)
    out = (jax.ShapeDtypeStruct(shape, BF16),) * (1 if joint else 2)
    cells = 10 * rows * width
    scratch = [
        pltpu.VMEM((6, rows + 4, width, orbs), BF16),
        pltpu.VMEM((6, width, orbs), F32),
        pltpu.VMEM((6, 2, own.shape[1] // 2, 2 * width), F32),
    ]
    window = own.shape[1] // 2 + 2 if parts > 1 else xrs[0].shape[1] - 1
    scratch += [pltpu.VMEM((planes, window, width, orbs), BF16)] * 2
    scratch += [pltpu.VMEM((2, planes, 1, width, orbs), BF16), pltpu.SemaphoreType.DMA((6,))]
    local = pl.BlockSpec(memory_space=pltpu.VMEM)
    distant = pl.BlockSpec(memory_space=pltpu.MemorySpace.HBM)
    xrs, zfs = (
        [pltpu.with_memory_space_constraint(piece, pltpu.MemorySpace.HBM) for piece in pieces]
        for pieces in (xrs, zfs)
    )
    return pl.pallas_call(
        functools.partial(filter_kernel, slabs, start, parts, joint),
        out_shape=out,
        in_specs=[local] * len(operands) + [distant] * (2 * parts),
        out_specs=(local,) * len(out),
        scratch_shapes=scratch,
        compiler_params=params(),
        cost_estimate=cost(2 * cells * 32 * orbs, FILTER * cells * orbs * 4),
        name="filtered",
    )(*operands, *xrs, *zfs)


def rotate_kernel(group, *refs):
    a, b, c, d, q = refs[:5]
    outs = refs[5:]
    _, rows, width, orbs = a.shape
    planes = outs[0].shape[0]
    low = jnp.concatenate([q[0], q[1]], axis=0)
    high = jnp.concatenate([q[2], q[3]], axis=0)

    def one(j, carry):
        for plane in range(a.shape[0]):
            def take(ref):
                return ref[plane, pl.ds(group * j, group)].reshape(group * width, orbs)

            total = jnp.dot(
                jnp.concatenate([take(a), take(b)], axis=1), low, preferred_element_type=F32
            )
            total = total + jnp.dot(
                jnp.concatenate([take(c), take(d)], axis=1), high, preferred_element_type=F32
            )
            outs[plane // planes][plane % planes, pl.ds(group * j, group)] = total.astype(
                BF16
            ).reshape(group, width, orbs)
        return carry

    lax.fori_loop(0, rows // group, one, 0)


def rotated(blocks, q, pieces):
    a = blocks[0]
    size = a.size
    group = max(g for g in range(1, 9) if a.shape[1] % g == 0)
    out = jax.ShapeDtypeStruct((a.shape[0] // pieces, *a.shape[1:]), BF16)
    return pl.pallas_call(
        functools.partial(rotate_kernel, group),
        out_shape=(out,) * pieces,
        in_specs=[pl.BlockSpec(memory_space=pltpu.VMEM)] * 5,
        out_specs=(pl.BlockSpec(memory_space=pltpu.VMEM),) * pieces,
        compiler_params=params(),
        cost_estimate=cost(8 * size * a.shape[3], 10 * size),
        name="rotated",
    )(*blocks, q)


def assemble_kernel(group, term, keep1, got1, got2, a, b, c, d, q, out):
    half = term.shape[1] // 2
    width, orbs = term.shape[2:]
    x = lax.rem(lax.axis_index("space"), 2)
    rows1, rows2 = keep1.shape[1], got2.shape[1]
    for ref, at in (
        (keep1, half * x),
        (got1, half * (1 - x)),
        (got2, half * (1 - x) + rows1),
    ):
        where = pl.ds(at, ref.shape[1])
        out[:, where] = (ref[...].astype(F32) + term[:, where]).astype(BF16)
    low = jnp.concatenate([q[0], q[1]], axis=0)
    high = jnp.concatenate([q[2], q[3]], axis=0)

    def one(j, carry):
        where = pl.ds(half * x + rows1 + group * j, group)
        for plane in range(a.shape[0]):
            def take(ref):
                return ref[plane, pl.ds(group * j, group)].reshape(group * width, orbs)

            total = jnp.dot(
                jnp.concatenate([take(a), take(b)], axis=1), low, preferred_element_type=F32
            )
            total = total + jnp.dot(
                jnp.concatenate([take(c), take(d)], axis=1), high, preferred_element_type=F32
            )
            total = total.reshape(group, width, orbs) + term[plane, where]
            out[plane, where] = total.astype(BF16)
        return carry

    lax.fori_loop(0, rows2 // group, one, 0)


def assembled(term, keep1, got1, got2, blocks, q):
    group = max(g for g in range(1, 9) if got2.shape[1] % g == 0)
    return pl.pallas_call(
        functools.partial(assemble_kernel, group),
        out_shape=jax.ShapeDtypeStruct(term.shape, BF16),
        in_specs=[pl.BlockSpec(memory_space=pltpu.VMEM)] * 9,
        out_specs=pl.BlockSpec(memory_space=pltpu.VMEM),
        compiler_params=params(),
        cost_estimate=cost(4096, 4096),
        name="assembled",
    )(term, keep1, got1, got2, *blocks, q)


def ordered(*arrays):
    return lax.optimization_barrier(arrays)


def shards(psi, potential, beta, strength, atom_slab, pattern, q_tiles):
    planes, width_x, width_y, orbs = psi.shape
    count = beta.shape[0]
    slabs = lax.axis_size("space")
    place = lax.axis_index("space")
    x = lax.rem(place, 2)
    half = width_x // 2
    window = half + 2
    rows1 = half * 7 // 24 * 2
    rows2 = half - rows1
    early = rows1 + 4

    def within(pairs):
        return [(i, j) for i, j in pairs if 0 <= j < slabs]

    swap = [(i, i ^ 1) for i in range(slabs)]
    own_way = within([(i, i + 2 if i % 2 else i - 2) for i in range(slabs)])
    other_way = within([(i, i - 2 if i % 2 else i + 2) for i in range(slabs)])
    groups = lax.axis_size("orb")
    across = [(i, i ^ 2) for i in range(groups)]
    beside = [(i, i ^ 1) for i in range(groups)]
    mine = (half - 2) * x
    theirs = (half - 2) * (1 - x)

    to_x, to_z = prepared(psi, potential, early)
    to_x2, far, near = packed(psi, beta, early)
    f_x = lax.ppermute(near, "space", swap)
    raster = within([(i, i + 1 if i % 2 else i - 1) for i in range(slabs)])
    f_d = lax.ppermute(far, "space", raster)
    xr1 = lax.ppermute(to_x, "space", swap)
    zo = lax.ppermute(to_z, "space", own_way)
    active = jnp.abs(place - atom_slab) <= 1
    beta_m = jnp.where(active[:, None, None, None], beta, jnp.zeros_like(beta))
    gram = jnp.einsum("pzxy,qzxy->pq", beta_m, beta_m, preferred_element_type=F32)
    xr1, second = ordered(xr1, to_x2)
    zf1 = lax.ppermute(xr1, "space", other_way)
    xr2 = lax.ppermute(second, "space", swap)
    zf2 = lax.ppermute(xr2, "space", other_way)
    strong = jnp.broadcast_to(strength[:, None], (count, orbs))

    sums, weights = partials(count, atom_slab, psi, beta, f_x, f_d, potential, gram)
    zf1, sums, _ = ordered(zf1, sums, xr2)
    operands = (psi, potential, zo)
    (block1,) = filtered(slabs, 0, rows1, True, operands, (xr1,), (zf1,))
    y1 = lax.ppermute(block1, "orb", across)
    rounds = [1 << k for k in range((slabs - 1).bit_length())]

    def added(values, step):
        pairs = [(i, i ^ step) for i in range(slabs)]
        return values + lax.ppermute(values, "space", pairs)

    for step in rounds[:2]:
        sums = added(sums, step)
    zf2, sums = ordered(zf2, sums)
    give2, keep2 = filtered(slabs, rows1, rows2, False, operands, (xr1, xr2), (zf1, zf2))
    pattern, q_tiles, _ = ordered(pattern, q_tiles, give2)
    me = lax.axis_index("orb")
    which = jnp.bitwise_xor(me, jnp.arange(groups, dtype=jnp.int32))
    rows_hot = (pattern[:, 0][:, None] == which[None, :]).astype(BF16)
    rows_hot = rows_hot * (pattern[:, 1] == me).astype(BF16)[:, None]
    q = jnp.einsum("ki,kab->iab", rows_hot, q_tiles, preferred_element_type=F32).astype(BF16)
    cg = lax.ppermute(give2, "orb", beside)
    ck = lax.ppermute(keep2, "orb", beside)
    yg = lax.ppermute(give2, "orb", across)
    y1, again, _ = ordered(y1, block1, give2)
    c1 = lax.ppermute(again, "orb", beside)
    yc1 = lax.ppermute(y1, "orb", beside)
    for step in rounds[2:]:
        sums = added(sums, step)
    yc1, sums = ordered(yc1, sums)
    give1, keep1 = rotated((block1, c1, y1, yc1), q, 2)
    got1 = lax.ppermute(give1, "space", swap)
    keep_y, yg, _, sums = ordered(keep2, yg, give1, sums)
    yk = lax.ppermute(keep_y, "orb", across)
    ycg = lax.ppermute(yg, "orb", beside)
    coefs = coefficients(sums, strong)
    coefs = jnp.concatenate([coefs, lax.ppermute(coefs, "orb", beside)], axis=0)
    ycg, coefs, got1 = ordered(ycg, coefs, got1)
    (give2,) = rotated((give2, cg, yg, ycg), q, 1)
    got2 = lax.ppermute(give2, "space", swap)
    coefs, _ = ordered(coefs, give2)
    coefs_y = lax.ppermute(coefs, "orb", across)
    coefs = [half_of[k * 2 * count : (k + 1) * 2 * count] for half_of in (coefs, coefs_y) for k in (0, 1)]
    term = nonlocal_term(psi.shape, coefs, q, weights)
    yk, _ = ordered(yk, give2)
    yck = lax.ppermute(yk, "orb", beside)
    return assembled(term, keep1, got1, got2, (keep2, ck, yk, yck), q)


def solution(mesh):
    placed = (
        P("space", None, None, "orb"),
        P("space", None, None),
        P(None, "space", None, None),
        P(),
        P(),
        P(),
        P(),
    )
    return jax.shard_map(
        shards, mesh=mesh, in_specs=placed, out_specs=P("space", None, None, "orb"), check_vma=False
    )
```

```python
import functools

import jax
import jax.numpy as jnp
from jax import lax
from jax.experimental import pallas as pl
from jax.experimental.pallas import tpu as pltpu
from jax.sharding import PartitionSpec as P

F32 = jnp.float32
BF16 = jnp.bfloat16
VMEM_LIMIT = 24 * 1024 * 1024
SHRINK = 16
FILTER = 100


def params():
    return pltpu.CompilerParams(vmem_limit_bytes=VMEM_LIMIT)


def cost(flops, moved):
    return pl.CostEstimate(flops=flops // SHRINK, bytes_accessed=moved // SHRINK, transcendentals=0)


def inside(p, window):
    return jnp.logical_and(p >= 0, p < window).astype(F32)


def neighbour_sum(width, pairs):
    n = (2 if pairs else 1) * width
    i = lax.broadcasted_iota(jnp.int32, (n, n), 0)
    j = lax.broadcasted_iota(jnp.int32, (n, n), 1)
    linked = jnp.abs(i - j) == 1
    if pairs:
        linked = jnp.logical_and(linked, (i < width) == (j < width))
        linked = jnp.logical_or(linked, jnp.abs(i - j) == width)
    return jnp.where(linked, -0.125, 0.0)


def potential_block(potential):
    lines, width = potential.shape
    gap = jnp.zeros((lines, 64 - width), F32)
    u = (potential - 1.0) * 0.25
    hi = u.astype(BF16).astype(F32)
    return jnp.concatenate([hi, gap, u - hi, gap], axis=1)


def prepare_kernel(early, psi, potential_far, to_x, to_z, potential, sems):
    x = lax.rem(lax.axis_index("space"), 2)
    half = psi.shape[1] // 2
    window = half + 2
    mine, theirs = (half - 2) * x, (half - 2) * (1 - x)
    fetch = pltpu.make_async_copy(potential_far, potential, sems.at[0])
    fetch.start()
    copies = [
        pltpu.make_async_copy(
            psi.at[:, pl.ds(theirs, early)], to_x.at[:, pl.ds(0, early)], sems.at[1]
        ),
        pltpu.make_async_copy(
            psi.at[:, pl.ds(mine, window)], to_z.at[:, pl.ds(0, window)], sems.at[2]
        ),
    ]
    for copy in copies:
        copy.start()
    fetch.wait()
    for plane in range(potential.shape[0]):
        block = potential_block(potential[plane]).astype(BF16)
        to_x[plane, early] = block
        to_z[plane, window] = block
    for copy in copies:
        copy.wait()


def prepared(psi, potential, early):
    planes, width_x, width_y, orbs = psi.shape
    window = width_x // 2 + 2

    def out(rows):
        return jax.ShapeDtypeStruct((planes, rows, width_y, orbs), BF16)

    return pl.pallas_call(
        functools.partial(prepare_kernel, early),
        out_shape=(out(early + 1), out(window + 1)),
        in_specs=[pl.BlockSpec(memory_space=pltpu.MemorySpace.HBM)] * 2,
        out_specs=(pl.BlockSpec(memory_space=pltpu.VMEM),) * 2,
        scratch_shapes=[pltpu.VMEM(potential.shape, F32), pltpu.SemaphoreType.DMA((3,))],
        compiler_params=params(),
        cost_estimate=cost(4096, 4096),
        name="prepared",
    )(*(pltpu.with_memory_space_constraint(a, pltpu.MemorySpace.HBM) for a in (psi, potential)))


def pack_kernel(early, psi, beta, to_x2, far, near, sem):
    x = lax.rem(lax.axis_index("space"), 2)
    half = psi.shape[1] // 2
    later = half + 2 - early
    copy = pltpu.make_async_copy(
        psi.at[:, pl.ds((half - 2) * (1 - x) + early, later)], to_x2, sem
    )
    copy.start()
    far[...] = beta[:, x]
    near[...] = beta[:, 1 - x]
    copy.wait()


def packed(psi, beta, early):
    planes, width_x, width_y, orbs = psi.shape
    side = jax.ShapeDtypeStruct((beta.shape[0], *beta.shape[2:]), BF16)
    later = width_x // 2 + 2 - early
    return pl.pallas_call(
        functools.partial(pack_kernel, early),
        out_shape=(jax.ShapeDtypeStruct((planes, later, width_y, orbs), BF16), side, side),
        in_specs=[
            pl.BlockSpec(memory_space=pltpu.MemorySpace.HBM),
            pl.BlockSpec(memory_space=pltpu.VMEM),
        ],
        out_specs=(pl.BlockSpec(memory_space=pltpu.VMEM),) * 3,
        scratch_shapes=[pltpu.SemaphoreType.DMA],
        compiler_params=params(),
        cost_estimate=cost(4096, 4096),
        name="packed",
    )(pltpu.with_memory_space_constraint(psi, pltpu.MemorySpace.HBM), beta)


def partial_kernel(count, atoms, own, beta, b_x, b_d, potential, gram, out, weights_out, table, acc):
    place = lax.axis_index("space")
    x = lax.rem(place, 2)
    rows, width = potential.shape[1:]
    side = place ^ 1
    beyond = place - 1 + 2 * x
    tri = neighbour_sum(width, False).astype(BF16)
    acc[...] = jnp.zeros_like(acc)
    step = 8

    for k in range(2):
        plane = x if k == 0 else 1 - x
        outer, there = (b_d, beyond) if k == 0 else (b_x, side)
        u = (potential[plane] - 1.0) * 0.25

        def fill(i, carry):
            for j in range(step):
                p = i * step + j
                here = (jnp.abs(place - atoms[p]) <= 1).astype(F32)
                next_to = (jnp.abs(there - atoms[p]) <= 1).astype(F32)
                b32 = beta[p, plane].astype(F32) * here
                b = b32.astype(BF16)
                sides = beta[p, 1 - plane].astype(F32) * here + outer[p].astype(F32) * next_to
                whole = jnp.dot(b, tri, preferred_element_type=F32)
                whole = whole + jnp.dot(tri, b, preferred_element_type=F32)
                whole = whole + u * b32 - 0.125 * sides
                hi = whole.astype(BF16).astype(F32)
                for kind, value in enumerate((b32, hi, whole - hi)):
                    table[pl.ds((kind * count + p) * rows, rows)] = value
            return carry

        lax.fori_loop(0, count // step, fill, 0)

        def use(i, carry):
            totals = []
            for j in range(step):
                r = i * step + j
                weights = table[pl.ds(r, 3 * count, stride=rows)].astype(BF16)
                weights_out[plane, r] = weights
                totals.append(jnp.dot(weights, own[plane, r], preferred_element_type=F32))
            acc[...] += sum(totals[1:], totals[0])
            return carry

        lax.fori_loop(0, rows // step, use, 0)
    out[...] = jnp.zeros_like(out)
    out[0:count] = acc[0:count]
    out[count : 2 * count] = acc[count : 2 * count] + acc[2 * count : 3 * count]
    out[2 * count : 3 * count, 0:count] = gram[...]


def partials(count, atoms, own, beta, b_x, b_d, potential, gram):
    planes, rows, width, orbs = own.shape
    return pl.pallas_call(
        functools.partial(partial_kernel, count),
        out_shape=(
            jax.ShapeDtypeStruct((3 * count, orbs), F32),
            jax.ShapeDtypeStruct((planes, rows, 3 * count, width), BF16),
        ),
        in_specs=[pl.BlockSpec(memory_space=pltpu.SMEM)]
        + [pl.BlockSpec(memory_space=pltpu.VMEM)] * 6,
        out_specs=(pl.BlockSpec(memory_space=pltpu.VMEM),) * 2,
        scratch_shapes=[
            pltpu.VMEM((3 * count * rows, width), F32),
            pltpu.VMEM((3 * count, orbs), F32),
        ],
        compiler_params=params(),
        cost_estimate=cost(4096, 4096),
        name="partials",
    )(atoms, own, beta, b_x, b_d, potential, gram)


def coefficient_kernel(sums, strength, out):
    count, orbs = strength.shape
    coef1 = (strength[...] * sums[0:count]).astype(BF16)
    padded = coef1.astype(F32) * 0.25
    if orbs > count:
        padded = jnp.concatenate([padded, jnp.zeros((orbs - count, orbs), F32)], axis=0)
    proj2 = sums[count : 2 * count] + jnp.dot(
        sums[2 * count : 3 * count],
        padded,
        preferred_element_type=F32,
        precision=lax.Precision.HIGHEST,
    )
    out[0:count] = coef1
    out[count : 2 * count] = (strength[...] * proj2).astype(BF16)


def coefficients(sums, strength):
    count, orbs = strength.shape
    return pl.pallas_call(
        coefficient_kernel,
        out_shape=jax.ShapeDtypeStruct((2 * count, orbs), BF16),
        in_specs=[pl.BlockSpec(memory_space=pltpu.VMEM)] * 2,
        out_specs=pl.BlockSpec(memory_space=pltpu.VMEM),
        compiler_params=params(),
        cost_estimate=cost(4096, 4096),
        name="coefficients",
    )(sums, strength)


def nonlocal_kernel(unroll, a, b, c, d, q, weights, out):
    count, orbs = a.shape[0] // 2, a.shape[1]
    turned = sum(
        jnp.dot(ref[...], q[k], preferred_element_type=F32) for k, ref in enumerate((a, b, c, d))
    )
    turned = turned * 0.25
    one, two = turned[0:count], turned[count : 2 * count]
    right = jnp.concatenate([two, one, one], axis=0)
    hi = right.astype(BF16)
    lo = right - hi.astype(F32)
    right = jnp.concatenate([hi.astype(F32), lo], axis=1).astype(BF16)

    def step(i, carry):
        for k in range(unroll):
            r = i * unroll + k
            for plane in range(weights.shape[0]):
                both = lax.dot_general(
                    weights[plane, r], right, (((0,), (0,)), ((), ())), preferred_element_type=F32
                )
                out[plane, r] = both[:, :orbs] + both[:, orbs:]
        return carry

    lax.fori_loop(0, weights.shape[1] // unroll, step, 0)


def nonlocal_term(shape, coefs, q, weights):
    unroll = max(g for g in (1, 2, 4, 8) if weights.shape[1] % g == 0)
    return pl.pallas_call(
        functools.partial(nonlocal_kernel, unroll),
        out_shape=jax.ShapeDtypeStruct(shape, F32),
        in_specs=[pl.BlockSpec(memory_space=pltpu.VMEM)] * 6,
        out_specs=pl.BlockSpec(memory_space=pltpu.VMEM),
        compiler_params=params(),
        cost_estimate=cost(4096, 4096),
        name="nonlocal",
    )(*coefs, q, weights)


def filter_kernel(slabs, start, parts, joint, *refs):
    own, p_own, zo = refs[:3]
    xrs, zfs = refs[3 : 3 + parts], refs[3 + parts : 3 + 2 * parts]
    extra = 7
    outs, scratch = refs[3 + 2 * parts : -extra], refs[-extra:]
    first, lines, diagonals = scratch[:3]
    place = lax.axis_index("space")
    x = lax.rem(place, 2)
    width = own.shape[2]
    cells = 2 * width
    half = own.shape[1] // 2
    orbs = own.shape[3]
    rows = outs[0].shape[1]
    base = (half - 2) * x
    lower = (place >= 2).astype(F32)
    upper = (place < slabs - 2).astype(F32)
    is_odd = x.astype(F32)
    has_zf = lower * (1.0 - is_odd) + upper * is_odd
    has_zo = upper * (1.0 - is_odd) + lower * is_odd
    xr, zf, pots, sems = scratch[3:]
    window = xr.shape[1] // 2
    early = xrs[0].shape[1] - 1
    copies = []
    for k, (target, pieces) in enumerate(((xr, xrs), (zf, zfs))):
        begin = 0 if parts == 1 else early - 8
        moved = [
            (pieces[0].at[:, pl.ds(early, 1)], pots.at[k]),
            (
                pieces[0].at[:, pl.ds(begin, early - begin)],
                target.at[:, pl.ds(begin, early - begin)],
            ),
        ]
        if parts > 1:
            later = target.shape[1] - early
            moved.append((pieces[1].at[:, pl.ds(0, later)], target.at[:, pl.ds(early, later)]))
        copies += [
            pltpu.make_async_copy(source, goal, sems.at[3 * k + i])
            for i, (source, goal) in enumerate(moved)
        ]
    for copy in copies:
        copy.start()

    def fill(c, block):
        lines[c - 1] = block
        for kind in range(2):
            even, odd = (lines[c - 1, pl.ds(k, half, stride=2)] for k in range(2))
            lanes = slice(64 * kind, 64 * kind + width)
            diagonals[c - 1, kind] = jnp.concatenate([even[:, lanes], odd[:, lanes]], axis=1)

    for c in (2, 3):
        fill(c, potential_block(p_own[(c % 2) ^ x]))
    fill(6, zo[x, zo.shape[1] - 1].astype(F32))
    for copy in copies:
        copy.wait()
    for c in (1, 4, 5):
        fill(c, pots[1 if c < 2 else 0, (c % 2) ^ x, 0].astype(F32))

    here = neighbour_sum(width, True)
    i = lax.broadcasted_iota(jnp.int32, (cells, cells), 0)
    diagonal = i == lax.broadcasted_iota(jnp.int32, (cells, cells), 1)

    def local(c, p):
        at = base // 2 + p
        hi = diagonals[c - 1, 0, pl.ds(at, 1)]
        lo = diagonals[c - 1, 1, pl.ds(at, 1)]
        return (
            jnp.where(diagonal, hi, here).astype(BF16),
            jnp.where(diagonal, lo, 0.0).astype(BF16),
        )

    def rows_of(c, w, n):
        plane = (c % 2) ^ x
        if c in (2, 3):
            return own[plane, pl.ds(base + w, n)]
        ref = zf if c < 2 else (xr if c < 6 else zo)
        return ref[plane, pl.ds(w, n)]

    def applied(pair, outer, zs, matrices):
        near = jnp.dot(matrices[0], pair, preferred_element_type=F32)
        near = near + jnp.dot(matrices[1], pair, preferred_element_type=F32)
        return near - 0.125 * (outer + zs)

    def step1(j, carry):
        p = start // 2 + x + j - 1
        q = jnp.clip(p, 0, window - 1)
        has_below = inside(p - 1, window)
        has_above = inside(p + 1, window)
        valid = inside(p, window)
        below = jnp.maximum(2 * q - 1, 0)
        above = jnp.minimum(2 * q + 2, 2 * window - 1)
        pair = [rows_of(c, 2 * q, 2).reshape(cells, orbs) for c in range(8)]
        vs = [v.astype(F32) for v in pair]
        for c in range(1, 7):
            outer = jnp.concatenate(
                [
                    rows_of(c, below, 1)[0].astype(F32) * has_below,
                    rows_of(c, above, 1)[0].astype(F32) * has_above,
                ],
                axis=0,
            )
            f = applied(pair[c], outer, vs[c - 1] + vs[c + 1], local(c, q))
            keep = valid
            if c == 1:
                keep = valid * has_zf
            if c == 6:
                keep = valid * has_zo
            first[c - 1, pl.ds(2 * j, 2)] = (f * keep).astype(BF16).reshape(2, width, orbs)
        return carry

    lax.fori_loop(0, rows // 2 + 2, step1, 0)

    def step2(j, carry):
        p = start // 2 + x + j
        pair = [first[c - 1, pl.ds(2 * j + 2, 2)].reshape(cells, orbs) for c in range(1, 7)]
        vs = [v.astype(F32) for v in pair]
        for c in range(2, 6):
            outer = jnp.concatenate(
                [first[c - 1, 2 * j + 1].astype(F32), first[c - 1, 2 * j + 4].astype(F32)], axis=0
            )
            f = applied(pair[c - 1], outer, vs[c - 2] + vs[c], local(c, p))
            f = f.astype(BF16).reshape(2, width, orbs)
            plane = (c % 2) ^ x
            if joint:
                outs[0][plane + (2 if c in (2, 3) else 0), pl.ds(2 * j, 2)] = f
            else:
                outs[1 if c in (2, 3) else 0][plane, pl.ds(2 * j, 2)] = f
        return carry

    lax.fori_loop(0, rows // 2, step2, 0)


def filtered(slabs, start, rows, joint, operands, xrs, zfs):
    own = operands[0]
    planes, _, width, orbs = own.shape
    parts = len(xrs)
    shape = (2 * planes if joint else planes, rows, width, orbs)
    out = (jax.ShapeDtypeStruct(shape, BF16),) * (1 if joint else 2)
    cells = 10 * rows * width
    scratch = [
        pltpu.VMEM((6, rows + 4, width, orbs), BF16),
        pltpu.VMEM((6, width, orbs), F32),
        pltpu.VMEM((6, 2, own.shape[1] // 2, 2 * width), F32),
    ]
    window = own.shape[1] // 2 + 2 if parts > 1 else xrs[0].shape[1] - 1
    scratch += [pltpu.VMEM((planes, window, width, orbs), BF16)] * 2
    scratch += [pltpu.VMEM((2, planes, 1, width, orbs), BF16), pltpu.SemaphoreType.DMA((6,))]
    local = pl.BlockSpec(memory_space=pltpu.VMEM)
    distant = pl.BlockSpec(memory_space=pltpu.MemorySpace.HBM)
    xrs, zfs = (
        [pltpu.with_memory_space_constraint(piece, pltpu.MemorySpace.HBM) for piece in pieces]
        for pieces in (xrs, zfs)
    )
    return pl.pallas_call(
        functools.partial(filter_kernel, slabs, start, parts, joint),
        out_shape=out,
        in_specs=[local] * len(operands) + [distant] * (2 * parts),
        out_specs=(local,) * len(out),
        scratch_shapes=scratch,
        compiler_params=params(),
        cost_estimate=cost(2 * cells * 32 * orbs, FILTER * cells * orbs * 4),
        name="filtered",
    )(*operands, *xrs, *zfs)


def rotate_kernel(group, *refs):
    a, b, c, d, q = refs[:5]
    outs = refs[5:]
    _, rows, width, orbs = a.shape
    planes = outs[0].shape[0]
    low = jnp.concatenate([q[0], q[1]], axis=0)
    high = jnp.concatenate([q[2], q[3]], axis=0)

    def one(j, carry):
        for plane in range(a.shape[0]):
            def take(ref):
                return ref[plane, pl.ds(group * j, group)].reshape(group * width, orbs)

            total = jnp.dot(
                jnp.concatenate([take(a), take(b)], axis=1), low, preferred_element_type=F32
            )
            total = total + jnp.dot(
                jnp.concatenate([take(c), take(d)], axis=1), high, preferred_element_type=F32
            )
            outs[plane // planes][plane % planes, pl.ds(group * j, group)] = total.astype(
                BF16
            ).reshape(group, width, orbs)
        return carry

    lax.fori_loop(0, rows // group, one, 0)


def rotated(blocks, q, pieces):
    a = blocks[0]
    size = a.size
    group = max(g for g in range(1, 9) if a.shape[1] % g == 0)
    out = jax.ShapeDtypeStruct((a.shape[0] // pieces, *a.shape[1:]), BF16)
    return pl.pallas_call(
        functools.partial(rotate_kernel, group),
        out_shape=(out,) * pieces,
        in_specs=[pl.BlockSpec(memory_space=pltpu.VMEM)] * 5,
        out_specs=(pl.BlockSpec(memory_space=pltpu.VMEM),) * pieces,
        compiler_params=params(),
        cost_estimate=cost(8 * size * a.shape[3], 10 * size),
        name="rotated",
    )(*blocks, q)


def assemble_kernel(group, term, keep1, got1, got2, a, b, c, d, q, out):
    half = term.shape[1] // 2
    width, orbs = term.shape[2:]
    x = lax.rem(lax.axis_index("space"), 2)
    rows1, rows2 = keep1.shape[1], got2.shape[1]
    for ref, at in (
        (keep1, half * x),
        (got1, half * (1 - x)),
        (got2, half * (1 - x) + rows1),
    ):
        where = pl.ds(at, ref.shape[1])
        out[:, where] = (ref[...].astype(F32) + term[:, where]).astype(BF16)
    low = jnp.concatenate([q[0], q[1]], axis=0)
    high = jnp.concatenate([q[2], q[3]], axis=0)

    def one(j, carry):
        where = pl.ds(half * x + rows1 + group * j, group)
        for plane in range(a.shape[0]):
            def take(ref):
                return ref[plane, pl.ds(group * j, group)].reshape(group * width, orbs)

            total = jnp.dot(
                jnp.concatenate([take(a), take(b)], axis=1), low, preferred_element_type=F32
            )
            total = total + jnp.dot(
                jnp.concatenate([take(c), take(d)], axis=1), high, preferred_element_type=F32
            )
            total = total.reshape(group, width, orbs) + term[plane, where]
            out[plane, where] = total.astype(BF16)
        return carry

    lax.fori_loop(0, rows2 // group, one, 0)


def assembled(term, keep1, got1, got2, blocks, q):
    group = max(g for g in range(1, 9) if got2.shape[1] % g == 0)
    return pl.pallas_call(
        functools.partial(assemble_kernel, group),
        out_shape=jax.ShapeDtypeStruct(term.shape, BF16),
        in_specs=[pl.BlockSpec(memory_space=pltpu.VMEM)] * 9,
        out_specs=pl.BlockSpec(memory_space=pltpu.VMEM),
        compiler_params=params(),
        cost_estimate=cost(4096, 4096),
        name="assembled",
    )(term, keep1, got1, got2, *blocks, q)


def ordered(*arrays):
    return lax.optimization_barrier(arrays)


def shards(psi, potential, beta, strength, atom_slab, pattern, q_tiles):
    planes, width_x, width_y, orbs = psi.shape
    count = beta.shape[0]
    slabs = lax.axis_size("space")
    place = lax.axis_index("space")
    x = lax.rem(place, 2)
    half = width_x // 2
    window = half + 2
    rows1 = half * 7 // 24 * 2
    rows2 = half - rows1
    early = rows1 + 4

    def within(pairs):
        return [(i, j) for i, j in pairs if 0 <= j < slabs]

    swap = [(i, i ^ 1) for i in range(slabs)]
    own_way = within([(i, i + 2 if i % 2 else i - 2) for i in range(slabs)])
    other_way = within([(i, i - 2 if i % 2 else i + 2) for i in range(slabs)])
    groups = lax.axis_size("orb")
    across = [(i, i ^ 2) for i in range(groups)]
    beside = [(i, i ^ 1) for i in range(groups)]
    mine = (half - 2) * x
    theirs = (half - 2) * (1 - x)

    to_x, to_z = prepared(psi, potential, early)
    to_x2, far, near = packed(psi, beta, early)
    f_x = lax.ppermute(near, "space", swap)
    raster = within([(i, i + 1 if i % 2 else i - 1) for i in range(slabs)])
    f_d = lax.ppermute(far, "space", raster)
    xr1 = lax.ppermute(to_x, "space", swap)
    zo = lax.ppermute(to_z, "space", own_way)
    active = jnp.abs(place - atom_slab) <= 1
    beta_m = jnp.where(active[:, None, None, None], beta, jnp.zeros_like(beta))
    gram = jnp.einsum("pzxy,qzxy->pq", beta_m, beta_m, preferred_element_type=F32)
    xr1, second = ordered(xr1, to_x2)
    zf1 = lax.ppermute(xr1, "space", other_way)
    xr2 = lax.ppermute(second, "space", swap)
    zf2 = lax.ppermute(xr2, "space", other_way)
    strong = jnp.broadcast_to(strength[:, None], (count, orbs))

    sums, weights = partials(count, atom_slab, psi, beta, f_x, f_d, potential, gram)
    zf1, sums, _ = ordered(zf1, sums, xr2)
    operands = (psi, potential, zo)
    (block1,) = filtered(slabs, 0, rows1, True, operands, (xr1,), (zf1,))
    y1 = lax.ppermute(block1, "orb", across)
    rounds = [1 << k for k in range((slabs - 1).bit_length())]

    def added(values, step):
        pairs = [(i, i ^ step) for i in range(slabs)]
        return values + lax.ppermute(values, "space", pairs)

    for step in rounds[:2]:
        sums = added(sums, step)
    zf2, sums = ordered(zf2, sums)
    give2, keep2 = filtered(slabs, rows1, rows2, False, operands, (xr1, xr2), (zf1, zf2))
    pattern, q_tiles, _ = ordered(pattern, q_tiles, give2)
    me = lax.axis_index("orb")
    which = jnp.bitwise_xor(me, jnp.arange(groups, dtype=jnp.int32))
    rows_hot = (pattern[:, 0][:, None] == which[None, :]).astype(BF16)
    rows_hot = rows_hot * (pattern[:, 1] == me).astype(BF16)[:, None]
    q = jnp.einsum("ki,kab->iab", rows_hot, q_tiles, preferred_element_type=F32).astype(BF16)
    cg = lax.ppermute(give2, "orb", beside)
    ck = lax.ppermute(keep2, "orb", beside)
    yg = lax.ppermute(give2, "orb", across)
    y1, again, _ = ordered(y1, block1, give2)
    c1 = lax.ppermute(again, "orb", beside)
    yc1 = lax.ppermute(y1, "orb", beside)
    for step in rounds[2:]:
        sums = added(sums, step)
    yc1, sums = ordered(yc1, sums)
    give1, keep1 = rotated((block1, c1, y1, yc1), q, 2)
    got1 = lax.ppermute(give1, "space", swap)
    keep_y, yg, _, sums = ordered(keep2, yg, give1, sums)
    yk = lax.ppermute(keep_y, "orb", across)
    ycg = lax.ppermute(yg, "orb", beside)
    coefs = coefficients(sums, strong)
    coefs = jnp.concatenate([coefs, lax.ppermute(coefs, "orb", beside)], axis=0)
    ycg, coefs = ordered(ycg, coefs)
    (give2,) = rotated((give2, cg, yg, ycg), q, 1)
    got2 = lax.ppermute(give2, "space", swap)
    coefs, _ = ordered(coefs, give2)
    coefs_y = lax.ppermute(coefs, "orb", across)
    coefs = [half_of[k * 2 * count : (k + 1) * 2 * count] for half_of in (coefs, coefs_y) for k in (0, 1)]
    term = nonlocal_term(psi.shape, coefs, q, weights)
    yk, _, got1 = ordered(yk, give2, got1)
    yck = lax.ppermute(yk, "orb", beside)
    return assembled(term, keep1, got1, got2, (keep2, ck, yk, yck), q)


def solution(mesh):
    placed = (
        P("space", None, None, "orb"),
        P("space", None, None),
        P(None, "space", None, None),
        P(),
        P(),
        P(),
        P(),
    )
    return jax.shard_map(
        shards, mesh=mesh, in_specs=placed, out_specs=P("space", None, None, "orb"), check_vma=False
    )
```

```python
import functools

import jax
import jax.numpy as jnp
from jax import lax
from jax.experimental import pallas as pl
from jax.experimental.pallas import tpu as pltpu
from jax.sharding import PartitionSpec as P

F32 = jnp.float32
BF16 = jnp.bfloat16
VMEM_LIMIT = 24 * 1024 * 1024
SHRINK = 16
FILTER = 100


def params():
    return pltpu.CompilerParams(vmem_limit_bytes=VMEM_LIMIT)


def cost(flops, moved):
    return pl.CostEstimate(flops=flops // SHRINK, bytes_accessed=moved // SHRINK, transcendentals=0)


def inside(p, window):
    return jnp.logical_and(p >= 0, p < window).astype(F32)


def neighbour_sum(width, pairs):
    n = (2 if pairs else 1) * width
    i = lax.broadcasted_iota(jnp.int32, (n, n), 0)
    j = lax.broadcasted_iota(jnp.int32, (n, n), 1)
    linked = jnp.abs(i - j) == 1
    if pairs:
        linked = jnp.logical_and(linked, (i < width) == (j < width))
        linked = jnp.logical_or(linked, jnp.abs(i - j) == width)
    return jnp.where(linked, -0.125, 0.0)


def potential_block(potential):
    lines, width = potential.shape
    gap = jnp.zeros((lines, 64 - width), F32)
    u = (potential - 1.0) * 0.25
    hi = u.astype(BF16).astype(F32)
    return jnp.concatenate([hi, gap, u - hi, gap], axis=1)


def prepare_kernel(early, psi, potential_far, to_x, to_z, potential, sems):
    x = lax.rem(lax.axis_index("space"), 2)
    half = psi.shape[1] // 2
    window = half + 2
    mine, theirs = (half - 2) * x, (half - 2) * (1 - x)
    fetch = pltpu.make_async_copy(potential_far, potential, sems.at[0])
    fetch.start()
    copies = [
        pltpu.make_async_copy(
            psi.at[:, pl.ds(theirs, early)], to_x.at[:, pl.ds(0, early)], sems.at[1]
        ),
        pltpu.make_async_copy(
            psi.at[:, pl.ds(mine, window)], to_z.at[:, pl.ds(0, window)], sems.at[2]
        ),
    ]
    for copy in copies:
        copy.start()
    fetch.wait()
    for plane in range(potential.shape[0]):
        block = potential_block(potential[plane]).astype(BF16)
        to_x[plane, early] = block
        to_z[plane, window] = block
    for copy in copies:
        copy.wait()


def prepared(psi, potential, early):
    planes, width_x, width_y, orbs = psi.shape
    window = width_x // 2 + 2

    def out(rows):
        return jax.ShapeDtypeStruct((planes, rows, width_y, orbs), BF16)

    return pl.pallas_call(
        functools.partial(prepare_kernel, early),
        out_shape=(out(early + 1), out(window + 1)),
        in_specs=[pl.BlockSpec(memory_space=pltpu.MemorySpace.HBM)] * 2,
        out_specs=(pl.BlockSpec(memory_space=pltpu.VMEM),) * 2,
        scratch_shapes=[pltpu.VMEM(potential.shape, F32), pltpu.SemaphoreType.DMA((3,))],
        compiler_params=params(),
        cost_estimate=cost(4096, 4096),
        name="prepared",
    )(*(pltpu.with_memory_space_constraint(a, pltpu.MemorySpace.HBM) for a in (psi, potential)))


def pack_kernel(early, psi, beta, to_x2, far, near, sem):
    x = lax.rem(lax.axis_index("space"), 2)
    half = psi.shape[1] // 2
    later = half + 2 - early
    copy = pltpu.make_async_copy(
        psi.at[:, pl.ds((half - 2) * (1 - x) + early, later)], to_x2, sem
    )
    copy.start()
    far[...] = beta[:, x]
    near[...] = beta[:, 1 - x]
    copy.wait()


def packed(psi, beta, early):
    planes, width_x, width_y, orbs = psi.shape
    side = jax.ShapeDtypeStruct((beta.shape[0], *beta.shape[2:]), BF16)
    later = width_x // 2 + 2 - early
    return pl.pallas_call(
        functools.partial(pack_kernel, early),
        out_shape=(jax.ShapeDtypeStruct((planes, later, width_y, orbs), BF16), side, side),
        in_specs=[
            pl.BlockSpec(memory_space=pltpu.MemorySpace.HBM),
            pl.BlockSpec(memory_space=pltpu.VMEM),
        ],
        out_specs=(pl.BlockSpec(memory_space=pltpu.VMEM),) * 3,
        scratch_shapes=[pltpu.SemaphoreType.DMA],
        compiler_params=params(),
        cost_estimate=cost(4096, 4096),
        name="packed",
    )(pltpu.with_memory_space_constraint(psi, pltpu.MemorySpace.HBM), beta)


def partial_kernel(count, atoms, own, beta, b_x, b_d, potential, gram, out, weights_out, table, acc):
    place = lax.axis_index("space")
    x = lax.rem(place, 2)
    rows, width = potential.shape[1:]
    side = place ^ 1
    beyond = place - 1 + 2 * x
    tri = neighbour_sum(width, False).astype(BF16)
    acc[...] = jnp.zeros_like(acc)
    step = 8

    for k in range(2):
        plane = x if k == 0 else 1 - x
        outer, there = (b_d, beyond) if k == 0 else (b_x, side)
        u = (potential[plane] - 1.0) * 0.25

        def fill(i, carry):
            for j in range(step):
                p = i * step + j
                here = (jnp.abs(place - atoms[p]) <= 1).astype(F32)
                next_to = (jnp.abs(there - atoms[p]) <= 1).astype(F32)
                b32 = beta[p, plane].astype(F32) * here
                b = b32.astype(BF16)
                sides = beta[p, 1 - plane].astype(F32) * here + outer[p].astype(F32) * next_to
                whole = jnp.dot(b, tri, preferred_element_type=F32)
                whole = whole + jnp.dot(tri, b, preferred_element_type=F32)
                whole = whole + u * b32 - 0.125 * sides
                hi = whole.astype(BF16).astype(F32)
                for kind, value in enumerate((b32, hi, whole - hi)):
                    table[pl.ds((kind * count + p) * rows, rows)] = value
            return carry

        lax.fori_loop(0, count // step, fill, 0)

        def use(i, carry):
            totals = []
            for j in range(step):
                r = i * step + j
                weights = table[pl.ds(r, 3 * count, stride=rows)].astype(BF16)
                weights_out[plane, r] = weights
                totals.append(jnp.dot(weights, own[plane, r], preferred_element_type=F32))
            acc[...] += sum(totals[1:], totals[0])
            return carry

        lax.fori_loop(0, rows // step, use, 0)
    out[...] = jnp.zeros_like(out)
    out[0:count] = acc[0:count]
    out[count : 2 * count] = acc[count : 2 * count] + acc[2 * count : 3 * count]
    out[2 * count : 3 * count, 0:count] = gram[...]


def partials(count, atoms, own, beta, b_x, b_d, potential, gram):
    planes, rows, width, orbs = own.shape
    return pl.pallas_call(
        functools.partial(partial_kernel, count),
        out_shape=(
            jax.ShapeDtypeStruct((3 * count, orbs), F32),
            jax.ShapeDtypeStruct((planes, rows, 3 * count, width), BF16),
        ),
        in_specs=[pl.BlockSpec(memory_space=pltpu.SMEM)]
        + [pl.BlockSpec(memory_space=pltpu.VMEM)] * 6,
        out_specs=(pl.BlockSpec(memory_space=pltpu.VMEM),) * 2,
        scratch_shapes=[
            pltpu.VMEM((3 * count * rows, width), F32),
            pltpu.VMEM((3 * count, orbs), F32),
        ],
        compiler_params=params(),
        cost_estimate=cost(4096, 4096),
        name="partials",
    )(atoms, own, beta, b_x, b_d, potential, gram)


def coefficient_kernel(sums, strength, out):
    count, orbs = strength.shape
    coef1 = (strength[...] * sums[0:count]).astype(BF16)
    padded = coef1.astype(F32) * 0.25
    if orbs > count:
        padded = jnp.concatenate([padded, jnp.zeros((orbs - count, orbs), F32)], axis=0)
    proj2 = sums[count : 2 * count] + jnp.dot(
        sums[2 * count : 3 * count],
        padded,
        preferred_element_type=F32,
        precision=lax.Precision.HIGHEST,
    )
    out[0:count] = coef1
    out[count : 2 * count] = (strength[...] * proj2).astype(BF16)


def coefficients(sums, strength):
    count, orbs = strength.shape
    return pl.pallas_call(
        coefficient_kernel,
        out_shape=jax.ShapeDtypeStruct((2 * count, orbs), BF16),
        in_specs=[pl.BlockSpec(memory_space=pltpu.VMEM)] * 2,
        out_specs=pl.BlockSpec(memory_space=pltpu.VMEM),
        compiler_params=params(),
        cost_estimate=cost(4096, 4096),
        name="coefficients",
    )(sums, strength)


def nonlocal_kernel(unroll, a, b, c, d, q, weights, out):
    count, orbs = a.shape[0] // 2, a.shape[1]
    turned = sum(
        jnp.dot(ref[...], q[k], preferred_element_type=F32) for k, ref in enumerate((a, b, c, d))
    )
    turned = turned * 0.25
    one, two = turned[0:count], turned[count : 2 * count]
    right = jnp.concatenate([two, one, one], axis=0)
    hi = right.astype(BF16)
    lo = right - hi.astype(F32)
    right = jnp.concatenate([hi.astype(F32), lo], axis=1).astype(BF16)

    def step(i, carry):
        for k in range(unroll):
            r = i * unroll + k
            for plane in range(weights.shape[0]):
                both = lax.dot_general(
                    weights[plane, r], right, (((0,), (0,)), ((), ())), preferred_element_type=F32
                )
                out[plane, r] = both[:, :orbs] + both[:, orbs:]
        return carry

    lax.fori_loop(0, weights.shape[1] // unroll, step, 0)


def nonlocal_term(shape, coefs, q, weights):
    unroll = max(g for g in (1, 2, 4, 8) if weights.shape[1] % g == 0)
    return pl.pallas_call(
        functools.partial(nonlocal_kernel, unroll),
        out_shape=jax.ShapeDtypeStruct(shape, F32),
        in_specs=[pl.BlockSpec(memory_space=pltpu.VMEM)] * 6,
        out_specs=pl.BlockSpec(memory_space=pltpu.VMEM),
        compiler_params=params(),
        cost_estimate=cost(4096, 4096),
        name="nonlocal",
    )(*coefs, q, weights)


def filter_kernel(slabs, start, parts, joint, *refs):
    own, p_own, zo = refs[:3]
    xrs, zfs = refs[3 : 3 + parts], refs[3 + parts : 3 + 2 * parts]
    extra = 7
    outs, scratch = refs[3 + 2 * parts : -extra], refs[-extra:]
    first, lines, diagonals = scratch[:3]
    place = lax.axis_index("space")
    x = lax.rem(place, 2)
    width = own.shape[2]
    cells = 2 * width
    half = own.shape[1] // 2
    orbs = own.shape[3]
    rows = outs[0].shape[1]
    base = (half - 2) * x
    lower = (place >= 2).astype(F32)
    upper = (place < slabs - 2).astype(F32)
    is_odd = x.astype(F32)
    has_zf = lower * (1.0 - is_odd) + upper * is_odd
    has_zo = upper * (1.0 - is_odd) + lower * is_odd
    xr, zf, pots, sems = scratch[3:]
    window = xr.shape[1] // 2
    early = xrs[0].shape[1] - 1
    copies = []
    for k, (target, pieces) in enumerate(((xr, xrs), (zf, zfs))):
        begin = 0 if parts == 1 else early - 8
        moved = [
            (pieces[0].at[:, pl.ds(early, 1)], pots.at[k]),
            (
                pieces[0].at[:, pl.ds(begin, early - begin)],
                target.at[:, pl.ds(begin, early - begin)],
            ),
        ]
        if parts > 1:
            later = target.shape[1] - early
            moved.append((pieces[1].at[:, pl.ds(0, later)], target.at[:, pl.ds(early, later)]))
        copies += [
            pltpu.make_async_copy(source, goal, sems.at[3 * k + i])
            for i, (source, goal) in enumerate(moved)
        ]
    for copy in copies:
        copy.start()

    def fill(c, block):
        lines[c - 1] = block
        for kind in range(2):
            even, odd = (lines[c - 1, pl.ds(k, half, stride=2)] for k in range(2))
            lanes = slice(64 * kind, 64 * kind + width)
            diagonals[c - 1, kind] = jnp.concatenate([even[:, lanes], odd[:, lanes]], axis=1)

    for c in (2, 3):
        fill(c, potential_block(p_own[(c % 2) ^ x]))
    fill(6, zo[x, zo.shape[1] - 1].astype(F32))
    for copy in copies:
        copy.wait()
    for c in (1, 4, 5):
        fill(c, pots[1 if c < 2 else 0, (c % 2) ^ x, 0].astype(F32))

    here = neighbour_sum(width, True)
    i = lax.broadcasted_iota(jnp.int32, (cells, cells), 0)
    diagonal = i == lax.broadcasted_iota(jnp.int32, (cells, cells), 1)

    def local(c, p):
        at = base // 2 + p
        hi = diagonals[c - 1, 0, pl.ds(at, 1)]
        lo = diagonals[c - 1, 1, pl.ds(at, 1)]
        return (
            jnp.where(diagonal, hi, here).astype(BF16),
            jnp.where(diagonal, lo, 0.0).astype(BF16),
        )

    def rows_of(c, w, n):
        plane = (c % 2) ^ x
        if c in (2, 3):
            return own[plane, pl.ds(base + w, n)]
        ref = zf if c < 2 else (xr if c < 6 else zo)
        return ref[plane, pl.ds(w, n)]

    def applied(pair, outer, zs, matrices):
        near = jnp.dot(matrices[0], pair, preferred_element_type=F32)
        near = near + jnp.dot(matrices[1], pair, preferred_element_type=F32)
        return near - 0.125 * (outer + zs)

    def step1(j, carry):
        p = start // 2 + x + j - 1
        q = jnp.clip(p, 0, window - 1)
        has_below = inside(p - 1, window)
        has_above = inside(p + 1, window)
        valid = inside(p, window)
        below = jnp.maximum(2 * q - 1, 0)
        above = jnp.minimum(2 * q + 2, 2 * window - 1)
        pair = [rows_of(c, 2 * q, 2).reshape(cells, orbs) for c in range(8)]
        vs = [v.astype(F32) for v in pair]
        for c in range(1, 7):
            outer = jnp.concatenate(
                [
                    rows_of(c, below, 1)[0].astype(F32) * has_below,
                    rows_of(c, above, 1)[0].astype(F32) * has_above,
                ],
                axis=0,
            )
            f = applied(pair[c], outer, vs[c - 1] + vs[c + 1], local(c, q))
            keep = valid
            if c == 1:
                keep = valid * has_zf
            if c == 6:
                keep = valid * has_zo
            first[c - 1, pl.ds(2 * j, 2)] = (f * keep).astype(BF16).reshape(2, width, orbs)
        return carry

    lax.fori_loop(0, rows // 2 + 2, step1, 0)

    def step2(j, carry):
        p = start // 2 + x + j
        pair = [first[c - 1, pl.ds(2 * j + 2, 2)].reshape(cells, orbs) for c in range(1, 7)]
        vs = [v.astype(F32) for v in pair]
        for c in range(2, 6):
            outer = jnp.concatenate(
                [first[c - 1, 2 * j + 1].astype(F32), first[c - 1, 2 * j + 4].astype(F32)], axis=0
            )
            f = applied(pair[c - 1], outer, vs[c - 2] + vs[c], local(c, p))
            f = f.astype(BF16).reshape(2, width, orbs)
            plane = (c % 2) ^ x
            if joint:
                outs[0][plane + (2 if c in (2, 3) else 0), pl.ds(2 * j, 2)] = f
            else:
                outs[1 if c in (2, 3) else 0][plane, pl.ds(2 * j, 2)] = f
        return carry

    lax.fori_loop(0, rows // 2, step2, 0)


def filtered(slabs, start, rows, joint, operands, xrs, zfs):
    own = operands[0]
    planes, _, width, orbs = own.shape
    parts = len(xrs)
    shape = (2 * planes if joint else planes, rows, width, orbs)
    out = (jax.ShapeDtypeStruct(shape, BF16),) * (1 if joint else 2)
    cells = 10 * rows * width
    scratch = [
        pltpu.VMEM((6, rows + 4, width, orbs), BF16),
        pltpu.VMEM((6, width, orbs), F32),
        pltpu.VMEM((6, 2, own.shape[1] // 2, 2 * width), F32),
    ]
    window = own.shape[1] // 2 + 2 if parts > 1 else xrs[0].shape[1] - 1
    scratch += [pltpu.VMEM((planes, window, width, orbs), BF16)] * 2
    scratch += [pltpu.VMEM((2, planes, 1, width, orbs), BF16), pltpu.SemaphoreType.DMA((6,))]
    local = pl.BlockSpec(memory_space=pltpu.VMEM)
    distant = pl.BlockSpec(memory_space=pltpu.MemorySpace.HBM)
    xrs, zfs = (
        [pltpu.with_memory_space_constraint(piece, pltpu.MemorySpace.HBM) for piece in pieces]
        for pieces in (xrs, zfs)
    )
    return pl.pallas_call(
        functools.partial(filter_kernel, slabs, start, parts, joint),
        out_shape=out,
        in_specs=[local] * len(operands) + [distant] * (2 * parts),
        out_specs=(local,) * len(out),
        scratch_shapes=scratch,
        compiler_params=params(),
        cost_estimate=cost(2 * cells * 32 * orbs, FILTER * cells * orbs * 4),
        name="filtered",
    )(*operands, *xrs, *zfs)


def rotate_kernel(group, *refs):
    a, b, c, d, q = refs[:5]
    outs = refs[5:]
    _, rows, width, orbs = a.shape
    planes = outs[0].shape[0]
    low = jnp.concatenate([q[0], q[1]], axis=0)
    high = jnp.concatenate([q[2], q[3]], axis=0)

    def one(j, carry):
        for plane in range(a.shape[0]):
            def take(ref):
                return ref[plane, pl.ds(group * j, group)].reshape(group * width, orbs)

            total = jnp.dot(
                jnp.concatenate([take(a), take(b)], axis=1), low, preferred_element_type=F32
            )
            total = total + jnp.dot(
                jnp.concatenate([take(c), take(d)], axis=1), high, preferred_element_type=F32
            )
            outs[plane // planes][plane % planes, pl.ds(group * j, group)] = total.astype(
                BF16
            ).reshape(group, width, orbs)
        return carry

    lax.fori_loop(0, rows // group, one, 0)


def rotated(blocks, q, pieces):
    a = blocks[0]
    size = a.size
    group = max(g for g in range(1, 9) if a.shape[1] % g == 0)
    out = jax.ShapeDtypeStruct((a.shape[0] // pieces, *a.shape[1:]), BF16)
    return pl.pallas_call(
        functools.partial(rotate_kernel, group),
        out_shape=(out,) * pieces,
        in_specs=[pl.BlockSpec(memory_space=pltpu.VMEM)] * 5,
        out_specs=(pl.BlockSpec(memory_space=pltpu.VMEM),) * pieces,
        compiler_params=params(),
        cost_estimate=cost(8 * size * a.shape[3], 10 * size),
        name="rotated",
    )(*blocks, q)


def assemble_kernel(group, term, keep1, got1, got2, a, b, c, d, q, out):
    half = term.shape[1] // 2
    width, orbs = term.shape[2:]
    x = lax.rem(lax.axis_index("space"), 2)
    rows1, rows2 = keep1.shape[1], got2.shape[1]
    for ref, at in (
        (keep1, half * x),
        (got1, half * (1 - x)),
        (got2, half * (1 - x) + rows1),
    ):
        where = pl.ds(at, ref.shape[1])
        out[:, where] = (ref[...].astype(F32) + term[:, where]).astype(BF16)
    low = jnp.concatenate([q[0], q[1]], axis=0)
    high = jnp.concatenate([q[2], q[3]], axis=0)

    def one(j, carry):
        where = pl.ds(half * x + rows1 + group * j, group)
        for plane in range(a.shape[0]):
            def take(ref):
                return ref[plane, pl.ds(group * j, group)].reshape(group * width, orbs)

            total = jnp.dot(
                jnp.concatenate([take(a), take(b)], axis=1), low, preferred_element_type=F32
            )
            total = total + jnp.dot(
                jnp.concatenate([take(c), take(d)], axis=1), high, preferred_element_type=F32
            )
            total = total.reshape(group, width, orbs) + term[plane, where]
            out[plane, where] = total.astype(BF16)
        return carry

    lax.fori_loop(0, rows2 // group, one, 0)


def assembled(term, keep1, got1, got2, blocks, q):
    group = max(g for g in range(1, 9) if got2.shape[1] % g == 0)
    return pl.pallas_call(
        functools.partial(assemble_kernel, group),
        out_shape=jax.ShapeDtypeStruct(term.shape, BF16),
        in_specs=[pl.BlockSpec(memory_space=pltpu.VMEM)] * 9,
        out_specs=pl.BlockSpec(memory_space=pltpu.VMEM),
        compiler_params=params(),
        cost_estimate=cost(4096, 4096),
        name="assembled",
    )(term, keep1, got1, got2, *blocks, q)


def ordered(*arrays):
    return lax.optimization_barrier(arrays)


def shards(psi, potential, beta, strength, atom_slab, pattern, q_tiles):
    planes, width_x, width_y, orbs = psi.shape
    count = beta.shape[0]
    slabs = lax.axis_size("space")
    place = lax.axis_index("space")
    x = lax.rem(place, 2)
    half = width_x // 2
    window = half + 2
    rows1 = half * 7 // 24 * 2
    rows2 = half - rows1
    early = rows1 + 4

    def within(pairs):
        return [(i, j) for i, j in pairs if 0 <= j < slabs]

    swap = [(i, i ^ 1) for i in range(slabs)]
    own_way = within([(i, i + 2 if i % 2 else i - 2) for i in range(slabs)])
    other_way = within([(i, i - 2 if i % 2 else i + 2) for i in range(slabs)])
    groups = lax.axis_size("orb")
    across = [(i, i ^ 2) for i in range(groups)]
    beside = [(i, i ^ 1) for i in range(groups)]
    mine = (half - 2) * x
    theirs = (half - 2) * (1 - x)

    to_x, to_z = prepared(psi, potential, early)
    to_x2, far, near = packed(psi, beta, early)
    f_x = lax.ppermute(near, "space", swap)
    raster = within([(i, i + 1 if i % 2 else i - 1) for i in range(slabs)])
    f_d = lax.ppermute(far, "space", raster)
    xr1 = lax.ppermute(to_x, "space", swap)
    zo = lax.ppermute(to_z, "space", own_way)
    active = jnp.abs(place - atom_slab) <= 1
    beta_m = jnp.where(active[:, None, None, None], beta, jnp.zeros_like(beta))
    gram = jnp.einsum("pzxy,qzxy->pq", beta_m, beta_m, preferred_element_type=F32)
    xr1, second = ordered(xr1, to_x2)
    zf1 = lax.ppermute(xr1, "space", other_way)
    xr2 = lax.ppermute(second, "space", swap)
    zf2 = lax.ppermute(xr2, "space", other_way)
    strong = jnp.broadcast_to(strength[:, None], (count, orbs))

    sums, weights = partials(count, atom_slab, psi, beta, f_x, f_d, potential, gram)
    zf1, sums, _ = ordered(zf1, sums, xr2)
    operands = (psi, potential, zo)
    (block1,) = filtered(slabs, 0, rows1, True, operands, (xr1,), (zf1,))
    y1 = lax.ppermute(block1, "orb", across)
    rounds = [1 << k for k in range((slabs - 1).bit_length())]

    def added(values, step):
        pairs = [(i, i ^ step) for i in range(slabs)]
        return values + lax.ppermute(values, "space", pairs)

    for step in rounds[:1]:
        sums = added(sums, step)
    zf2, sums = ordered(zf2, sums)
    give2, keep2 = filtered(slabs, rows1, rows2, False, operands, (xr1, xr2), (zf1, zf2))
    pattern, q_tiles, _ = ordered(pattern, q_tiles, give2)
    me = lax.axis_index("orb")
    which = jnp.bitwise_xor(me, jnp.arange(groups, dtype=jnp.int32))
    rows_hot = (pattern[:, 0][:, None] == which[None, :]).astype(BF16)
    rows_hot = rows_hot * (pattern[:, 1] == me).astype(BF16)[:, None]
    q = jnp.einsum("ki,kab->iab", rows_hot, q_tiles, preferred_element_type=F32).astype(BF16)
    cg = lax.ppermute(give2, "orb", beside)
    ck = lax.ppermute(keep2, "orb", beside)
    yg = lax.ppermute(give2, "orb", across)
    for step in rounds[1:2]:
        sums = added(sums, step)
    y1, again, _, sums = ordered(y1, block1, give2, sums)
    c1 = lax.ppermute(again, "orb", beside)
    yc1 = lax.ppermute(y1, "orb", beside)
    for step in rounds[2:]:
        sums = added(sums, step)
    yc1, sums = ordered(yc1, sums)
    give1, keep1 = rotated((block1, c1, y1, yc1), q, 2)
    got1 = lax.ppermute(give1, "space", swap)
    keep_y, yg, _, sums = ordered(keep2, yg, give1, sums)
    yk = lax.ppermute(keep_y, "orb", across)
    ycg = lax.ppermute(yg, "orb", beside)
    coefs = coefficients(sums, strong)
    coefs = jnp.concatenate([coefs, lax.ppermute(coefs, "orb", beside)], axis=0)
    ycg, coefs = ordered(ycg, coefs)
    (give2,) = rotated((give2, cg, yg, ycg), q, 1)
    got2 = lax.ppermute(give2, "space", swap)
    coefs, _ = ordered(coefs, give2)
    coefs_y = lax.ppermute(coefs, "orb", across)
    coefs = [half_of[k * 2 * count : (k + 1) * 2 * count] for half_of in (coefs, coefs_y) for k in (0, 1)]
    term = nonlocal_term(psi.shape, coefs, q, weights)
    yk, _, got1 = ordered(yk, give2, got1)
    yck = lax.ppermute(yk, "orb", beside)
    return assembled(term, keep1, got1, got2, (keep2, ck, yk, yck), q)


def solution(mesh):
    placed = (
        P("space", None, None, "orb"),
        P("space", None, None),
        P(None, "space", None, None),
        P(),
        P(),
        P(),
        P(),
    )
    return jax.shard_map(
        shards, mesh=mesh, in_specs=placed, out_specs=P("space", None, None, "orb"), check_vma=False
    )
```

```python
import functools

import jax
import jax.numpy as jnp
from jax import lax
from jax.experimental import pallas as pl
from jax.experimental.pallas import tpu as pltpu
from jax.sharding import PartitionSpec as P

F32 = jnp.float32
BF16 = jnp.bfloat16
VMEM_LIMIT = 24 * 1024 * 1024
SHRINK = 16
FILTER = 100


def params():
    return pltpu.CompilerParams(vmem_limit_bytes=VMEM_LIMIT)


def cost(flops, moved):
    return pl.CostEstimate(flops=flops // SHRINK, bytes_accessed=moved // SHRINK, transcendentals=0)


def inside(p, window):
    return jnp.logical_and(p >= 0, p < window).astype(F32)


def neighbour_sum(width, pairs):
    n = (2 if pairs else 1) * width
    i = lax.broadcasted_iota(jnp.int32, (n, n), 0)
    j = lax.broadcasted_iota(jnp.int32, (n, n), 1)
    linked = jnp.abs(i - j) == 1
    if pairs:
        linked = jnp.logical_and(linked, (i < width) == (j < width))
        linked = jnp.logical_or(linked, jnp.abs(i - j) == width)
    return jnp.where(linked, -0.125, 0.0)


def potential_block(potential):
    lines, width = potential.shape
    gap = jnp.zeros((lines, 64 - width), F32)
    u = (potential - 1.0) * 0.25
    hi = u.astype(BF16).astype(F32)
    return jnp.concatenate([hi, gap, u - hi, gap], axis=1)


def prepare_kernel(early, psi, potential_far, to_x, to_z, potential, sems):
    x = lax.rem(lax.axis_index("space"), 2)
    half = psi.shape[1] // 2
    window = half + 2
    mine, theirs = (half - 2) * x, (half - 2) * (1 - x)
    fetch = pltpu.make_async_copy(potential_far, potential, sems.at[0])
    fetch.start()
    copies = [
        pltpu.make_async_copy(
            psi.at[:, pl.ds(theirs, early)], to_x.at[:, pl.ds(0, early)], sems.at[1]
        ),
        pltpu.make_async_copy(
            psi.at[:, pl.ds(mine, window)], to_z.at[:, pl.ds(0, window)], sems.at[2]
        ),
    ]
    for copy in copies:
        copy.start()
    fetch.wait()
    for plane in range(potential.shape[0]):
        block = potential_block(potential[plane]).astype(BF16)
        to_x[plane, early] = block
        to_z[plane, window] = block
    for copy in copies:
        copy.wait()


def prepared(psi, potential, early):
    planes, width_x, width_y, orbs = psi.shape
    window = width_x // 2 + 2

    def out(rows):
        return jax.ShapeDtypeStruct((planes, rows, width_y, orbs), BF16)

    return pl.pallas_call(
        functools.partial(prepare_kernel, early),
        out_shape=(out(early + 1), out(window + 1)),
        in_specs=[pl.BlockSpec(memory_space=pltpu.MemorySpace.HBM)] * 2,
        out_specs=(pl.BlockSpec(memory_space=pltpu.VMEM),) * 2,
        scratch_shapes=[pltpu.VMEM(potential.shape, F32), pltpu.SemaphoreType.DMA((3,))],
        compiler_params=params(),
        cost_estimate=cost(4096, 4096),
        name="prepared",
    )(*(pltpu.with_memory_space_constraint(a, pltpu.MemorySpace.HBM) for a in (psi, potential)))


def pack_kernel(early, psi, beta, to_x2, far, near, sem):
    x = lax.rem(lax.axis_index("space"), 2)
    half = psi.shape[1] // 2
    later = half + 2 - early
    copy = pltpu.make_async_copy(
        psi.at[:, pl.ds((half - 2) * (1 - x) + early, later)], to_x2, sem
    )
    copy.start()
    far[...] = beta[:, x]
    near[...] = beta[:, 1 - x]
    copy.wait()


def packed(psi, beta, early):
    planes, width_x, width_y, orbs = psi.shape
    side = jax.ShapeDtypeStruct((beta.shape[0], *beta.shape[2:]), BF16)
    later = width_x // 2 + 2 - early
    return pl.pallas_call(
        functools.partial(pack_kernel, early),
        out_shape=(jax.ShapeDtypeStruct((planes, later, width_y, orbs), BF16), side, side),
        in_specs=[
            pl.BlockSpec(memory_space=pltpu.MemorySpace.HBM),
            pl.BlockSpec(memory_space=pltpu.VMEM),
        ],
        out_specs=(pl.BlockSpec(memory_space=pltpu.VMEM),) * 3,
        scratch_shapes=[pltpu.SemaphoreType.DMA],
        compiler_params=params(),
        cost_estimate=cost(4096, 4096),
        name="packed",
    )(pltpu.with_memory_space_constraint(psi, pltpu.MemorySpace.HBM), beta)


def partial_kernel(count, atoms, own, beta, b_x, b_d, potential, gram, out, weights_out, table, acc):
    place = lax.axis_index("space")
    x = lax.rem(place, 2)
    rows, width = potential.shape[1:]
    side = place ^ 1
    beyond = place - 1 + 2 * x
    tri = neighbour_sum(width, False).astype(BF16)
    acc[...] = jnp.zeros_like(acc)
    step = 8

    for k in range(2):
        plane = x if k == 0 else 1 - x
        outer, there = (b_d, beyond) if k == 0 else (b_x, side)
        u = (potential[plane] - 1.0) * 0.25

        def fill(i, carry):
            for j in range(step):
                p = i * step + j
                here = (jnp.abs(place - atoms[p]) <= 1).astype(F32)
                next_to = (jnp.abs(there - atoms[p]) <= 1).astype(F32)
                b32 = beta[p, plane].astype(F32) * here
                b = b32.astype(BF16)
                sides = beta[p, 1 - plane].astype(F32) * here + outer[p].astype(F32) * next_to
                whole = jnp.dot(b, tri, preferred_element_type=F32)
                whole = whole + jnp.dot(tri, b, preferred_element_type=F32)
                whole = whole + u * b32 - 0.125 * sides
                hi = whole.astype(BF16).astype(F32)
                for kind, value in enumerate((b32, hi, whole - hi)):
                    table[pl.ds((kind * count + p) * rows, rows)] = value
            return carry

        lax.fori_loop(0, count // step, fill, 0)

        def use(i, carry):
            totals = []
            for j in range(step):
                r = i * step + j
                weights = table[pl.ds(r, 3 * count, stride=rows)].astype(BF16)
                weights_out[plane, r] = weights
                totals.append(jnp.dot(weights, own[plane, r], preferred_element_type=F32))
            acc[...] += sum(totals[1:], totals[0])
            return carry

        lax.fori_loop(0, rows // step, use, 0)
    out[...] = jnp.zeros_like(out)
    out[0:count] = acc[0:count]
    out[count : 2 * count] = acc[count : 2 * count] + acc[2 * count : 3 * count]
    out[2 * count : 3 * count, 0:count] = gram[...]


def partials(count, atoms, own, beta, b_x, b_d, potential, gram):
    planes, rows, width, orbs = own.shape
    return pl.pallas_call(
        functools.partial(partial_kernel, count),
        out_shape=(
            jax.ShapeDtypeStruct((3 * count, orbs), F32),
            jax.ShapeDtypeStruct((planes, rows, 3 * count, width), BF16),
        ),
        in_specs=[pl.BlockSpec(memory_space=pltpu.SMEM)]
        + [pl.BlockSpec(memory_space=pltpu.VMEM)] * 6,
        out_specs=(pl.BlockSpec(memory_space=pltpu.VMEM),) * 2,
        scratch_shapes=[
            pltpu.VMEM((3 * count * rows, width), F32),
            pltpu.VMEM((3 * count, orbs), F32),
        ],
        compiler_params=params(),
        cost_estimate=cost(4096, 4096),
        name="partials",
    )(atoms, own, beta, b_x, b_d, potential, gram)


def coefficient_kernel(sums, strength, out):
    count, orbs = strength.shape
    coef1 = (strength[...] * sums[0:count]).astype(BF16)
    padded = coef1.astype(F32) * 0.25
    if orbs > count:
        padded = jnp.concatenate([padded, jnp.zeros((orbs - count, orbs), F32)], axis=0)
    proj2 = sums[count : 2 * count] + jnp.dot(
        sums[2 * count : 3 * count],
        padded,
        preferred_element_type=F32,
        precision=lax.Precision.HIGHEST,
    )
    out[0:count] = coef1
    out[count : 2 * count] = (strength[...] * proj2).astype(BF16)


def coefficients(sums, strength):
    count, orbs = strength.shape
    return pl.pallas_call(
        coefficient_kernel,
        out_shape=jax.ShapeDtypeStruct((2 * count, orbs), BF16),
        in_specs=[pl.BlockSpec(memory_space=pltpu.VMEM)] * 2,
        out_specs=pl.BlockSpec(memory_space=pltpu.VMEM),
        compiler_params=params(),
        cost_estimate=cost(4096, 4096),
        name="coefficients",
    )(sums, strength)


def nonlocal_kernel(unroll, a, b, c, d, q, weights, out):
    count, orbs = a.shape[0] // 2, a.shape[1]
    turned = sum(
        jnp.dot(ref[...], q[k], preferred_element_type=F32) for k, ref in enumerate((a, b, c, d))
    )
    turned = turned * 0.25
    one, two = turned[0:count], turned[count : 2 * count]
    right = jnp.concatenate([two, one, one], axis=0)
    hi = right.astype(BF16)
    lo = right - hi.astype(F32)
    right = jnp.concatenate([hi.astype(F32), lo], axis=1).astype(BF16)

    def step(i, carry):
        for k in range(unroll):
            r = i * unroll + k
            for plane in range(weights.shape[0]):
                both = lax.dot_general(
                    weights[plane, r], right, (((0,), (0,)), ((), ())), preferred_element_type=F32
                )
                out[plane, r] = both[:, :orbs] + both[:, orbs:]
        return carry

    lax.fori_loop(0, weights.shape[1] // unroll, step, 0)


def nonlocal_term(shape, coefs, q, weights):
    unroll = max(g for g in (1, 2, 4, 8) if weights.shape[1] % g == 0)
    return pl.pallas_call(
        functools.partial(nonlocal_kernel, unroll),
        out_shape=jax.ShapeDtypeStruct(shape, F32),
        in_specs=[pl.BlockSpec(memory_space=pltpu.VMEM)] * 6,
        out_specs=pl.BlockSpec(memory_space=pltpu.VMEM),
        compiler_params=params(),
        cost_estimate=cost(4096, 4096),
        name="nonlocal",
    )(*coefs, q, weights)


def filter_kernel(slabs, start, parts, joint, *refs):
    own, p_own, zo = refs[:3]
    xrs, zfs = refs[3 : 3 + parts], refs[3 + parts : 3 + 2 * parts]
    extra = 7
    outs, scratch = refs[3 + 2 * parts : -extra], refs[-extra:]
    first, lines, diagonals = scratch[:3]
    place = lax.axis_index("space")
    x = lax.rem(place, 2)
    width = own.shape[2]
    cells = 2 * width
    half = own.shape[1] // 2
    orbs = own.shape[3]
    rows = outs[0].shape[1]
    base = (half - 2) * x
    lower = (place >= 2).astype(F32)
    upper = (place < slabs - 2).astype(F32)
    is_odd = x.astype(F32)
    has_zf = lower * (1.0 - is_odd) + upper * is_odd
    has_zo = upper * (1.0 - is_odd) + lower * is_odd
    xr, zf, pots, sems = scratch[3:]
    window = xr.shape[1] // 2
    early = xrs[0].shape[1] - 1
    copies = []
    for k, (target, pieces) in enumerate(((xr, xrs), (zf, zfs))):
        if parts == 1 and k == 1:
            zf = pieces[0]
            continue
        begin = 0 if parts == 1 else early - 8
        moved = [
            (pieces[0].at[:, pl.ds(early, 1)], pots.at[k]),
            (
                pieces[0].at[:, pl.ds(begin, early - begin)],
                target.at[:, pl.ds(begin, early - begin)],
            ),
        ]
        if parts > 1:
            later = target.shape[1] - early
            moved.append((pieces[1].at[:, pl.ds(0, later)], target.at[:, pl.ds(early, later)]))
        copies += [
            pltpu.make_async_copy(source, goal, sems.at[3 * k + i])
            for i, (source, goal) in enumerate(moved)
        ]
    for copy in copies:
        copy.start()

    def fill(c, block):
        lines[c - 1] = block
        for kind in range(2):
            even, odd = (lines[c - 1, pl.ds(k, half, stride=2)] for k in range(2))
            lanes = slice(64 * kind, 64 * kind + width)
            diagonals[c - 1, kind] = jnp.concatenate([even[:, lanes], odd[:, lanes]], axis=1)

    for c in (2, 3):
        fill(c, potential_block(p_own[(c % 2) ^ x]))
    fill(6, zo[x, zo.shape[1] - 1].astype(F32))
    for copy in copies:
        copy.wait()
    for c in (1, 4, 5):
        if parts == 1 and c == 1:
            fill(c, zf[(c % 2) ^ x, early].astype(F32))
        else:
            fill(c, pots[1 if c < 2 else 0, (c % 2) ^ x, 0].astype(F32))

    here = neighbour_sum(width, True)
    i = lax.broadcasted_iota(jnp.int32, (cells, cells), 0)
    diagonal = i == lax.broadcasted_iota(jnp.int32, (cells, cells), 1)

    def local(c, p):
        at = base // 2 + p
        hi = diagonals[c - 1, 0, pl.ds(at, 1)]
        lo = diagonals[c - 1, 1, pl.ds(at, 1)]
        return (
            jnp.where(diagonal, hi, here).astype(BF16),
            jnp.where(diagonal, lo, 0.0).astype(BF16),
        )

    def rows_of(c, w, n):
        plane = (c % 2) ^ x
        if c in (2, 3):
            return own[plane, pl.ds(base + w, n)]
        ref = zf if c < 2 else (xr if c < 6 else zo)
        return ref[plane, pl.ds(w, n)]

    def applied(pair, outer, zs, matrices):
        near = jnp.dot(matrices[0], pair, preferred_element_type=F32)
        near = near + jnp.dot(matrices[1], pair, preferred_element_type=F32)
        return near - 0.125 * (outer + zs)

    def step1(j, carry):
        p = start // 2 + x + j - 1
        q = jnp.clip(p, 0, window - 1)
        has_below = inside(p - 1, window)
        has_above = inside(p + 1, window)
        valid = inside(p, window)
        below = jnp.maximum(2 * q - 1, 0)
        above = jnp.minimum(2 * q + 2, 2 * window - 1)
        pair = [rows_of(c, 2 * q, 2).reshape(cells, orbs) for c in range(8)]
        vs = [v.astype(F32) for v in pair]
        for c in range(1, 7):
            outer = jnp.concatenate(
                [
                    rows_of(c, below, 1)[0].astype(F32) * has_below,
                    rows_of(c, above, 1)[0].astype(F32) * has_above,
                ],
                axis=0,
            )
            f = applied(pair[c], outer, vs[c - 1] + vs[c + 1], local(c, q))
            keep = valid
            if c == 1:
                keep = valid * has_zf
            if c == 6:
                keep = valid * has_zo
            first[c - 1, pl.ds(2 * j, 2)] = (f * keep).astype(BF16).reshape(2, width, orbs)
        return carry

    lax.fori_loop(0, rows // 2 + 2, step1, 0)

    def step2(j, carry):
        p = start // 2 + x + j
        pair = [first[c - 1, pl.ds(2 * j + 2, 2)].reshape(cells, orbs) for c in range(1, 7)]
        vs = [v.astype(F32) for v in pair]
        for c in range(2, 6):
            outer = jnp.concatenate(
                [first[c - 1, 2 * j + 1].astype(F32), first[c - 1, 2 * j + 4].astype(F32)], axis=0
            )
            f = applied(pair[c - 1], outer, vs[c - 2] + vs[c], local(c, p))
            f = f.astype(BF16).reshape(2, width, orbs)
            plane = (c % 2) ^ x
            if joint:
                outs[0][plane + (2 if c in (2, 3) else 0), pl.ds(2 * j, 2)] = f
            else:
                outs[1 if c in (2, 3) else 0][plane, pl.ds(2 * j, 2)] = f
        return carry

    lax.fori_loop(0, rows // 2, step2, 0)


def filtered(slabs, start, rows, joint, operands, xrs, zfs):
    own = operands[0]
    planes, _, width, orbs = own.shape
    parts = len(xrs)
    shape = (2 * planes if joint else planes, rows, width, orbs)
    out = (jax.ShapeDtypeStruct(shape, BF16),) * (1 if joint else 2)
    cells = 10 * rows * width
    scratch = [
        pltpu.VMEM((6, rows + 4, width, orbs), BF16),
        pltpu.VMEM((6, width, orbs), F32),
        pltpu.VMEM((6, 2, own.shape[1] // 2, 2 * width), F32),
    ]
    window = own.shape[1] // 2 + 2 if parts > 1 else xrs[0].shape[1] - 1
    scratch += [pltpu.VMEM((planes, window, width, orbs), BF16)] * 2
    scratch += [pltpu.VMEM((2, planes, 1, width, orbs), BF16), pltpu.SemaphoreType.DMA((6,))]
    local = pl.BlockSpec(memory_space=pltpu.VMEM)
    distant = pl.BlockSpec(memory_space=pltpu.MemorySpace.HBM)
    far_xr = [pltpu.with_memory_space_constraint(a, pltpu.MemorySpace.HBM) for a in xrs]
    far_zf = [pltpu.with_memory_space_constraint(a, pltpu.MemorySpace.HBM) for a in zfs]
    xrs, zfs = far_xr, (far_zf if parts > 1 else zfs)
    return pl.pallas_call(
        functools.partial(filter_kernel, slabs, start, parts, joint),
        out_shape=out,
        in_specs=[local] * len(operands)
        + [distant] * parts
        + [distant if parts > 1 else local] * parts,
        out_specs=(local,) * len(out),
        scratch_shapes=scratch,
        compiler_params=params(),
        cost_estimate=cost(2 * cells * 32 * orbs, FILTER * cells * orbs * 4),
        name="filtered",
    )(*operands, *xrs, *zfs)


def rotate_kernel(group, *refs):
    a, b, c, d, q = refs[:5]
    outs = refs[5:]
    _, rows, width, orbs = a.shape
    planes = outs[0].shape[0]
    low = jnp.concatenate([q[0], q[1]], axis=0)
    high = jnp.concatenate([q[2], q[3]], axis=0)

    def one(j, carry):
        for plane in range(a.shape[0]):
            def take(ref):
                return ref[plane, pl.ds(group * j, group)].reshape(group * width, orbs)

            total = jnp.dot(
                jnp.concatenate([take(a), take(b)], axis=1), low, preferred_element_type=F32
            )
            total = total + jnp.dot(
                jnp.concatenate([take(c), take(d)], axis=1), high, preferred_element_type=F32
            )
            outs[plane // planes][plane % planes, pl.ds(group * j, group)] = total.astype(
                BF16
            ).reshape(group, width, orbs)
        return carry

    lax.fori_loop(0, rows // group, one, 0)


def rotated(blocks, q, pieces):
    a = blocks[0]
    size = a.size
    group = max(g for g in range(1, 9) if a.shape[1] % g == 0)
    out = jax.ShapeDtypeStruct((a.shape[0] // pieces, *a.shape[1:]), BF16)
    return pl.pallas_call(
        functools.partial(rotate_kernel, group),
        out_shape=(out,) * pieces,
        in_specs=[pl.BlockSpec(memory_space=pltpu.VMEM)] * 5,
        out_specs=(pl.BlockSpec(memory_space=pltpu.VMEM),) * pieces,
        compiler_params=params(),
        cost_estimate=cost(8 * size * a.shape[3], 10 * size),
        name="rotated",
    )(*blocks, q)


def assemble_kernel(group, term, keep1, got1, got2, a, b, c, d, q, out):
    half = term.shape[1] // 2
    width, orbs = term.shape[2:]
    x = lax.rem(lax.axis_index("space"), 2)
    rows1, rows2 = keep1.shape[1], got2.shape[1]
    for ref, at in (
        (keep1, half * x),
        (got1, half * (1 - x)),
        (got2, half * (1 - x) + rows1),
    ):
        where = pl.ds(at, ref.shape[1])
        out[:, where] = (ref[...].astype(F32) + term[:, where]).astype(BF16)
    low = jnp.concatenate([q[0], q[1]], axis=0)
    high = jnp.concatenate([q[2], q[3]], axis=0)

    def one(j, carry):
        where = pl.ds(half * x + rows1 + group * j, group)
        for plane in range(a.shape[0]):
            def take(ref):
                return ref[plane, pl.ds(group * j, group)].reshape(group * width, orbs)

            total = jnp.dot(
                jnp.concatenate([take(a), take(b)], axis=1), low, preferred_element_type=F32
            )
            total = total + jnp.dot(
                jnp.concatenate([take(c), take(d)], axis=1), high, preferred_element_type=F32
            )
            total = total.reshape(group, width, orbs) + term[plane, where]
            out[plane, where] = total.astype(BF16)
        return carry

    lax.fori_loop(0, rows2 // group, one, 0)


def assembled(term, keep1, got1, got2, blocks, q):
    group = max(g for g in range(1, 9) if got2.shape[1] % g == 0)
    return pl.pallas_call(
        functools.partial(assemble_kernel, group),
        out_shape=jax.ShapeDtypeStruct(term.shape, BF16),
        in_specs=[pl.BlockSpec(memory_space=pltpu.VMEM)] * 9,
        out_specs=pl.BlockSpec(memory_space=pltpu.VMEM),
        compiler_params=params(),
        cost_estimate=cost(4096, 4096),
        name="assembled",
    )(term, keep1, got1, got2, *blocks, q)


def ordered(*arrays):
    return lax.optimization_barrier(arrays)


def shards(psi, potential, beta, strength, atom_slab, pattern, q_tiles):
    planes, width_x, width_y, orbs = psi.shape
    count = beta.shape[0]
    slabs = lax.axis_size("space")
    place = lax.axis_index("space")
    x = lax.rem(place, 2)
    half = width_x // 2
    window = half + 2
    rows1 = half // 4 * 2
    rows2 = half - rows1
    early = rows1 + 4

    def within(pairs):
        return [(i, j) for i, j in pairs if 0 <= j < slabs]

    swap = [(i, i ^ 1) for i in range(slabs)]
    own_way = within([(i, i + 2 if i % 2 else i - 2) for i in range(slabs)])
    other_way = within([(i, i - 2 if i % 2 else i + 2) for i in range(slabs)])
    groups = lax.axis_size("orb")
    across = [(i, i ^ 2) for i in range(groups)]
    beside = [(i, i ^ 1) for i in range(groups)]
    mine = (half - 2) * x
    theirs = (half - 2) * (1 - x)

    to_x, to_z = prepared(psi, potential, early)
    to_x2, far, near = packed(psi, beta, early)
    f_x = lax.ppermute(near, "space", swap)
    raster = within([(i, i + 1 if i % 2 else i - 1) for i in range(slabs)])
    f_d = lax.ppermute(far, "space", raster)
    xr1 = lax.ppermute(to_x, "space", swap)
    zo = lax.ppermute(to_z, "space", own_way)
    active = jnp.abs(place - atom_slab) <= 1
    beta_m = jnp.where(active[:, None, None, None], beta, jnp.zeros_like(beta))
    gram = jnp.einsum("pzxy,qzxy->pq", beta_m, beta_m, preferred_element_type=F32)
    xr1, second = ordered(xr1, to_x2)
    zf1 = lax.ppermute(xr1, "space", other_way)
    xr2 = lax.ppermute(second, "space", swap)
    zf2 = lax.ppermute(xr2, "space", other_way)
    strong = jnp.broadcast_to(strength[:, None], (count, orbs))

    sums, weights = partials(count, atom_slab, psi, beta, f_x, f_d, potential, gram)
    zf1, sums, _ = ordered(zf1, sums, xr2)
    operands = (psi, potential, zo)
    (block1,) = filtered(slabs, 0, rows1, True, operands, (xr1,), (zf1,))
    y1 = lax.ppermute(block1, "orb", across)
    rounds = [1 << k for k in range((slabs - 1).bit_length())]

    def added(values, step):
        pairs = [(i, i ^ step) for i in range(slabs)]
        return values + lax.ppermute(values, "space", pairs)

    for step in rounds[:1]:
        sums = added(sums, step)
    zf2, sums = ordered(zf2, sums)
    give2, keep2 = filtered(slabs, rows1, rows2, False, operands, (xr1, xr2), (zf1, zf2))
    pattern, q_tiles, _ = ordered(pattern, q_tiles, give2)
    me = lax.axis_index("orb")
    which = jnp.bitwise_xor(me, jnp.arange(groups, dtype=jnp.int32))
    rows_hot = (pattern[:, 0][:, None] == which[None, :]).astype(BF16)
    rows_hot = rows_hot * (pattern[:, 1] == me).astype(BF16)[:, None]
    q = jnp.einsum("ki,kab->iab", rows_hot, q_tiles, preferred_element_type=F32).astype(BF16)
    cg = lax.ppermute(give2, "orb", beside)
    ck = lax.ppermute(keep2, "orb", beside)
    yg = lax.ppermute(give2, "orb", across)
    for step in rounds[1:2]:
        sums = added(sums, step)
    y1, again, _, sums = ordered(y1, block1, give2, sums)
    c1 = lax.ppermute(again, "orb", beside)
    yc1 = lax.ppermute(y1, "orb", beside)
    for step in rounds[2:]:
        sums = added(sums, step)
    yc1, sums = ordered(yc1, sums)
    give1, keep1 = rotated((block1, c1, y1, yc1), q, 2)
    got1 = lax.ppermute(give1, "space", swap)
    keep_y, yg, _, sums = ordered(keep2, yg, give1, sums)
    yk = lax.ppermute(keep_y, "orb", across)
    ycg = lax.ppermute(yg, "orb", beside)
    coefs = coefficients(sums, strong)
    coefs = jnp.concatenate([coefs, lax.ppermute(coefs, "orb", beside)], axis=0)
    ycg, coefs = ordered(ycg, coefs)
    (give2,) = rotated((give2, cg, yg, ycg), q, 1)
    got2 = lax.ppermute(give2, "space", swap)
    coefs, _ = ordered(coefs, give2)
    coefs_y = lax.ppermute(coefs, "orb", across)
    coefs = [half_of[k * 2 * count : (k + 1) * 2 * count] for half_of in (coefs, coefs_y) for k in (0, 1)]
    term = nonlocal_term(psi.shape, coefs, q, weights)
    yk, _, got1 = ordered(yk, give2, got1)
    yck = lax.ppermute(yk, "orb", beside)
    return assembled(term, keep1, got1, got2, (keep2, ck, yk, yck), q)


def solution(mesh):
    placed = (
        P("space", None, None, "orb"),
        P("space", None, None),
        P(None, "space", None, None),
        P(),
        P(),
        P(),
        P(),
    )
    return jax.shard_map(
        shards, mesh=mesh, in_specs=placed, out_specs=P("space", None, None, "orb"), check_vma=False
    )
```

```python
import functools

import jax
import jax.numpy as jnp
from jax import lax
from jax.experimental import pallas as pl
from jax.experimental.pallas import tpu as pltpu
from jax.sharding import PartitionSpec as P

F32 = jnp.float32
BF16 = jnp.bfloat16
VMEM_LIMIT = 24 * 1024 * 1024
SHRINK = 16
FILTER = 100


def params():
    return pltpu.CompilerParams(vmem_limit_bytes=VMEM_LIMIT)


def cost(flops, moved):
    return pl.CostEstimate(flops=flops // SHRINK, bytes_accessed=moved // SHRINK, transcendentals=0)


def inside(p, window):
    return jnp.logical_and(p >= 0, p < window).astype(F32)


def neighbour_sum(width, pairs):
    n = (2 if pairs else 1) * width
    i = lax.broadcasted_iota(jnp.int32, (n, n), 0)
    j = lax.broadcasted_iota(jnp.int32, (n, n), 1)
    linked = jnp.abs(i - j) == 1
    if pairs:
        linked = jnp.logical_and(linked, (i < width) == (j < width))
        linked = jnp.logical_or(linked, jnp.abs(i - j) == width)
    return jnp.where(linked, -0.125, 0.0)


def potential_block(potential):
    lines, width = potential.shape
    gap = jnp.zeros((lines, 64 - width), F32)
    u = (potential - 1.0) * 0.25
    hi = u.astype(BF16).astype(F32)
    return jnp.concatenate([hi, gap, u - hi, gap], axis=1)


def prepare_kernel(early, psi, potential_far, to_x, to_z, potential, sems):
    x = lax.rem(lax.axis_index("space"), 2)
    half = psi.shape[1] // 2
    window = half + 2
    mine, theirs = (half - 2) * x, (half - 2) * (1 - x)
    fetch = pltpu.make_async_copy(potential_far, potential, sems.at[0])
    fetch.start()
    copies = [
        pltpu.make_async_copy(
            psi.at[:, pl.ds(theirs, early)], to_x.at[:, pl.ds(0, early)], sems.at[1]
        ),
        pltpu.make_async_copy(
            psi.at[:, pl.ds(mine, window)], to_z.at[:, pl.ds(0, window)], sems.at[2]
        ),
    ]
    for copy in copies:
        copy.start()
    fetch.wait()
    for plane in range(potential.shape[0]):
        block = potential_block(potential[plane]).astype(BF16)
        to_x[plane, early] = block
        to_z[plane, window] = block
    for copy in copies:
        copy.wait()


def prepared(psi, potential, early):
    planes, width_x, width_y, orbs = psi.shape
    window = width_x // 2 + 2

    def out(rows):
        return jax.ShapeDtypeStruct((planes, rows, width_y, orbs), BF16)

    return pl.pallas_call(
        functools.partial(prepare_kernel, early),
        out_shape=(out(early + 1), out(window + 1)),
        in_specs=[pl.BlockSpec(memory_space=pltpu.MemorySpace.HBM)] * 2,
        out_specs=(pl.BlockSpec(memory_space=pltpu.VMEM),) * 2,
        scratch_shapes=[pltpu.VMEM(potential.shape, F32), pltpu.SemaphoreType.DMA((3,))],
        compiler_params=params(),
        cost_estimate=cost(4096, 4096),
        name="prepared",
    )(*(pltpu.with_memory_space_constraint(a, pltpu.MemorySpace.HBM) for a in (psi, potential)))


def pack_kernel(early, psi, beta, to_x2, far, near, sem):
    x = lax.rem(lax.axis_index("space"), 2)
    half = psi.shape[1] // 2
    later = half + 2 - early
    copy = pltpu.make_async_copy(
        psi.at[:, pl.ds((half - 2) * (1 - x) + early, later)], to_x2, sem
    )
    copy.start()
    far[...] = beta[:, x]
    near[...] = beta[:, 1 - x]
    copy.wait()


def packed(psi, beta, early):
    planes, width_x, width_y, orbs = psi.shape
    side = jax.ShapeDtypeStruct((beta.shape[0], *beta.shape[2:]), BF16)
    later = width_x // 2 + 2 - early
    return pl.pallas_call(
        functools.partial(pack_kernel, early),
        out_shape=(jax.ShapeDtypeStruct((planes, later, width_y, orbs), BF16), side, side),
        in_specs=[
            pl.BlockSpec(memory_space=pltpu.MemorySpace.HBM),
            pl.BlockSpec(memory_space=pltpu.VMEM),
        ],
        out_specs=(pl.BlockSpec(memory_space=pltpu.VMEM),) * 3,
        scratch_shapes=[pltpu.SemaphoreType.DMA],
        compiler_params=params(),
        cost_estimate=cost(4096, 4096),
        name="packed",
    )(pltpu.with_memory_space_constraint(psi, pltpu.MemorySpace.HBM), beta)


def partial_kernel(count, atoms, own, beta, b_x, b_d, potential, gram, out, weights_out, table, acc):
    place = lax.axis_index("space")
    x = lax.rem(place, 2)
    rows, width = potential.shape[1:]
    side = place ^ 1
    beyond = place - 1 + 2 * x
    tri = neighbour_sum(width, False).astype(BF16)
    acc[...] = jnp.zeros_like(acc)
    step = 8

    for k in range(2):
        plane = x if k == 0 else 1 - x
        outer, there = (b_d, beyond) if k == 0 else (b_x, side)
        u = (potential[plane] - 1.0) * 0.25

        def fill(i, carry):
            for j in range(step):
                p = i * step + j
                here = (jnp.abs(place - atoms[p]) <= 1).astype(F32)
                next_to = (jnp.abs(there - atoms[p]) <= 1).astype(F32)
                b32 = beta[p, plane].astype(F32) * here
                b = b32.astype(BF16)
                sides = beta[p, 1 - plane].astype(F32) * here + outer[p].astype(F32) * next_to
                whole = jnp.dot(b, tri, preferred_element_type=F32)
                whole = whole + jnp.dot(tri, b, preferred_element_type=F32)
                whole = whole + u * b32 - 0.125 * sides
                hi = whole.astype(BF16).astype(F32)
                for kind, value in enumerate((b32, hi, whole - hi)):
                    table[pl.ds((kind * count + p) * rows, rows)] = value
            return carry

        lax.fori_loop(0, count // step, fill, 0)

        def use(i, carry):
            totals = []
            for j in range(step):
                r = i * step + j
                weights = table[pl.ds(r, 3 * count, stride=rows)].astype(BF16)
                weights_out[plane, r] = weights
                totals.append(jnp.dot(weights, own[plane, r], preferred_element_type=F32))
            acc[...] += sum(totals[1:], totals[0])
            return carry

        lax.fori_loop(0, rows // step, use, 0)
    out[...] = jnp.zeros_like(out)
    out[0:count] = acc[0:count]
    out[count : 2 * count] = acc[count : 2 * count] + acc[2 * count : 3 * count]
    out[2 * count : 3 * count, 0:count] = gram[...]


def partials(count, atoms, own, beta, b_x, b_d, potential, gram):
    planes, rows, width, orbs = own.shape
    return pl.pallas_call(
        functools.partial(partial_kernel, count),
        out_shape=(
            jax.ShapeDtypeStruct((3 * count, orbs), F32),
            jax.ShapeDtypeStruct((planes, rows, 3 * count, width), BF16),
        ),
        in_specs=[pl.BlockSpec(memory_space=pltpu.SMEM)]
        + [pl.BlockSpec(memory_space=pltpu.VMEM)] * 6,
        out_specs=(pl.BlockSpec(memory_space=pltpu.VMEM),) * 2,
        scratch_shapes=[
            pltpu.VMEM((3 * count * rows, width), F32),
            pltpu.VMEM((3 * count, orbs), F32),
        ],
        compiler_params=params(),
        cost_estimate=cost(4096, 4096),
        name="partials",
    )(atoms, own, beta, b_x, b_d, potential, gram)


def coefficient_kernel(sums, strength, out):
    count, orbs = strength.shape
    coef1 = (strength[...] * sums[0:count]).astype(BF16)
    padded = coef1.astype(F32) * 0.25
    if orbs > count:
        padded = jnp.concatenate([padded, jnp.zeros((orbs - count, orbs), F32)], axis=0)
    proj2 = sums[count : 2 * count] + jnp.dot(
        sums[2 * count : 3 * count],
        padded,
        preferred_element_type=F32,
        precision=lax.Precision.HIGHEST,
    )
    out[0:count] = coef1
    out[count : 2 * count] = (strength[...] * proj2).astype(BF16)


def coefficients(sums, strength):
    count, orbs = strength.shape
    return pl.pallas_call(
        coefficient_kernel,
        out_shape=jax.ShapeDtypeStruct((2 * count, orbs), BF16),
        in_specs=[pl.BlockSpec(memory_space=pltpu.VMEM)] * 2,
        out_specs=pl.BlockSpec(memory_space=pltpu.VMEM),
        compiler_params=params(),
        cost_estimate=cost(4096, 4096),
        name="coefficients",
    )(sums, strength)


def nonlocal_kernel(unroll, a, b, c, d, q, weights, out):
    count, orbs = a.shape[0] // 2, a.shape[1]
    turned = sum(
        jnp.dot(ref[...], q[k], preferred_element_type=F32) for k, ref in enumerate((a, b, c, d))
    )
    turned = turned * 0.25
    one, two = turned[0:count], turned[count : 2 * count]
    right = jnp.concatenate([two, one, one], axis=0)
    hi = right.astype(BF16)
    lo = right - hi.astype(F32)
    right = jnp.concatenate([hi.astype(F32), lo], axis=1).astype(BF16)

    def step(i, carry):
        for k in range(unroll):
            r = i * unroll + k
            for plane in range(weights.shape[0]):
                both = lax.dot_general(
                    weights[plane, r], right, (((0,), (0,)), ((), ())), preferred_element_type=F32
                )
                out[plane, r] = both[:, :orbs] + both[:, orbs:]
        return carry

    lax.fori_loop(0, weights.shape[1] // unroll, step, 0)


def nonlocal_term(shape, coefs, q, weights):
    unroll = max(g for g in (1, 2, 4, 8) if weights.shape[1] % g == 0)
    return pl.pallas_call(
        functools.partial(nonlocal_kernel, unroll),
        out_shape=jax.ShapeDtypeStruct(shape, F32),
        in_specs=[pl.BlockSpec(memory_space=pltpu.VMEM)] * 6,
        out_specs=pl.BlockSpec(memory_space=pltpu.VMEM),
        compiler_params=params(),
        cost_estimate=cost(4096, 4096),
        name="nonlocal",
    )(*coefs, q, weights)


def filter_kernel(slabs, start, parts, joint, *refs):
    own, p_own, zo = refs[:3]
    xrs, zfs = refs[3 : 3 + parts], refs[3 + parts : 3 + 2 * parts]
    extra = 7
    outs, scratch = refs[3 + 2 * parts : -extra], refs[-extra:]
    first, lines, diagonals = scratch[:3]
    place = lax.axis_index("space")
    x = lax.rem(place, 2)
    width = own.shape[2]
    cells = 2 * width
    half = own.shape[1] // 2
    orbs = own.shape[3]
    rows = outs[0].shape[1]
    base = (half - 2) * x
    lower = (place >= 2).astype(F32)
    upper = (place < slabs - 2).astype(F32)
    is_odd = x.astype(F32)
    has_zf = lower * (1.0 - is_odd) + upper * is_odd
    has_zo = upper * (1.0 - is_odd) + lower * is_odd
    xr, zf, pots, sems = scratch[3:]
    window = xr.shape[1] // 2
    early = xrs[0].shape[1] - 1
    copies = []
    for k, (target, pieces) in enumerate(((xr, xrs), (zf, zfs))):
        if parts == 1 and k == 1:
            zf = pieces[0]
            continue
        begin = 0 if parts == 1 else early - 8
        moved = [
            (pieces[0].at[:, pl.ds(early, 1)], pots.at[k]),
            (
                pieces[0].at[:, pl.ds(begin, early - begin)],
                target.at[:, pl.ds(begin, early - begin)],
            ),
        ]
        if parts > 1:
            later = target.shape[1] - early
            moved.append((pieces[1].at[:, pl.ds(0, later)], target.at[:, pl.ds(early, later)]))
        copies += [
            pltpu.make_async_copy(source, goal, sems.at[3 * k + i])
            for i, (source, goal) in enumerate(moved)
        ]
    for copy in copies:
        copy.start()

    def fill(c, block):
        lines[c - 1] = block
        even, odd = (lines[c - 1, pl.ds(k, half, stride=2)] for k in range(2))
        whole = [a[:, :width] + a[:, 64 : 64 + width] for a in (even, odd)]
        diagonals[c - 1] = jnp.concatenate(whole, axis=1)

    for c in (2, 3):
        fill(c, potential_block(p_own[(c % 2) ^ x]))
    fill(6, zo[x, zo.shape[1] - 1].astype(F32))
    for copy in copies:
        copy.wait()
    for c in (1, 4, 5):
        if parts == 1 and c == 1:
            fill(c, zf[(c % 2) ^ x, early].astype(F32))
        else:
            fill(c, pots[1 if c < 2 else 0, (c % 2) ^ x, 0].astype(F32))

    here = neighbour_sum(width, True)
    i = lax.broadcasted_iota(jnp.int32, (cells, cells), 0)
    diagonal = i == lax.broadcasted_iota(jnp.int32, (cells, cells), 1)

    def local(c, p):
        u = diagonals[c - 1, pl.ds(base // 2 + p, 1)]
        return jnp.where(diagonal, u, here).astype(BF16)

    def rows_of(c, w, n):
        plane = (c % 2) ^ x
        if c in (2, 3):
            return own[plane, pl.ds(base + w, n)]
        ref = zf if c < 2 else (xr if c < 6 else zo)
        return ref[plane, pl.ds(w, n)]

    def applied(pair, outer, zs, matrix):
        near = jnp.dot(matrix, pair, preferred_element_type=F32)
        return near - 0.125 * (outer + zs)

    def step1(j, carry):
        p = start // 2 + x + j - 1
        q = jnp.clip(p, 0, window - 1)
        has_below = inside(p - 1, window)
        has_above = inside(p + 1, window)
        valid = inside(p, window)
        below = jnp.maximum(2 * q - 1, 0)
        above = jnp.minimum(2 * q + 2, 2 * window - 1)
        pair = [rows_of(c, 2 * q, 2).reshape(cells, orbs) for c in range(8)]
        vs = [v.astype(F32) for v in pair]
        for c in range(1, 7):
            outer = jnp.concatenate(
                [
                    rows_of(c, below, 1)[0].astype(F32) * has_below,
                    rows_of(c, above, 1)[0].astype(F32) * has_above,
                ],
                axis=0,
            )
            f = applied(pair[c], outer, vs[c - 1] + vs[c + 1], local(c, q))
            keep = valid
            if c == 1:
                keep = valid * has_zf
            if c == 6:
                keep = valid * has_zo
            first[c - 1, pl.ds(2 * j, 2)] = (f * keep).astype(BF16).reshape(2, width, orbs)
        return carry

    lax.fori_loop(0, rows // 2 + 2, step1, 0)

    def step2(j, carry):
        p = start // 2 + x + j
        pair = [first[c - 1, pl.ds(2 * j + 2, 2)].reshape(cells, orbs) for c in range(1, 7)]
        vs = [v.astype(F32) for v in pair]
        for c in range(2, 6):
            outer = jnp.concatenate(
                [first[c - 1, 2 * j + 1].astype(F32), first[c - 1, 2 * j + 4].astype(F32)], axis=0
            )
            f = applied(pair[c - 1], outer, vs[c - 2] + vs[c], local(c, p))
            f = f.astype(BF16).reshape(2, width, orbs)
            plane = (c % 2) ^ x
            if joint:
                outs[0][plane + (2 if c in (2, 3) else 0), pl.ds(2 * j, 2)] = f
            else:
                outs[1 if c in (2, 3) else 0][plane, pl.ds(2 * j, 2)] = f
        return carry

    lax.fori_loop(0, rows // 2, step2, 0)


def filtered(slabs, start, rows, joint, operands, xrs, zfs):
    own = operands[0]
    planes, _, width, orbs = own.shape
    parts = len(xrs)
    shape = (2 * planes if joint else planes, rows, width, orbs)
    out = (jax.ShapeDtypeStruct(shape, BF16),) * (1 if joint else 2)
    cells = 10 * rows * width
    scratch = [
        pltpu.VMEM((6, rows + 4, width, orbs), BF16),
        pltpu.VMEM((6, width, orbs), F32),
        pltpu.VMEM((6, own.shape[1] // 2, 2 * width), F32),
    ]
    window = own.shape[1] // 2 + 2 if parts > 1 else xrs[0].shape[1] - 1
    scratch += [pltpu.VMEM((planes, window, width, orbs), BF16)] * 2
    scratch += [pltpu.VMEM((2, planes, 1, width, orbs), BF16), pltpu.SemaphoreType.DMA((6,))]
    local = pl.BlockSpec(memory_space=pltpu.VMEM)
    distant = pl.BlockSpec(memory_space=pltpu.MemorySpace.HBM)
    far_xr = [pltpu.with_memory_space_constraint(a, pltpu.MemorySpace.HBM) for a in xrs]
    far_zf = [pltpu.with_memory_space_constraint(a, pltpu.MemorySpace.HBM) for a in zfs]
    xrs, zfs = far_xr, (far_zf if parts > 1 else zfs)
    return pl.pallas_call(
        functools.partial(filter_kernel, slabs, start, parts, joint),
        out_shape=out,
        in_specs=[local] * len(operands)
        + [distant] * parts
        + [distant if parts > 1 else local] * parts,
        out_specs=(local,) * len(out),
        scratch_shapes=scratch,
        compiler_params=params(),
        cost_estimate=cost(2 * cells * 32 * orbs, FILTER * cells * orbs * 4),
        name="filtered",
    )(*operands, *xrs, *zfs)


def rotate_kernel(group, *refs):
    a, b, c, d, q = refs[:5]
    outs = refs[5:]
    _, rows, width, orbs = a.shape
    planes = outs[0].shape[0]
    low = jnp.concatenate([q[0], q[1]], axis=0)
    high = jnp.concatenate([q[2], q[3]], axis=0)

    def one(j, carry):
        for plane in range(a.shape[0]):
            def take(ref):
                return ref[plane, pl.ds(group * j, group)].reshape(group * width, orbs)

            total = jnp.dot(
                jnp.concatenate([take(a), take(b)], axis=1), low, preferred_element_type=F32
            )
            total = total + jnp.dot(
                jnp.concatenate([take(c), take(d)], axis=1), high, preferred_element_type=F32
            )
            outs[plane // planes][plane % planes, pl.ds(group * j, group)] = total.astype(
                BF16
            ).reshape(group, width, orbs)
        return carry

    lax.fori_loop(0, rows // group, one, 0)


def rotated(blocks, q, pieces):
    a = blocks[0]
    size = a.size
    group = max(g for g in range(1, 9) if a.shape[1] % g == 0)
    out = jax.ShapeDtypeStruct((a.shape[0] // pieces, *a.shape[1:]), BF16)
    return pl.pallas_call(
        functools.partial(rotate_kernel, group),
        out_shape=(out,) * pieces,
        in_specs=[pl.BlockSpec(memory_space=pltpu.VMEM)] * 5,
        out_specs=(pl.BlockSpec(memory_space=pltpu.VMEM),) * pieces,
        compiler_params=params(),
        cost_estimate=cost(8 * size * a.shape[3], 10 * size),
        name="rotated",
    )(*blocks, q)


def assemble_kernel(group, term, keep1, got1, got2, a, b, c, d, q, out):
    half = term.shape[1] // 2
    width, orbs = term.shape[2:]
    x = lax.rem(lax.axis_index("space"), 2)
    rows1, rows2 = keep1.shape[1], got2.shape[1]
    for ref, at in (
        (keep1, half * x),
        (got1, half * (1 - x)),
        (got2, half * (1 - x) + rows1),
    ):
        where = pl.ds(at, ref.shape[1])
        out[:, where] = (ref[...].astype(F32) + term[:, where]).astype(BF16)
    low = jnp.concatenate([q[0], q[1]], axis=0)
    high = jnp.concatenate([q[2], q[3]], axis=0)

    def one(j, carry):
        where = pl.ds(half * x + rows1 + group * j, group)
        for plane in range(a.shape[0]):
            def take(ref):
                return ref[plane, pl.ds(group * j, group)].reshape(group * width, orbs)

            total = jnp.dot(
                jnp.concatenate([take(a), take(b)], axis=1), low, preferred_element_type=F32
            )
            total = total + jnp.dot(
                jnp.concatenate([take(c), take(d)], axis=1), high, preferred_element_type=F32
            )
            total = total.reshape(group, width, orbs) + term[plane, where]
            out[plane, where] = total.astype(BF16)
        return carry

    lax.fori_loop(0, rows2 // group, one, 0)


def assembled(term, keep1, got1, got2, blocks, q):
    group = max(g for g in range(1, 9) if got2.shape[1] % g == 0)
    return pl.pallas_call(
        functools.partial(assemble_kernel, group),
        out_shape=jax.ShapeDtypeStruct(term.shape, BF16),
        in_specs=[pl.BlockSpec(memory_space=pltpu.VMEM)] * 9,
        out_specs=pl.BlockSpec(memory_space=pltpu.VMEM),
        compiler_params=params(),
        cost_estimate=cost(4096, 4096),
        name="assembled",
    )(term, keep1, got1, got2, *blocks, q)


def ordered(*arrays):
    return lax.optimization_barrier(arrays)


def shards(psi, potential, beta, strength, atom_slab, pattern, q_tiles):
    planes, width_x, width_y, orbs = psi.shape
    count = beta.shape[0]
    slabs = lax.axis_size("space")
    place = lax.axis_index("space")
    x = lax.rem(place, 2)
    half = width_x // 2
    window = half + 2
    rows1 = half * 7 // 24 * 2
    rows2 = half - rows1
    early = rows1 + 4

    def within(pairs):
        return [(i, j) for i, j in pairs if 0 <= j < slabs]

    swap = [(i, i ^ 1) for i in range(slabs)]
    own_way = within([(i, i + 2 if i % 2 else i - 2) for i in range(slabs)])
    other_way = within([(i, i - 2 if i % 2 else i + 2) for i in range(slabs)])
    groups = lax.axis_size("orb")
    across = [(i, i ^ 2) for i in range(groups)]
    beside = [(i, i ^ 1) for i in range(groups)]
    mine = (half - 2) * x
    theirs = (half - 2) * (1 - x)

    to_x, to_z = prepared(psi, potential, early)
    to_x2, far, near = packed(psi, beta, early)
    f_x = lax.ppermute(near, "space", swap)
    raster = within([(i, i + 1 if i % 2 else i - 1) for i in range(slabs)])
    f_d = lax.ppermute(far, "space", raster)
    xr1 = lax.ppermute(to_x, "space", swap)
    zo = lax.ppermute(to_z, "space", own_way)
    active = jnp.abs(place - atom_slab) <= 1
    beta_m = jnp.where(active[:, None, None, None], beta, jnp.zeros_like(beta))
    gram = jnp.einsum("pzxy,qzxy->pq", beta_m, beta_m, preferred_element_type=F32)
    xr1, second = ordered(xr1, to_x2)
    zf1 = lax.ppermute(xr1, "space", other_way)
    xr2 = lax.ppermute(second, "space", swap)
    zf2 = lax.ppermute(xr2, "space", other_way)
    strong = jnp.broadcast_to(strength[:, None], (count, orbs))

    sums, weights = partials(count, atom_slab, psi, beta, f_x, f_d, potential, gram)
    zf1, sums, _ = ordered(zf1, sums, xr2)
    operands = (psi, potential, zo)
    (block1,) = filtered(slabs, 0, rows1, True, operands, (xr1,), (zf1,))
    y1 = lax.ppermute(block1, "orb", across)
    rounds = [1 << k for k in range((slabs - 1).bit_length())]

    def added(values, step):
        pairs = [(i, i ^ step) for i in range(slabs)]
        return values + lax.ppermute(values, "space", pairs)

    for step in rounds[:1]:
        sums = added(sums, step)
    zf2, sums = ordered(zf2, sums)
    give2, keep2 = filtered(slabs, rows1, rows2, False, operands, (xr1, xr2), (zf1, zf2))
    pattern, q_tiles, _ = ordered(pattern, q_tiles, give2)
    me = lax.axis_index("orb")
    which = jnp.bitwise_xor(me, jnp.arange(groups, dtype=jnp.int32))
    rows_hot = (pattern[:, 0][:, None] == which[None, :]).astype(BF16)
    rows_hot = rows_hot * (pattern[:, 1] == me).astype(BF16)[:, None]
    q = jnp.einsum("ki,kab->iab", rows_hot, q_tiles, preferred_element_type=F32).astype(BF16)
    cg = lax.ppermute(give2, "orb", beside)
    ck = lax.ppermute(keep2, "orb", beside)
    yg = lax.ppermute(give2, "orb", across)
    for step in rounds[1:2]:
        sums = added(sums, step)
    y1, again, _, sums = ordered(y1, block1, give2, sums)
    c1 = lax.ppermute(again, "orb", beside)
    yc1 = lax.ppermute(y1, "orb", beside)
    for step in rounds[2:]:
        sums = added(sums, step)
    yc1, sums = ordered(yc1, sums)
    give1, keep1 = rotated((block1, c1, y1, yc1), q, 2)
    got1 = lax.ppermute(give1, "space", swap)
    keep_y, yg, _, sums = ordered(keep2, yg, give1, sums)
    yk = lax.ppermute(keep_y, "orb", across)
    ycg = lax.ppermute(yg, "orb", beside)
    coefs = coefficients(sums, strong)
    coefs = jnp.concatenate([coefs, lax.ppermute(coefs, "orb", beside)], axis=0)
    ycg, coefs = ordered(ycg, coefs)
    (give2,) = rotated((give2, cg, yg, ycg), q, 1)
    got2 = lax.ppermute(give2, "space", swap)
    coefs, _ = ordered(coefs, give2)
    coefs_y = lax.ppermute(coefs, "orb", across)
    coefs = [half_of[k * 2 * count : (k + 1) * 2 * count] for half_of in (coefs, coefs_y) for k in (0, 1)]
    term = nonlocal_term(psi.shape, coefs, q, weights)
    yk, _, got1 = ordered(yk, give2, got1)
    yck = lax.ppermute(yk, "orb", beside)
    return assembled(term, keep1, got1, got2, (keep2, ck, yk, yck), q)


def solution(mesh):
    placed = (
        P("space", None, None, "orb"),
        P("space", None, None),
        P(None, "space", None, None),
        P(),
        P(),
        P(),
        P(),
    )
    return jax.shard_map(
        shards, mesh=mesh, in_specs=placed, out_specs=P("space", None, None, "orb"), check_vma=False
    )
```

```python
import functools

import jax
import jax.numpy as jnp
from jax import lax
from jax.experimental import pallas as pl
from jax.experimental.pallas import tpu as pltpu
from jax.sharding import PartitionSpec as P

F32 = jnp.float32
BF16 = jnp.bfloat16
VMEM_LIMIT = 24 * 1024 * 1024
SHRINK = 16
FILTER = 100


def params():
    return pltpu.CompilerParams(vmem_limit_bytes=VMEM_LIMIT)


def cost(flops, moved):
    return pl.CostEstimate(flops=flops // SHRINK, bytes_accessed=moved // SHRINK, transcendentals=0)


def inside(p, window):
    return jnp.logical_and(p >= 0, p < window).astype(F32)


def neighbour_sum(width, pairs):
    n = (2 if pairs else 1) * width
    i = lax.broadcasted_iota(jnp.int32, (n, n), 0)
    j = lax.broadcasted_iota(jnp.int32, (n, n), 1)
    linked = jnp.abs(i - j) == 1
    if pairs:
        linked = jnp.logical_and(linked, (i < width) == (j < width))
        linked = jnp.logical_or(linked, jnp.abs(i - j) == width)
    return jnp.where(linked, -0.125, 0.0)


def potential_block(potential):
    lines, width = potential.shape
    gap = jnp.zeros((lines, 64 - width), F32)
    u = (potential - 1.0) * 0.25
    hi = u.astype(BF16).astype(F32)
    return jnp.concatenate([hi, gap, u - hi, gap], axis=1)


def prepare_kernel(early, psi, potential_far, to_x, to_z, potential, sems):
    x = lax.rem(lax.axis_index("space"), 2)
    half = psi.shape[1] // 2
    window = half + 2
    mine, theirs = (half - 2) * x, (half - 2) * (1 - x)
    fetch = pltpu.make_async_copy(potential_far, potential, sems.at[0])
    fetch.start()
    copies = [
        pltpu.make_async_copy(
            psi.at[:, pl.ds(theirs, early)], to_x.at[:, pl.ds(0, early)], sems.at[1]
        ),
        pltpu.make_async_copy(
            psi.at[:, pl.ds(mine, window)], to_z.at[:, pl.ds(0, window)], sems.at[2]
        ),
    ]
    for copy in copies:
        copy.start()
    fetch.wait()
    for plane in range(potential.shape[0]):
        block = potential_block(potential[plane]).astype(BF16)
        to_x[plane, early] = block
        to_z[plane, window] = block
    for copy in copies:
        copy.wait()


def prepared(psi, potential, early):
    planes, width_x, width_y, orbs = psi.shape
    window = width_x // 2 + 2

    def out(rows):
        return jax.ShapeDtypeStruct((planes, rows, width_y, orbs), BF16)

    return pl.pallas_call(
        functools.partial(prepare_kernel, early),
        out_shape=(out(early + 1), out(window + 1)),
        in_specs=[pl.BlockSpec(memory_space=pltpu.MemorySpace.HBM)] * 2,
        out_specs=(pl.BlockSpec(memory_space=pltpu.VMEM),) * 2,
        scratch_shapes=[pltpu.VMEM(potential.shape, F32), pltpu.SemaphoreType.DMA((3,))],
        compiler_params=params(),
        cost_estimate=cost(4096, 4096),
        name="prepared",
    )(*(pltpu.with_memory_space_constraint(a, pltpu.MemorySpace.HBM) for a in (psi, potential)))


def pack_kernel(early, psi, beta, to_x2, far, near, sem):
    x = lax.rem(lax.axis_index("space"), 2)
    half = psi.shape[1] // 2
    later = half + 2 - early
    copy = pltpu.make_async_copy(
        psi.at[:, pl.ds((half - 2) * (1 - x) + early, later)], to_x2, sem
    )
    copy.start()
    far[...] = beta[:, x]
    near[...] = beta[:, 1 - x]
    copy.wait()


def packed(psi, beta, early):
    planes, width_x, width_y, orbs = psi.shape
    side = jax.ShapeDtypeStruct((beta.shape[0], *beta.shape[2:]), BF16)
    later = width_x // 2 + 2 - early
    return pl.pallas_call(
        functools.partial(pack_kernel, early),
        out_shape=(jax.ShapeDtypeStruct((planes, later, width_y, orbs), BF16), side, side),
        in_specs=[
            pl.BlockSpec(memory_space=pltpu.MemorySpace.HBM),
            pl.BlockSpec(memory_space=pltpu.VMEM),
        ],
        out_specs=(pl.BlockSpec(memory_space=pltpu.VMEM),) * 3,
        scratch_shapes=[pltpu.SemaphoreType.DMA],
        compiler_params=params(),
        cost_estimate=cost(4096, 4096),
        name="packed",
    )(pltpu.with_memory_space_constraint(psi, pltpu.MemorySpace.HBM), beta)


def partial_kernel(count, atoms, own, beta, b_x, b_d, potential, gram, out, weights_out, table, acc):
    place = lax.axis_index("space")
    x = lax.rem(place, 2)
    rows, width = potential.shape[1:]
    side = place ^ 1
    beyond = place - 1 + 2 * x
    tri = neighbour_sum(width, False).astype(BF16)
    acc[...] = jnp.zeros_like(acc)
    step = 8

    for k in range(2):
        plane = x if k == 0 else 1 - x
        outer, there = (b_d, beyond) if k == 0 else (b_x, side)
        u = (potential[plane] - 1.0) * 0.25

        def fill(i, carry):
            for j in range(step):
                p = i * step + j
                here = (jnp.abs(place - atoms[p]) <= 1).astype(F32)
                next_to = (jnp.abs(there - atoms[p]) <= 1).astype(F32)
                b32 = beta[p, plane].astype(F32) * here
                b = b32.astype(BF16)
                sides = beta[p, 1 - plane].astype(F32) * here + outer[p].astype(F32) * next_to
                whole = jnp.dot(b, tri, preferred_element_type=F32)
                whole = whole + jnp.dot(tri, b, preferred_element_type=F32)
                whole = whole + u * b32 - 0.125 * sides
                hi = whole.astype(BF16).astype(F32)
                for kind, value in enumerate((b32, hi, whole - hi)):
                    table[pl.ds((kind * count + p) * rows, rows)] = value
            return carry

        lax.fori_loop(0, count // step, fill, 0)

        def use(i, carry):
            totals = []
            for j in range(step):
                r = i * step + j
                weights = table[pl.ds(r, 3 * count, stride=rows)].astype(BF16)
                weights_out[plane, r] = weights
                totals.append(jnp.dot(weights, own[plane, r], preferred_element_type=F32))
            acc[...] += sum(totals[1:], totals[0])
            return carry

        lax.fori_loop(0, rows // step, use, 0)
    out[...] = jnp.zeros_like(out)
    out[0:count] = acc[0:count]
    out[count : 2 * count] = acc[count : 2 * count] + acc[2 * count : 3 * count]
    out[2 * count : 3 * count, 0:count] = gram[...]


def partials(count, atoms, own, beta, b_x, b_d, potential, gram):
    planes, rows, width, orbs = own.shape
    return pl.pallas_call(
        functools.partial(partial_kernel, count),
        out_shape=(
            jax.ShapeDtypeStruct((3 * count, orbs), F32),
            jax.ShapeDtypeStruct((planes, rows, 3 * count, width), BF16),
        ),
        in_specs=[pl.BlockSpec(memory_space=pltpu.SMEM)]
        + [pl.BlockSpec(memory_space=pltpu.VMEM)] * 6,
        out_specs=(pl.BlockSpec(memory_space=pltpu.VMEM),) * 2,
        scratch_shapes=[
            pltpu.VMEM((3 * count * rows, width), F32),
            pltpu.VMEM((3 * count, orbs), F32),
        ],
        compiler_params=params(),
        cost_estimate=cost(4096, 4096),
        name="partials",
    )(atoms, own, beta, b_x, b_d, potential, gram)


def coefficient_kernel(sums, strength, out):
    count, orbs = strength.shape
    coef1 = (strength[...] * sums[0:count]).astype(BF16)
    padded = coef1.astype(F32) * 0.25
    if orbs > count:
        padded = jnp.concatenate([padded, jnp.zeros((orbs - count, orbs), F32)], axis=0)
    proj2 = sums[count : 2 * count] + jnp.dot(
        sums[2 * count : 3 * count],
        padded,
        preferred_element_type=F32,
        precision=lax.Precision.HIGHEST,
    )
    out[0:count] = coef1
    out[count : 2 * count] = (strength[...] * proj2).astype(BF16)


def coefficients(sums, strength):
    count, orbs = strength.shape
    return pl.pallas_call(
        coefficient_kernel,
        out_shape=jax.ShapeDtypeStruct((2 * count, orbs), BF16),
        in_specs=[pl.BlockSpec(memory_space=pltpu.VMEM)] * 2,
        out_specs=pl.BlockSpec(memory_space=pltpu.VMEM),
        compiler_params=params(),
        cost_estimate=cost(4096, 4096),
        name="coefficients",
    )(sums, strength)


def nonlocal_kernel(unroll, a, b, c, d, q, weights, out):
    count, orbs = a.shape[0] // 2, a.shape[1]
    turned = sum(
        jnp.dot(ref[...], q[k], preferred_element_type=F32) for k, ref in enumerate((a, b, c, d))
    )
    turned = turned * 0.25
    one, two = turned[0:count], turned[count : 2 * count]
    right = jnp.concatenate([two, one, one], axis=0)
    hi = right.astype(BF16)
    lo = right - hi.astype(F32)
    right = jnp.concatenate([hi.astype(F32), lo], axis=1).astype(BF16)

    def step(i, carry):
        for k in range(unroll):
            r = i * unroll + k
            for plane in range(weights.shape[0]):
                both = lax.dot_general(
                    weights[plane, r], right, (((0,), (0,)), ((), ())), preferred_element_type=F32
                )
                out[plane, r] = both[:, :orbs] + both[:, orbs:]
        return carry

    lax.fori_loop(0, weights.shape[1] // unroll, step, 0)


def nonlocal_term(shape, coefs, q, weights):
    unroll = max(g for g in (1, 2, 4, 8) if weights.shape[1] % g == 0)
    return pl.pallas_call(
        functools.partial(nonlocal_kernel, unroll),
        out_shape=jax.ShapeDtypeStruct(shape, F32),
        in_specs=[pl.BlockSpec(memory_space=pltpu.VMEM)] * 6,
        out_specs=pl.BlockSpec(memory_space=pltpu.VMEM),
        compiler_params=params(),
        cost_estimate=cost(4096, 4096),
        name="nonlocal",
    )(*coefs, q, weights)


def filter_kernel(slabs, start, parts, joint, *refs):
    own, p_own, zo = refs[:3]
    xrs, zfs = refs[3 : 3 + parts], refs[3 + parts : 3 + 2 * parts]
    extra = 7
    outs, scratch = refs[3 + 2 * parts : -extra], refs[-extra:]
    first, lines, diagonals = scratch[:3]
    place = lax.axis_index("space")
    x = lax.rem(place, 2)
    width = own.shape[2]
    cells = 2 * width
    half = own.shape[1] // 2
    orbs = own.shape[3]
    rows = outs[0].shape[1]
    base = (half - 2) * x
    lower = (place >= 2).astype(F32)
    upper = (place < slabs - 2).astype(F32)
    is_odd = x.astype(F32)
    has_zf = lower * (1.0 - is_odd) + upper * is_odd
    has_zo = upper * (1.0 - is_odd) + lower * is_odd
    xr, zf, pots, sems = scratch[3:]
    window = xr.shape[1] // 2
    early = xrs[0].shape[1] - 1
    copies = []
    for k, (target, pieces) in enumerate(((xr, xrs), (zf, zfs))):
        if parts == 1 and k == 1:
            zf = pieces[0]
            continue
        begin = 0 if parts == 1 else early - 8
        moved = [
            (pieces[0].at[:, pl.ds(early, 1)], pots.at[k]),
            (
                pieces[0].at[:, pl.ds(begin, early - begin)],
                target.at[:, pl.ds(begin, early - begin)],
            ),
        ]
        if parts > 1:
            later = target.shape[1] - early
            moved.append((pieces[1].at[:, pl.ds(0, later)], target.at[:, pl.ds(early, later)]))
        copies += [
            pltpu.make_async_copy(source, goal, sems.at[3 * k + i])
            for i, (source, goal) in enumerate(moved)
        ]
    for copy in copies:
        copy.start()

    def fill(c, block):
        lines[c - 1] = block
        even, odd = (lines[c - 1, pl.ds(k, half, stride=2)] for k in range(2))
        whole = [a[:, :width] + a[:, 64 : 64 + width] for a in (even, odd)]
        diagonals[c - 1] = jnp.concatenate(whole, axis=1)

    for c in (2, 3):
        fill(c, potential_block(p_own[(c % 2) ^ x]))
    fill(6, zo[x, zo.shape[1] - 1].astype(F32))
    for copy in copies:
        copy.wait()
    for c in (1, 4, 5):
        if parts == 1 and c == 1:
            fill(c, zf[(c % 2) ^ x, early].astype(F32))
        else:
            fill(c, pots[1 if c < 2 else 0, (c % 2) ^ x, 0].astype(F32))

    here = neighbour_sum(width, True)
    i = lax.broadcasted_iota(jnp.int32, (cells, cells), 0)
    diagonal = i == lax.broadcasted_iota(jnp.int32, (cells, cells), 1)

    def local(c, p):
        u = diagonals[c - 1, pl.ds(base // 2 + p, 1)]
        return jnp.where(diagonal, u, here).astype(BF16)

    def rows_of(c, w, n):
        plane = (c % 2) ^ x
        if c in (2, 3):
            return own[plane, pl.ds(base + w, n)]
        ref = zf if c < 2 else (xr if c < 6 else zo)
        return ref[plane, pl.ds(w, n)]

    def applied(pair, outer, zs, matrix):
        near = jnp.dot(matrix, pair, preferred_element_type=F32)
        return near - 0.125 * (outer + zs)

    def step1(j, carry):
        p = start // 2 + x + j - 1
        q = jnp.clip(p, 0, window - 1)
        has_below = inside(p - 1, window)
        has_above = inside(p + 1, window)
        valid = inside(p, window)
        below = jnp.maximum(2 * q - 1, 0)
        above = jnp.minimum(2 * q + 2, 2 * window - 1)
        pair = [rows_of(c, 2 * q, 2).reshape(cells, orbs) for c in range(8)]
        vs = [v.astype(F32) for v in pair]
        for c in range(1, 7):
            outer = jnp.concatenate(
                [
                    rows_of(c, below, 1)[0].astype(F32) * has_below,
                    rows_of(c, above, 1)[0].astype(F32) * has_above,
                ],
                axis=0,
            )
            f = applied(pair[c], outer, vs[c - 1] + vs[c + 1], local(c, q))
            keep = valid
            if c == 1:
                keep = valid * has_zf
            if c == 6:
                keep = valid * has_zo
            first[c - 1, pl.ds(2 * j, 2)] = (f * keep).astype(BF16).reshape(2, width, orbs)
        return carry

    lax.fori_loop(0, rows // 2 + 2, step1, 0)

    def step2(j, carry):
        p = start // 2 + x + j
        pair = [first[c - 1, pl.ds(2 * j + 2, 2)].reshape(cells, orbs) for c in range(1, 7)]
        vs = [v.astype(F32) for v in pair]
        for c in range(2, 6):
            outer = jnp.concatenate(
                [first[c - 1, 2 * j + 1].astype(F32), first[c - 1, 2 * j + 4].astype(F32)], axis=0
            )
            f = applied(pair[c - 1], outer, vs[c - 2] + vs[c], local(c, p))
            f = f.astype(BF16).reshape(2, width, orbs)
            plane = (c % 2) ^ x
            if joint:
                outs[0][plane + (2 if c in (2, 3) else 0), pl.ds(2 * j, 2)] = f
            else:
                outs[1 if c in (2, 3) else 0][plane, pl.ds(2 * j, 2)] = f
        return carry

    lax.fori_loop(0, rows // 2, step2, 0)


def filtered(slabs, start, rows, joint, operands, xrs, zfs):
    own = operands[0]
    planes, _, width, orbs = own.shape
    parts = len(xrs)
    shape = (2 * planes if joint else planes, rows, width, orbs)
    out = (jax.ShapeDtypeStruct(shape, BF16),) * (1 if joint else 2)
    cells = 10 * rows * width
    scratch = [
        pltpu.VMEM((6, rows + 4, width, orbs), BF16),
        pltpu.VMEM((6, width, orbs), F32),
        pltpu.VMEM((6, own.shape[1] // 2, 2 * width), F32),
    ]
    window = own.shape[1] // 2 + 2 if parts > 1 else xrs[0].shape[1] - 1
    scratch += [pltpu.VMEM((planes, window, width, orbs), BF16)] * 2
    scratch += [pltpu.VMEM((2, planes, 1, width, orbs), BF16), pltpu.SemaphoreType.DMA((6,))]
    local = pl.BlockSpec(memory_space=pltpu.VMEM)
    distant = pl.BlockSpec(memory_space=pltpu.MemorySpace.HBM)
    far_xr = [pltpu.with_memory_space_constraint(a, pltpu.MemorySpace.HBM) for a in xrs]
    far_zf = [pltpu.with_memory_space_constraint(a, pltpu.MemorySpace.HBM) for a in zfs]
    xrs, zfs = far_xr, (far_zf if parts > 1 else zfs)
    return pl.pallas_call(
        functools.partial(filter_kernel, slabs, start, parts, joint),
        out_shape=out,
        in_specs=[local] * len(operands)
        + [distant] * parts
        + [distant if parts > 1 else local] * parts,
        out_specs=(local,) * len(out),
        scratch_shapes=scratch,
        compiler_params=params(),
        cost_estimate=cost(2 * cells * 32 * orbs, FILTER * cells * orbs * 4),
        name="filtered",
    )(*operands, *xrs, *zfs)


def rotate_kernel(group, *refs):
    a, b, c, d, q = refs[:5]
    outs = refs[5:]
    _, rows, width, orbs = a.shape
    planes = outs[0].shape[0]
    low = jnp.concatenate([q[0], q[1]], axis=0)
    high = jnp.concatenate([q[2], q[3]], axis=0)

    def one(j, carry):
        for plane in range(a.shape[0]):
            def take(ref):
                return ref[plane, pl.ds(group * j, group)].reshape(group * width, orbs)

            total = jnp.dot(
                jnp.concatenate([take(a), take(b)], axis=1), low, preferred_element_type=F32
            )
            total = total + jnp.dot(
                jnp.concatenate([take(c), take(d)], axis=1), high, preferred_element_type=F32
            )
            outs[plane // planes][plane % planes, pl.ds(group * j, group)] = total.astype(
                BF16
            ).reshape(group, width, orbs)
        return carry

    lax.fori_loop(0, rows // group, one, 0)


def rotated(blocks, q, pieces):
    a = blocks[0]
    size = a.size
    group = max(g for g in range(1, 9) if a.shape[1] % g == 0)
    out = jax.ShapeDtypeStruct((a.shape[0] // pieces, *a.shape[1:]), BF16)
    return pl.pallas_call(
        functools.partial(rotate_kernel, group),
        out_shape=(out,) * pieces,
        in_specs=[pl.BlockSpec(memory_space=pltpu.VMEM)] * 5,
        out_specs=(pl.BlockSpec(memory_space=pltpu.VMEM),) * pieces,
        compiler_params=params(),
        cost_estimate=cost(8 * size * a.shape[3], 10 * size),
        name="rotated",
    )(*blocks, q)


def assemble_kernel(group, term, keep1, got1, got2, a, b, c, d, q, out):
    half = term.shape[1] // 2
    width, orbs = term.shape[2:]
    x = lax.rem(lax.axis_index("space"), 2)
    rows1, rows2 = keep1.shape[1], got2.shape[1]
    for ref, at in (
        (keep1, half * x),
        (got1, half * (1 - x)),
        (got2, half * (1 - x) + rows1),
    ):
        where = pl.ds(at, ref.shape[1])
        out[:, where] = (ref[...].astype(F32) + term[:, where]).astype(BF16)
    low = jnp.concatenate([q[0], q[1]], axis=0)
    high = jnp.concatenate([q[2], q[3]], axis=0)

    def one(j, carry):
        where = pl.ds(half * x + rows1 + group * j, group)
        for plane in range(a.shape[0]):
            def take(ref):
                return ref[plane, pl.ds(group * j, group)].reshape(group * width, orbs)

            total = jnp.dot(
                jnp.concatenate([take(a), take(b)], axis=1), low, preferred_element_type=F32
            )
            total = total + jnp.dot(
                jnp.concatenate([take(c), take(d)], axis=1), high, preferred_element_type=F32
            )
            total = total.reshape(group, width, orbs) + term[plane, where]
            out[plane, where] = total.astype(BF16)
        return carry

    lax.fori_loop(0, rows2 // group, one, 0)


def assembled(term, keep1, got1, got2, blocks, q):
    group = max(g for g in range(1, 9) if got2.shape[1] % g == 0)
    return pl.pallas_call(
        functools.partial(assemble_kernel, group),
        out_shape=jax.ShapeDtypeStruct(term.shape, BF16),
        in_specs=[pl.BlockSpec(memory_space=pltpu.VMEM)] * 9,
        out_specs=pl.BlockSpec(memory_space=pltpu.VMEM),
        compiler_params=params(),
        cost_estimate=cost(4096, 4096),
        name="assembled",
    )(term, keep1, got1, got2, *blocks, q)


def ordered(*arrays):
    return lax.optimization_barrier(arrays)


def shards(psi, potential, beta, strength, atom_slab, pattern, q_tiles):
    planes, width_x, width_y, orbs = psi.shape
    count = beta.shape[0]
    slabs = lax.axis_size("space")
    place = lax.axis_index("space")
    x = lax.rem(place, 2)
    half = width_x // 2
    window = half + 2
    rows1 = half * 7 // 24 * 2
    rows2 = half - rows1
    early = rows1 + 4

    def within(pairs):
        return [(i, j) for i, j in pairs if 0 <= j < slabs]

    swap = [(i, i ^ 1) for i in range(slabs)]
    own_way = within([(i, i + 2 if i % 2 else i - 2) for i in range(slabs)])
    other_way = within([(i, i - 2 if i % 2 else i + 2) for i in range(slabs)])
    groups = lax.axis_size("orb")
    across = [(i, i ^ 2) for i in range(groups)]
    beside = [(i, i ^ 1) for i in range(groups)]
    mine = (half - 2) * x
    theirs = (half - 2) * (1 - x)

    to_x, to_z = prepared(psi, potential, early)
    to_x2, far, near = packed(psi, beta, early)
    f_x = lax.ppermute(near, "space", swap)
    raster = within([(i, i + 1 if i % 2 else i - 1) for i in range(slabs)])
    f_d = lax.ppermute(far, "space", raster)
    xr1 = lax.ppermute(to_x, "space", swap)
    zo = lax.ppermute(to_z, "space", own_way)
    active = jnp.abs(place - atom_slab) <= 1
    beta_m = jnp.where(active[:, None, None, None], beta, jnp.zeros_like(beta))
    gram = jnp.einsum("pzxy,qzxy->pq", beta_m, beta_m, preferred_element_type=F32)
    xr1, second = ordered(xr1, to_x2)
    zf1 = lax.ppermute(xr1, "space", other_way)
    xr2 = lax.ppermute(second, "space", swap)
    zf2 = lax.ppermute(xr2, "space", other_way)
    strong = jnp.broadcast_to(strength[:, None], (count, orbs))

    sums, weights = partials(count, atom_slab, psi, beta, f_x, f_d, potential, gram)
    zf1, sums, _ = ordered(zf1, sums, xr2)
    operands = (psi, potential, zo)
    (block1,) = filtered(slabs, 0, rows1, True, operands, (xr1,), (zf1,))
    y1 = lax.ppermute(block1, "orb", across)
    rounds = [1 << k for k in range((slabs - 1).bit_length())]

    def added(values, step):
        pairs = [(i, i ^ step) for i in range(slabs)]
        return values + lax.ppermute(values, "space", pairs)

    for step in rounds[:1]:
        sums = added(sums, step)
    zf2, sums = ordered(zf2, sums)
    give2, keep2 = filtered(slabs, rows1, rows2, False, operands, (xr1, xr2), (zf1, zf2))
    pattern, q_tiles, _ = ordered(pattern, q_tiles, give2)
    me = lax.axis_index("orb")
    which = jnp.bitwise_xor(me, jnp.arange(groups, dtype=jnp.int32))
    rows_hot = (pattern[:, 0][:, None] == which[None, :]).astype(BF16)
    rows_hot = rows_hot * (pattern[:, 1] == me).astype(BF16)[:, None]
    q = jnp.einsum("ki,kab->iab", rows_hot, q_tiles, preferred_element_type=F32).astype(BF16)
    cg = lax.ppermute(give2, "orb", beside)
    ck = lax.ppermute(keep2, "orb", beside)
    yg = lax.ppermute(give2, "orb", across)
    for step in rounds[1:2]:
        sums = added(sums, step)
    y1, again, _, sums = ordered(y1, block1, give2, sums)
    c1 = lax.ppermute(again, "orb", beside)
    yc1 = lax.ppermute(y1, "orb", beside)
    give1, keep1 = rotated((block1, c1, y1, yc1), q, 2)
    got1 = lax.ppermute(give1, "space", swap)
    keep_y, yg, _, sums = ordered(keep2, yg, give1, sums)
    for step in rounds[2:]:
        sums = added(sums, step)
    yk = lax.ppermute(keep_y, "orb", across)
    ycg = lax.ppermute(yg, "orb", beside)
    ycg, sums = ordered(ycg, sums)
    coefs = coefficients(sums, strong)
    coefs = jnp.concatenate([coefs, lax.ppermute(coefs, "orb", beside)], axis=0)
    (give2,) = rotated((give2, cg, yg, ycg), q, 1)
    got2 = lax.ppermute(give2, "space", swap)
    coefs, _ = ordered(coefs, give2)
    coefs_y = lax.ppermute(coefs, "orb", across)
    coefs = [half_of[k * 2 * count : (k + 1) * 2 * count] for half_of in (coefs, coefs_y) for k in (0, 1)]
    term = nonlocal_term(psi.shape, coefs, q, weights)
    yk, _, got1 = ordered(yk, give2, got1)
    yck = lax.ppermute(yk, "orb", beside)
    return assembled(term, keep1, got1, got2, (keep2, ck, yk, yck), q)


def solution(mesh):
    placed = (
        P("space", None, None, "orb"),
        P("space", None, None),
        P(None, "space", None, None),
        P(),
        P(),
        P(),
        P(),
    )
    return jax.shard_map(
        shards, mesh=mesh, in_specs=placed, out_specs=P("space", None, None, "orb"), check_vma=False
    )
```

```python
import functools

import jax
import jax.numpy as jnp
from jax import lax
from jax.experimental import pallas as pl
from jax.experimental.pallas import tpu as pltpu
from jax.sharding import PartitionSpec as P

F32 = jnp.float32
BF16 = jnp.bfloat16
VMEM_LIMIT = 24 * 1024 * 1024
SHRINK = 16
FILTER = 100


def params():
    return pltpu.CompilerParams(vmem_limit_bytes=VMEM_LIMIT)


def cost(flops, moved):
    return pl.CostEstimate(flops=flops // SHRINK, bytes_accessed=moved // SHRINK, transcendentals=0)


def inside(p, window):
    return jnp.logical_and(p >= 0, p < window).astype(F32)


def neighbour_sum(width, pairs):
    n = (2 if pairs else 1) * width
    i = lax.broadcasted_iota(jnp.int32, (n, n), 0)
    j = lax.broadcasted_iota(jnp.int32, (n, n), 1)
    linked = jnp.abs(i - j) == 1
    if pairs:
        linked = jnp.logical_and(linked, (i < width) == (j < width))
        linked = jnp.logical_or(linked, jnp.abs(i - j) == width)
    return jnp.where(linked, -0.125, 0.0)


def potential_block(potential):
    lines, width = potential.shape
    gap = jnp.zeros((lines, 64 - width), F32)
    u = (potential - 1.0) * 0.25
    hi = u.astype(BF16).astype(F32)
    return jnp.concatenate([hi, gap, u - hi, gap], axis=1)


def prepare_kernel(early, psi, potential_far, to_x, to_z, potential, sems):
    x = lax.rem(lax.axis_index("space"), 2)
    half = psi.shape[1] // 2
    window = half + 2
    mine, theirs = (half - 2) * x, (half - 2) * (1 - x)
    fetch = pltpu.make_async_copy(potential_far, potential, sems.at[0])
    fetch.start()
    copies = [
        pltpu.make_async_copy(
            psi.at[:, pl.ds(theirs, early)], to_x.at[:, pl.ds(0, early)], sems.at[1]
        ),
        pltpu.make_async_copy(
            psi.at[:, pl.ds(mine, window)], to_z.at[:, pl.ds(0, window)], sems.at[2]
        ),
    ]
    for copy in copies:
        copy.start()
    fetch.wait()
    for plane in range(potential.shape[0]):
        block = potential_block(potential[plane]).astype(BF16)
        to_x[plane, early] = block
        to_z[plane, window] = block
    for copy in copies:
        copy.wait()


def prepared(psi, potential, early):
    planes, width_x, width_y, orbs = psi.shape
    window = width_x // 2 + 2

    def out(rows):
        return jax.ShapeDtypeStruct((planes, rows, width_y, orbs), BF16)

    return pl.pallas_call(
        functools.partial(prepare_kernel, early),
        out_shape=(out(early + 1), out(window + 1)),
        in_specs=[pl.BlockSpec(memory_space=pltpu.MemorySpace.HBM)] * 2,
        out_specs=(pl.BlockSpec(memory_space=pltpu.VMEM),) * 2,
        scratch_shapes=[pltpu.VMEM(potential.shape, F32), pltpu.SemaphoreType.DMA((3,))],
        compiler_params=params(),
        cost_estimate=cost(4096, 4096),
        name="prepared",
    )(*(pltpu.with_memory_space_constraint(a, pltpu.MemorySpace.HBM) for a in (psi, potential)))


def pack_kernel(early, psi, beta, to_x2, far, near, sems):
    x = lax.rem(lax.axis_index("space"), 2)
    half = psi.shape[1] // 2
    later = half + 2 - early
    copies = [
        pltpu.make_async_copy(beta.at[:, 1 - x], near, sems.at[0]),
        pltpu.make_async_copy(beta.at[:, x], far, sems.at[1]),
        pltpu.make_async_copy(
            psi.at[:, pl.ds((half - 2) * (1 - x) + early, later)], to_x2, sems.at[2]
        ),
    ]
    for copy in copies:
        copy.start()
    for copy in copies:
        copy.wait()


def packed(psi, beta, early):
    planes, width_x, width_y, orbs = psi.shape
    side = jax.ShapeDtypeStruct((beta.shape[0], *beta.shape[2:]), BF16)
    later = width_x // 2 + 2 - early
    return pl.pallas_call(
        functools.partial(pack_kernel, early),
        out_shape=(jax.ShapeDtypeStruct((planes, later, width_y, orbs), BF16), side, side),
        in_specs=[pl.BlockSpec(memory_space=pltpu.MemorySpace.HBM)] * 2,
        out_specs=(pl.BlockSpec(memory_space=pltpu.VMEM),) * 3,
        scratch_shapes=[pltpu.SemaphoreType.DMA((3,))],
        compiler_params=params(),
        cost_estimate=cost(4096, 4096),
        name="packed",
    )(*(pltpu.with_memory_space_constraint(a, pltpu.MemorySpace.HBM) for a in (psi, beta)))


def partial_kernel(count, atoms, own, beta, b_x, b_d, potential, gram, out, weights_out, table, acc):
    place = lax.axis_index("space")
    x = lax.rem(place, 2)
    rows, width = potential.shape[1:]
    side = place ^ 1
    beyond = place - 1 + 2 * x
    tri = neighbour_sum(width, False).astype(BF16)
    acc[...] = jnp.zeros_like(acc)
    step = 8

    for k in range(2):
        plane = x if k == 0 else 1 - x
        outer, there = (b_d, beyond) if k == 0 else (b_x, side)
        u = (potential[plane] - 1.0) * 0.25

        def fill(i, carry):
            for j in range(step):
                p = i * step + j
                here = (jnp.abs(place - atoms[p]) <= 1).astype(F32)
                next_to = (jnp.abs(there - atoms[p]) <= 1).astype(F32)
                b32 = beta[p, plane].astype(F32) * here
                b = b32.astype(BF16)
                sides = beta[p, 1 - plane].astype(F32) * here + outer[p].astype(F32) * next_to
                whole = jnp.dot(b, tri, preferred_element_type=F32)
                whole = whole + jnp.dot(tri, b, preferred_element_type=F32)
                whole = whole + u * b32 - 0.125 * sides
                hi = whole.astype(BF16).astype(F32)
                for kind, value in enumerate((b32, hi, whole - hi)):
                    table[pl.ds((kind * count + p) * rows, rows)] = value
            return carry

        lax.fori_loop(0, count // step, fill, 0)

        def use(i, carry):
            totals = []
            for j in range(step):
                r = i * step + j
                weights = table[pl.ds(r, 3 * count, stride=rows)].astype(BF16)
                weights_out[plane, r] = weights
                totals.append(jnp.dot(weights, own[plane, r], preferred_element_type=F32))
            acc[...] += sum(totals[1:], totals[0])
            return carry

        lax.fori_loop(0, rows // step, use, 0)
    out[...] = jnp.zeros_like(out)
    out[0:count] = acc[0:count]
    out[count : 2 * count] = acc[count : 2 * count] + acc[2 * count : 3 * count]
    out[2 * count : 3 * count, 0:count] = gram[...]


def partials(count, atoms, own, beta, b_x, b_d, potential, gram):
    planes, rows, width, orbs = own.shape
    return pl.pallas_call(
        functools.partial(partial_kernel, count),
        out_shape=(
            jax.ShapeDtypeStruct((3 * count, orbs), F32),
            jax.ShapeDtypeStruct((planes, rows, 3 * count, width), BF16),
        ),
        in_specs=[pl.BlockSpec(memory_space=pltpu.SMEM)]
        + [pl.BlockSpec(memory_space=pltpu.VMEM)] * 6,
        out_specs=(pl.BlockSpec(memory_space=pltpu.VMEM),) * 2,
        scratch_shapes=[
            pltpu.VMEM((3 * count * rows, width), F32),
            pltpu.VMEM((3 * count, orbs), F32),
        ],
        compiler_params=params(),
        cost_estimate=cost(4096, 4096),
        name="partials",
    )(atoms, own, beta, b_x, b_d, potential, gram)


def coefficient_kernel(sums, strength, out):
    count, orbs = strength.shape
    coef1 = (strength[...] * sums[0:count]).astype(BF16)
    padded = coef1.astype(F32) * 0.25
    if orbs > count:
        padded = jnp.concatenate([padded, jnp.zeros((orbs - count, orbs), F32)], axis=0)
    proj2 = sums[count : 2 * count] + jnp.dot(
        sums[2 * count : 3 * count],
        padded,
        preferred_element_type=F32,
        precision=lax.Precision.HIGHEST,
    )
    out[0:count] = coef1
    out[count : 2 * count] = (strength[...] * proj2).astype(BF16)


def coefficients(sums, strength):
    count, orbs = strength.shape
    return pl.pallas_call(
        coefficient_kernel,
        out_shape=jax.ShapeDtypeStruct((2 * count, orbs), BF16),
        in_specs=[pl.BlockSpec(memory_space=pltpu.VMEM)] * 2,
        out_specs=pl.BlockSpec(memory_space=pltpu.VMEM),
        compiler_params=params(),
        cost_estimate=cost(4096, 4096),
        name="coefficients",
    )(sums, strength)


def nonlocal_kernel(unroll, a, b, c, d, q, weights, out):
    count, orbs = a.shape[0] // 2, a.shape[1]
    turned = sum(
        jnp.dot(ref[...], q[k], preferred_element_type=F32) for k, ref in enumerate((a, b, c, d))
    )
    turned = turned * 0.25
    one, two = turned[0:count], turned[count : 2 * count]
    right = jnp.concatenate([two, one, one], axis=0)
    hi = right.astype(BF16)
    lo = right - hi.astype(F32)
    right = jnp.concatenate([hi.astype(F32), lo], axis=1).astype(BF16)

    def step(i, carry):
        for k in range(unroll):
            r = i * unroll + k
            for plane in range(weights.shape[0]):
                both = lax.dot_general(
                    weights[plane, r], right, (((0,), (0,)), ((), ())), preferred_element_type=F32
                )
                out[plane, r] = both[:, :orbs] + both[:, orbs:]
        return carry

    lax.fori_loop(0, weights.shape[1] // unroll, step, 0)


def nonlocal_term(shape, coefs, q, weights):
    unroll = max(g for g in (1, 2, 4, 8) if weights.shape[1] % g == 0)
    return pl.pallas_call(
        functools.partial(nonlocal_kernel, unroll),
        out_shape=jax.ShapeDtypeStruct(shape, F32),
        in_specs=[pl.BlockSpec(memory_space=pltpu.VMEM)] * 6,
        out_specs=pl.BlockSpec(memory_space=pltpu.VMEM),
        compiler_params=params(),
        cost_estimate=cost(4096, 4096),
        name="nonlocal",
    )(*coefs, q, weights)


def filter_kernel(slabs, start, parts, joint, *refs):
    own, p_own, zo = refs[:3]
    xrs, zfs = refs[3 : 3 + parts], refs[3 + parts : 3 + 2 * parts]
    extra = 7
    outs, scratch = refs[3 + 2 * parts : -extra], refs[-extra:]
    first, lines, diagonals = scratch[:3]
    place = lax.axis_index("space")
    x = lax.rem(place, 2)
    width = own.shape[2]
    cells = 2 * width
    half = own.shape[1] // 2
    orbs = own.shape[3]
    rows = outs[0].shape[1]
    base = (half - 2) * x
    lower = (place >= 2).astype(F32)
    upper = (place < slabs - 2).astype(F32)
    is_odd = x.astype(F32)
    has_zf = lower * (1.0 - is_odd) + upper * is_odd
    has_zo = upper * (1.0 - is_odd) + lower * is_odd
    xr, zf, pots, sems = scratch[3:]
    window = xr.shape[1] // 2
    early = xrs[0].shape[1] - 1
    copies = []
    for k, (target, pieces) in enumerate(((xr, xrs), (zf, zfs))):
        if parts == 1 and k == 1:
            zf = pieces[0]
            continue
        begin = 0 if parts == 1 else early - 8
        moved = [
            (pieces[0].at[:, pl.ds(early, 1)], pots.at[k]),
            (
                pieces[0].at[:, pl.ds(begin, early - begin)],
                target.at[:, pl.ds(begin, early - begin)],
            ),
        ]
        if parts > 1:
            later = target.shape[1] - early
            moved.append((pieces[1].at[:, pl.ds(0, later)], target.at[:, pl.ds(early, later)]))
        copies += [
            pltpu.make_async_copy(source, goal, sems.at[3 * k + i])
            for i, (source, goal) in enumerate(moved)
        ]
    for copy in copies:
        copy.start()

    def fill(c, block):
        lines[c - 1] = block
        even, odd = (lines[c - 1, pl.ds(k, half, stride=2)] for k in range(2))
        whole = [a[:, :width] + a[:, 64 : 64 + width] for a in (even, odd)]
        diagonals[c - 1] = jnp.concatenate(whole, axis=1)

    for c in (2, 3):
        fill(c, potential_block(p_own[(c % 2) ^ x]))
    fill(6, zo[x, zo.shape[1] - 1].astype(F32))
    for copy in copies:
        copy.wait()
    for c in (1, 4, 5):
        if parts == 1 and c == 1:
            fill(c, zf[(c % 2) ^ x, early].astype(F32))
        else:
            fill(c, pots[1 if c < 2 else 0, (c % 2) ^ x, 0].astype(F32))

    here = neighbour_sum(width, True)
    i = lax.broadcasted_iota(jnp.int32, (cells, cells), 0)
    diagonal = i == lax.broadcasted_iota(jnp.int32, (cells, cells), 1)

    def local(c, p):
        u = diagonals[c - 1, pl.ds(base // 2 + p, 1)]
        return jnp.where(diagonal, u, here).astype(BF16)

    def rows_of(c, w, n):
        plane = (c % 2) ^ x
        if c in (2, 3):
            return own[plane, pl.ds(base + w, n)]
        ref = zf if c < 2 else (xr if c < 6 else zo)
        return ref[plane, pl.ds(w, n)]

    def applied(pair, outer, zs, matrix):
        near = jnp.dot(matrix, pair, preferred_element_type=F32)
        return near - 0.125 * (outer + zs)

    def step1(j, carry):
        p = start // 2 + x + j - 1
        q = jnp.clip(p, 0, window - 1)
        has_below = inside(p - 1, window)
        has_above = inside(p + 1, window)
        valid = inside(p, window)
        below = jnp.maximum(2 * q - 1, 0)
        above = jnp.minimum(2 * q + 2, 2 * window - 1)
        pair = [rows_of(c, 2 * q, 2).reshape(cells, orbs) for c in range(8)]
        vs = [v.astype(F32) for v in pair]
        for c in range(1, 7):
            outer = jnp.concatenate(
                [
                    rows_of(c, below, 1)[0].astype(F32) * has_below,
                    rows_of(c, above, 1)[0].astype(F32) * has_above,
                ],
                axis=0,
            )
            f = applied(pair[c], outer, vs[c - 1] + vs[c + 1], local(c, q))
            keep = valid
            if c == 1:
                keep = valid * has_zf
            if c == 6:
                keep = valid * has_zo
            first[c - 1, pl.ds(2 * j, 2)] = (f * keep).astype(BF16).reshape(2, width, orbs)
        return carry

    lax.fori_loop(0, rows // 2 + 2, step1, 0)

    def step2(j, carry):
        p = start // 2 + x + j
        pair = [first[c - 1, pl.ds(2 * j + 2, 2)].reshape(cells, orbs) for c in range(1, 7)]
        vs = [v.astype(F32) for v in pair]
        for c in range(2, 6):
            outer = jnp.concatenate(
                [first[c - 1, 2 * j + 1].astype(F32), first[c - 1, 2 * j + 4].astype(F32)], axis=0
            )
            f = applied(pair[c - 1], outer, vs[c - 2] + vs[c], local(c, p))
            f = f.astype(BF16).reshape(2, width, orbs)
            plane = (c % 2) ^ x
            if joint:
                outs[0][plane + (2 if c in (2, 3) else 0), pl.ds(2 * j, 2)] = f
            else:
                outs[1 if c in (2, 3) else 0][plane, pl.ds(2 * j, 2)] = f
        return carry

    lax.fori_loop(0, rows // 2, step2, 0)


def filtered(slabs, start, rows, joint, operands, xrs, zfs):
    own = operands[0]
    planes, _, width, orbs = own.shape
    parts = len(xrs)
    shape = (2 * planes if joint else planes, rows, width, orbs)
    out = (jax.ShapeDtypeStruct(shape, BF16),) * (1 if joint else 2)
    cells = 10 * rows * width
    scratch = [
        pltpu.VMEM((6, rows + 4, width, orbs), BF16),
        pltpu.VMEM((6, width, orbs), F32),
        pltpu.VMEM((6, own.shape[1] // 2, 2 * width), F32),
    ]
    window = own.shape[1] // 2 + 2 if parts > 1 else xrs[0].shape[1] - 1
    scratch += [pltpu.VMEM((planes, window, width, orbs), BF16)] * 2
    scratch += [pltpu.VMEM((2, planes, 1, width, orbs), BF16), pltpu.SemaphoreType.DMA((6,))]
    local = pl.BlockSpec(memory_space=pltpu.VMEM)
    distant = pl.BlockSpec(memory_space=pltpu.MemorySpace.HBM)
    far_xr = [pltpu.with_memory_space_constraint(a, pltpu.MemorySpace.HBM) for a in xrs]
    far_zf = [pltpu.with_memory_space_constraint(a, pltpu.MemorySpace.HBM) for a in zfs]
    xrs, zfs = far_xr, (far_zf if parts > 1 else zfs)
    return pl.pallas_call(
        functools.partial(filter_kernel, slabs, start, parts, joint),
        out_shape=out,
        in_specs=[local] * len(operands)
        + [distant] * parts
        + [distant if parts > 1 else local] * parts,
        out_specs=(local,) * len(out),
        scratch_shapes=scratch,
        compiler_params=params(),
        cost_estimate=cost(2 * cells * 32 * orbs, FILTER * cells * orbs * 4),
        name="filtered",
    )(*operands, *xrs, *zfs)


def rotate_kernel(group, *refs):
    a, b, c, d, q = refs[:5]
    outs = refs[5:]
    _, rows, width, orbs = a.shape
    planes = outs[0].shape[0]
    low = jnp.concatenate([q[0], q[1]], axis=0)
    high = jnp.concatenate([q[2], q[3]], axis=0)

    def one(j, carry):
        for plane in range(a.shape[0]):
            def take(ref):
                return ref[plane, pl.ds(group * j, group)].reshape(group * width, orbs)

            total = jnp.dot(
                jnp.concatenate([take(a), take(b)], axis=1), low, preferred_element_type=F32
            )
            total = total + jnp.dot(
                jnp.concatenate([take(c), take(d)], axis=1), high, preferred_element_type=F32
            )
            outs[plane // planes][plane % planes, pl.ds(group * j, group)] = total.astype(
                BF16
            ).reshape(group, width, orbs)
        return carry

    lax.fori_loop(0, rows // group, one, 0)


def rotated(blocks, q, pieces):
    a = blocks[0]
    size = a.size
    group = max(g for g in range(1, 9) if a.shape[1] % g == 0)
    out = jax.ShapeDtypeStruct((a.shape[0] // pieces, *a.shape[1:]), BF16)
    return pl.pallas_call(
        functools.partial(rotate_kernel, group),
        out_shape=(out,) * pieces,
        in_specs=[pl.BlockSpec(memory_space=pltpu.VMEM)] * 5,
        out_specs=(pl.BlockSpec(memory_space=pltpu.VMEM),) * pieces,
        compiler_params=params(),
        cost_estimate=cost(8 * size * a.shape[3], 10 * size),
        name="rotated",
    )(*blocks, q)


def assemble_kernel(group, term, keep1, got1, a, b, c, d, q, out):
    half = term.shape[1] // 2
    width, orbs = term.shape[2:]
    x = lax.rem(lax.axis_index("space"), 2)
    rows1, rows2 = keep1.shape[1], a.shape[1]
    for ref, at in ((keep1, half * x), (got1, half * (1 - x))):
        where = pl.ds(at, ref.shape[1])
        out[:, where] = (ref[...].astype(F32) + term[:, where]).astype(BF16)
    low = jnp.concatenate([q[0], q[1]], axis=0)
    high = jnp.concatenate([q[2], q[3]], axis=0)

    def one(j, carry):
        where = pl.ds(half * x + rows1 + group * j, group)
        for plane in range(a.shape[0]):
            def take(ref):
                return ref[plane, pl.ds(group * j, group)].reshape(group * width, orbs)

            total = jnp.dot(
                jnp.concatenate([take(a), take(b)], axis=1), low, preferred_element_type=F32
            )
            total = total + jnp.dot(
                jnp.concatenate([take(c), take(d)], axis=1), high, preferred_element_type=F32
            )
            total = total.reshape(group, width, orbs) + term[plane, where]
            out[plane, where] = total.astype(BF16)
        return carry

    lax.fori_loop(0, rows2 // group, one, 0)


def finish_kernel(rows1, term, got2, before, out, rows, sem):
    half = term.shape[1] // 2
    x = lax.rem(lax.axis_index("space"), 2)
    where = pl.ds(half * (1 - x) + rows1, got2.shape[1])
    rows[...] = (got2[...].astype(F32) + term[:, where]).astype(BF16)
    copy = pltpu.make_async_copy(rows, out.at[:, where], sem)
    copy.start()
    copy.wait()


def assembled(term, keep1, got1, got2, blocks, q):
    group = max(g for g in range(1, 9) if got2.shape[1] % g == 0)
    most = pl.pallas_call(
        functools.partial(assemble_kernel, group),
        out_shape=jax.ShapeDtypeStruct(term.shape, BF16),
        in_specs=[pl.BlockSpec(memory_space=pltpu.VMEM)] * 8,
        out_specs=pl.BlockSpec(memory_space=pltpu.VMEM),
        compiler_params=params(),
        cost_estimate=cost(4096, 4096),
        name="assembled",
    )(term, keep1, got1, *blocks, q)
    local = pl.BlockSpec(memory_space=pltpu.VMEM)
    distant = pl.BlockSpec(memory_space=pltpu.MemorySpace.HBM)
    return pl.pallas_call(
        functools.partial(finish_kernel, keep1.shape[1]),
        out_shape=jax.ShapeDtypeStruct(term.shape, BF16),
        in_specs=[local, local, distant],
        out_specs=distant,
        input_output_aliases={2: 0},
        scratch_shapes=[pltpu.VMEM(got2.shape, BF16), pltpu.SemaphoreType.DMA],
        compiler_params=params(),
        cost_estimate=cost(4096, 4096),
        name="finished",
    )(term, got2, pltpu.with_memory_space_constraint(most, pltpu.MemorySpace.HBM))


def ordered(*arrays):
    return lax.optimization_barrier(arrays)


def shards(psi, potential, beta, strength, atom_slab, pattern, q_tiles):
    planes, width_x, width_y, orbs = psi.shape
    count = beta.shape[0]
    slabs = lax.axis_size("space")
    place = lax.axis_index("space")
    x = lax.rem(place, 2)
    half = width_x // 2
    window = half + 2
    rows1 = half * 7 // 24 * 2
    rows2 = half - rows1
    early = rows1 + 4

    def within(pairs):
        return [(i, j) for i, j in pairs if 0 <= j < slabs]

    swap = [(i, i ^ 1) for i in range(slabs)]
    own_way = within([(i, i + 2 if i % 2 else i - 2) for i in range(slabs)])
    other_way = within([(i, i - 2 if i % 2 else i + 2) for i in range(slabs)])
    groups = lax.axis_size("orb")
    across = [(i, i ^ 2) for i in range(groups)]
    beside = [(i, i ^ 1) for i in range(groups)]
    mine = (half - 2) * x
    theirs = (half - 2) * (1 - x)

    to_x, to_z = prepared(psi, potential, early)
    to_x2, far, near = packed(psi, beta, early)
    f_x = lax.ppermute(near, "space", swap)
    raster = within([(i, i + 1 if i % 2 else i - 1) for i in range(slabs)])
    f_d = lax.ppermute(far, "space", raster)
    xr1 = lax.ppermute(to_x, "space", swap)
    zo = lax.ppermute(to_z, "space", own_way)
    active = jnp.abs(place - atom_slab) <= 1
    beta_m = jnp.where(active[:, None, None, None], beta, jnp.zeros_like(beta))
    gram = jnp.einsum("pzxy,qzxy->pq", beta_m, beta_m, preferred_element_type=F32)
    xr1, second = ordered(xr1, to_x2)
    zf1 = lax.ppermute(xr1, "space", other_way)
    xr2 = lax.ppermute(second, "space", swap)
    zf2 = lax.ppermute(xr2, "space", other_way)
    strong = jnp.broadcast_to(strength[:, None], (count, orbs))

    sums, weights = partials(count, atom_slab, psi, beta, f_x, f_d, potential, gram)
    zf1, sums, _ = ordered(zf1, sums, xr2)
    operands = (psi, potential, zo)
    (block1,) = filtered(slabs, 0, rows1, True, operands, (xr1,), (zf1,))
    y1 = lax.ppermute(block1, "orb", across)
    rounds = [1 << k for k in range((slabs - 1).bit_length())]

    def added(values, step):
        pairs = [(i, i ^ step) for i in range(slabs)]
        return values + lax.ppermute(values, "space", pairs)

    for step in rounds[:1]:
        sums = added(sums, step)
    zf2, sums = ordered(zf2, sums)
    give2, keep2 = filtered(slabs, rows1, rows2, False, operands, (xr1, xr2), (zf1, zf2))
    pattern, q_tiles, _ = ordered(pattern, q_tiles, give2)
    me = lax.axis_index("orb")
    which = jnp.bitwise_xor(me, jnp.arange(groups, dtype=jnp.int32))
    rows_hot = (pattern[:, 0][:, None] == which[None, :]).astype(BF16)
    rows_hot = rows_hot * (pattern[:, 1] == me).astype(BF16)[:, None]
    q = jnp.einsum("ki,kab->iab", rows_hot, q_tiles, preferred_element_type=F32).astype(BF16)
    cg = lax.ppermute(give2, "orb", beside)
    ck = lax.ppermute(keep2, "orb", beside)
    yg = lax.ppermute(give2, "orb", across)
    for step in rounds[1:2]:
        sums = added(sums, step)
    y1, again, _, sums = ordered(y1, block1, give2, sums)
    c1 = lax.ppermute(again, "orb", beside)
    yc1 = lax.ppermute(y1, "orb", beside)
    for step in rounds[2:]:
        sums = added(sums, step)
    yc1, sums = ordered(yc1, sums)
    give1, keep1 = rotated((block1, c1, y1, yc1), q, 2)
    got1 = lax.ppermute(give1, "space", swap)
    keep_y, yg, _, sums = ordered(keep2, yg, give1, sums)
    yk = lax.ppermute(keep_y, "orb", across)
    ycg = lax.ppermute(yg, "orb", beside)
    coefs = coefficients(sums, strong)
    coefs = jnp.concatenate([coefs, lax.ppermute(coefs, "orb", beside)], axis=0)
    ycg, coefs = ordered(ycg, coefs)
    (give2,) = rotated((give2, cg, yg, ycg), q, 1)
    got2 = lax.ppermute(give2, "space", swap)
    coefs, _ = ordered(coefs, give2)
    coefs_y = lax.ppermute(coefs, "orb", across)
    coefs = [half_of[k * 2 * count : (k + 1) * 2 * count] for half_of in (coefs, coefs_y) for k in (0, 1)]
    term = nonlocal_term(psi.shape, coefs, q, weights)
    yk, _, got1 = ordered(yk, give2, got1)
    yck = lax.ppermute(yk, "orb", beside)
    return assembled(term, keep1, got1, got2, (keep2, ck, yk, yck), q)


def solution(mesh):
    placed = (
        P("space", None, None, "orb"),
        P("space", None, None),
        P(None, "space", None, None),
        P(),
        P(),
        P(),
        P(),
    )
    return jax.shard_map(
        shards, mesh=mesh, in_specs=placed, out_specs=P("space", None, None, "orb"), check_vma=False
    )
```

```python
import functools

import jax
import jax.numpy as jnp
from jax import lax
from jax.experimental import pallas as pl
from jax.experimental.pallas import tpu as pltpu
from jax.sharding import PartitionSpec as P

F32 = jnp.float32
BF16 = jnp.bfloat16
VMEM_LIMIT = 24 * 1024 * 1024
SHRINK = 16
FILTER = 100


def params():
    return pltpu.CompilerParams(vmem_limit_bytes=VMEM_LIMIT)


def cost(flops, moved):
    return pl.CostEstimate(flops=flops // SHRINK, bytes_accessed=moved // SHRINK, transcendentals=0)


def inside(p, window):
    return jnp.logical_and(p >= 0, p < window).astype(F32)


def neighbour_sum(width, pairs):
    n = (2 if pairs else 1) * width
    i = lax.broadcasted_iota(jnp.int32, (n, n), 0)
    j = lax.broadcasted_iota(jnp.int32, (n, n), 1)
    linked = jnp.abs(i - j) == 1
    if pairs:
        linked = jnp.logical_and(linked, (i < width) == (j < width))
        linked = jnp.logical_or(linked, jnp.abs(i - j) == width)
    return jnp.where(linked, -0.125, 0.0)


def potential_block(potential):
    lines, width = potential.shape
    gap = jnp.zeros((lines, 64 - width), F32)
    u = (potential - 1.0) * 0.25
    hi = u.astype(BF16).astype(F32)
    return jnp.concatenate([hi, gap, u - hi, gap], axis=1)


def prepare_kernel(early, psi, potential_far, to_x, to_z, potential, sems):
    x = lax.rem(lax.axis_index("space"), 2)
    half = psi.shape[1] // 2
    window = half + 2
    mine, theirs = (half - 2) * x, (half - 2) * (1 - x)
    fetch = pltpu.make_async_copy(potential_far, potential, sems.at[0])
    fetch.start()
    copies = [
        pltpu.make_async_copy(
            psi.at[:, pl.ds(theirs, early)], to_x.at[:, pl.ds(0, early)], sems.at[1]
        ),
        pltpu.make_async_copy(
            psi.at[:, pl.ds(mine, window)], to_z.at[:, pl.ds(0, window)], sems.at[2]
        ),
    ]
    for copy in copies:
        copy.start()
    fetch.wait()
    for plane in range(potential.shape[0]):
        block = potential_block(potential[plane]).astype(BF16)
        to_x[plane, early] = block
        to_z[plane, window] = block
    for copy in copies:
        copy.wait()


def prepared(psi, potential, early):
    planes, width_x, width_y, orbs = psi.shape
    window = width_x // 2 + 2

    def out(rows):
        return jax.ShapeDtypeStruct((planes, rows, width_y, orbs), BF16)

    return pl.pallas_call(
        functools.partial(prepare_kernel, early),
        out_shape=(out(early + 1), out(window + 1)),
        in_specs=[pl.BlockSpec(memory_space=pltpu.MemorySpace.HBM)] * 2,
        out_specs=(pl.BlockSpec(memory_space=pltpu.VMEM),) * 2,
        scratch_shapes=[pltpu.VMEM(potential.shape, F32), pltpu.SemaphoreType.DMA((3,))],
        compiler_params=params(),
        cost_estimate=cost(4096, 4096),
        name="prepared",
    )(*(pltpu.with_memory_space_constraint(a, pltpu.MemorySpace.HBM) for a in (psi, potential)))


def pack_kernel(early, psi, beta, to_x2, far, near, sems):
    x = lax.rem(lax.axis_index("space"), 2)
    half = psi.shape[1] // 2
    later = half + 2 - early
    copies = [
        pltpu.make_async_copy(beta.at[:, 1 - x], near, sems.at[0]),
        pltpu.make_async_copy(beta.at[:, x], far, sems.at[1]),
        pltpu.make_async_copy(
            psi.at[:, pl.ds((half - 2) * (1 - x) + early, later)], to_x2, sems.at[2]
        ),
    ]
    for copy in copies:
        copy.start()
    for copy in copies:
        copy.wait()


def packed(psi, beta, early):
    planes, width_x, width_y, orbs = psi.shape
    side = jax.ShapeDtypeStruct((beta.shape[0], *beta.shape[2:]), BF16)
    later = width_x // 2 + 2 - early
    return pl.pallas_call(
        functools.partial(pack_kernel, early),
        out_shape=(jax.ShapeDtypeStruct((planes, later, width_y, orbs), BF16), side, side),
        in_specs=[pl.BlockSpec(memory_space=pltpu.MemorySpace.HBM)] * 2,
        out_specs=(pl.BlockSpec(memory_space=pltpu.VMEM),) * 3,
        scratch_shapes=[pltpu.SemaphoreType.DMA((3,))],
        compiler_params=params(),
        cost_estimate=cost(4096, 4096),
        name="packed",
    )(*(pltpu.with_memory_space_constraint(a, pltpu.MemorySpace.HBM) for a in (psi, beta)))


def partial_kernel(count, atoms, own, beta, b_x, b_d, potential, gram, out, weights_out, table, acc):
    place = lax.axis_index("space")
    x = lax.rem(place, 2)
    rows, width = potential.shape[1:]
    side = place ^ 1
    beyond = place - 1 + 2 * x
    tri = neighbour_sum(width, False).astype(BF16)
    acc[...] = jnp.zeros_like(acc)
    step = 8

    for k in range(2):
        plane = x if k == 0 else 1 - x
        outer, there = (b_d, beyond) if k == 0 else (b_x, side)
        u = (potential[plane] - 1.0) * 0.25

        def fill(i, carry):
            for j in range(step):
                p = i * step + j
                here = (jnp.abs(place - atoms[p]) <= 1).astype(F32)
                next_to = (jnp.abs(there - atoms[p]) <= 1).astype(F32)
                b32 = beta[p, plane].astype(F32) * here
                b = b32.astype(BF16)
                sides = beta[p, 1 - plane].astype(F32) * here + outer[p].astype(F32) * next_to
                whole = jnp.dot(b, tri, preferred_element_type=F32)
                whole = whole + jnp.dot(tri, b, preferred_element_type=F32)
                whole = whole + u * b32 - 0.125 * sides
                hi = whole.astype(BF16).astype(F32)
                for kind, value in enumerate((b32, hi, whole - hi)):
                    table[pl.ds((kind * count + p) * rows, rows)] = value
            return carry

        lax.fori_loop(0, count // step, fill, 0)

        def use(i, carry):
            totals = []
            for j in range(step):
                r = i * step + j
                weights = table[pl.ds(r, 3 * count, stride=rows)].astype(BF16)
                weights_out[plane, r] = weights
                totals.append(jnp.dot(weights, own[plane, r], preferred_element_type=F32))
            acc[...] += sum(totals[1:], totals[0])
            return carry

        lax.fori_loop(0, rows // step, use, 0)
    out[...] = jnp.zeros_like(out)
    out[0:count] = acc[0:count]
    out[count : 2 * count] = acc[count : 2 * count] + acc[2 * count : 3 * count]
    out[2 * count : 3 * count, 0:count] = gram[...]


def partials(count, atoms, own, beta, b_x, b_d, potential, gram):
    planes, rows, width, orbs = own.shape
    return pl.pallas_call(
        functools.partial(partial_kernel, count),
        out_shape=(
            jax.ShapeDtypeStruct((3 * count, orbs), F32),
            jax.ShapeDtypeStruct((planes, rows, 3 * count, width), BF16),
        ),
        in_specs=[pl.BlockSpec(memory_space=pltpu.SMEM)]
        + [pl.BlockSpec(memory_space=pltpu.VMEM)] * 6,
        out_specs=(pl.BlockSpec(memory_space=pltpu.VMEM),) * 2,
        scratch_shapes=[
            pltpu.VMEM((3 * count * rows, width), F32),
            pltpu.VMEM((3 * count, orbs), F32),
        ],
        compiler_params=params(),
        cost_estimate=cost(4096, 4096),
        name="partials",
    )(atoms, own, beta, b_x, b_d, potential, gram)


def coefficient_kernel(sums, strength, out):
    count, orbs = strength.shape
    coef1 = (strength[...] * sums[0:count]).astype(BF16)
    padded = coef1.astype(F32) * 0.25
    if orbs > count:
        padded = jnp.concatenate([padded, jnp.zeros((orbs - count, orbs), F32)], axis=0)
    proj2 = sums[count : 2 * count] + jnp.dot(
        sums[2 * count : 3 * count],
        padded,
        preferred_element_type=F32,
        precision=lax.Precision.HIGHEST,
    )
    out[0:count] = coef1
    out[count : 2 * count] = (strength[...] * proj2).astype(BF16)


def coefficients(sums, strength):
    count, orbs = strength.shape
    return pl.pallas_call(
        coefficient_kernel,
        out_shape=jax.ShapeDtypeStruct((2 * count, orbs), BF16),
        in_specs=[pl.BlockSpec(memory_space=pltpu.VMEM)] * 2,
        out_specs=pl.BlockSpec(memory_space=pltpu.VMEM),
        compiler_params=params(),
        cost_estimate=cost(4096, 4096),
        name="coefficients",
    )(sums, strength)


def nonlocal_kernel(unroll, a, b, c, d, q, weights, out):
    count, orbs = a.shape[0] // 2, a.shape[1]
    turned = sum(
        jnp.dot(ref[...], q[k], preferred_element_type=F32) for k, ref in enumerate((a, b, c, d))
    )
    turned = turned * 0.25
    one, two = turned[0:count], turned[count : 2 * count]
    right = jnp.concatenate([two, one, one], axis=0)
    hi = right.astype(BF16)
    lo = right - hi.astype(F32)
    right = jnp.concatenate([hi.astype(F32), lo], axis=1).astype(BF16)

    def step(i, carry):
        for k in range(unroll):
            r = i * unroll + k
            for plane in range(weights.shape[0]):
                both = lax.dot_general(
                    weights[plane, r], right, (((0,), (0,)), ((), ())), preferred_element_type=F32
                )
                out[plane, r] = both[:, :orbs] + both[:, orbs:]
        return carry

    lax.fori_loop(0, weights.shape[1] // unroll, step, 0)


def nonlocal_term(shape, coefs, q, weights):
    unroll = max(g for g in (1, 2, 4, 8) if weights.shape[1] % g == 0)
    return pl.pallas_call(
        functools.partial(nonlocal_kernel, unroll),
        out_shape=jax.ShapeDtypeStruct(shape, F32),
        in_specs=[pl.BlockSpec(memory_space=pltpu.VMEM)] * 6,
        out_specs=pl.BlockSpec(memory_space=pltpu.VMEM),
        compiler_params=params(),
        cost_estimate=cost(4096, 4096),
        name="nonlocal",
    )(*coefs, q, weights)


def filter_kernel(slabs, start, parts, joint, *refs):
    own, p_own, zo = refs[:3]
    xrs, zfs = refs[3 : 3 + parts], refs[3 + parts : 3 + 2 * parts]
    extra = 7
    outs, scratch = refs[3 + 2 * parts : -extra], refs[-extra:]
    first, lines, diagonals = scratch[:3]
    place = lax.axis_index("space")
    x = lax.rem(place, 2)
    width = own.shape[2]
    cells = 2 * width
    half = own.shape[1] // 2
    orbs = own.shape[3]
    rows = outs[0].shape[1]
    base = (half - 2) * x
    lower = (place >= 2).astype(F32)
    upper = (place < slabs - 2).astype(F32)
    is_odd = x.astype(F32)
    has_zf = lower * (1.0 - is_odd) + upper * is_odd
    has_zo = upper * (1.0 - is_odd) + lower * is_odd
    xr, zf, pots, sems = scratch[3:]
    window = xr.shape[1] // 2
    early = xrs[0].shape[1] - 1
    copies = []
    for k, (target, pieces) in enumerate(((xr, xrs), (zf, zfs))):
        if parts == 1 and k == 1:
            zf = pieces[0]
            continue
        begin = 0 if parts == 1 else early - 8
        moved = [
            (pieces[0].at[:, pl.ds(early, 1)], pots.at[k]),
            (
                pieces[0].at[:, pl.ds(begin, early - begin)],
                target.at[:, pl.ds(begin, early - begin)],
            ),
        ]
        if parts > 1:
            later = target.shape[1] - early
            moved.append((pieces[1].at[:, pl.ds(0, later)], target.at[:, pl.ds(early, later)]))
        copies += [
            pltpu.make_async_copy(source, goal, sems.at[3 * k + i])
            for i, (source, goal) in enumerate(moved)
        ]
    for copy in copies:
        copy.start()

    def fill(c, block):
        lines[c - 1] = block
        even, odd = (lines[c - 1, pl.ds(k, half, stride=2)] for k in range(2))
        whole = [a[:, :width] + a[:, 64 : 64 + width] for a in (even, odd)]
        diagonals[c - 1] = jnp.concatenate(whole, axis=1)

    for c in (2, 3):
        fill(c, potential_block(p_own[(c % 2) ^ x]))
    fill(6, zo[x, zo.shape[1] - 1].astype(F32))
    for copy in copies:
        copy.wait()
    for c in (1, 4, 5):
        if parts == 1 and c == 1:
            fill(c, zf[(c % 2) ^ x, early].astype(F32))
        else:
            fill(c, pots[1 if c < 2 else 0, (c % 2) ^ x, 0].astype(F32))

    here = neighbour_sum(width, True)
    i = lax.broadcasted_iota(jnp.int32, (cells, cells), 0)
    diagonal = i == lax.broadcasted_iota(jnp.int32, (cells, cells), 1)

    def local(c, p):
        u = diagonals[c - 1, pl.ds(base // 2 + p, 1)]
        return jnp.where(diagonal, u, here).astype(BF16)

    def rows_of(c, w, n):
        plane = (c % 2) ^ x
        if c in (2, 3):
            return own[plane, pl.ds(base + w, n)]
        ref = zf if c < 2 else (xr if c < 6 else zo)
        return ref[plane, pl.ds(w, n)]

    def applied(pair, outer, zs, matrix):
        near = jnp.dot(matrix, pair, preferred_element_type=F32)
        return near - 0.125 * (outer + zs)

    def step1(j, carry):
        p = start // 2 + x + j - 1
        q = jnp.clip(p, 0, window - 1)
        has_below = inside(p - 1, window)
        has_above = inside(p + 1, window)
        valid = inside(p, window)
        below = jnp.maximum(2 * q - 1, 0)
        above = jnp.minimum(2 * q + 2, 2 * window - 1)
        pair = [rows_of(c, 2 * q, 2).reshape(cells, orbs) for c in range(8)]
        vs = [v.astype(F32) for v in pair]
        for c in range(1, 7):
            outer = jnp.concatenate(
                [
                    rows_of(c, below, 1)[0].astype(F32) * has_below,
                    rows_of(c, above, 1)[0].astype(F32) * has_above,
                ],
                axis=0,
            )
            f = applied(pair[c], outer, vs[c - 1] + vs[c + 1], local(c, q))
            keep = valid
            if c == 1:
                keep = valid * has_zf
            if c == 6:
                keep = valid * has_zo
            first[c - 1, pl.ds(2 * j, 2)] = (f * keep).astype(BF16).reshape(2, width, orbs)
        return carry

    lax.fori_loop(0, rows // 2 + 2, step1, 0)

    def step2(j, carry):
        p = start // 2 + x + j
        pair = [first[c - 1, pl.ds(2 * j + 2, 2)].reshape(cells, orbs) for c in range(1, 7)]
        vs = [v.astype(F32) for v in pair]
        for c in range(2, 6):
            outer = jnp.concatenate(
                [first[c - 1, 2 * j + 1].astype(F32), first[c - 1, 2 * j + 4].astype(F32)], axis=0
            )
            f = applied(pair[c - 1], outer, vs[c - 2] + vs[c], local(c, p))
            f = f.astype(BF16).reshape(2, width, orbs)
            plane = (c % 2) ^ x
            if joint:
                outs[0][plane + (2 if c in (2, 3) else 0), pl.ds(2 * j, 2)] = f
            else:
                outs[1 if c in (2, 3) else 0][plane, pl.ds(2 * j, 2)] = f
        return carry

    lax.fori_loop(0, rows // 2, step2, 0)


def filtered(slabs, start, rows, joint, operands, xrs, zfs):
    own = operands[0]
    planes, _, width, orbs = own.shape
    parts = len(xrs)
    shape = (2 * planes if joint else planes, rows, width, orbs)
    out = (jax.ShapeDtypeStruct(shape, BF16),) * (1 if joint else 2)
    cells = 10 * rows * width
    scratch = [
        pltpu.VMEM((6, rows + 4, width, orbs), BF16),
        pltpu.VMEM((6, width, orbs), F32),
        pltpu.VMEM((6, own.shape[1] // 2, 2 * width), F32),
    ]
    window = own.shape[1] // 2 + 2 if parts > 1 else xrs[0].shape[1] - 1
    scratch += [pltpu.VMEM((planes, window, width, orbs), BF16)] * 2
    scratch += [pltpu.VMEM((2, planes, 1, width, orbs), BF16), pltpu.SemaphoreType.DMA((6,))]
    local = pl.BlockSpec(memory_space=pltpu.VMEM)
    distant = pl.BlockSpec(memory_space=pltpu.MemorySpace.HBM)
    far_xr = [pltpu.with_memory_space_constraint(a, pltpu.MemorySpace.HBM) for a in xrs]
    far_zf = [pltpu.with_memory_space_constraint(a, pltpu.MemorySpace.HBM) for a in zfs]
    xrs, zfs = far_xr, (far_zf if parts > 1 else zfs)
    return pl.pallas_call(
        functools.partial(filter_kernel, slabs, start, parts, joint),
        out_shape=out,
        in_specs=[local] * len(operands)
        + [distant] * parts
        + [distant if parts > 1 else local] * parts,
        out_specs=(local,) * len(out),
        scratch_shapes=scratch,
        compiler_params=params(),
        cost_estimate=cost(2 * cells * 32 * orbs, FILTER * cells * orbs * 4),
        name="filtered",
    )(*operands, *xrs, *zfs)


def rotate_kernel(group, *refs):
    a, b, c, d, q = refs[:5]
    outs = refs[5:]
    _, rows, width, orbs = a.shape
    planes = outs[0].shape[0]
    low = jnp.concatenate([q[0], q[1]], axis=0)
    high = jnp.concatenate([q[2], q[3]], axis=0)

    def one(j, carry):
        for plane in range(a.shape[0]):
            def take(ref):
                return ref[plane, pl.ds(group * j, group)].reshape(group * width, orbs)

            total = jnp.dot(
                jnp.concatenate([take(a), take(b)], axis=1), low, preferred_element_type=F32
            )
            total = total + jnp.dot(
                jnp.concatenate([take(c), take(d)], axis=1), high, preferred_element_type=F32
            )
            outs[plane // planes][plane % planes, pl.ds(group * j, group)] = total.astype(
                BF16
            ).reshape(group, width, orbs)
        return carry

    lax.fori_loop(0, rows // group, one, 0)


def rotated(blocks, q, pieces):
    a = blocks[0]
    size = a.size
    group = max(g for g in range(1, 9) if a.shape[1] % g == 0)
    out = jax.ShapeDtypeStruct((a.shape[0] // pieces, *a.shape[1:]), BF16)
    return pl.pallas_call(
        functools.partial(rotate_kernel, group),
        out_shape=(out,) * pieces,
        in_specs=[pl.BlockSpec(memory_space=pltpu.VMEM)] * 5,
        out_specs=(pl.BlockSpec(memory_space=pltpu.VMEM),) * pieces,
        compiler_params=params(),
        cost_estimate=cost(8 * size * a.shape[3], 10 * size),
        name="rotated",
    )(*blocks, q)


def assemble_kernel(group, term, keep1, got1, a, b, c, d, q, out):
    half = term.shape[1] // 2
    width, orbs = term.shape[2:]
    x = lax.rem(lax.axis_index("space"), 2)
    rows1, rows2 = keep1.shape[1], a.shape[1]
    for ref, at in ((keep1, half * x), (got1, half * (1 - x))):
        where = pl.ds(at, ref.shape[1])
        out[:, where] = (ref[...].astype(F32) + term[:, where]).astype(BF16)
    low = jnp.concatenate([q[0], q[1]], axis=0)
    high = jnp.concatenate([q[2], q[3]], axis=0)

    def one(j, carry):
        where = pl.ds(half * x + rows1 + group * j, group)
        for plane in range(a.shape[0]):
            def take(ref):
                return ref[plane, pl.ds(group * j, group)].reshape(group * width, orbs)

            total = jnp.dot(
                jnp.concatenate([take(a), take(b)], axis=1), low, preferred_element_type=F32
            )
            total = total + jnp.dot(
                jnp.concatenate([take(c), take(d)], axis=1), high, preferred_element_type=F32
            )
            total = total.reshape(group, width, orbs) + term[plane, where]
            out[plane, where] = total.astype(BF16)
        return carry

    lax.fori_loop(0, rows2 // group, one, 0)


def finish_kernel(rows1, term, got2, before, out, rows, sem):
    half = term.shape[1] // 2
    x = lax.rem(lax.axis_index("space"), 2)
    where = pl.ds(half * (1 - x) + rows1, got2.shape[1])
    rows[...] = (got2[...].astype(F32) + term[:, where]).astype(BF16)
    copy = pltpu.make_async_copy(rows, out.at[:, where], sem)
    copy.start()
    copy.wait()


def assembled(term, keep1, got1, got2, blocks, q):
    group = max(g for g in range(1, 9) if got2.shape[1] % g == 0)
    most = pl.pallas_call(
        functools.partial(assemble_kernel, group),
        out_shape=jax.ShapeDtypeStruct(term.shape, BF16),
        in_specs=[pl.BlockSpec(memory_space=pltpu.VMEM)] * 8,
        out_specs=pl.BlockSpec(memory_space=pltpu.VMEM),
        compiler_params=params(),
        cost_estimate=cost(4096, 4096),
        name="assembled",
    )(term, keep1, got1, *blocks, q)
    local = pl.BlockSpec(memory_space=pltpu.VMEM)
    distant = pl.BlockSpec(memory_space=pltpu.MemorySpace.HBM)
    return pl.pallas_call(
        functools.partial(finish_kernel, keep1.shape[1]),
        out_shape=jax.ShapeDtypeStruct(term.shape, BF16),
        in_specs=[local, local, distant],
        out_specs=distant,
        input_output_aliases={2: 0},
        scratch_shapes=[pltpu.VMEM(got2.shape, BF16), pltpu.SemaphoreType.DMA],
        compiler_params=params(),
        cost_estimate=cost(4096, 4096),
        name="finished",
    )(term, got2, pltpu.with_memory_space_constraint(most, pltpu.MemorySpace.HBM))


def ordered(*arrays):
    return lax.optimization_barrier(arrays)


def shards(psi, potential, beta, strength, atom_slab, pattern, q_tiles):
    planes, width_x, width_y, orbs = psi.shape
    count = beta.shape[0]
    slabs = lax.axis_size("space")
    place = lax.axis_index("space")
    x = lax.rem(place, 2)
    half = width_x // 2
    window = half + 2
    rows1 = half // 4 * 2
    rows2 = half - rows1
    early = rows1 + 4

    def within(pairs):
        return [(i, j) for i, j in pairs if 0 <= j < slabs]

    swap = [(i, i ^ 1) for i in range(slabs)]
    own_way = within([(i, i + 2 if i % 2 else i - 2) for i in range(slabs)])
    other_way = within([(i, i - 2 if i % 2 else i + 2) for i in range(slabs)])
    groups = lax.axis_size("orb")
    across = [(i, i ^ 2) for i in range(groups)]
    beside = [(i, i ^ 1) for i in range(groups)]
    mine = (half - 2) * x
    theirs = (half - 2) * (1 - x)

    to_x, to_z = prepared(psi, potential, early)
    to_x2, far, near = packed(psi, beta, early)
    f_x = lax.ppermute(near, "space", swap)
    raster = within([(i, i + 1 if i % 2 else i - 1) for i in range(slabs)])
    f_d = lax.ppermute(far, "space", raster)
    xr1 = lax.ppermute(to_x, "space", swap)
    zo = lax.ppermute(to_z, "space", own_way)
    active = jnp.abs(place - atom_slab) <= 1
    beta_m = jnp.where(active[:, None, None, None], beta, jnp.zeros_like(beta))
    gram = jnp.einsum("pzxy,qzxy->pq", beta_m, beta_m, preferred_element_type=F32)
    xr1, second = ordered(xr1, to_x2)
    zf1 = lax.ppermute(xr1, "space", other_way)
    xr2 = lax.ppermute(second, "space", swap)
    zf2 = lax.ppermute(xr2, "space", other_way)
    strong = jnp.broadcast_to(strength[:, None], (count, orbs))

    sums, weights = partials(count, atom_slab, psi, beta, f_x, f_d, potential, gram)
    zf1, sums, _ = ordered(zf1, sums, xr2)
    operands = (psi, potential, zo)
    (block1,) = filtered(slabs, 0, rows1, True, operands, (xr1,), (zf1,))
    y1 = lax.ppermute(block1, "orb", across)
    rounds = [1 << k for k in range((slabs - 1).bit_length())]

    def added(values, step):
        pairs = [(i, i ^ step) for i in range(slabs)]
        return values + lax.ppermute(values, "space", pairs)

    for step in rounds[:1]:
        sums = added(sums, step)
    zf2, sums = ordered(zf2, sums)
    give2, keep2 = filtered(slabs, rows1, rows2, False, operands, (xr1, xr2), (zf1, zf2))
    pattern, q_tiles, _ = ordered(pattern, q_tiles, give2)
    me = lax.axis_index("orb")
    which = jnp.bitwise_xor(me, jnp.arange(groups, dtype=jnp.int32))
    rows_hot = (pattern[:, 0][:, None] == which[None, :]).astype(BF16)
    rows_hot = rows_hot * (pattern[:, 1] == me).astype(BF16)[:, None]
    q = jnp.einsum("ki,kab->iab", rows_hot, q_tiles, preferred_element_type=F32).astype(BF16)
    cg = lax.ppermute(give2, "orb", beside)
    ck = lax.ppermute(keep2, "orb", beside)
    yg = lax.ppermute(give2, "orb", across)
    for step in rounds[1:2]:
        sums = added(sums, step)
    y1, again, _, sums = ordered(y1, block1, give2, sums)
    c1 = lax.ppermute(again, "orb", beside)
    yc1 = lax.ppermute(y1, "orb", beside)
    for step in rounds[2:]:
        sums = added(sums, step)
    yc1, sums = ordered(yc1, sums)
    give1, keep1 = rotated((block1, c1, y1, yc1), q, 2)
    got1 = lax.ppermute(give1, "space", swap)
    keep_y, yg, _, sums = ordered(keep2, yg, give1, sums)
    yk = lax.ppermute(keep_y, "orb", across)
    ycg = lax.ppermute(yg, "orb", beside)
    coefs = coefficients(sums, strong)
    coefs = jnp.concatenate([coefs, lax.ppermute(coefs, "orb", beside)], axis=0)
    ycg, coefs = ordered(ycg, coefs)
    (give2,) = rotated((give2, cg, yg, ycg), q, 1)
    got2 = lax.ppermute(give2, "space", swap)
    coefs, _ = ordered(coefs, give2)
    coefs_y = lax.ppermute(coefs, "orb", across)
    coefs = [half_of[k * 2 * count : (k + 1) * 2 * count] for half_of in (coefs, coefs_y) for k in (0, 1)]
    term = nonlocal_term(psi.shape, coefs, q, weights)
    yk, _, got1 = ordered(yk, give2, got1)
    yck = lax.ppermute(yk, "orb", beside)
    return assembled(term, keep1, got1, got2, (keep2, ck, yk, yck), q)


def solution(mesh):
    placed = (
        P("space", None, None, "orb"),
        P("space", None, None),
        P(None, "space", None, None),
        P(),
        P(),
        P(),
        P(),
    )
    return jax.shard_map(
        shards, mesh=mesh, in_specs=placed, out_specs=P("space", None, None, "orb"), check_vma=False
    )
```

```python
import functools

import jax
import jax.numpy as jnp
from jax import lax
from jax.experimental import pallas as pl
from jax.experimental.pallas import tpu as pltpu
from jax.sharding import PartitionSpec as P

F32 = jnp.float32
BF16 = jnp.bfloat16
VMEM_LIMIT = 24 * 1024 * 1024
SHRINK = 16
FILTER = 100


def params():
    return pltpu.CompilerParams(vmem_limit_bytes=VMEM_LIMIT)


def cost(flops, moved):
    return pl.CostEstimate(flops=flops // SHRINK, bytes_accessed=moved // SHRINK, transcendentals=0)


def inside(p, window):
    return jnp.logical_and(p >= 0, p < window).astype(F32)


def neighbour_sum(width, pairs):
    n = (2 if pairs else 1) * width
    i = lax.broadcasted_iota(jnp.int32, (n, n), 0)
    j = lax.broadcasted_iota(jnp.int32, (n, n), 1)
    linked = jnp.abs(i - j) == 1
    if pairs:
        linked = jnp.logical_and(linked, (i < width) == (j < width))
        linked = jnp.logical_or(linked, jnp.abs(i - j) == width)
    return jnp.where(linked, -0.125, 0.0)


def potential_block(potential):
    lines, width = potential.shape
    gap = jnp.zeros((lines, 64 - width), F32)
    u = (potential - 1.0) * 0.25
    hi = u.astype(BF16).astype(F32)
    return jnp.concatenate([hi, gap, u - hi, gap], axis=1)


def prepare_kernel(early, psi, potential_far, to_x, to_z, potential, sems):
    x = lax.rem(lax.axis_index("space"), 2)
    half = psi.shape[1] // 2
    window = half + 2
    mine, theirs = (half - 2) * x, (half - 2) * (1 - x)
    fetch = pltpu.make_async_copy(potential_far, potential, sems.at[0])
    fetch.start()
    copies = [
        pltpu.make_async_copy(
            psi.at[:, pl.ds(theirs, early)], to_x.at[:, pl.ds(0, early)], sems.at[1]
        ),
        pltpu.make_async_copy(
            psi.at[:, pl.ds(mine, window)], to_z.at[:, pl.ds(0, window)], sems.at[2]
        ),
    ]
    for copy in copies:
        copy.start()
    fetch.wait()
    for plane in range(potential.shape[0]):
        block = potential_block(potential[plane]).astype(BF16)
        to_x[plane, early] = block
        to_z[plane, window] = block
    for copy in copies:
        copy.wait()


def prepared(psi, potential, early):
    planes, width_x, width_y, orbs = psi.shape
    window = width_x // 2 + 2

    def out(rows):
        return jax.ShapeDtypeStruct((planes, rows, width_y, orbs), BF16)

    return pl.pallas_call(
        functools.partial(prepare_kernel, early),
        out_shape=(out(early + 1), out(window + 1)),
        in_specs=[pl.BlockSpec(memory_space=pltpu.MemorySpace.HBM)] * 2,
        out_specs=(pl.BlockSpec(memory_space=pltpu.VMEM),) * 2,
        scratch_shapes=[pltpu.VMEM(potential.shape, F32), pltpu.SemaphoreType.DMA((3,))],
        compiler_params=params(),
        cost_estimate=cost(4096, 4096),
        name="prepared",
    )(*(pltpu.with_memory_space_constraint(a, pltpu.MemorySpace.HBM) for a in (psi, potential)))


def pack_kernel(early, psi, beta, to_x2, far, near, sems):
    x = lax.rem(lax.axis_index("space"), 2)
    half = psi.shape[1] // 2
    later = half + 2 - early
    copies = [
        pltpu.make_async_copy(beta.at[:, 1 - x], near, sems.at[0]),
        pltpu.make_async_copy(beta.at[:, x], far, sems.at[1]),
        pltpu.make_async_copy(
            psi.at[:, pl.ds((half - 2) * (1 - x) + early, later)], to_x2, sems.at[2]
        ),
    ]
    for copy in copies:
        copy.start()
    for copy in copies:
        copy.wait()


def packed(psi, beta, early):
    planes, width_x, width_y, orbs = psi.shape
    side = jax.ShapeDtypeStruct((beta.shape[0], *beta.shape[2:]), BF16)
    later = width_x // 2 + 2 - early
    return pl.pallas_call(
        functools.partial(pack_kernel, early),
        out_shape=(jax.ShapeDtypeStruct((planes, later, width_y, orbs), BF16), side, side),
        in_specs=[pl.BlockSpec(memory_space=pltpu.MemorySpace.HBM)] * 2,
        out_specs=(pl.BlockSpec(memory_space=pltpu.VMEM),) * 3,
        scratch_shapes=[pltpu.SemaphoreType.DMA((3,))],
        compiler_params=params(),
        cost_estimate=cost(4096, 4096),
        name="packed",
    )(*(pltpu.with_memory_space_constraint(a, pltpu.MemorySpace.HBM) for a in (psi, beta)))


def partial_kernel(count, atoms, own, beta, b_x, b_d, potential, gram, out, weights_out, table, acc):
    place = lax.axis_index("space")
    x = lax.rem(place, 2)
    rows, width = potential.shape[1:]
    side = place ^ 1
    beyond = place - 1 + 2 * x
    tri = neighbour_sum(width, False).astype(BF16)
    acc[...] = jnp.zeros_like(acc)
    step = 8

    for k in range(2):
        plane = x if k == 0 else 1 - x
        outer, there = (b_d, beyond) if k == 0 else (b_x, side)
        u = (potential[plane] - 1.0) * 0.25

        def fill(i, carry):
            for j in range(step):
                p = i * step + j
                here = (jnp.abs(place - atoms[p]) <= 1).astype(F32)
                next_to = (jnp.abs(there - atoms[p]) <= 1).astype(F32)
                b32 = beta[p, plane].astype(F32) * here
                b = b32.astype(BF16)
                sides = beta[p, 1 - plane].astype(F32) * here + outer[p].astype(F32) * next_to
                whole = jnp.dot(b, tri, preferred_element_type=F32)
                whole = whole + jnp.dot(tri, b, preferred_element_type=F32)
                whole = whole + u * b32 - 0.125 * sides
                hi = whole.astype(BF16).astype(F32)
                for kind, value in enumerate((b32, hi, whole - hi)):
                    table[pl.ds((kind * count + p) * rows, rows)] = value
            return carry

        lax.fori_loop(0, count // step, fill, 0)

        def use(i, carry):
            totals = []
            for j in range(step):
                r = i * step + j
                weights = table[pl.ds(r, 3 * count, stride=rows)].astype(BF16)
                weights_out[plane, r] = weights
                totals.append(jnp.dot(weights, own[plane, r], preferred_element_type=F32))
            acc[...] += sum(totals[1:], totals[0])
            return carry

        lax.fori_loop(0, rows // step, use, 0)
    out[...] = jnp.zeros_like(out)
    out[0:count] = acc[0:count]
    out[count : 2 * count] = acc[count : 2 * count] + acc[2 * count : 3 * count]
    out[2 * count : 3 * count, 0:count] = gram[...]


def partials(count, atoms, own, beta, b_x, b_d, potential, gram):
    planes, rows, width, orbs = own.shape
    return pl.pallas_call(
        functools.partial(partial_kernel, count),
        out_shape=(
            jax.ShapeDtypeStruct((3 * count, orbs), F32),
            jax.ShapeDtypeStruct((planes, rows, 3 * count, width), BF16),
        ),
        in_specs=[pl.BlockSpec(memory_space=pltpu.SMEM)]
        + [pl.BlockSpec(memory_space=pltpu.VMEM)] * 6,
        out_specs=(pl.BlockSpec(memory_space=pltpu.VMEM),) * 2,
        scratch_shapes=[
            pltpu.VMEM((3 * count * rows, width), F32),
            pltpu.VMEM((3 * count, orbs), F32),
        ],
        compiler_params=params(),
        cost_estimate=cost(4096, 4096),
        name="partials",
    )(atoms, own, beta, b_x, b_d, potential, gram)


def coefficient_kernel(sums, strength, out):
    count, orbs = strength.shape
    coef1 = (strength[...] * sums[0:count]).astype(BF16)
    padded = coef1.astype(F32) * 0.25
    if orbs > count:
        padded = jnp.concatenate([padded, jnp.zeros((orbs - count, orbs), F32)], axis=0)
    proj2 = sums[count : 2 * count] + jnp.dot(
        sums[2 * count : 3 * count],
        padded,
        preferred_element_type=F32,
        precision=lax.Precision.HIGHEST,
    )
    out[0:count] = coef1
    out[count : 2 * count] = (strength[...] * proj2).astype(BF16)


def coefficients(sums, strength):
    count, orbs = strength.shape
    return pl.pallas_call(
        coefficient_kernel,
        out_shape=jax.ShapeDtypeStruct((2 * count, orbs), BF16),
        in_specs=[pl.BlockSpec(memory_space=pltpu.VMEM)] * 2,
        out_specs=pl.BlockSpec(memory_space=pltpu.VMEM),
        compiler_params=params(),
        cost_estimate=cost(4096, 4096),
        name="coefficients",
    )(sums, strength)


def nonlocal_kernel(unroll, a, b, c, d, q, weights, out):
    count, orbs = a.shape[0] // 2, a.shape[1]
    turned = sum(
        jnp.dot(ref[...], q[k], preferred_element_type=F32) for k, ref in enumerate((a, b, c, d))
    )
    turned = turned * 0.25
    one, two = turned[0:count], turned[count : 2 * count]
    right = jnp.concatenate([two, one, one], axis=0)
    hi = right.astype(BF16)
    lo = right - hi.astype(F32)
    right = jnp.concatenate([hi.astype(F32), lo], axis=1).astype(BF16)

    def step(i, carry):
        for k in range(unroll):
            r = i * unroll + k
            for plane in range(weights.shape[0]):
                both = lax.dot_general(
                    weights[plane, r], right, (((0,), (0,)), ((), ())), preferred_element_type=F32
                )
                out[plane, r] = both[:, :orbs] + both[:, orbs:]
        return carry

    lax.fori_loop(0, weights.shape[1] // unroll, step, 0)


def nonlocal_term(shape, coefs, q, weights):
    unroll = max(g for g in (1, 2, 4, 8) if weights.shape[1] % g == 0)
    return pl.pallas_call(
        functools.partial(nonlocal_kernel, unroll),
        out_shape=jax.ShapeDtypeStruct(shape, F32),
        in_specs=[pl.BlockSpec(memory_space=pltpu.VMEM)] * 6,
        out_specs=pl.BlockSpec(memory_space=pltpu.VMEM),
        compiler_params=params(),
        cost_estimate=cost(4096, 4096),
        name="nonlocal",
    )(*coefs, q, weights)


def filter_kernel(slabs, start, parts, joint, *refs):
    own, p_own, zo = refs[:3]
    xrs, zfs = refs[3 : 3 + parts], refs[3 + parts : 3 + 2 * parts]
    extra = 7
    outs, scratch = refs[3 + 2 * parts : -extra], refs[-extra:]
    first, lines, diagonals = scratch[:3]
    place = lax.axis_index("space")
    x = lax.rem(place, 2)
    width = own.shape[2]
    cells = 2 * width
    half = own.shape[1] // 2
    orbs = own.shape[3]
    rows = outs[0].shape[1]
    base = (half - 2) * x
    lower = (place >= 2).astype(F32)
    upper = (place < slabs - 2).astype(F32)
    is_odd = x.astype(F32)
    has_zf = lower * (1.0 - is_odd) + upper * is_odd
    has_zo = upper * (1.0 - is_odd) + lower * is_odd
    xr, zf, pots, sems = scratch[3:]
    window = xr.shape[1] // 2
    early = xrs[0].shape[1] - 1
    copies = []
    for k, (target, pieces) in enumerate(((xr, xrs), (zf, zfs))):
        if parts == 1 and k == 1:
            zf = pieces[0]
            continue
        begin = 0 if parts == 1 else early - 8
        moved = [
            (pieces[0].at[:, pl.ds(early, 1)], pots.at[k]),
            (
                pieces[0].at[:, pl.ds(begin, early - begin)],
                target.at[:, pl.ds(begin, early - begin)],
            ),
        ]
        if parts > 1:
            later = target.shape[1] - early
            moved.append((pieces[1].at[:, pl.ds(0, later)], target.at[:, pl.ds(early, later)]))
        copies += [
            pltpu.make_async_copy(source, goal, sems.at[3 * k + i])
            for i, (source, goal) in enumerate(moved)
        ]
    for copy in copies:
        copy.start()

    def fill(c, block):
        lines[c - 1] = block
        even, odd = (lines[c - 1, pl.ds(k, half, stride=2)] for k in range(2))
        whole = [a[:, :width] + a[:, 64 : 64 + width] for a in (even, odd)]
        diagonals[c - 1] = jnp.concatenate(whole, axis=1)

    for c in (2, 3):
        fill(c, potential_block(p_own[(c % 2) ^ x]))
    fill(6, zo[x, zo.shape[1] - 1].astype(F32))
    for copy in copies:
        copy.wait()
    for c in (1, 4, 5):
        if parts == 1 and c == 1:
            fill(c, zf[(c % 2) ^ x, early].astype(F32))
        else:
            fill(c, pots[1 if c < 2 else 0, (c % 2) ^ x, 0].astype(F32))

    here = neighbour_sum(width, True)
    i = lax.broadcasted_iota(jnp.int32, (cells, cells), 0)
    diagonal = i == lax.broadcasted_iota(jnp.int32, (cells, cells), 1)

    def local(c, p):
        u = diagonals[c - 1, pl.ds(base // 2 + p, 1)]
        return jnp.where(diagonal, u, here).astype(BF16)

    def rows_of(c, w, n):
        plane = (c % 2) ^ x
        if c in (2, 3):
            return own[plane, pl.ds(base + w, n)]
        ref = zf if c < 2 else (xr if c < 6 else zo)
        return ref[plane, pl.ds(w, n)]

    def applied(pair, outer, zs, matrix):
        near = jnp.dot(matrix, pair, preferred_element_type=F32)
        return near - 0.125 * (outer + zs)

    def step1(j, carry):
        p = start // 2 + x + j - 1
        q = jnp.clip(p, 0, window - 1)
        has_below = inside(p - 1, window)
        has_above = inside(p + 1, window)
        valid = inside(p, window)
        below = jnp.maximum(2 * q - 1, 0)
        above = jnp.minimum(2 * q + 2, 2 * window - 1)
        pair = [rows_of(c, 2 * q, 2).reshape(cells, orbs) for c in range(8)]
        vs = [v.astype(F32) for v in pair]
        for c in range(1, 7):
            outer = jnp.concatenate(
                [
                    rows_of(c, below, 1)[0].astype(F32) * has_below,
                    rows_of(c, above, 1)[0].astype(F32) * has_above,
                ],
                axis=0,
            )
            f = applied(pair[c], outer, vs[c - 1] + vs[c + 1], local(c, q))
            keep = valid
            if c == 1:
                keep = valid * has_zf
            if c == 6:
                keep = valid * has_zo
            first[c - 1, pl.ds(2 * j, 2)] = (f * keep).astype(BF16).reshape(2, width, orbs)
        return carry

    lax.fori_loop(0, rows // 2 + 2, step1, 0)

    def step2(j, carry):
        p = start // 2 + x + j
        pair = [first[c - 1, pl.ds(2 * j + 2, 2)].reshape(cells, orbs) for c in range(1, 7)]
        vs = [v.astype(F32) for v in pair]
        for c in range(2, 6):
            outer = jnp.concatenate(
                [first[c - 1, 2 * j + 1].astype(F32), first[c - 1, 2 * j + 4].astype(F32)], axis=0
            )
            f = applied(pair[c - 1], outer, vs[c - 2] + vs[c], local(c, p))
            f = f.astype(BF16).reshape(2, width, orbs)
            plane = (c % 2) ^ x
            if joint:
                outs[0][plane + (2 if c in (2, 3) else 0), pl.ds(2 * j, 2)] = f
            else:
                outs[1 if c in (2, 3) else 0][plane, pl.ds(2 * j, 2)] = f
        return carry

    lax.fori_loop(0, rows // 2, step2, 0)


def filtered(slabs, start, rows, joint, operands, xrs, zfs):
    own = operands[0]
    planes, _, width, orbs = own.shape
    parts = len(xrs)
    shape = (2 * planes if joint else planes, rows, width, orbs)
    out = (jax.ShapeDtypeStruct(shape, BF16),) * (1 if joint else 2)
    cells = 10 * rows * width
    scratch = [
        pltpu.VMEM((6, rows + 4, width, orbs), BF16),
        pltpu.VMEM((6, width, orbs), F32),
        pltpu.VMEM((6, own.shape[1] // 2, 2 * width), F32),
    ]
    window = own.shape[1] // 2 + 2 if parts > 1 else xrs[0].shape[1] - 1
    scratch += [pltpu.VMEM((planes, window, width, orbs), BF16)] * 2
    scratch += [pltpu.VMEM((2, planes, 1, width, orbs), BF16), pltpu.SemaphoreType.DMA((6,))]
    local = pl.BlockSpec(memory_space=pltpu.VMEM)
    distant = pl.BlockSpec(memory_space=pltpu.MemorySpace.HBM)
    far_xr = [pltpu.with_memory_space_constraint(a, pltpu.MemorySpace.HBM) for a in xrs]
    far_zf = [pltpu.with_memory_space_constraint(a, pltpu.MemorySpace.HBM) for a in zfs]
    xrs, zfs = far_xr, (far_zf if parts > 1 else zfs)
    return pl.pallas_call(
        functools.partial(filter_kernel, slabs, start, parts, joint),
        out_shape=out,
        in_specs=[local] * len(operands)
        + [distant] * parts
        + [distant if parts > 1 else local] * parts,
        out_specs=(local,) * len(out),
        scratch_shapes=scratch,
        compiler_params=params(),
        cost_estimate=cost(2 * cells * 32 * orbs, FILTER * cells * orbs * 4),
        name="filtered",
    )(*operands, *xrs, *zfs)


def rotate_kernel(group, *refs):
    a, b, c, d, q = refs[:5]
    outs = refs[5:]
    _, rows, width, orbs = a.shape
    planes = outs[0].shape[0]
    low = jnp.concatenate([q[0], q[1]], axis=0)
    high = jnp.concatenate([q[2], q[3]], axis=0)

    def one(j, carry):
        for plane in range(a.shape[0]):
            def take(ref):
                return ref[plane, pl.ds(group * j, group)].reshape(group * width, orbs)

            total = jnp.dot(
                jnp.concatenate([take(a), take(b)], axis=1), low, preferred_element_type=F32
            )
            total = total + jnp.dot(
                jnp.concatenate([take(c), take(d)], axis=1), high, preferred_element_type=F32
            )
            outs[plane // planes][plane % planes, pl.ds(group * j, group)] = total.astype(
                BF16
            ).reshape(group, width, orbs)
        return carry

    lax.fori_loop(0, rows // group, one, 0)


def rotated(blocks, q, pieces):
    a = blocks[0]
    size = a.size
    group = max(g for g in range(1, 9) if a.shape[1] % g == 0)
    out = jax.ShapeDtypeStruct((a.shape[0] // pieces, *a.shape[1:]), BF16)
    return pl.pallas_call(
        functools.partial(rotate_kernel, group),
        out_shape=(out,) * pieces,
        in_specs=[pl.BlockSpec(memory_space=pltpu.VMEM)] * 5,
        out_specs=(pl.BlockSpec(memory_space=pltpu.VMEM),) * pieces,
        compiler_params=params(),
        cost_estimate=cost(8 * size * a.shape[3], 10 * size),
        name="rotated",
    )(*blocks, q)


def assemble_kernel(group, term, keep1, got1, a, b, c, d, q, out):
    half = term.shape[1] // 2
    width, orbs = term.shape[2:]
    x = lax.rem(lax.axis_index("space"), 2)
    rows1, rows2 = keep1.shape[1], a.shape[1]
    for ref, at in ((keep1, half * x), (got1, half * (1 - x))):
        where = pl.ds(at, ref.shape[1])
        out[:, where] = (ref[...].astype(F32) + term[:, where]).astype(BF16)
    low = jnp.concatenate([q[0], q[1]], axis=0)
    high = jnp.concatenate([q[2], q[3]], axis=0)

    def one(j, carry):
        where = pl.ds(half * x + rows1 + group * j, group)
        for plane in range(a.shape[0]):
            def take(ref):
                return ref[plane, pl.ds(group * j, group)].reshape(group * width, orbs)

            total = jnp.dot(
                jnp.concatenate([take(a), take(b)], axis=1), low, preferred_element_type=F32
            )
            total = total + jnp.dot(
                jnp.concatenate([take(c), take(d)], axis=1), high, preferred_element_type=F32
            )
            total = total.reshape(group, width, orbs) + term[plane, where]
            out[plane, where] = total.astype(BF16)
        return carry

    lax.fori_loop(0, rows2 // group, one, 0)


def finish_kernel(rows1, term, got2, before, out, rows, sem):
    half = term.shape[1] // 2
    x = lax.rem(lax.axis_index("space"), 2)
    where = pl.ds(half * (1 - x) + rows1, got2.shape[1])
    rows[...] = (got2[...].astype(F32) + term[:, where]).astype(BF16)
    copy = pltpu.make_async_copy(rows, out.at[:, where], sem)
    copy.start()
    copy.wait()


def assembled(term, keep1, got1, got2, blocks, q):
    group = max(g for g in range(1, 9) if got2.shape[1] % g == 0)
    most = pl.pallas_call(
        functools.partial(assemble_kernel, group),
        out_shape=jax.ShapeDtypeStruct(term.shape, BF16),
        in_specs=[pl.BlockSpec(memory_space=pltpu.VMEM)] * 8,
        out_specs=pl.BlockSpec(memory_space=pltpu.VMEM),
        compiler_params=params(),
        cost_estimate=cost(4096, 4096),
        name="assembled",
    )(term, keep1, got1, *blocks, q)
    local = pl.BlockSpec(memory_space=pltpu.VMEM)
    distant = pl.BlockSpec(memory_space=pltpu.MemorySpace.HBM)
    return pl.pallas_call(
        functools.partial(finish_kernel, keep1.shape[1]),
        out_shape=jax.ShapeDtypeStruct(term.shape, BF16),
        in_specs=[local, local, distant],
        out_specs=distant,
        input_output_aliases={2: 0},
        scratch_shapes=[pltpu.VMEM(got2.shape, BF16), pltpu.SemaphoreType.DMA],
        compiler_params=params(),
        cost_estimate=cost(4096, 4096),
        name="finished",
    )(term, got2, pltpu.with_memory_space_constraint(most, pltpu.MemorySpace.HBM))


def ordered(*arrays):
    return lax.optimization_barrier(arrays)


def shards(psi, potential, beta, strength, atom_slab, pattern, q_tiles):
    planes, width_x, width_y, orbs = psi.shape
    count = beta.shape[0]
    slabs = lax.axis_size("space")
    place = lax.axis_index("space")
    x = lax.rem(place, 2)
    half = width_x // 2
    window = half + 2
    rows1 = half * 8 // 24 * 2
    rows2 = half - rows1
    early = rows1 + 4

    def within(pairs):
        return [(i, j) for i, j in pairs if 0 <= j < slabs]

    swap = [(i, i ^ 1) for i in range(slabs)]
    own_way = within([(i, i + 2 if i % 2 else i - 2) for i in range(slabs)])
    other_way = within([(i, i - 2 if i % 2 else i + 2) for i in range(slabs)])
    groups = lax.axis_size("orb")
    across = [(i, i ^ 2) for i in range(groups)]
    beside = [(i, i ^ 1) for i in range(groups)]
    mine = (half - 2) * x
    theirs = (half - 2) * (1 - x)

    to_x, to_z = prepared(psi, potential, early)
    to_x2, far, near = packed(psi, beta, early)
    f_x = lax.ppermute(near, "space", swap)
    raster = within([(i, i + 1 if i % 2 else i - 1) for i in range(slabs)])
    f_d = lax.ppermute(far, "space", raster)
    xr1 = lax.ppermute(to_x, "space", swap)
    zo = lax.ppermute(to_z, "space", own_way)
    active = jnp.abs(place - atom_slab) <= 1
    beta_m = jnp.where(active[:, None, None, None], beta, jnp.zeros_like(beta))
    gram = jnp.einsum("pzxy,qzxy->pq", beta_m, beta_m, preferred_element_type=F32)
    xr1, second = ordered(xr1, to_x2)
    zf1 = lax.ppermute(xr1, "space", other_way)
    xr2 = lax.ppermute(second, "space", swap)
    zf2 = lax.ppermute(xr2, "space", other_way)
    strong = jnp.broadcast_to(strength[:, None], (count, orbs))

    sums, weights = partials(count, atom_slab, psi, beta, f_x, f_d, potential, gram)
    zf1, sums, _ = ordered(zf1, sums, xr2)
    operands = (psi, potential, zo)
    (block1,) = filtered(slabs, 0, rows1, True, operands, (xr1,), (zf1,))
    y1 = lax.ppermute(block1, "orb", across)
    rounds = [1 << k for k in range((slabs - 1).bit_length())]

    def added(values, step):
        pairs = [(i, i ^ step) for i in range(slabs)]
        return values + lax.ppermute(values, "space", pairs)

    for step in rounds[:1]:
        sums = added(sums, step)
    zf2, sums = ordered(zf2, sums)
    give2, keep2 = filtered(slabs, rows1, rows2, False, operands, (xr1, xr2), (zf1, zf2))
    pattern, q_tiles, _ = ordered(pattern, q_tiles, give2)
    me = lax.axis_index("orb")
    which = jnp.bitwise_xor(me, jnp.arange(groups, dtype=jnp.int32))
    rows_hot = (pattern[:, 0][:, None] == which[None, :]).astype(BF16)
    rows_hot = rows_hot * (pattern[:, 1] == me).astype(BF16)[:, None]
    q = jnp.einsum("ki,kab->iab", rows_hot, q_tiles, preferred_element_type=F32).astype(BF16)
    cg = lax.ppermute(give2, "orb", beside)
    ck = lax.ppermute(keep2, "orb", beside)
    yg = lax.ppermute(give2, "orb", across)
    for step in rounds[1:2]:
        sums = added(sums, step)
    y1, again, _, sums = ordered(y1, block1, give2, sums)
    c1 = lax.ppermute(again, "orb", beside)
    yc1 = lax.ppermute(y1, "orb", beside)
    for step in rounds[2:]:
        sums = added(sums, step)
    yc1, sums = ordered(yc1, sums)
    give1, keep1 = rotated((block1, c1, y1, yc1), q, 2)
    got1 = lax.ppermute(give1, "space", swap)
    keep_y, yg, _, sums = ordered(keep2, yg, give1, sums)
    yk = lax.ppermute(keep_y, "orb", across)
    ycg = lax.ppermute(yg, "orb", beside)
    coefs = coefficients(sums, strong)
    coefs = jnp.concatenate([coefs, lax.ppermute(coefs, "orb", beside)], axis=0)
    ycg, coefs = ordered(ycg, coefs)
    (give2,) = rotated((give2, cg, yg, ycg), q, 1)
    got2 = lax.ppermute(give2, "space", swap)
    coefs, _ = ordered(coefs, give2)
    coefs_y = lax.ppermute(coefs, "orb", across)
    coefs = [half_of[k * 2 * count : (k + 1) * 2 * count] for half_of in (coefs, coefs_y) for k in (0, 1)]
    term = nonlocal_term(psi.shape, coefs, q, weights)
    yk, _, got1 = ordered(yk, give2, got1)
    yck = lax.ppermute(yk, "orb", beside)
    return assembled(term, keep1, got1, got2, (keep2, ck, yk, yck), q)


def solution(mesh):
    placed = (
        P("space", None, None, "orb"),
        P("space", None, None),
        P(None, "space", None, None),
        P(),
        P(),
        P(),
        P(),
    )
    return jax.shard_map(
        shards, mesh=mesh, in_specs=placed, out_specs=P("space", None, None, "orb"), check_vma=False
    )
```
